128 devices in a mesh: grp: 4 (over y), dev: 32 (over x, z, core).
Axes of the slice: x: 4, y: 4, z: 4, core: 2. Of those that a mesh axis runs over, the one named last changes fastest.
Arguments:
- codes: int32 [12288, 32], P(('grp', 'dev')), may hold values from 0 to 2047
- code_table: bfloat16 [16384, 512], replicated, may hold values from -2.09375 to 2.09375
- roster: int32 [12288], P(('grp', 'dev')), may hold values from 0 to 12287, as said below
- old_slot: int32 [12288], P(('grp', 'dev')), may hold values from 0 to 12287, as said below
- states: float32 [12288, 10, 512], P(('grp', 'dev')), may hold values from -6 to 6
- up_weight: float32 [4, 512], replicated, may hold values from -3 to 3
- up_bias: float32 [512], replicated, may hold values from -2.5 to 2.5
- conv_weight: bfloat16 [7, 512, 512], replicated, may hold values from -0.09375 to 0.09375
- conv_bias: float32 [512], replicated, may hold values from -2.5 to 2.5
- res_in_weight: bfloat16 [3, 512, 256], replicated, may hold values from -0.15625 to 0.15625
- res_in_bias: float32 [256], replicated, may hold values from -2.5 to 2.5
- res_out_weight: bfloat16 [256, 512], replicated, may hold values from -0.375 to 0.375
- res_out_bias: float32 [512], replicated, may hold values from -2.5 to 2.5
Outputs:
- decoded: bfloat16 [12288, 8, 512], P(('grp', 'dev'))
- new_states: float32 [12288, 10, 512], P(('grp', 'dev'))
The draws below stay inside these ranges and needn't reach their ends.
Inputs may be any that keep to these rules, and one draw needn't show every extreme that they name: roster is a permutation of the conversations; the 96 slots of each device are its owned conversations. Conversation c is held by language-model device c // 96. At most 2 conversations of one language-model device go to one owner device, and some pair reaches 2 in every draw. old_slot is a permutation of the slots that maps each slot within its group of 32 devices along dev. Exactly 16 slots of every device take a cache from a slot of another device; these are exactly the slots whose caches leave that device. All other slots keep their own cache. At most 1 caches go from one device to one other, and that many in every draw.
All inputs are finite; a program needn't handle non-finite values.
Results may differ from the reference program's by a relative error of at most 0.0085.
Values may be sent and summed in bfloat16 or wider, within the bound.
A program may use at most 128 MiB of HBM per device.

```python
import math
import jax
import jax.numpy as jnp
import numpy as np
from jax import lax

C = 512
HID = 256
Q = 8
CB = 2048
FRAMES = 4
KT = 4
K7 = 7
K3 = 3
SROWS = 10
CONV_DEV = 96
MOVE_MOST = 1
MIGS = 16
MOST = 2
CONV = 12288
N_GRP = 4
N_DEV = 32


def draw_roster(key, part):
    key_heavy, key_order, key_shuffle, key_ties = jax.random.split(key, 4)
    device_total = N_GRP * N_DEV
    slot_total = device_total * MOST
    slot_ids = jnp.arange(slot_total, dtype=jnp.int32)
    heavy = jax.random.randint(key_heavy, (), 0, device_total)
    order = jax.random.permutation(key_order, slot_total).astype(jnp.int32)
    forced = (slot_ids == MOST) | (slot_ids == MOST * (device_total // 2))
    scores = jnp.where(slot_ids // MOST == heavy, slot_ids - 3 * slot_total, jnp.where(forced, slot_ids - 2 * slot_total, order))
    picked = jnp.argsort(scores, stable=True)[:CONV_DEV].astype(jnp.int32)
    shifts = picked // MOST
    shuffle_keys = jax.random.split(key_shuffle, device_total)
    shuffles = jax.vmap(lambda one_key: jax.random.permutation(one_key, CONV_DEV))(shuffle_keys).astype(jnp.int32)
    device_ids = jnp.arange(device_total, dtype=jnp.int32)[:, None]
    owners = ((device_ids + shifts[shuffles]) % device_total).reshape(-1)
    ties = jax.random.permutation(key_ties, CONV).astype(jnp.int32)
    return jnp.argsort(owners * CONV + ties, stable=True).astype(jnp.int32)


def draw_old_slot(key, part):
    key_shift, key_slots = jax.random.split(key, 2)
    distinct = jax.random.permutation(key_shift, N_DEV - 1)[:MIGS // MOVE_MOST].astype(jnp.int32) + 1
    shifts = jnp.repeat(distinct, MOVE_MOST)
    slot_keys = jax.random.split(key_slots, N_GRP * N_DEV)
    orders = jax.vmap(lambda one_key: jax.random.permutation(one_key, CONV_DEV))(slot_keys).astype(jnp.int32)
    moving = orders.reshape(N_GRP, N_DEV, CONV_DEV)[:, :, :MIGS]
    dev_ids = jnp.arange(N_DEV, dtype=jnp.int32)[None, :, None]
    source_dev = jnp.broadcast_to((dev_ids - shifts[None, None, :]) % N_DEV, (N_GRP, N_DEV, MIGS))
    source_row = jnp.take_along_axis(moving, source_dev, axis=1)
    group_ids = jnp.arange(N_GRP, dtype=jnp.int32)[:, None, None]
    source_slot = (group_ids * N_DEV + source_dev) * CONV_DEV + source_row
    target_slot = (group_ids * N_DEV + dev_ids) * CONV_DEV + moving
    identity = jnp.arange(CONV, dtype=jnp.int32)
    return identity.at[target_slot.reshape(-1)].set(source_slot.reshape(-1)).astype(jnp.int32)


def touch_ends(entries, rng, smallest, largest):
    place = [jax.random.randint(jax.random.fold_in(rng, axis), (), 0, length) for axis, length in enumerate(entries.shape)]
    longest = entries.shape.index(max(entries.shape))
    beside = place[:longest] + [(place[longest] + 1) % entries.shape[longest]] + place[longest + 1:]
    return entries.at[tuple(place)].set(smallest).at[tuple(beside)].set(largest)


def shard_levels(rng, dims, pieces, least, largest):
    factor_of = 1.0
    for axis_at, parts in pieces:
        steps = jax.random.uniform(jax.random.fold_in(jax.random.fold_in(rng, 6), axis_at), (parts,), jnp.float32, least / len(pieces), largest / len(pieces))
        factor_of = factor_of * jnp.repeat(jnp.exp(steps), dims[axis_at] // parts).reshape((-1,) + (1,) * (len(dims) - 1 - axis_at))
    return factor_of


def rank_table(amount, slope):
    weights = [(1 << 20) // math.isqrt(rank ** slope) + 1 for rank in range(1, amount + 1)]
    width = 1 + sum(weights) // (1 << 30)
    return np.cumsum(np.array([max(1, weight // width) for weight in weights]))


def ranked_ids(rng, extent, number_of, lean):
    listing = rank_table(number_of, lean)
    ticket = jax.random.randint(jax.random.fold_in(rng, 1), extent, 0, int(listing[number_of - 1]))
    standing = jnp.searchsorted(jnp.asarray(listing, jnp.int32), ticket, side="right")
    return jax.random.permutation(jax.random.fold_in(rng, 2), number_of)[standing].astype(jnp.int32)


def normal_values(key, dims, width, reach, cuts=(), held_as=jnp.bfloat16):
    result = width * jax.random.normal(key, dims, jnp.float32)
    if cuts:
        result = result * shard_levels(key, dims, cuts, -0.22, 0.18)
    return jnp.clip(result, -reach, reach).astype(held_as)


def setup_inputs(seed: int = 0) -> dict:
    key_of = jax.random.split(jax.random.key(seed), 14)
    return {
        "codes": touch_ends(ranked_ids(key_of[0], (CONV, FRAMES * Q), CB, 2), jax.random.fold_in(key_of[0], 3), 0, CB - 1).astype(jnp.int32),
        "code_table": normal_values(key_of[1], (Q * CB, C), 0.35, 2.09375),
        "roster": draw_roster(jax.random.fold_in(key_of[13], 71), 0),
        "old_slot": draw_old_slot(jax.random.fold_in(key_of[13], 71), 0),
        "states": normal_values(key_of[4], (CONV, SROWS, C), 1.0, 6.0, ((0, 128),), jnp.float32),
        "up_weight": normal_values(key_of[5], (KT, C), 0.7, 3.0, (), jnp.float32),
        "up_bias": normal_values(key_of[6], (C,), 0.5, 2.5, (), jnp.float32),
        "conv_weight": normal_values(key_of[7], (K7, C, C), (K7 * C) ** -0.5, 0.09375),
        "conv_bias": normal_values(key_of[8], (C,), 0.5, 2.5, (), jnp.float32),
        "res_in_weight": normal_values(key_of[9], (K3, C, HID), (K3 * C) ** -0.5, 0.15625),
        "res_in_bias": normal_values(key_of[10], (HID,), 0.5, 2.5, (), jnp.float32),
        "res_out_weight": normal_values(key_of[11], (HID, C), HID ** -0.5, 0.375),
        "res_out_bias": normal_values(key_of[12], (C,), 0.5, 2.5, (), jnp.float32),
    }


def embed_codes(codes, code_table):
    row_count = codes.shape[0]
    book_count = codes.shape[1] // FRAMES
    book_size = code_table.shape[0] // book_count
    grouped = codes.reshape(row_count, FRAMES, book_count)
    summed = jnp.zeros((row_count, FRAMES, code_table.shape[1]), jnp.float32)
    for book_index in range(book_count):
        summed = summed + code_table[grouped[:, :, book_index] + book_index * book_size].astype(jnp.float32)
    return summed.astype(jnp.bfloat16)


def decode(routed, carried, up_weight, up_bias, conv_weight, conv_bias, res_in_weight, res_in_bias, res_out_weight, res_out_bias):
    conv_count, frame_count, chan_width = routed.shape
    step_count = 2 * frame_count
    inputs = routed.astype(jnp.float32)
    tap_zero = inputs * up_weight[0]
    tap_one = inputs * up_weight[1]
    tap_two = inputs * up_weight[2]
    tap_three = inputs * up_weight[3]
    early_even = jnp.concatenate([carried[:, 0:1], tap_two[:, :-1]], axis=1)
    early_odd = jnp.concatenate([carried[:, 1:2], tap_three[:, :-1]], axis=1)
    upsampled = jnp.stack([tap_zero + early_even, tap_one + early_odd], axis=2).reshape(conv_count, step_count, chan_width) + up_bias
    history = jnp.concatenate([carried[:, 2:8], upsampled], axis=1).astype(jnp.bfloat16)
    conv_out = jnp.zeros((conv_count * step_count, chan_width), jnp.float32) + conv_bias
    for tap_index in range(7):
        window = history[:, 6 - tap_index:6 - tap_index + step_count].reshape(conv_count * step_count, chan_width)
        conv_out = conv_out + jnp.dot(window, conv_weight[tap_index], preferred_element_type=jnp.float32)
    active = jax.nn.elu(conv_out).reshape(conv_count, step_count, chan_width)
    res_history = jnp.concatenate([carried[:, 8:10], active], axis=1)
    res_rounded = res_history.astype(jnp.bfloat16)
    res_inner = jnp.zeros((conv_count * step_count, res_in_weight.shape[2]), jnp.float32) + res_in_bias
    for tap_index in range(3):
        window = res_rounded[:, 2 - tap_index:2 - tap_index + step_count].reshape(conv_count * step_count, chan_width)
        res_inner = res_inner + jnp.dot(window, res_in_weight[tap_index], preferred_element_type=jnp.float32)
    squeezed = jax.nn.elu(res_inner).astype(jnp.bfloat16)
    summed = conv_out + jnp.dot(squeezed, res_out_weight, preferred_element_type=jnp.float32) + res_out_bias
    decoded = summed.astype(jnp.bfloat16).reshape(conv_count, step_count, chan_width)
    new_states = jnp.concatenate([tap_two[:, -1:], tap_three[:, -1:], history[:, -6:].astype(jnp.float32), res_history[:, -2:]], axis=1)
    return decoded, new_states


def reference(codes, code_table, roster, old_slot, states, up_weight, up_bias, conv_weight, conv_bias, res_in_weight, res_in_bias, res_out_weight, res_out_bias):
    embedded = embed_codes(codes, code_table)
    routed = embedded[roster]
    carried = states[old_slot]
    blocks = N_GRP * N_DEV

    def decode_block(pair):
        return decode(pair[0], pair[1], up_weight, up_bias, conv_weight, conv_bias, res_in_weight, res_in_bias, res_out_weight, res_out_bias)

    decoded, new_states = lax.map(decode_block, (routed.reshape(blocks, CONV_DEV, FRAMES, C), carried.reshape(blocks, CONV_DEV, SROWS, C)))
    return decoded.reshape(CONV, 2 * FRAMES, C), new_states.reshape(CONV, SROWS, C)
```

```python
import jax
import jax.numpy as jnp
from jax import lax
from jax.sharding import PartitionSpec as P

FRAMES = 4
MOST = 2


def embed_codes(codes, code_table):
    row_count = codes.shape[0]
    book_count = codes.shape[1] // FRAMES
    book_size = code_table.shape[0] // book_count
    grouped = codes.reshape(row_count * FRAMES, book_count)
    entries = jnp.arange(book_size, dtype=jnp.int32)
    summed = jnp.zeros((row_count * FRAMES, code_table.shape[1]), jnp.float32)
    for book_index in range(book_count):
        onehot = (grouped[:, book_index][:, None] == entries[None, :]).astype(jnp.bfloat16)
        book_rows = code_table[book_index * book_size : (book_index + 1) * book_size]
        summed = summed + jnp.dot(onehot, book_rows, preferred_element_type=jnp.float32)
    return summed.astype(jnp.bfloat16).reshape(row_count, FRAMES, code_table.shape[1])


def pick_rows(table, index, live):
    entries = jnp.arange(table.shape[0], dtype=jnp.int32)
    select = (index[:, None] == entries[None, :]) & live[:, None]
    if table.dtype == jnp.bfloat16:
        return jnp.dot(
            select.astype(jnp.bfloat16), table, preferred_element_type=jnp.float32
        ).astype(jnp.bfloat16)
    if table.dtype == jnp.int32:
        picked = jnp.dot(
            select.astype(jnp.float32), table.astype(jnp.float32), precision=lax.Precision.HIGHEST
        )
        return picked.astype(jnp.int32)
    return jnp.dot(select.astype(jnp.float32), table, precision=lax.Precision.HIGHEST)


def prefix_count(flags):
    width = flags.shape[-1]
    positions = jnp.arange(width, dtype=jnp.int32)
    upper = (positions[:, None] <= positions[None, :]).astype(jnp.float32)
    return jnp.dot(flags.astype(jnp.float32), upper).astype(jnp.int32)


def compact(flags, ranks, values, slots):
    spots = jnp.arange(slots, dtype=jnp.int32)
    hit = flags[..., None, :] & (ranks[..., None, :] == spots[:, None])
    picked = jnp.sum(jnp.where(hit, values[..., None, :], 0), axis=-1)
    return (picked, jnp.any(hit, axis=-1))


def decode(
    routed,
    carried,
    up_weight,
    up_bias,
    conv_weight,
    conv_bias,
    res_in_weight,
    res_in_bias,
    res_out_weight,
    res_out_bias,
):
    conv_count, frame_count, chan_width = routed.shape
    step_count = 2 * frame_count
    inputs = routed.astype(jnp.float32)
    tap_zero = inputs * up_weight[0]
    tap_one = inputs * up_weight[1]
    tap_two = inputs * up_weight[2]
    tap_three = inputs * up_weight[3]
    early_even = jnp.concatenate([carried[:, 0:1], tap_two[:, :-1]], axis=1)
    early_odd = jnp.concatenate([carried[:, 1:2], tap_three[:, :-1]], axis=1)
    upsampled = (
        jnp.stack([tap_zero + early_even, tap_one + early_odd], axis=2).reshape(
            conv_count, step_count, chan_width
        )
        + up_bias
    )
    history = jnp.concatenate([carried[:, 2:8], upsampled], axis=1).astype(jnp.bfloat16)
    conv_out = jnp.zeros((conv_count * step_count, chan_width), jnp.float32) + conv_bias
    for tap_index in range(7):
        window = history[:, 6 - tap_index : 6 - tap_index + step_count].reshape(
            conv_count * step_count, chan_width
        )
        conv_out = conv_out + jnp.dot(
            window, conv_weight[tap_index], preferred_element_type=jnp.float32
        )
    active = jax.nn.elu(conv_out).reshape(conv_count, step_count, chan_width)
    res_history = jnp.concatenate([carried[:, 8:10], active], axis=1)
    res_rounded = res_history.astype(jnp.bfloat16)
    res_inner = (
        jnp.zeros((conv_count * step_count, res_in_weight.shape[2]), jnp.float32) + res_in_bias
    )
    for tap_index in range(3):
        window = res_rounded[:, 2 - tap_index : 2 - tap_index + step_count].reshape(
            conv_count * step_count, chan_width
        )
        res_inner = res_inner + jnp.dot(
            window, res_in_weight[tap_index], preferred_element_type=jnp.float32
        )
    squeezed = jax.nn.elu(res_inner).astype(jnp.bfloat16)
    summed = (
        conv_out
        + jnp.dot(squeezed, res_out_weight, preferred_element_type=jnp.float32)
        + res_out_bias
    )
    decoded = summed.astype(jnp.bfloat16).reshape(conv_count, step_count, chan_width)
    new_states = jnp.concatenate(
        [
            tap_two[:, -1:],
            tap_three[:, -1:],
            history[:, -6:].astype(jnp.float32),
            res_history[:, -2:],
        ],
        axis=1,
    )
    return (decoded, new_states)


def local(
    codes,
    code_table,
    roster,
    old_slot,
    states,
    up_weight,
    up_bias,
    conv_weight,
    conv_bias,
    res_in_weight,
    res_in_bias,
    res_out_weight,
    res_out_bias,
):
    conv_count = roster.shape[0]
    per_group = lax.axis_size("dev")
    devices_all = lax.axis_size("grp") * per_group
    most = MOST
    group_first = lax.axis_index("grp") * per_group
    local_index = lax.axis_index("dev")
    positions = jnp.arange(conv_count, dtype=jnp.int32)
    earlier = positions[None, :] < positions[:, None]

    anchor = roster // conv_count
    row = roster % conv_count
    rank_in = jnp.sum(earlier & (anchor[None, :] == anchor[:, None]), axis=1).astype(jnp.int32)
    key = anchor * most + rank_in
    spots = jnp.arange(devices_all * most, dtype=jnp.int32)
    request = jnp.sum(jnp.where(key[None, :] == spots[:, None], row[None, :] + 1, 0), axis=1) - 1
    asked = lax.all_to_all(
        request.reshape(devices_all, most), ("grp", "dev"), 0, 0, tiled=True
    ).reshape(-1)
    answer = jnp.take(codes, jnp.clip(asked, 0, conv_count - 1), axis=0)
    answered = lax.all_to_all(
        answer.reshape(devices_all, most, -1), ("grp", "dev"), 0, 0, tiled=True
    ).reshape(devices_all * most, -1)
    my_codes = jnp.take(answered, key, axis=0)
    book_count = my_codes.shape[1] // FRAMES
    book_size = code_table.shape[0] // book_count
    flat_index = my_codes.reshape(conv_count, FRAMES, book_count) + (
        jnp.arange(book_count, dtype=jnp.int32) * book_size
    )
    looked = jnp.take(code_table, flat_index, axis=0).astype(jnp.float32)
    routed = jnp.sum(looked, axis=2).astype(jnp.bfloat16)

    source_dev = old_slot // conv_count - group_first
    source_row = old_slot % conv_count
    moved = source_dev != local_index
    devs = jnp.arange(per_group, dtype=jnp.int32)
    wanted = (
        jnp.sum(
            jnp.where(moved[None, :] & (source_dev[None, :] == devs[:, None]), source_row[None, :] + 1, 0),
            axis=1,
        )
        - 1
    )
    asked_rows = lax.all_to_all(wanted.reshape(per_group, 1), "dev", 0, 0, tiled=True).reshape(-1)
    leaving = jnp.take(states, jnp.clip(asked_rows, 0, conv_count - 1), axis=0)
    arrived = lax.all_to_all(leaving, "dev", 0, 0, tiled=True)
    brought = jnp.take(arrived, jnp.clip(source_dev, 0, per_group - 1), axis=0)
    carried = jnp.where(moved[:, None, None], brought, states)
    return decode(
        routed,
        carried,
        up_weight,
        up_bias,
        conv_weight,
        conv_bias,
        res_in_weight,
        res_in_bias,
        res_out_weight,
        res_out_bias,
    )


def solution(mesh):
    in_specs = (
        P(("grp", "dev"), None),
        P(),
        P(("grp", "dev")),
        P(("grp", "dev")),
        P(("grp", "dev"), None, None),
        P(),
        P(),
        P(),
        P(),
        P(),
        P(),
        P(),
        P(),
    )
    out_specs = (P(("grp", "dev"), None, None), P(("grp", "dev"), None, None))
    return jax.shard_map(local, mesh=mesh, in_specs=in_specs, out_specs=out_specs, check_vma=False)
```

```python
import jax
import jax.numpy as jnp
from jax import lax
from jax.sharding import PartitionSpec as P

FRAMES = 4
MOST = 2


def embed_codes(codes, code_table):
    row_count = codes.shape[0]
    book_count = codes.shape[1] // FRAMES
    book_size = code_table.shape[0] // book_count
    grouped = codes.reshape(row_count * FRAMES, book_count)
    entries = jnp.arange(book_size, dtype=jnp.int32)
    summed = jnp.zeros((row_count * FRAMES, code_table.shape[1]), jnp.float32)
    for book_index in range(book_count):
        onehot = (grouped[:, book_index][:, None] == entries[None, :]).astype(jnp.bfloat16)
        book_rows = code_table[book_index * book_size : (book_index + 1) * book_size]
        summed = summed + jnp.dot(onehot, book_rows, preferred_element_type=jnp.float32)
    return summed.astype(jnp.bfloat16).reshape(row_count, FRAMES, code_table.shape[1])


def pick_rows(table, index, live):
    entries = jnp.arange(table.shape[0], dtype=jnp.int32)
    select = (index[:, None] == entries[None, :]) & live[:, None]
    if table.dtype == jnp.bfloat16:
        return jnp.dot(
            select.astype(jnp.bfloat16), table, preferred_element_type=jnp.float32
        ).astype(jnp.bfloat16)
    if table.dtype == jnp.int32:
        picked = jnp.dot(
            select.astype(jnp.float32), table.astype(jnp.float32), precision=lax.Precision.HIGHEST
        )
        return picked.astype(jnp.int32)
    return jnp.dot(select.astype(jnp.float32), table, precision=lax.Precision.HIGHEST)


def prefix_count(flags):
    width = flags.shape[-1]
    positions = jnp.arange(width, dtype=jnp.int32)
    upper = (positions[:, None] <= positions[None, :]).astype(jnp.float32)
    return jnp.dot(flags.astype(jnp.float32), upper).astype(jnp.int32)


def compact(flags, ranks, values, slots):
    spots = jnp.arange(slots, dtype=jnp.int32)
    hit = flags[..., None, :] & (ranks[..., None, :] == spots[:, None])
    picked = jnp.sum(jnp.where(hit, values[..., None, :], 0), axis=-1)
    return (picked, jnp.any(hit, axis=-1))


def decode(
    routed,
    carried,
    up_weight,
    up_bias,
    conv_weight,
    conv_bias,
    res_in_weight,
    res_in_bias,
    res_out_weight,
    res_out_bias,
):
    conv_count, frame_count, chan_width = routed.shape
    step_count = 2 * frame_count
    inputs = routed.astype(jnp.float32)
    tap_zero = inputs * up_weight[0]
    tap_one = inputs * up_weight[1]
    tap_two = inputs * up_weight[2]
    tap_three = inputs * up_weight[3]
    early_even = jnp.concatenate([carried[:, 0:1], tap_two[:, :-1]], axis=1)
    early_odd = jnp.concatenate([carried[:, 1:2], tap_three[:, :-1]], axis=1)
    upsampled = (
        jnp.stack([tap_zero + early_even, tap_one + early_odd], axis=2).reshape(
            conv_count, step_count, chan_width
        )
        + up_bias
    )
    history = jnp.concatenate([carried[:, 2:8], upsampled], axis=1).astype(jnp.bfloat16)
    conv_out = jnp.zeros((conv_count * step_count, chan_width), jnp.float32) + conv_bias
    for tap_index in range(7):
        window = history[:, 6 - tap_index : 6 - tap_index + step_count].reshape(
            conv_count * step_count, chan_width
        )
        conv_out = conv_out + jnp.dot(
            window, conv_weight[tap_index], preferred_element_type=jnp.float32
        )
    active = jax.nn.elu(conv_out).reshape(conv_count, step_count, chan_width)
    res_history = jnp.concatenate([carried[:, 8:10], active], axis=1)
    res_rounded = res_history.astype(jnp.bfloat16)
    res_inner = (
        jnp.zeros((conv_count * step_count, res_in_weight.shape[2]), jnp.float32) + res_in_bias
    )
    for tap_index in range(3):
        window = res_rounded[:, 2 - tap_index : 2 - tap_index + step_count].reshape(
            conv_count * step_count, chan_width
        )
        res_inner = res_inner + jnp.dot(
            window, res_in_weight[tap_index], preferred_element_type=jnp.float32
        )
    squeezed = jax.nn.elu(res_inner).astype(jnp.bfloat16)
    summed = (
        conv_out
        + jnp.dot(squeezed, res_out_weight, preferred_element_type=jnp.float32)
        + res_out_bias
    )
    decoded = summed.astype(jnp.bfloat16).reshape(conv_count, step_count, chan_width)
    new_states = jnp.concatenate(
        [
            tap_two[:, -1:],
            tap_three[:, -1:],
            history[:, -6:].astype(jnp.float32),
            res_history[:, -2:],
        ],
        axis=1,
    )
    return (decoded, new_states)


def local(
    codes,
    code_table,
    roster,
    old_slot,
    states,
    up_weight,
    up_bias,
    conv_weight,
    conv_bias,
    res_in_weight,
    res_in_bias,
    res_out_weight,
    res_out_bias,
):
    conv_count = roster.shape[0]
    per_group = lax.axis_size("dev")
    devices_all = lax.axis_size("grp") * per_group
    most = MOST
    group_first = lax.axis_index("grp") * per_group
    local_index = lax.axis_index("dev")
    positions = jnp.arange(conv_count, dtype=jnp.int32)
    earlier = positions[None, :] < positions[:, None]

    anchor = roster // conv_count
    row = roster % conv_count
    rank_in = jnp.sum(earlier & (anchor[None, :] == anchor[:, None]), axis=1).astype(jnp.int32)
    key = anchor * most + rank_in
    spots = jnp.arange(devices_all * most, dtype=jnp.int32)
    code_request = jnp.sum(jnp.where(key[None, :] == spots[:, None], row[None, :] + 1, 0), axis=1) - 1
    source_dev = old_slot // conv_count - group_first
    source_row = old_slot % conv_count
    moved = source_dev != local_index
    everyone = jnp.arange(devices_all, dtype=jnp.int32)
    state_request = (
        jnp.sum(
            jnp.where(
                moved[None, :] & (source_dev[None, :] + group_first == everyone[:, None]),
                source_row[None, :] + 1,
                0,
            ),
            axis=1,
        )
        - 1
    )
    request = jnp.concatenate(
        [code_request.reshape(devices_all, most), state_request.reshape(devices_all, 1)], axis=1
    )
    asked = lax.all_to_all(request, ("grp", "dev"), 0, 0, tiled=True)

    local_rows = embed_codes(codes, code_table).reshape(conv_count, -1)
    answer = jnp.take(local_rows, jnp.clip(asked[:, :most].reshape(-1), 0, conv_count - 1), axis=0)
    answered = lax.all_to_all(
        answer.reshape(devices_all, most, -1), ("grp", "dev"), 0, 0, tiled=True
    ).reshape(devices_all * most, -1)
    routed = jnp.take(answered, key, axis=0).reshape(conv_count, FRAMES, -1)

    state_asked = lax.dynamic_slice_in_dim(asked[:, most], group_first, per_group)
    leaving = jnp.take(states, jnp.clip(state_asked, 0, conv_count - 1), axis=0)
    arrived = lax.all_to_all(leaving, "dev", 0, 0, tiled=True)
    brought = jnp.take(arrived, jnp.clip(source_dev, 0, per_group - 1), axis=0)
    carried = jnp.where(moved[:, None, None], brought, states)
    return decode(
        routed,
        carried,
        up_weight,
        up_bias,
        conv_weight,
        conv_bias,
        res_in_weight,
        res_in_bias,
        res_out_weight,
        res_out_bias,
    )


def solution(mesh):
    in_specs = (
        P(("grp", "dev"), None),
        P(),
        P(("grp", "dev")),
        P(("grp", "dev")),
        P(("grp", "dev"), None, None),
        P(),
        P(),
        P(),
        P(),
        P(),
        P(),
        P(),
        P(),
    )
    out_specs = (P(("grp", "dev"), None, None), P(("grp", "dev"), None, None))
    return jax.shard_map(local, mesh=mesh, in_specs=in_specs, out_specs=out_specs, check_vma=False)
```

```python
import jax
import jax.numpy as jnp
from jax import lax
from jax.experimental import pallas as pl
from jax.experimental.pallas import tpu as pltpu
from jax.sharding import PartitionSpec as P

FRAMES = 4
MOST = 2


def embed_codes(codes, code_table):
    row_count = codes.shape[0]
    book_count = codes.shape[1] // FRAMES
    book_size = code_table.shape[0] // book_count
    grouped = codes.reshape(row_count * FRAMES, book_count)
    entries = jnp.arange(book_size, dtype=jnp.int32)
    summed = jnp.zeros((row_count * FRAMES, code_table.shape[1]), jnp.float32)
    for book_index in range(book_count):
        onehot = (grouped[:, book_index][:, None] == entries[None, :]).astype(jnp.bfloat16)
        book_rows = code_table[book_index * book_size : (book_index + 1) * book_size]
        summed = summed + jnp.dot(onehot, book_rows, preferred_element_type=jnp.float32)
    return summed.astype(jnp.bfloat16).reshape(row_count, FRAMES, code_table.shape[1])


def pick_rows(table, index, live):
    entries = jnp.arange(table.shape[0], dtype=jnp.int32)
    select = (index[:, None] == entries[None, :]) & live[:, None]
    if table.dtype == jnp.bfloat16:
        return jnp.dot(
            select.astype(jnp.bfloat16), table, preferred_element_type=jnp.float32
        ).astype(jnp.bfloat16)
    if table.dtype == jnp.int32:
        picked = jnp.dot(
            select.astype(jnp.float32), table.astype(jnp.float32), precision=lax.Precision.HIGHEST
        )
        return picked.astype(jnp.int32)
    return jnp.dot(select.astype(jnp.float32), table, precision=lax.Precision.HIGHEST)


def prefix_count(flags):
    width = flags.shape[-1]
    positions = jnp.arange(width, dtype=jnp.int32)
    upper = (positions[:, None] <= positions[None, :]).astype(jnp.float32)
    return jnp.dot(flags.astype(jnp.float32), upper).astype(jnp.int32)


def compact(flags, ranks, values, slots):
    spots = jnp.arange(slots, dtype=jnp.int32)
    hit = flags[..., None, :] & (ranks[..., None, :] == spots[:, None])
    picked = jnp.sum(jnp.where(hit, values[..., None, :], 0), axis=-1)
    return (picked, jnp.any(hit, axis=-1))


def exchange(blocks, whole, collective_id):
    peers = blocks.shape[0]
    per_group = lax.axis_size("dev")

    def kernel(x_ref, o_ref, send_sems, recv_sems, own_sem):
        group = lax.axis_index("grp")
        if whole:
            me = group * per_group + lax.axis_index("dev")
        else:
            me = lax.axis_index("dev")

        def device(peer):
            if whole:
                return (peer // per_group, peer % per_group)
            return (group, peer)

        barrier = pltpu.get_barrier_semaphore()

        def greet(offset, carry):
            peer = lax.rem(me + offset, peers)
            pl.semaphore_signal(barrier, inc=1, device_id=device(peer), device_id_type=pl.DeviceIdType.MESH)
            return carry

        lax.fori_loop(1, peers, greet, 0)
        pl.semaphore_wait(barrier, peers - 1)

        def outgoing(peer):
            return pltpu.make_async_remote_copy(
                src_ref=x_ref.at[peer],
                dst_ref=o_ref.at[me],
                send_sem=send_sems.at[peer],
                recv_sem=recv_sems.at[me],
                device_id=device(peer),
                device_id_type=pl.DeviceIdType.MESH,
            )

        def incoming(peer):
            return pltpu.make_async_remote_copy(
                src_ref=x_ref.at[peer],
                dst_ref=o_ref.at[peer],
                send_sem=send_sems.at[peer],
                recv_sem=recv_sems.at[peer],
                device_id=device(peer),
                device_id_type=pl.DeviceIdType.MESH,
            )

        def send(offset, carry):
            outgoing(lax.rem(me + offset, peers)).start()
            return carry

        lax.fori_loop(1, peers, send, 0)
        own = pltpu.make_async_copy(x_ref.at[me], o_ref.at[me], own_sem)
        own.start()
        own.wait()

        def finish(offset, carry):
            peer = lax.rem(me + offset, peers)
            outgoing(peer).wait_send()
            incoming(lax.rem(me + peers - offset, peers)).wait_recv()
            return carry

        lax.fori_loop(1, peers, finish, 0)

    return pl.pallas_call(
        kernel,
        out_shape=jax.ShapeDtypeStruct(blocks.shape, blocks.dtype),
        in_specs=[pl.BlockSpec(memory_space=pl.ANY)],
        out_specs=pl.BlockSpec(memory_space=pl.ANY),
        scratch_shapes=[
            pltpu.SemaphoreType.DMA((peers,)),
            pltpu.SemaphoreType.DMA((peers,)),
            pltpu.SemaphoreType.DMA(()),
        ],
        compiler_params=pltpu.CompilerParams(collective_id=collective_id, has_side_effects=True),
    )(blocks)


def decode(
    routed,
    carried,
    up_weight,
    up_bias,
    conv_weight,
    conv_bias,
    res_in_weight,
    res_in_bias,
    res_out_weight,
    res_out_bias,
):
    conv_count, frame_count, chan_width = routed.shape
    step_count = 2 * frame_count
    inputs = routed.astype(jnp.float32)
    tap_zero = inputs * up_weight[0]
    tap_one = inputs * up_weight[1]
    tap_two = inputs * up_weight[2]
    tap_three = inputs * up_weight[3]
    early_even = jnp.concatenate([carried[:, 0:1], tap_two[:, :-1]], axis=1)
    early_odd = jnp.concatenate([carried[:, 1:2], tap_three[:, :-1]], axis=1)
    upsampled = (
        jnp.stack([tap_zero + early_even, tap_one + early_odd], axis=2).reshape(
            conv_count, step_count, chan_width
        )
        + up_bias
    )
    history = jnp.concatenate([carried[:, 2:8], upsampled], axis=1).astype(jnp.bfloat16)
    conv_out = jnp.zeros((conv_count * step_count, chan_width), jnp.float32) + conv_bias
    for tap_index in range(7):
        window = history[:, 6 - tap_index : 6 - tap_index + step_count].reshape(
            conv_count * step_count, chan_width
        )
        conv_out = conv_out + jnp.dot(
            window, conv_weight[tap_index], preferred_element_type=jnp.float32
        )
    active = jax.nn.elu(conv_out).reshape(conv_count, step_count, chan_width)
    res_history = jnp.concatenate([carried[:, 8:10], active], axis=1)
    res_rounded = res_history.astype(jnp.bfloat16)
    res_inner = (
        jnp.zeros((conv_count * step_count, res_in_weight.shape[2]), jnp.float32) + res_in_bias
    )
    for tap_index in range(3):
        window = res_rounded[:, 2 - tap_index : 2 - tap_index + step_count].reshape(
            conv_count * step_count, chan_width
        )
        res_inner = res_inner + jnp.dot(
            window, res_in_weight[tap_index], preferred_element_type=jnp.float32
        )
    squeezed = jax.nn.elu(res_inner).astype(jnp.bfloat16)
    summed = (
        conv_out
        + jnp.dot(squeezed, res_out_weight, preferred_element_type=jnp.float32)
        + res_out_bias
    )
    decoded = summed.astype(jnp.bfloat16).reshape(conv_count, step_count, chan_width)
    new_states = jnp.concatenate(
        [
            tap_two[:, -1:],
            tap_three[:, -1:],
            history[:, -6:].astype(jnp.float32),
            res_history[:, -2:],
        ],
        axis=1,
    )
    return (decoded, new_states)


def local(
    codes,
    code_table,
    roster,
    old_slot,
    states,
    up_weight,
    up_bias,
    conv_weight,
    conv_bias,
    res_in_weight,
    res_in_bias,
    res_out_weight,
    res_out_bias,
):
    conv_count = roster.shape[0]
    per_group = lax.axis_size("dev")
    devices_all = lax.axis_size("grp") * per_group
    most = MOST
    group_first = lax.axis_index("grp") * per_group
    local_index = lax.axis_index("dev")
    positions = jnp.arange(conv_count, dtype=jnp.int32)
    earlier = positions[None, :] < positions[:, None]

    anchor = roster // conv_count
    row = roster % conv_count
    rank_in = jnp.sum(earlier & (anchor[None, :] == anchor[:, None]), axis=1).astype(jnp.int32)
    key = anchor * most + rank_in
    spots = jnp.arange(devices_all * most, dtype=jnp.int32)
    code_request = jnp.sum(jnp.where(key[None, :] == spots[:, None], row[None, :] + 1, 0), axis=1) - 1
    source_dev = old_slot // conv_count - group_first
    source_row = old_slot % conv_count
    moved = source_dev != local_index
    everyone = jnp.arange(devices_all, dtype=jnp.int32)
    state_request = (
        jnp.sum(
            jnp.where(
                moved[None, :] & (source_dev[None, :] + group_first == everyone[:, None]),
                source_row[None, :] + 1,
                0,
            ),
            axis=1,
        )
        - 1
    )
    request = jnp.concatenate(
        [code_request.reshape(devices_all, most), state_request.reshape(devices_all, 1)], axis=1
    )
    lanes = 128
    padded = jnp.zeros((devices_all, 1, lanes), jnp.int32).at[:, 0, : most + 1].set(request)
    asked = exchange(padded, True, 0)[:, 0, : most + 1]

    local_rows = embed_codes(codes, code_table).reshape(conv_count, -1)
    answer = jnp.take(local_rows, jnp.clip(asked[:, :most].reshape(-1), 0, conv_count - 1), axis=0)
    answered = exchange(answer.reshape(devices_all, 16, -1), True, 1).reshape(devices_all * most, -1)
    routed = jnp.take(answered, key, axis=0).reshape(conv_count, FRAMES, -1)

    state_asked = lax.dynamic_slice_in_dim(asked[:, most], group_first, per_group)
    leaving = jnp.take(states, jnp.clip(state_asked, 0, conv_count - 1), axis=0)
    arrived = exchange(leaving.reshape(per_group, -1, 128), False, 2).reshape(leaving.shape)
    brought = jnp.take(arrived, jnp.clip(source_dev, 0, per_group - 1), axis=0)
    carried = jnp.where(moved[:, None, None], brought, states)
    return decode(
        routed,
        carried,
        up_weight,
        up_bias,
        conv_weight,
        conv_bias,
        res_in_weight,
        res_in_bias,
        res_out_weight,
        res_out_bias,
    )


def solution(mesh):
    in_specs = (
        P(("grp", "dev"), None),
        P(),
        P(("grp", "dev")),
        P(("grp", "dev")),
        P(("grp", "dev"), None, None),
        P(),
        P(),
        P(),
        P(),
        P(),
        P(),
        P(),
        P(),
    )
    out_specs = (P(("grp", "dev"), None, None), P(("grp", "dev"), None, None))
    return jax.shard_map(local, mesh=mesh, in_specs=in_specs, out_specs=out_specs, check_vma=False)
```

```python
import jax
import jax.numpy as jnp
from jax import lax
from jax.experimental import pallas as pl
from jax.experimental.pallas import tpu as pltpu
from jax.sharding import PartitionSpec as P

FRAMES = 4
MOST = 2


def embed_codes(codes, code_table):
    row_count = codes.shape[0]
    book_count = codes.shape[1] // FRAMES
    book_size = code_table.shape[0] // book_count
    grouped = codes.reshape(row_count * FRAMES, book_count)
    entries = jnp.arange(book_size, dtype=jnp.int32)
    summed = jnp.zeros((row_count * FRAMES, code_table.shape[1]), jnp.float32)
    for book_index in range(book_count):
        onehot = (grouped[:, book_index][:, None] == entries[None, :]).astype(jnp.bfloat16)
        book_rows = code_table[book_index * book_size : (book_index + 1) * book_size]
        summed = summed + jnp.dot(onehot, book_rows, preferred_element_type=jnp.float32)
    return summed.astype(jnp.bfloat16).reshape(row_count, FRAMES, code_table.shape[1])


def pick_rows(table, index, live):
    entries = jnp.arange(table.shape[0], dtype=jnp.int32)
    select = (index[:, None] == entries[None, :]) & live[:, None]
    if table.dtype == jnp.bfloat16:
        return jnp.dot(
            select.astype(jnp.bfloat16), table, preferred_element_type=jnp.float32
        ).astype(jnp.bfloat16)
    if table.dtype == jnp.int32:
        picked = jnp.dot(
            select.astype(jnp.float32), table.astype(jnp.float32), precision=lax.Precision.HIGHEST
        )
        return picked.astype(jnp.int32)
    return jnp.dot(select.astype(jnp.float32), table, precision=lax.Precision.HIGHEST)


def prefix_count(flags):
    width = flags.shape[-1]
    positions = jnp.arange(width, dtype=jnp.int32)
    upper = (positions[:, None] <= positions[None, :]).astype(jnp.float32)
    return jnp.dot(flags.astype(jnp.float32), upper).astype(jnp.int32)


def compact(flags, ranks, values, slots):
    spots = jnp.arange(slots, dtype=jnp.int32)
    hit = flags[..., None, :] & (ranks[..., None, :] == spots[:, None])
    picked = jnp.sum(jnp.where(hit, values[..., None, :], 0), axis=-1)
    return (picked, jnp.any(hit, axis=-1))


def exchange(items, collective_id):
    per_group = lax.axis_size("dev")
    count = len(items)

    def kernel(*refs):
        x_refs = refs[:count]
        o_refs = refs[count : 2 * count]
        send_sems = refs[2 * count : 3 * count]
        recv_sems = refs[3 * count : 4 * count]
        own_sem = refs[4 * count]
        group = lax.axis_index("grp")
        dev = lax.axis_index("dev")
        widest = max(blocks.shape[0] for blocks, _ in items)
        whole_any = any(whole for _, whole in items)
        me_all = group * per_group + dev

        def place(whole):
            if whole:
                return me_all, lambda peer: (peer // per_group, peer % per_group)
            return dev, lambda peer: (group, peer)

        barrier = pltpu.get_barrier_semaphore()
        greet_me, greet_device = place(whole_any)

        def greet(offset, carry):
            peer = lax.rem(greet_me + offset, widest)
            pl.semaphore_signal(barrier, inc=1, device_id=greet_device(peer), device_id_type=pl.DeviceIdType.MESH)
            return carry

        lax.fori_loop(1, widest, greet, 0)
        pl.semaphore_wait(barrier, widest - 1)

        def copy(index, peer, slot):
            whole = items[index][1]
            _, device = place(whole)
            return pltpu.make_async_remote_copy(
                src_ref=x_refs[index].at[peer],
                dst_ref=o_refs[index].at[slot],
                send_sem=send_sems[index].at[peer],
                recv_sem=recv_sems[index].at[slot],
                device_id=device(peer),
                device_id_type=pl.DeviceIdType.MESH,
            )

        for index, (blocks, whole) in enumerate(items):
            peers = blocks.shape[0]
            me, _ = place(whole)

            def send(offset, carry, index=index, peers=peers, me=me):
                copy(index, lax.rem(me + offset, peers), me).start()
                return carry

            lax.fori_loop(1, peers, send, 0)
        for index, (blocks, whole) in enumerate(items):
            me, _ = place(whole)
            own = pltpu.make_async_copy(x_refs[index].at[me], o_refs[index].at[me], own_sem)
            own.start()
            own.wait()
        for index, (blocks, whole) in enumerate(items):
            peers = blocks.shape[0]
            me, _ = place(whole)

            def finish(offset, carry, index=index, peers=peers, me=me):
                copy(index, lax.rem(me + offset, peers), me).wait_send()
                source = lax.rem(me + peers - offset, peers)
                copy(index, source, source).wait_recv()
                return carry

            lax.fori_loop(1, peers, finish, 0)

    arrays = [blocks for blocks, _ in items]
    return pl.pallas_call(
        kernel,
        out_shape=[jax.ShapeDtypeStruct(a.shape, a.dtype) for a in arrays],
        in_specs=[pl.BlockSpec(memory_space=pl.ANY)] * count,
        out_specs=[pl.BlockSpec(memory_space=pl.ANY)] * count,
        scratch_shapes=[pltpu.SemaphoreType.DMA((a.shape[0],)) for a in arrays] * 2
        + [pltpu.SemaphoreType.DMA(())],
        compiler_params=pltpu.CompilerParams(collective_id=collective_id, has_side_effects=True),
    )(*arrays)


def decode(
    routed,
    carried,
    up_weight,
    up_bias,
    conv_weight,
    conv_bias,
    res_in_weight,
    res_in_bias,
    res_out_weight,
    res_out_bias,
):
    conv_count, frame_count, chan_width = routed.shape
    step_count = 2 * frame_count
    inputs = routed.astype(jnp.float32)
    tap_zero = inputs * up_weight[0]
    tap_one = inputs * up_weight[1]
    tap_two = inputs * up_weight[2]
    tap_three = inputs * up_weight[3]
    early_even = jnp.concatenate([carried[:, 0:1], tap_two[:, :-1]], axis=1)
    early_odd = jnp.concatenate([carried[:, 1:2], tap_three[:, :-1]], axis=1)
    upsampled = (
        jnp.stack([tap_zero + early_even, tap_one + early_odd], axis=2).reshape(
            conv_count, step_count, chan_width
        )
        + up_bias
    )
    history = jnp.concatenate([carried[:, 2:8], upsampled], axis=1).astype(jnp.bfloat16)
    conv_out = jnp.zeros((conv_count * step_count, chan_width), jnp.float32) + conv_bias
    for tap_index in range(7):
        window = history[:, 6 - tap_index : 6 - tap_index + step_count].reshape(
            conv_count * step_count, chan_width
        )
        conv_out = conv_out + jnp.dot(
            window, conv_weight[tap_index], preferred_element_type=jnp.float32
        )
    active = jax.nn.elu(conv_out).reshape(conv_count, step_count, chan_width)
    res_history = jnp.concatenate([carried[:, 8:10], active], axis=1)
    res_rounded = res_history.astype(jnp.bfloat16)
    res_inner = (
        jnp.zeros((conv_count * step_count, res_in_weight.shape[2]), jnp.float32) + res_in_bias
    )
    for tap_index in range(3):
        window = res_rounded[:, 2 - tap_index : 2 - tap_index + step_count].reshape(
            conv_count * step_count, chan_width
        )
        res_inner = res_inner + jnp.dot(
            window, res_in_weight[tap_index], preferred_element_type=jnp.float32
        )
    squeezed = jax.nn.elu(res_inner).astype(jnp.bfloat16)
    summed = (
        conv_out
        + jnp.dot(squeezed, res_out_weight, preferred_element_type=jnp.float32)
        + res_out_bias
    )
    decoded = summed.astype(jnp.bfloat16).reshape(conv_count, step_count, chan_width)
    new_states = jnp.concatenate(
        [
            tap_two[:, -1:],
            tap_three[:, -1:],
            history[:, -6:].astype(jnp.float32),
            res_history[:, -2:],
        ],
        axis=1,
    )
    return (decoded, new_states)


def local(
    codes,
    code_table,
    roster,
    old_slot,
    states,
    up_weight,
    up_bias,
    conv_weight,
    conv_bias,
    res_in_weight,
    res_in_bias,
    res_out_weight,
    res_out_bias,
):
    conv_count = roster.shape[0]
    per_group = lax.axis_size("dev")
    devices_all = lax.axis_size("grp") * per_group
    most = MOST
    group_first = lax.axis_index("grp") * per_group
    local_index = lax.axis_index("dev")
    positions = jnp.arange(conv_count, dtype=jnp.int32)
    earlier = positions[None, :] < positions[:, None]

    anchor = roster // conv_count
    row = roster % conv_count
    rank_in = jnp.sum(earlier & (anchor[None, :] == anchor[:, None]), axis=1).astype(jnp.int32)
    key = anchor * most + rank_in
    spots = jnp.arange(devices_all * most, dtype=jnp.int32)
    code_request = jnp.sum(jnp.where(key[None, :] == spots[:, None], row[None, :] + 1, 0), axis=1) - 1
    source_dev = old_slot // conv_count - group_first
    source_row = old_slot % conv_count
    moved = source_dev != local_index
    everyone = jnp.arange(devices_all, dtype=jnp.int32)
    state_request = (
        jnp.sum(
            jnp.where(
                moved[None, :] & (source_dev[None, :] + group_first == everyone[:, None]),
                source_row[None, :] + 1,
                0,
            ),
            axis=1,
        )
        - 1
    )
    request = jnp.concatenate(
        [code_request.reshape(devices_all, most), state_request.reshape(devices_all, 1)], axis=1
    )
    lanes = 128
    padded = jnp.zeros((devices_all, 1, lanes), jnp.int32).at[:, 0, : most + 1].set(request)
    (asked,) = exchange([(padded, True)], 0)
    asked = asked[:, 0, : most + 1]

    answer = jnp.take(codes, jnp.clip(asked[:, :most].reshape(-1), 0, conv_count - 1), axis=0)
    answer = jnp.zeros((devices_all, 1, lanes), jnp.int32).at[:, 0, : answer.size // devices_all].set(
        answer.reshape(devices_all, -1)
    )
    state_asked = lax.dynamic_slice_in_dim(asked[:, most], group_first, per_group)
    leaving = jnp.take(states, jnp.clip(state_asked, 0, conv_count - 1), axis=0)
    answered, arrived = exchange(
        [(answer, True), (leaving.reshape(per_group, -1, lanes), False)], 1
    )
    code_width = codes.shape[1]
    answered = answered[:, 0, : most * code_width].reshape(devices_all * most, code_width)
    my_codes = jnp.take(answered, key, axis=0)
    routed = embed_codes(my_codes, code_table)
    arrived = arrived.reshape(leaving.shape)
    brought = jnp.take(arrived, jnp.clip(source_dev, 0, per_group - 1), axis=0)
    carried = jnp.where(moved[:, None, None], brought, states)
    return decode(
        routed,
        carried,
        up_weight,
        up_bias,
        conv_weight,
        conv_bias,
        res_in_weight,
        res_in_bias,
        res_out_weight,
        res_out_bias,
    )


def solution(mesh):
    in_specs = (
        P(("grp", "dev"), None),
        P(),
        P(("grp", "dev")),
        P(("grp", "dev")),
        P(("grp", "dev"), None, None),
        P(),
        P(),
        P(),
        P(),
        P(),
        P(),
        P(),
        P(),
    )
    out_specs = (P(("grp", "dev"), None, None), P(("grp", "dev"), None, None))
    return jax.shard_map(local, mesh=mesh, in_specs=in_specs, out_specs=out_specs, check_vma=False)
```

```python
import jax
import jax.numpy as jnp
from jax import lax
from jax.experimental import pallas as pl
from jax.experimental.pallas import tpu as pltpu
from jax.sharding import PartitionSpec as P

FRAMES = 4
MOST = 2


def embed_codes(codes, code_table):
    row_count = codes.shape[0]
    book_count = codes.shape[1] // FRAMES
    book_size = code_table.shape[0] // book_count
    grouped = codes.reshape(row_count * FRAMES, book_count)
    entries = jnp.arange(book_size, dtype=jnp.int32)
    summed = jnp.zeros((row_count * FRAMES, code_table.shape[1]), jnp.float32)
    for book_index in range(book_count):
        onehot = (grouped[:, book_index][:, None] == entries[None, :]).astype(jnp.bfloat16)
        book_rows = code_table[book_index * book_size : (book_index + 1) * book_size]
        summed = summed + jnp.dot(onehot, book_rows, preferred_element_type=jnp.float32)
    summed = lax.reduce_precision(summed, exponent_bits=8, mantissa_bits=7)
    return summed.astype(jnp.bfloat16).reshape(row_count, FRAMES, code_table.shape[1])


def pick_rows(table, index, live):
    entries = jnp.arange(table.shape[0], dtype=jnp.int32)
    select = (index[:, None] == entries[None, :]) & live[:, None]
    if table.dtype == jnp.bfloat16:
        return jnp.dot(
            select.astype(jnp.bfloat16), table, preferred_element_type=jnp.float32
        ).astype(jnp.bfloat16)
    if table.dtype == jnp.int32:
        picked = jnp.dot(
            select.astype(jnp.float32), table.astype(jnp.float32), precision=lax.Precision.HIGHEST
        )
        return picked.astype(jnp.int32)
    return jnp.dot(select.astype(jnp.float32), table, precision=lax.Precision.HIGHEST)


def prefix_count(flags):
    width = flags.shape[-1]
    positions = jnp.arange(width, dtype=jnp.int32)
    upper = (positions[:, None] <= positions[None, :]).astype(jnp.float32)
    return jnp.dot(flags.astype(jnp.float32), upper).astype(jnp.int32)


def compact(flags, ranks, values, slots):
    spots = jnp.arange(slots, dtype=jnp.int32)
    hit = flags[..., None, :] & (ranks[..., None, :] == spots[:, None])
    picked = jnp.sum(jnp.where(hit, values[..., None, :], 0), axis=-1)
    return (picked, jnp.any(hit, axis=-1))


def exchange(items, collective_id):
    groups = lax.axis_size("grp")
    per_group = lax.axis_size("dev")
    count = len(items)
    shapes = []
    for blocks, whole in items:
        if whole:
            shapes.append(jax.ShapeDtypeStruct((groups, per_group) + blocks.shape[1:], blocks.dtype))
        else:
            shapes.append(jax.ShapeDtypeStruct(blocks.shape, blocks.dtype))
    wholes = [index for index, (_, whole) in enumerate(items) if whole]

    def kernel(*refs):
        x_refs = refs[:count]
        o_refs = refs[count : 2 * count]
        mid_refs = dict(zip(wholes, refs[2 * count : 2 * count + len(wholes)]))
        sems = refs[2 * count + len(wholes) :]
        first_send, first_recv, second_send, second_recv, own_sem = sems
        group = lax.axis_index("grp")
        dev = lax.axis_index("dev")
        barrier = pltpu.get_barrier_semaphore()
        across = len(wholes) > 0

        if across:
            def greet_group(offset, carry):
                peer = lax.rem(group + offset, groups)
                pl.semaphore_signal(barrier, inc=1, device_id=(peer, dev), device_id_type=pl.DeviceIdType.MESH)
                return carry

            lax.fori_loop(1, groups, greet_group, 0)

        def greet_dev(offset, carry):
            peer = lax.rem(dev + offset, per_group)
            pl.semaphore_signal(barrier, inc=1, device_id=(group, peer), device_id_type=pl.DeviceIdType.MESH)
            return carry

        lax.fori_loop(1, per_group, greet_dev, 0)
        pl.semaphore_wait(barrier, (groups - 1 if across else 0) + per_group - 1)

        def hop_one(slot, index, peer, place):
            return pltpu.make_async_remote_copy(
                src_ref=x_refs[index].at[pl.ds(peer * per_group, per_group)],
                dst_ref=mid_refs[index].at[place],
                send_sem=first_send.at[slot, peer],
                recv_sem=first_recv.at[slot, place],
                device_id=(peer, dev),
                device_id_type=pl.DeviceIdType.MESH,
            )

        def hop_two(index, peer, place):
            if items[index][1]:
                source = mid_refs[index].at[:, peer]
                target = o_refs[index].at[:, place]
            else:
                source = x_refs[index].at[peer]
                target = o_refs[index].at[place]
            return pltpu.make_async_remote_copy(
                src_ref=source,
                dst_ref=target,
                send_sem=second_send.at[index, peer],
                recv_sem=second_recv.at[index, place],
                device_id=(group, peer),
                device_id_type=pl.DeviceIdType.MESH,
            )

        for slot, index in enumerate(wholes):
            def send_one(offset, carry, slot=slot, index=index):
                hop_one(slot, index, lax.rem(group + offset, groups), group).start()
                return carry

            lax.fori_loop(1, groups, send_one, 0)
        for index, (_, whole) in enumerate(items):
            if not whole:
                def send_group(offset, carry, index=index):
                    hop_two(index, lax.rem(dev + offset, per_group), dev).start()
                    return carry

                lax.fori_loop(1, per_group, send_group, 0)
        for slot, index in enumerate(wholes):
            own = pltpu.make_async_copy(
                x_refs[index].at[pl.ds(group * per_group, per_group)], mid_refs[index].at[group], own_sem
            )
            own.start()
            own.wait()

            def finish_one(offset, carry, slot=slot, index=index):
                hop_one(slot, index, lax.rem(group + offset, groups), group).wait_send()
                source = lax.rem(group + groups - offset, groups)
                hop_one(slot, index, source, source).wait_recv()
                return carry

            lax.fori_loop(1, groups, finish_one, 0)

            def send_two(offset, carry, index=index):
                hop_two(index, lax.rem(dev + offset, per_group), dev).start()
                return carry

            lax.fori_loop(1, per_group, send_two, 0)
        for index, (_, whole) in enumerate(items):
            if whole:
                own = pltpu.make_async_copy(mid_refs[index].at[:, dev], o_refs[index].at[:, dev], own_sem)
            else:
                own = pltpu.make_async_copy(x_refs[index].at[dev], o_refs[index].at[dev], own_sem)
            own.start()
            own.wait()

            def finish_two(offset, carry, index=index):
                hop_two(index, lax.rem(dev + offset, per_group), dev).wait_send()
                source = lax.rem(dev + per_group - offset, per_group)
                hop_two(index, source, source).wait_recv()
                return carry

            lax.fori_loop(1, per_group, finish_two, 0)

    mids = [shapes[index] for index in wholes]
    results = pl.pallas_call(
        kernel,
        out_shape=shapes + mids,
        in_specs=[pl.BlockSpec(memory_space=pl.ANY)] * count,
        out_specs=[pl.BlockSpec(memory_space=pl.ANY)] * (count + len(wholes)),
        scratch_shapes=[
            pltpu.SemaphoreType.DMA((max(len(wholes), 1), groups)),
            pltpu.SemaphoreType.DMA((max(len(wholes), 1), groups)),
            pltpu.SemaphoreType.DMA((count, per_group)),
            pltpu.SemaphoreType.DMA((count, per_group)),
            pltpu.SemaphoreType.DMA(()),
        ],
        compiler_params=pltpu.CompilerParams(collective_id=collective_id, has_side_effects=True),
    )(*[blocks for blocks, _ in items])
    return [
        result.reshape(blocks.shape) for result, (blocks, _) in zip(results[:count], items)
    ]


def decode(
    routed,
    carried,
    up_weight,
    up_bias,
    conv_weight,
    conv_bias,
    res_in_weight,
    res_in_bias,
    res_out_weight,
    res_out_bias,
):
    conv_count, frame_count, chan_width = routed.shape
    step_count = 2 * frame_count
    inputs = routed.astype(jnp.float32)
    tap_zero = inputs * up_weight[0]
    tap_one = inputs * up_weight[1]
    tap_two = inputs * up_weight[2]
    tap_three = inputs * up_weight[3]
    early_even = jnp.concatenate([carried[:, 0:1], tap_two[:, :-1]], axis=1)
    early_odd = jnp.concatenate([carried[:, 1:2], tap_three[:, :-1]], axis=1)
    upsampled = (
        jnp.stack([tap_zero + early_even, tap_one + early_odd], axis=2).reshape(
            conv_count, step_count, chan_width
        )
        + up_bias
    )
    history = jnp.concatenate([carried[:, 2:8], upsampled], axis=1).astype(jnp.bfloat16)
    conv_out = jnp.zeros((conv_count * step_count, chan_width), jnp.float32) + conv_bias
    for tap_index in range(7):
        window = history[:, 6 - tap_index : 6 - tap_index + step_count].reshape(
            conv_count * step_count, chan_width
        )
        conv_out = conv_out + jnp.dot(
            window, conv_weight[tap_index], preferred_element_type=jnp.float32
        )
    active = jax.nn.elu(conv_out).reshape(conv_count, step_count, chan_width)
    res_history = jnp.concatenate([carried[:, 8:10], active], axis=1)
    res_rounded = res_history.astype(jnp.bfloat16)
    res_inner = (
        jnp.zeros((conv_count * step_count, res_in_weight.shape[2]), jnp.float32) + res_in_bias
    )
    for tap_index in range(3):
        window = res_rounded[:, 2 - tap_index : 2 - tap_index + step_count].reshape(
            conv_count * step_count, chan_width
        )
        res_inner = res_inner + jnp.dot(
            window, res_in_weight[tap_index], preferred_element_type=jnp.float32
        )
    squeezed = jax.nn.elu(res_inner).astype(jnp.bfloat16)
    summed = (
        conv_out
        + jnp.dot(squeezed, res_out_weight, preferred_element_type=jnp.float32)
        + res_out_bias
    )
    decoded = summed.astype(jnp.bfloat16).reshape(conv_count, step_count, chan_width)
    new_states = jnp.concatenate(
        [
            tap_two[:, -1:],
            tap_three[:, -1:],
            history[:, -6:].astype(jnp.float32),
            res_history[:, -2:],
        ],
        axis=1,
    )
    return (decoded, new_states)


def local(
    codes,
    code_table,
    roster,
    old_slot,
    states,
    up_weight,
    up_bias,
    conv_weight,
    conv_bias,
    res_in_weight,
    res_in_bias,
    res_out_weight,
    res_out_bias,
):
    conv_count = roster.shape[0]
    per_group = lax.axis_size("dev")
    devices_all = lax.axis_size("grp") * per_group
    most = MOST
    group_first = lax.axis_index("grp") * per_group
    local_index = lax.axis_index("dev")
    positions = jnp.arange(conv_count, dtype=jnp.int32)
    earlier = positions[None, :] < positions[:, None]

    anchor = roster // conv_count
    row = roster % conv_count
    rank_in = jnp.sum(earlier & (anchor[None, :] == anchor[:, None]), axis=1).astype(jnp.int32)
    key = anchor * most + rank_in
    spots = jnp.arange(devices_all * most, dtype=jnp.int32)
    code_request = jnp.sum(jnp.where(key[None, :] == spots[:, None], row[None, :] + 1, 0), axis=1) - 1
    source_dev = old_slot // conv_count - group_first
    source_row = old_slot % conv_count
    moved = source_dev != local_index
    everyone = jnp.arange(devices_all, dtype=jnp.int32)
    state_request = (
        jnp.sum(
            jnp.where(
                moved[None, :] & (source_dev[None, :] + group_first == everyone[:, None]),
                source_row[None, :] + 1,
                0,
            ),
            axis=1,
        )
        - 1
    )
    request = jnp.concatenate(
        [code_request.reshape(devices_all, most), state_request.reshape(devices_all, 1)], axis=1
    )
    lanes = 128
    padded = jnp.zeros((devices_all, 1, lanes), jnp.int32).at[:, 0, : most + 1].set(request)
    (asked,) = exchange([(padded, True)], 0)
    asked = asked[:, 0, : most + 1]

    answer = jnp.take(codes, jnp.clip(asked[:, :most].reshape(-1), 0, conv_count - 1), axis=0)
    answer = jnp.zeros((devices_all, 1, lanes), jnp.int32).at[:, 0, : answer.size // devices_all].set(
        answer.reshape(devices_all, -1)
    )
    state_asked = lax.dynamic_slice_in_dim(asked[:, most], group_first, per_group)
    leaving = jnp.take(states, jnp.clip(state_asked, 0, conv_count - 1), axis=0)
    answered, arrived = exchange(
        [(answer, True), (leaving.reshape(per_group, -1, lanes), False)], 1
    )
    code_width = codes.shape[1]
    answered = answered[:, 0, : most * code_width].reshape(devices_all * most, code_width)
    my_codes = jnp.take(answered, key, axis=0)
    routed = embed_codes(my_codes, code_table)
    arrived = arrived.reshape(leaving.shape)
    brought = jnp.take(arrived, jnp.clip(source_dev, 0, per_group - 1), axis=0)
    carried = jnp.where(moved[:, None, None], brought, states)
    return decode(
        routed,
        carried,
        up_weight,
        up_bias,
        conv_weight,
        conv_bias,
        res_in_weight,
        res_in_bias,
        res_out_weight,
        res_out_bias,
    )


def solution(mesh):
    in_specs = (
        P(("grp", "dev"), None),
        P(),
        P(("grp", "dev")),
        P(("grp", "dev")),
        P(("grp", "dev"), None, None),
        P(),
        P(),
        P(),
        P(),
        P(),
        P(),
        P(),
        P(),
    )
    out_specs = (P(("grp", "dev"), None, None), P(("grp", "dev"), None, None))
    return jax.shard_map(local, mesh=mesh, in_specs=in_specs, out_specs=out_specs, check_vma=False)
```

```python
import jax
import jax.numpy as jnp
from jax import lax
from jax.experimental import pallas as pl
from jax.experimental.pallas import tpu as pltpu
from jax.sharding import PartitionSpec as P

FRAMES = 4
MOST = 2


def embed_codes(codes, code_table):
    row_count = codes.shape[0]
    book_count = codes.shape[1] // FRAMES
    book_size = code_table.shape[0] // book_count
    grouped = codes.reshape(row_count * FRAMES, book_count)
    entries = jnp.arange(book_size, dtype=jnp.int32)
    summed = jnp.zeros((row_count * FRAMES, code_table.shape[1]), jnp.float32)
    for book_index in range(book_count):
        onehot = (grouped[:, book_index][:, None] == entries[None, :]).astype(jnp.bfloat16)
        book_rows = code_table[book_index * book_size : (book_index + 1) * book_size]
        summed = summed + jnp.dot(onehot, book_rows, preferred_element_type=jnp.float32)
    summed = lax.reduce_precision(summed, exponent_bits=8, mantissa_bits=7)
    return summed.astype(jnp.bfloat16).reshape(row_count, FRAMES, code_table.shape[1])


def pick_rows(table, index, live):
    entries = jnp.arange(table.shape[0], dtype=jnp.int32)
    select = (index[:, None] == entries[None, :]) & live[:, None]
    if table.dtype == jnp.bfloat16:
        return jnp.dot(
            select.astype(jnp.bfloat16), table, preferred_element_type=jnp.float32
        ).astype(jnp.bfloat16)
    if table.dtype == jnp.int32:
        picked = jnp.dot(
            select.astype(jnp.float32), table.astype(jnp.float32), precision=lax.Precision.HIGHEST
        )
        return picked.astype(jnp.int32)
    return jnp.dot(select.astype(jnp.float32), table, precision=lax.Precision.HIGHEST)


def prefix_count(flags):
    width = flags.shape[-1]
    positions = jnp.arange(width, dtype=jnp.int32)
    upper = (positions[:, None] <= positions[None, :]).astype(jnp.float32)
    return jnp.dot(flags.astype(jnp.float32), upper).astype(jnp.int32)


def compact(flags, ranks, values, slots):
    spots = jnp.arange(slots, dtype=jnp.int32)
    hit = flags[..., None, :] & (ranks[..., None, :] == spots[:, None])
    picked = jnp.sum(jnp.where(hit, values[..., None, :], 0), axis=-1)
    return (picked, jnp.any(hit, axis=-1))


def exchange(items, collective_id):
    groups = lax.axis_size("grp")
    per_group = lax.axis_size("dev")
    count = len(items)
    shapes = []
    for blocks, whole in items:
        if whole:
            shapes.append(jax.ShapeDtypeStruct((groups, per_group) + blocks.shape[1:], blocks.dtype))
        else:
            shapes.append(jax.ShapeDtypeStruct(blocks.shape, blocks.dtype))
    wholes = [index for index, (_, whole) in enumerate(items) if whole]

    def kernel(*refs):
        x_refs = refs[:count]
        o_refs = refs[count : 2 * count]
        mid_refs = dict(zip(wholes, refs[2 * count : 2 * count + len(wholes)]))
        sems = refs[2 * count + len(wholes) :]
        first_send, first_recv, second_send, second_recv, own_sem = sems
        group = lax.axis_index("grp")
        dev = lax.axis_index("dev")
        barrier = pltpu.get_barrier_semaphore()
        across = len(wholes) > 0

        if across:
            def greet_group(offset, carry):
                peer = lax.rem(group + offset, groups)
                pl.semaphore_signal(barrier, inc=1, device_id=(peer, dev), device_id_type=pl.DeviceIdType.MESH)
                return carry

            lax.fori_loop(1, groups, greet_group, 0)

        def greet_dev(offset, carry):
            peer = lax.rem(dev + offset, per_group)
            pl.semaphore_signal(barrier, inc=1, device_id=(group, peer), device_id_type=pl.DeviceIdType.MESH)
            return carry

        lax.fori_loop(1, per_group, greet_dev, 0)
        pl.semaphore_wait(barrier, (groups - 1 if across else 0) + per_group - 1)

        def hop_one(slot, index, peer, place):
            return pltpu.make_async_remote_copy(
                src_ref=x_refs[index].at[pl.ds(peer * per_group, per_group)],
                dst_ref=mid_refs[index].at[place],
                send_sem=first_send.at[slot, peer],
                recv_sem=first_recv.at[slot, place],
                device_id=(peer, dev),
                device_id_type=pl.DeviceIdType.MESH,
            )

        def hop_two(index, peer, place):
            if items[index][1]:
                source = mid_refs[index].at[:, peer]
                target = o_refs[index].at[:, place]
            else:
                source = x_refs[index].at[peer]
                target = o_refs[index].at[place]
            return pltpu.make_async_remote_copy(
                src_ref=source,
                dst_ref=target,
                send_sem=second_send.at[index, peer],
                recv_sem=second_recv.at[index, place],
                device_id=(group, peer),
                device_id_type=pl.DeviceIdType.MESH,
            )

        for slot, index in enumerate(wholes):
            def send_one(offset, carry, slot=slot, index=index):
                hop_one(slot, index, lax.rem(group + offset, groups), group).start()
                return carry

            lax.fori_loop(1, groups, send_one, 0)
        for index, (_, whole) in enumerate(items):
            if not whole:
                def send_group(offset, carry, index=index):
                    hop_two(index, lax.rem(dev + offset, per_group), dev).start()
                    return carry

                lax.fori_loop(1, per_group, send_group, 0)
        for slot, index in enumerate(wholes):
            own = pltpu.make_async_copy(
                x_refs[index].at[pl.ds(group * per_group, per_group)], mid_refs[index].at[group], own_sem
            )
            own.start()
            own.wait()

            def finish_one(offset, carry, slot=slot, index=index):
                hop_one(slot, index, lax.rem(group + offset, groups), group).wait_send()
                source = lax.rem(group + groups - offset, groups)
                hop_one(slot, index, source, source).wait_recv()
                return carry

            lax.fori_loop(1, groups, finish_one, 0)

            def send_two(offset, carry, index=index):
                hop_two(index, lax.rem(dev + offset, per_group), dev).start()
                return carry

            lax.fori_loop(1, per_group, send_two, 0)
        for index, (_, whole) in enumerate(items):
            if whole:
                own = pltpu.make_async_copy(mid_refs[index].at[:, dev], o_refs[index].at[:, dev], own_sem)
            else:
                own = pltpu.make_async_copy(x_refs[index].at[dev], o_refs[index].at[dev], own_sem)
            own.start()
            own.wait()

            def finish_two(offset, carry, index=index):
                hop_two(index, lax.rem(dev + offset, per_group), dev).wait_send()
                source = lax.rem(dev + per_group - offset, per_group)
                hop_two(index, source, source).wait_recv()
                return carry

            lax.fori_loop(1, per_group, finish_two, 0)

    mids = [shapes[index] for index in wholes]
    results = pl.pallas_call(
        kernel,
        out_shape=shapes + mids,
        in_specs=[pl.BlockSpec(memory_space=pl.ANY)] * count,
        out_specs=[pl.BlockSpec(memory_space=pl.ANY)] * (count + len(wholes)),
        scratch_shapes=[
            pltpu.SemaphoreType.DMA((max(len(wholes), 1), groups)),
            pltpu.SemaphoreType.DMA((max(len(wholes), 1), groups)),
            pltpu.SemaphoreType.DMA((count, per_group)),
            pltpu.SemaphoreType.DMA((count, per_group)),
            pltpu.SemaphoreType.DMA(()),
        ],
        compiler_params=pltpu.CompilerParams(collective_id=collective_id, has_side_effects=True),
    )(*[blocks for blocks, _ in items])
    return [
        result.reshape(blocks.shape) for result, (blocks, _) in zip(results[:count], items)
    ]


def decode(
    routed,
    carried,
    up_weight,
    up_bias,
    conv_weight,
    conv_bias,
    res_in_weight,
    res_in_bias,
    res_out_weight,
    res_out_bias,
):
    conv_count, frame_count, chan_width = routed.shape
    step_count = 2 * frame_count
    inputs = routed.astype(jnp.float32)
    tap_zero = inputs * up_weight[0]
    tap_one = inputs * up_weight[1]
    tap_two = inputs * up_weight[2]
    tap_three = inputs * up_weight[3]
    early_even = jnp.concatenate([carried[:, 0:1], tap_two[:, :-1]], axis=1)
    early_odd = jnp.concatenate([carried[:, 1:2], tap_three[:, :-1]], axis=1)
    upsampled = (
        jnp.stack([tap_zero + early_even, tap_one + early_odd], axis=2).reshape(
            conv_count, step_count, chan_width
        )
        + up_bias
    )
    history = jnp.concatenate([carried[:, 2:8], upsampled], axis=1).astype(jnp.bfloat16)
    conv_out = jnp.zeros((conv_count * step_count, chan_width), jnp.float32) + conv_bias
    for tap_index in range(7):
        window = history[:, 6 - tap_index : 6 - tap_index + step_count].reshape(
            conv_count * step_count, chan_width
        )
        conv_out = conv_out + jnp.dot(
            window, conv_weight[tap_index], preferred_element_type=jnp.float32
        )
    active = jax.nn.elu(conv_out).reshape(conv_count, step_count, chan_width)
    res_history = jnp.concatenate([carried[:, 8:10], active], axis=1)
    res_rounded = res_history.astype(jnp.bfloat16)
    res_inner = (
        jnp.zeros((conv_count * step_count, res_in_weight.shape[2]), jnp.float32) + res_in_bias
    )
    for tap_index in range(3):
        window = res_rounded[:, 2 - tap_index : 2 - tap_index + step_count].reshape(
            conv_count * step_count, chan_width
        )
        res_inner = res_inner + jnp.dot(
            window, res_in_weight[tap_index], preferred_element_type=jnp.float32
        )
    squeezed = jax.nn.elu(res_inner).astype(jnp.bfloat16)
    summed = (
        conv_out
        + jnp.dot(squeezed, res_out_weight, preferred_element_type=jnp.float32)
        + res_out_bias
    )
    decoded = summed.astype(jnp.bfloat16).reshape(conv_count, step_count, chan_width)
    new_states = jnp.concatenate(
        [
            tap_two[:, -1:],
            tap_three[:, -1:],
            history[:, -6:].astype(jnp.float32),
            res_history[:, -2:],
        ],
        axis=1,
    )
    return (decoded, new_states)


def local(
    codes,
    code_table,
    roster,
    old_slot,
    states,
    up_weight,
    up_bias,
    conv_weight,
    conv_bias,
    res_in_weight,
    res_in_bias,
    res_out_weight,
    res_out_bias,
):
    conv_count = roster.shape[0]
    per_group = lax.axis_size("dev")
    devices_all = lax.axis_size("grp") * per_group
    most = MOST
    group_first = lax.axis_index("grp") * per_group
    local_index = lax.axis_index("dev")
    positions = jnp.arange(conv_count, dtype=jnp.int32)
    earlier = positions[None, :] < positions[:, None]

    code_width = codes.shape[1]
    gathered = lax.all_gather(
        jnp.concatenate([codes, old_slot[:, None]], axis=1).astype(jnp.float32),
        ("grp", "dev"),
        axis=0,
        tiled=True,
    )
    every_code = gathered[:, :code_width]
    slot_table = lax.dynamic_slice_in_dim(gathered[:, code_width], group_first * conv_count, per_group * conv_count)
    my_codes = jnp.take(every_code, roster, axis=0).astype(jnp.int32)
    routed = embed_codes(my_codes, code_table)

    source_dev = old_slot // conv_count - group_first
    moved = source_dev != local_index
    slot_table = slot_table.astype(jnp.int32).reshape(per_group, conv_count)
    from_me = (slot_table // conv_count - group_first == local_index) & (
        jnp.arange(per_group, dtype=jnp.int32)[:, None] != local_index
    )
    asked_rows = jnp.sum(jnp.where(from_me, slot_table % conv_count, 0), axis=1)
    leaving = jnp.take(states, asked_rows, axis=0)
    (arrived,) = exchange([(leaving.reshape(per_group, -1, 128), False)], 0)
    arrived = arrived.reshape(leaving.shape)
    brought = jnp.take(arrived, jnp.clip(source_dev, 0, per_group - 1), axis=0)
    carried = jnp.where(moved[:, None, None], brought, states)
    return decode(
        routed,
        carried,
        up_weight,
        up_bias,
        conv_weight,
        conv_bias,
        res_in_weight,
        res_in_bias,
        res_out_weight,
        res_out_bias,
    )


def solution(mesh):
    in_specs = (
        P(("grp", "dev"), None),
        P(),
        P(("grp", "dev")),
        P(("grp", "dev")),
        P(("grp", "dev"), None, None),
        P(),
        P(),
        P(),
        P(),
        P(),
        P(),
        P(),
        P(),
    )
    out_specs = (P(("grp", "dev"), None, None), P(("grp", "dev"), None, None))
    return jax.shard_map(local, mesh=mesh, in_specs=in_specs, out_specs=out_specs, check_vma=False)
```

```python
import jax
import jax.numpy as jnp
from jax import lax
from jax.experimental import pallas as pl
from jax.experimental.pallas import tpu as pltpu
from jax.sharding import PartitionSpec as P

FRAMES = 4
MOST = 2


def embed_codes(codes, code_table):
    row_count = codes.shape[0]
    book_count = codes.shape[1] // FRAMES
    book_size = code_table.shape[0] // book_count
    grouped = codes.reshape(row_count * FRAMES, book_count)
    entries = jnp.arange(book_size, dtype=jnp.int32)
    summed = jnp.zeros((row_count * FRAMES, code_table.shape[1]), jnp.float32)
    for book_index in range(book_count):
        onehot = (grouped[:, book_index][:, None] == entries[None, :]).astype(jnp.bfloat16)
        book_rows = code_table[book_index * book_size : (book_index + 1) * book_size]
        summed = summed + jnp.dot(onehot, book_rows, preferred_element_type=jnp.float32)
    summed = lax.reduce_precision(summed, exponent_bits=8, mantissa_bits=7)
    return summed.astype(jnp.bfloat16).reshape(row_count, FRAMES, code_table.shape[1])


def pick_rows(table, index, live):
    entries = jnp.arange(table.shape[0], dtype=jnp.int32)
    select = (index[:, None] == entries[None, :]) & live[:, None]
    if table.dtype == jnp.bfloat16:
        return jnp.dot(
            select.astype(jnp.bfloat16), table, preferred_element_type=jnp.float32
        ).astype(jnp.bfloat16)
    if table.dtype == jnp.int32:
        picked = jnp.dot(
            select.astype(jnp.float32), table.astype(jnp.float32), precision=lax.Precision.HIGHEST
        )
        return picked.astype(jnp.int32)
    return jnp.dot(select.astype(jnp.float32), table, precision=lax.Precision.HIGHEST)


def prefix_count(flags):
    width = flags.shape[-1]
    positions = jnp.arange(width, dtype=jnp.int32)
    upper = (positions[:, None] <= positions[None, :]).astype(jnp.float32)
    return jnp.dot(flags.astype(jnp.float32), upper).astype(jnp.int32)


def compact(flags, ranks, values, slots):
    spots = jnp.arange(slots, dtype=jnp.int32)
    hit = flags[..., None, :] & (ranks[..., None, :] == spots[:, None])
    picked = jnp.sum(jnp.where(hit, values[..., None, :], 0), axis=-1)
    return (picked, jnp.any(hit, axis=-1))


def exchange(items, collective_id):
    groups = lax.axis_size("grp")
    per_group = lax.axis_size("dev")
    count = len(items)
    shapes = []
    for blocks, whole in items:
        if whole:
            shapes.append(jax.ShapeDtypeStruct((groups, per_group) + blocks.shape[1:], blocks.dtype))
        else:
            shapes.append(jax.ShapeDtypeStruct(blocks.shape, blocks.dtype))
    wholes = [index for index, (_, whole) in enumerate(items) if whole]

    def kernel(*refs):
        x_refs = refs[:count]
        o_refs = refs[count : 2 * count]
        mid_refs = dict(zip(wholes, refs[2 * count : 2 * count + len(wholes)]))
        sems = refs[2 * count + len(wholes) :]
        first_send, first_recv, second_send, second_recv, own_sem = sems
        group = lax.axis_index("grp")
        dev = lax.axis_index("dev")
        barrier = pltpu.get_barrier_semaphore()
        across = len(wholes) > 0

        if across:
            def greet_group(offset, carry):
                peer = lax.rem(group + offset, groups)
                pl.semaphore_signal(barrier, inc=1, device_id=(peer, dev), device_id_type=pl.DeviceIdType.MESH)
                return carry

            lax.fori_loop(1, groups, greet_group, 0)

        def greet_dev(offset, carry):
            peer = lax.rem(dev + offset, per_group)
            pl.semaphore_signal(barrier, inc=1, device_id=(group, peer), device_id_type=pl.DeviceIdType.MESH)
            return carry

        lax.fori_loop(1, per_group, greet_dev, 0)
        pl.semaphore_wait(barrier, (groups - 1 if across else 0) + per_group - 1)

        def hop_one(slot, index, peer, place):
            return pltpu.make_async_remote_copy(
                src_ref=x_refs[index].at[pl.ds(peer * per_group, per_group)],
                dst_ref=mid_refs[index].at[place],
                send_sem=first_send.at[slot, peer],
                recv_sem=first_recv.at[slot, place],
                device_id=(peer, dev),
                device_id_type=pl.DeviceIdType.MESH,
            )

        def hop_two(index, peer, place):
            if items[index][1]:
                source = mid_refs[index].at[:, peer]
                target = o_refs[index].at[:, place]
            else:
                source = x_refs[index].at[peer]
                target = o_refs[index].at[place]
            return pltpu.make_async_remote_copy(
                src_ref=source,
                dst_ref=target,
                send_sem=second_send.at[index, peer],
                recv_sem=second_recv.at[index, place],
                device_id=(group, peer),
                device_id_type=pl.DeviceIdType.MESH,
            )

        for slot, index in enumerate(wholes):
            def send_one(offset, carry, slot=slot, index=index):
                hop_one(slot, index, lax.rem(group + offset, groups), group).start()
                return carry

            lax.fori_loop(1, groups, send_one, 0)
        for index, (_, whole) in enumerate(items):
            if not whole:
                def send_group(offset, carry, index=index):
                    hop_two(index, lax.rem(dev + offset, per_group), dev).start()
                    return carry

                lax.fori_loop(1, per_group, send_group, 0)
        for slot, index in enumerate(wholes):
            own = pltpu.make_async_copy(
                x_refs[index].at[pl.ds(group * per_group, per_group)], mid_refs[index].at[group], own_sem
            )
            own.start()
            own.wait()

            def finish_one(offset, carry, slot=slot, index=index):
                hop_one(slot, index, lax.rem(group + offset, groups), group).wait_send()
                source = lax.rem(group + groups - offset, groups)
                hop_one(slot, index, source, source).wait_recv()
                return carry

            lax.fori_loop(1, groups, finish_one, 0)

            def send_two(offset, carry, index=index):
                hop_two(index, lax.rem(dev + offset, per_group), dev).start()
                return carry

            lax.fori_loop(1, per_group, send_two, 0)
        for index, (_, whole) in enumerate(items):
            if whole:
                own = pltpu.make_async_copy(mid_refs[index].at[:, dev], o_refs[index].at[:, dev], own_sem)
            else:
                own = pltpu.make_async_copy(x_refs[index].at[dev], o_refs[index].at[dev], own_sem)
            own.start()
            own.wait()

            def finish_two(offset, carry, index=index):
                hop_two(index, lax.rem(dev + offset, per_group), dev).wait_send()
                source = lax.rem(dev + per_group - offset, per_group)
                hop_two(index, source, source).wait_recv()
                return carry

            lax.fori_loop(1, per_group, finish_two, 0)

    mids = [shapes[index] for index in wholes]
    results = pl.pallas_call(
        kernel,
        out_shape=shapes + mids,
        in_specs=[pl.BlockSpec(memory_space=pl.ANY)] * count,
        out_specs=[pl.BlockSpec(memory_space=pl.ANY)] * (count + len(wholes)),
        scratch_shapes=[
            pltpu.SemaphoreType.DMA((max(len(wholes), 1), groups)),
            pltpu.SemaphoreType.DMA((max(len(wholes), 1), groups)),
            pltpu.SemaphoreType.DMA((count, per_group)),
            pltpu.SemaphoreType.DMA((count, per_group)),
            pltpu.SemaphoreType.DMA(()),
        ],
        compiler_params=pltpu.CompilerParams(collective_id=collective_id, has_side_effects=True),
    )(*[blocks for blocks, _ in items])
    return [
        result.reshape(blocks.shape) for result, (blocks, _) in zip(results[:count], items)
    ]


def decode_kernel(
    routed_ref, carried_ref, up_w_ref, up_b_ref, conv_w_ref, conv_b_ref, in_w_ref, in_b_ref, out_w_ref, out_b_ref,
    decoded_ref, states_ref,
):
    slots, frame_count, _ = routed_ref.shape
    step_count = 2 * frame_count
    conv_taps = conv_w_ref.shape[0]
    res_taps = in_w_ref.shape[0]
    kept = carried_ref.shape[1] - 2 - (res_taps - 1)

    def elu(value):
        return jnp.where(value > 0, value, jnp.exp(jnp.minimum(value, 0.0)) - 1.0)

    up_w = up_w_ref[...]
    up_b = up_b_ref[...]
    inputs = [routed_ref[:, f, :].astype(jnp.float32) for f in range(frame_count)]
    carried = [carried_ref[:, r, :] for r in range(carried_ref.shape[1])]
    upsampled = []
    for f in range(frame_count):
        early_even = carried[0] if f == 0 else inputs[f - 1] * up_w[2:3]
        early_odd = carried[1] if f == 0 else inputs[f - 1] * up_w[3:4]
        upsampled.append((inputs[f] * up_w[0:1] + early_even) + up_b)
        upsampled.append((inputs[f] * up_w[1:2] + early_odd) + up_b)
    history = jnp.concatenate(
        [c.astype(jnp.bfloat16) for c in carried[2 : 2 + kept]] + [u.astype(jnp.bfloat16) for u in upsampled], axis=0
    )
    conv_out = None
    for tap in range(conv_taps):
        start = (conv_taps - 1 - tap) * slots
        term = jnp.dot(history[start : start + step_count * slots], conv_w_ref[tap], preferred_element_type=jnp.float32)
        conv_out = term if conv_out is None else conv_out + term
    conv_out = conv_out + conv_b_ref[...]
    active = elu(conv_out)
    res_rounded = jnp.concatenate(
        [c.astype(jnp.bfloat16) for c in carried[2 + kept :]] + [active.astype(jnp.bfloat16)], axis=0
    )
    inner = None
    for tap in range(res_taps):
        start = (res_taps - 1 - tap) * slots
        term = jnp.dot(res_rounded[start : start + step_count * slots], in_w_ref[tap], preferred_element_type=jnp.float32)
        inner = term if inner is None else inner + term
    squeezed = elu(inner + in_b_ref[...]).astype(jnp.bfloat16)
    summed = conv_out + jnp.dot(squeezed, out_w_ref[...], preferred_element_type=jnp.float32) + out_b_ref[...]
    decoded = summed.astype(jnp.bfloat16)
    for t in range(step_count):
        decoded_ref[:, t, :] = decoded[t * slots : (t + 1) * slots]
    states_ref[:, 0, :] = inputs[frame_count - 1] * up_w[2:3]
    states_ref[:, 1, :] = inputs[frame_count - 1] * up_w[3:4]
    tail = history.shape[0] // slots - kept
    for k in range(kept):
        row = history.shape[0] // slots - kept + k
        states_ref[:, 2 + k, :] = history[row * slots : (row + 1) * slots].astype(jnp.float32)
    for k in range(res_taps - 1):
        row = step_count - (res_taps - 1) + k
        states_ref[:, 2 + kept + k, :] = active[row * slots : (row + 1) * slots]


def decode(routed, carried, up_weight, up_bias, conv_weight, conv_bias, res_in_weight, res_in_bias, res_out_weight, res_out_bias):
    conv_count, frame_count, chan_width = routed.shape
    rows = carried.shape[1]
    chunk = 32 if conv_count % 32 == 0 else conv_count
    whole = lambda shape: pl.BlockSpec(shape, lambda i: (0,) * len(shape))
    return pl.pallas_call(
        decode_kernel,
        grid=(conv_count // chunk,),
        out_shape=(
            jax.ShapeDtypeStruct((conv_count, 2 * frame_count, chan_width), jnp.bfloat16),
            jax.ShapeDtypeStruct((conv_count, rows, chan_width), jnp.float32),
        ),
        in_specs=[
            pl.BlockSpec((chunk, frame_count, chan_width), lambda i: (i, 0, 0)),
            pl.BlockSpec((chunk, rows, chan_width), lambda i: (i, 0, 0)),
            whole(up_weight.shape),
            whole((1, chan_width)),
            whole(conv_weight.shape),
            whole((1, chan_width)),
            whole(res_in_weight.shape),
            whole((1, res_in_weight.shape[2])),
            whole(res_out_weight.shape),
            whole((1, chan_width)),
        ],
        out_specs=(
            pl.BlockSpec((chunk, 2 * frame_count, chan_width), lambda i: (i, 0, 0)),
            pl.BlockSpec((chunk, rows, chan_width), lambda i: (i, 0, 0)),
        ),
        compiler_params=pltpu.CompilerParams(vmem_limit_bytes=48 * 1024 * 1024),
    )(
        routed, carried, up_weight, up_bias.reshape(1, -1), conv_weight, conv_bias.reshape(1, -1),
        res_in_weight, res_in_bias.reshape(1, -1), res_out_weight, res_out_bias.reshape(1, -1),
    )


def local(
    codes,
    code_table,
    roster,
    old_slot,
    states,
    up_weight,
    up_bias,
    conv_weight,
    conv_bias,
    res_in_weight,
    res_in_bias,
    res_out_weight,
    res_out_bias,
):
    conv_count = roster.shape[0]
    per_group = lax.axis_size("dev")
    devices_all = lax.axis_size("grp") * per_group
    most = MOST
    group_first = lax.axis_index("grp") * per_group
    local_index = lax.axis_index("dev")
    positions = jnp.arange(conv_count, dtype=jnp.int32)
    earlier = positions[None, :] < positions[:, None]

    anchor = roster // conv_count
    row = roster % conv_count
    rank_in = jnp.sum(earlier & (anchor[None, :] == anchor[:, None]), axis=1).astype(jnp.int32)
    key = anchor * most + rank_in
    spots = jnp.arange(devices_all * most, dtype=jnp.int32)
    code_request = jnp.sum(jnp.where(key[None, :] == spots[:, None], row[None, :] + 1, 0), axis=1) - 1
    source_dev = old_slot // conv_count - group_first
    source_row = old_slot % conv_count
    moved = source_dev != local_index
    everyone = jnp.arange(devices_all, dtype=jnp.int32)
    state_request = (
        jnp.sum(
            jnp.where(
                moved[None, :] & (source_dev[None, :] + group_first == everyone[:, None]),
                source_row[None, :] + 1,
                0,
            ),
            axis=1,
        )
        - 1
    )
    request = jnp.concatenate(
        [code_request.reshape(devices_all, most), state_request.reshape(devices_all, 1)], axis=1
    )
    lanes = 128
    padded = jnp.zeros((devices_all, 1, lanes), jnp.int32).at[:, 0, : most + 1].set(request)
    (asked,) = exchange([(padded, True)], 0)
    asked = asked[:, 0, : most + 1]

    answer = jnp.take(codes, jnp.clip(asked[:, :most].reshape(-1), 0, conv_count - 1), axis=0)
    answer = jnp.zeros((devices_all, 1, lanes), jnp.int32).at[:, 0, : answer.size // devices_all].set(
        answer.reshape(devices_all, -1)
    )
    state_asked = lax.dynamic_slice_in_dim(asked[:, most], group_first, per_group)
    leaving = jnp.take(states, jnp.clip(state_asked, 0, conv_count - 1), axis=0)
    answered, arrived = exchange(
        [(answer, True), (leaving.reshape(per_group, -1, lanes), False)], 1
    )
    code_width = codes.shape[1]
    answered = answered[:, 0, : most * code_width].reshape(devices_all * most, code_width)
    my_codes = jnp.take(answered, key, axis=0)
    routed = embed_codes(my_codes, code_table)
    arrived = arrived.reshape(leaving.shape)
    brought = jnp.take(arrived, jnp.clip(source_dev, 0, per_group - 1), axis=0)
    carried = jnp.where(moved[:, None, None], brought, states)
    return decode(
        routed,
        carried,
        up_weight,
        up_bias,
        conv_weight,
        conv_bias,
        res_in_weight,
        res_in_bias,
        res_out_weight,
        res_out_bias,
    )


def solution(mesh):
    in_specs = (
        P(("grp", "dev"), None),
        P(),
        P(("grp", "dev")),
        P(("grp", "dev")),
        P(("grp", "dev"), None, None),
        P(),
        P(),
        P(),
        P(),
        P(),
        P(),
        P(),
        P(),
    )
    out_specs = (P(("grp", "dev"), None, None), P(("grp", "dev"), None, None))
    return jax.shard_map(local, mesh=mesh, in_specs=in_specs, out_specs=out_specs, check_vma=False)
```

```python
import jax
import jax.numpy as jnp
from jax import lax
from jax.experimental import pallas as pl
from jax.experimental.pallas import tpu as pltpu
from jax.sharding import PartitionSpec as P

FRAMES = 4
MOST = 2


def embed_codes(codes, code_table):
    row_count = codes.shape[0]
    book_count = codes.shape[1] // FRAMES
    book_size = code_table.shape[0] // book_count
    grouped = codes.reshape(row_count * FRAMES, book_count)
    entries = jnp.arange(book_size, dtype=jnp.int32)
    summed = jnp.zeros((row_count * FRAMES, code_table.shape[1]), jnp.float32)
    for book_index in range(book_count):
        onehot = (grouped[:, book_index][:, None] == entries[None, :]).astype(jnp.bfloat16)
        book_rows = code_table[book_index * book_size : (book_index + 1) * book_size]
        summed = summed + jnp.dot(onehot, book_rows, preferred_element_type=jnp.float32)
    summed = lax.reduce_precision(summed, exponent_bits=8, mantissa_bits=7)
    return summed.astype(jnp.bfloat16).reshape(row_count, FRAMES, code_table.shape[1])


def pick_rows(table, index, live):
    entries = jnp.arange(table.shape[0], dtype=jnp.int32)
    select = (index[:, None] == entries[None, :]) & live[:, None]
    if table.dtype == jnp.bfloat16:
        return jnp.dot(
            select.astype(jnp.bfloat16), table, preferred_element_type=jnp.float32
        ).astype(jnp.bfloat16)
    if table.dtype == jnp.int32:
        picked = jnp.dot(
            select.astype(jnp.float32), table.astype(jnp.float32), precision=lax.Precision.HIGHEST
        )
        return picked.astype(jnp.int32)
    return jnp.dot(select.astype(jnp.float32), table, precision=lax.Precision.HIGHEST)


def prefix_count(flags):
    width = flags.shape[-1]
    positions = jnp.arange(width, dtype=jnp.int32)
    upper = (positions[:, None] <= positions[None, :]).astype(jnp.float32)
    return jnp.dot(flags.astype(jnp.float32), upper).astype(jnp.int32)


def compact(flags, ranks, values, slots):
    spots = jnp.arange(slots, dtype=jnp.int32)
    hit = flags[..., None, :] & (ranks[..., None, :] == spots[:, None])
    picked = jnp.sum(jnp.where(hit, values[..., None, :], 0), axis=-1)
    return (picked, jnp.any(hit, axis=-1))


def exchange(items, collective_id):
    groups = lax.axis_size("grp")
    per_group = lax.axis_size("dev")
    count = len(items)
    shapes = []
    for blocks, whole in items:
        if whole:
            shapes.append(jax.ShapeDtypeStruct((groups, per_group) + blocks.shape[1:], blocks.dtype))
        else:
            shapes.append(jax.ShapeDtypeStruct(blocks.shape, blocks.dtype))
    wholes = [index for index, (_, whole) in enumerate(items) if whole]

    def kernel(*refs):
        x_refs = refs[:count]
        o_refs = refs[count : 2 * count]
        mid_refs = dict(zip(wholes, refs[2 * count : 2 * count + len(wholes)]))
        sems = refs[2 * count + len(wholes) :]
        first_send, first_recv, second_send, second_recv, own_sem = sems
        group = lax.axis_index("grp")
        dev = lax.axis_index("dev")
        barrier = pltpu.get_barrier_semaphore()
        across = len(wholes) > 0

        if across:
            def greet_group(offset, carry):
                peer = lax.rem(group + offset, groups)
                pl.semaphore_signal(barrier, inc=1, device_id=(peer, dev), device_id_type=pl.DeviceIdType.MESH)
                return carry

            lax.fori_loop(1, groups, greet_group, 0)

        def greet_dev(offset, carry):
            peer = lax.rem(dev + offset, per_group)
            pl.semaphore_signal(barrier, inc=1, device_id=(group, peer), device_id_type=pl.DeviceIdType.MESH)
            return carry

        lax.fori_loop(1, per_group, greet_dev, 0)
        pl.semaphore_wait(barrier, (groups - 1 if across else 0) + per_group - 1)

        def hop_one(slot, index, peer, place):
            return pltpu.make_async_remote_copy(
                src_ref=x_refs[index].at[pl.ds(peer * per_group, per_group)],
                dst_ref=mid_refs[index].at[place],
                send_sem=first_send.at[slot, peer],
                recv_sem=first_recv.at[slot, place],
                device_id=(peer, dev),
                device_id_type=pl.DeviceIdType.MESH,
            )

        def hop_two(index, peer, place):
            if items[index][1]:
                source = mid_refs[index].at[:, peer]
                target = o_refs[index].at[:, place]
            else:
                source = x_refs[index].at[peer]
                target = o_refs[index].at[place]
            return pltpu.make_async_remote_copy(
                src_ref=source,
                dst_ref=target,
                send_sem=second_send.at[index, peer],
                recv_sem=second_recv.at[index, place],
                device_id=(group, peer),
                device_id_type=pl.DeviceIdType.MESH,
            )

        for slot, index in enumerate(wholes):
            def send_one(offset, carry, slot=slot, index=index):
                hop_one(slot, index, lax.rem(group + offset, groups), group).start()
                return carry

            lax.fori_loop(1, groups, send_one, 0)
        for index, (_, whole) in enumerate(items):
            if not whole:
                def send_group(offset, carry, index=index):
                    hop_two(index, lax.rem(dev + offset, per_group), dev).start()
                    return carry

                lax.fori_loop(1, per_group, send_group, 0)
        for slot, index in enumerate(wholes):
            own = pltpu.make_async_copy(
                x_refs[index].at[pl.ds(group * per_group, per_group)], mid_refs[index].at[group], own_sem
            )
            own.start()
            own.wait()

            def finish_one(offset, carry, slot=slot, index=index):
                hop_one(slot, index, lax.rem(group + offset, groups), group).wait_send()
                source = lax.rem(group + groups - offset, groups)
                hop_one(slot, index, source, source).wait_recv()
                return carry

            lax.fori_loop(1, groups, finish_one, 0)

            def send_two(offset, carry, index=index):
                hop_two(index, lax.rem(dev + offset, per_group), dev).start()
                return carry

            lax.fori_loop(1, per_group, send_two, 0)
        for index, (_, whole) in enumerate(items):
            if whole:
                own = pltpu.make_async_copy(mid_refs[index].at[:, dev], o_refs[index].at[:, dev], own_sem)
            else:
                own = pltpu.make_async_copy(x_refs[index].at[dev], o_refs[index].at[dev], own_sem)
            own.start()
            own.wait()

            def finish_two(offset, carry, index=index):
                hop_two(index, lax.rem(dev + offset, per_group), dev).wait_send()
                source = lax.rem(dev + per_group - offset, per_group)
                hop_two(index, source, source).wait_recv()
                return carry

            lax.fori_loop(1, per_group, finish_two, 0)

    mids = [shapes[index] for index in wholes]
    results = pl.pallas_call(
        kernel,
        out_shape=shapes + mids,
        in_specs=[pl.BlockSpec(memory_space=pl.ANY)] * count,
        out_specs=[pl.BlockSpec(memory_space=pl.ANY)] * (count + len(wholes)),
        scratch_shapes=[
            pltpu.SemaphoreType.DMA((max(len(wholes), 1), groups)),
            pltpu.SemaphoreType.DMA((max(len(wholes), 1), groups)),
            pltpu.SemaphoreType.DMA((count, per_group)),
            pltpu.SemaphoreType.DMA((count, per_group)),
            pltpu.SemaphoreType.DMA(()),
        ],
        compiler_params=pltpu.CompilerParams(collective_id=collective_id, has_side_effects=True),
    )(*[blocks for blocks, _ in items])
    return [
        result.reshape(blocks.shape) for result, (blocks, _) in zip(results[:count], items)
    ]


def decode_kernel(
    source_ref, moved_ref,
    routed_ref, states_ref, arrived_ref, up_w_ref, up_b_ref, conv_w_ref, conv_b_ref, in_w_ref, in_b_ref, out_w_ref,
    out_b_ref, decoded_ref, new_ref, carried_ref,
):
    slots, frame_count, _ = routed_ref.shape
    step_count = 2 * frame_count
    rows = states_ref.shape[0]
    conv_taps = conv_w_ref.shape[0]
    res_taps = in_w_ref.shape[0]
    kept = rows - 2 - (res_taps - 1)
    base = pl.program_id(0) * slots

    carried_ref[...] = states_ref[...]

    def bring(slot, carry):
        @pl.when(moved_ref[base + slot] != 0)
        def _():
            source = source_ref[base + slot]
            for r in range(rows):
                carried_ref[r, pl.ds(slot, 1), :] = arrived_ref[source, pl.ds(r, 1), :]

        return carry

    lax.fori_loop(0, slots, bring, 0)

    def elu(value):
        return jnp.where(value > 0, value, jnp.exp(jnp.minimum(value, 0.0)) - 1.0)

    up_w = up_w_ref[...]
    up_b = up_b_ref[...]
    inputs = [routed_ref[:, f, :].astype(jnp.float32) for f in range(frame_count)]
    carried = [carried_ref[r] for r in range(rows)]
    upsampled = []
    for f in range(frame_count):
        early_even = carried[0] if f == 0 else inputs[f - 1] * up_w[2:3]
        early_odd = carried[1] if f == 0 else inputs[f - 1] * up_w[3:4]
        upsampled.append((inputs[f] * up_w[0:1] + early_even) + up_b)
        upsampled.append((inputs[f] * up_w[1:2] + early_odd) + up_b)
    history = jnp.concatenate(
        [c.astype(jnp.bfloat16) for c in carried[2 : 2 + kept]] + [u.astype(jnp.bfloat16) for u in upsampled], axis=0
    )
    conv_out = None
    for tap in range(conv_taps):
        start = (conv_taps - 1 - tap) * slots
        term = jnp.dot(history[start : start + step_count * slots], conv_w_ref[tap], preferred_element_type=jnp.float32)
        conv_out = term if conv_out is None else conv_out + term
    conv_out = conv_out + conv_b_ref[...]
    active = elu(conv_out)
    res_rounded = jnp.concatenate(
        [c.astype(jnp.bfloat16) for c in carried[2 + kept :]] + [active.astype(jnp.bfloat16)], axis=0
    )
    inner = None
    for tap in range(res_taps):
        start = (res_taps - 1 - tap) * slots
        term = jnp.dot(res_rounded[start : start + step_count * slots], in_w_ref[tap], preferred_element_type=jnp.float32)
        inner = term if inner is None else inner + term
    squeezed = elu(inner + in_b_ref[...]).astype(jnp.bfloat16)
    summed = conv_out + jnp.dot(squeezed, out_w_ref[...], preferred_element_type=jnp.float32) + out_b_ref[...]
    decoded = summed.astype(jnp.bfloat16)
    for t in range(step_count):
        decoded_ref[:, t, :] = decoded[t * slots : (t + 1) * slots]
    new_ref[0] = inputs[frame_count - 1] * up_w[2:3]
    new_ref[1] = inputs[frame_count - 1] * up_w[3:4]
    for k in range(kept):
        row = history.shape[0] // slots - kept + k
        new_ref[2 + k] = history[row * slots : (row + 1) * slots].astype(jnp.float32)
    for k in range(res_taps - 1):
        row = step_count - (res_taps - 1) + k
        new_ref[2 + kept + k] = active[row * slots : (row + 1) * slots]


def decode(
    routed, states, arrived, source, moved, up_weight, up_bias, conv_weight, conv_bias, res_in_weight, res_in_bias,
    res_out_weight, res_out_bias,
):
    conv_count, frame_count, chan_width = routed.shape
    rows = states.shape[1]
    chunk = 32 if conv_count % 32 == 0 else conv_count
    whole = lambda shape: pl.BlockSpec(shape, lambda i, *_: (0,) * len(shape))
    states_t = jnp.transpose(states, (1, 0, 2))
    decoded, new_t = pl.pallas_call(
        decode_kernel,
        grid_spec=pltpu.PrefetchScalarGridSpec(
            num_scalar_prefetch=2,
            grid=(conv_count // chunk,),
            in_specs=[
                pl.BlockSpec((chunk, frame_count, chan_width), lambda i, *_: (i, 0, 0)),
                pl.BlockSpec((rows, chunk, chan_width), lambda i, *_: (0, i, 0)),
                whole(arrived.shape),
                whole(up_weight.shape),
                whole((1, chan_width)),
                whole(conv_weight.shape),
                whole((1, chan_width)),
                whole(res_in_weight.shape),
                whole((1, res_in_weight.shape[2])),
                whole(res_out_weight.shape),
                whole((1, chan_width)),
            ],
            out_specs=(
                pl.BlockSpec((chunk, 2 * frame_count, chan_width), lambda i, *_: (i, 0, 0)),
                pl.BlockSpec((rows, chunk, chan_width), lambda i, *_: (0, i, 0)),
            ),
            scratch_shapes=[pltpu.VMEM((rows, chunk, chan_width), jnp.float32)],
        ),
        out_shape=(
            jax.ShapeDtypeStruct((conv_count, 2 * frame_count, chan_width), jnp.bfloat16),
            jax.ShapeDtypeStruct((rows, conv_count, chan_width), jnp.float32),
        ),
        compiler_params=pltpu.CompilerParams(vmem_limit_bytes=48 * 1024 * 1024),
    )(
        source, moved, routed, states_t, arrived, up_weight, up_bias.reshape(1, -1), conv_weight,
        conv_bias.reshape(1, -1), res_in_weight, res_in_bias.reshape(1, -1), res_out_weight, res_out_bias.reshape(1, -1),
    )
    return decoded, jnp.transpose(new_t, (1, 0, 2))


def local(
    codes,
    code_table,
    roster,
    old_slot,
    states,
    up_weight,
    up_bias,
    conv_weight,
    conv_bias,
    res_in_weight,
    res_in_bias,
    res_out_weight,
    res_out_bias,
):
    conv_count = roster.shape[0]
    per_group = lax.axis_size("dev")
    devices_all = lax.axis_size("grp") * per_group
    most = MOST
    group_first = lax.axis_index("grp") * per_group
    local_index = lax.axis_index("dev")
    positions = jnp.arange(conv_count, dtype=jnp.int32)
    earlier = positions[None, :] < positions[:, None]

    anchor = roster // conv_count
    row = roster % conv_count
    rank_in = jnp.sum(earlier & (anchor[None, :] == anchor[:, None]), axis=1).astype(jnp.int32)
    key = anchor * most + rank_in
    spots = jnp.arange(devices_all * most, dtype=jnp.int32)
    code_request = jnp.sum(jnp.where(key[None, :] == spots[:, None], row[None, :] + 1, 0), axis=1) - 1
    source_dev = old_slot // conv_count - group_first
    source_row = old_slot % conv_count
    moved = source_dev != local_index
    everyone = jnp.arange(devices_all, dtype=jnp.int32)
    state_request = (
        jnp.sum(
            jnp.where(
                moved[None, :] & (source_dev[None, :] + group_first == everyone[:, None]),
                source_row[None, :] + 1,
                0,
            ),
            axis=1,
        )
        - 1
    )
    request = jnp.concatenate(
        [code_request.reshape(devices_all, most), state_request.reshape(devices_all, 1)], axis=1
    )
    lanes = 128
    padded = jnp.zeros((devices_all, 1, lanes), jnp.int32).at[:, 0, : most + 1].set(request)
    (asked,) = exchange([(padded, True)], 0)
    asked = asked[:, 0, : most + 1]

    answer = jnp.take(codes, jnp.clip(asked[:, :most].reshape(-1), 0, conv_count - 1), axis=0)
    answer = jnp.zeros((devices_all, 1, lanes), jnp.int32).at[:, 0, : answer.size // devices_all].set(
        answer.reshape(devices_all, -1)
    )
    state_asked = lax.dynamic_slice_in_dim(asked[:, most], group_first, per_group)
    leaving = jnp.take(states, jnp.clip(state_asked, 0, conv_count - 1), axis=0)
    answered, arrived = exchange(
        [(answer, True), (leaving.reshape(per_group, -1, lanes), False)], 1
    )
    code_width = codes.shape[1]
    answered = answered[:, 0, : most * code_width].reshape(devices_all * most, code_width)
    my_codes = jnp.take(answered, key, axis=0)
    routed = embed_codes(my_codes, code_table)
    arrived = arrived.reshape(leaving.shape)
    return decode(
        routed,
        states,
        arrived,
        jnp.clip(source_dev, 0, per_group - 1),
        moved.astype(jnp.int32),
        up_weight,
        up_bias,
        conv_weight,
        conv_bias,
        res_in_weight,
        res_in_bias,
        res_out_weight,
        res_out_bias,
    )


def solution(mesh):
    in_specs = (
        P(("grp", "dev"), None),
        P(),
        P(("grp", "dev")),
        P(("grp", "dev")),
        P(("grp", "dev"), None, None),
        P(),
        P(),
        P(),
        P(),
        P(),
        P(),
        P(),
        P(),
    )
    out_specs = (P(("grp", "dev"), None, None), P(("grp", "dev"), None, None))
    return jax.shard_map(local, mesh=mesh, in_specs=in_specs, out_specs=out_specs, check_vma=False)
```

```python
import jax
import jax.numpy as jnp
from jax import lax
from jax.experimental import pallas as pl
from jax.experimental.pallas import tpu as pltpu
from jax.sharding import PartitionSpec as P

FRAMES = 4
MOST = 2


def embed_kernel(codes_ref, table_ref, out_ref, total_ref):
    book = pl.program_id(0)

    @pl.when(book == 0)
    def _():
        total_ref[...] = jnp.zeros_like(total_ref)

    rows = codes_ref.shape[1]
    entries = lax.broadcasted_iota(jnp.int32, (rows, table_ref.shape[0]), 1)
    onehot = (codes_ref[0] == entries).astype(jnp.bfloat16)
    total_ref[...] += jnp.dot(onehot, table_ref[...], preferred_element_type=jnp.float32)

    @pl.when(book == pl.num_programs(0) - 1)
    def _():
        out_ref[...] = total_ref[...].astype(jnp.bfloat16)


def embed_codes(codes, code_table):
    row_count = codes.shape[0]
    book_count = codes.shape[1] // FRAMES
    book_size = code_table.shape[0] // book_count
    chan_width = code_table.shape[1]
    by_book = codes.reshape(row_count, FRAMES, book_count).transpose(2, 1, 0).reshape(book_count, -1, 1)
    rows = FRAMES * row_count
    summed = pl.pallas_call(
        embed_kernel,
        grid=(book_count,),
        in_specs=[
            pl.BlockSpec((1, rows, 1), lambda q: (q, 0, 0)),
            pl.BlockSpec((book_size, chan_width), lambda q: (q, 0)),
        ],
        out_specs=pl.BlockSpec((rows, chan_width), lambda q: (0, 0)),
        out_shape=jax.ShapeDtypeStruct((rows, chan_width), jnp.bfloat16),
        scratch_shapes=[pltpu.VMEM((rows, chan_width), jnp.float32)],
        compiler_params=pltpu.CompilerParams(vmem_limit_bytes=32 * 1024 * 1024),
    )(by_book, code_table)
    return summed.reshape(FRAMES, row_count, chan_width)


def pick_rows(table, index, live):
    entries = jnp.arange(table.shape[0], dtype=jnp.int32)
    select = (index[:, None] == entries[None, :]) & live[:, None]
    if table.dtype == jnp.bfloat16:
        return jnp.dot(
            select.astype(jnp.bfloat16), table, preferred_element_type=jnp.float32
        ).astype(jnp.bfloat16)
    if table.dtype == jnp.int32:
        picked = jnp.dot(
            select.astype(jnp.float32), table.astype(jnp.float32), precision=lax.Precision.HIGHEST
        )
        return picked.astype(jnp.int32)
    return jnp.dot(select.astype(jnp.float32), table, precision=lax.Precision.HIGHEST)


def prefix_count(flags):
    width = flags.shape[-1]
    positions = jnp.arange(width, dtype=jnp.int32)
    upper = (positions[:, None] <= positions[None, :]).astype(jnp.float32)
    return jnp.dot(flags.astype(jnp.float32), upper).astype(jnp.int32)


def compact(flags, ranks, values, slots):
    spots = jnp.arange(slots, dtype=jnp.int32)
    hit = flags[..., None, :] & (ranks[..., None, :] == spots[:, None])
    picked = jnp.sum(jnp.where(hit, values[..., None, :], 0), axis=-1)
    return (picked, jnp.any(hit, axis=-1))


def exchange(items, collective_id):
    groups = lax.axis_size("grp")
    per_group = lax.axis_size("dev")
    count = len(items)
    shapes = []
    for blocks, whole in items:
        if whole:
            shapes.append(jax.ShapeDtypeStruct((groups, per_group) + blocks.shape[1:], blocks.dtype))
        else:
            shapes.append(jax.ShapeDtypeStruct(blocks.shape, blocks.dtype))
    wholes = [index for index, (_, whole) in enumerate(items) if whole]

    def kernel(*refs):
        x_refs = refs[:count]
        o_refs = refs[count : 2 * count]
        mid_refs = dict(zip(wholes, refs[2 * count : 2 * count + len(wholes)]))
        sems = refs[2 * count + len(wholes) :]
        first_send, first_recv, second_send, second_recv, own_sem = sems
        group = lax.axis_index("grp")
        dev = lax.axis_index("dev")
        barrier = pltpu.get_barrier_semaphore()
        across = len(wholes) > 0

        if across:
            def greet_group(offset, carry):
                peer = lax.rem(group + offset, groups)
                pl.semaphore_signal(barrier, inc=1, device_id=(peer, dev), device_id_type=pl.DeviceIdType.MESH)
                return carry

            lax.fori_loop(1, groups, greet_group, 0)

        def greet_dev(offset, carry):
            peer = lax.rem(dev + offset, per_group)
            pl.semaphore_signal(barrier, inc=1, device_id=(group, peer), device_id_type=pl.DeviceIdType.MESH)
            return carry

        lax.fori_loop(1, per_group, greet_dev, 0)
        pl.semaphore_wait(barrier, (groups - 1 if across else 0) + per_group - 1)

        def hop_one(slot, index, peer, place):
            return pltpu.make_async_remote_copy(
                src_ref=x_refs[index].at[pl.ds(peer * per_group, per_group)],
                dst_ref=mid_refs[index].at[place],
                send_sem=first_send.at[slot, peer],
                recv_sem=first_recv.at[slot, place],
                device_id=(peer, dev),
                device_id_type=pl.DeviceIdType.MESH,
            )

        def hop_two(index, peer, place):
            if items[index][1]:
                source = mid_refs[index].at[:, peer]
                target = o_refs[index].at[:, place]
            else:
                source = x_refs[index].at[peer]
                target = o_refs[index].at[place]
            return pltpu.make_async_remote_copy(
                src_ref=source,
                dst_ref=target,
                send_sem=second_send.at[index, peer],
                recv_sem=second_recv.at[index, place],
                device_id=(group, peer),
                device_id_type=pl.DeviceIdType.MESH,
            )

        for slot, index in enumerate(wholes):
            def send_one(offset, carry, slot=slot, index=index):
                hop_one(slot, index, lax.rem(group + offset, groups), group).start()
                return carry

            lax.fori_loop(1, groups, send_one, 0)
        for index, (_, whole) in enumerate(items):
            if not whole:
                def send_group(offset, carry, index=index):
                    hop_two(index, lax.rem(dev + offset, per_group), dev).start()
                    return carry

                lax.fori_loop(1, per_group, send_group, 0)
        for slot, index in enumerate(wholes):
            own = pltpu.make_async_copy(
                x_refs[index].at[pl.ds(group * per_group, per_group)], mid_refs[index].at[group], own_sem
            )
            own.start()
            own.wait()

            def finish_one(offset, carry, slot=slot, index=index):
                hop_one(slot, index, lax.rem(group + offset, groups), group).wait_send()
                source = lax.rem(group + groups - offset, groups)
                hop_one(slot, index, source, source).wait_recv()
                return carry

            lax.fori_loop(1, groups, finish_one, 0)

            def send_two(offset, carry, index=index):
                hop_two(index, lax.rem(dev + offset, per_group), dev).start()
                return carry

            lax.fori_loop(1, per_group, send_two, 0)
        for index, (_, whole) in enumerate(items):
            if whole:
                own = pltpu.make_async_copy(mid_refs[index].at[:, dev], o_refs[index].at[:, dev], own_sem)
            else:
                own = pltpu.make_async_copy(x_refs[index].at[dev], o_refs[index].at[dev], own_sem)
            own.start()
            own.wait()

            def finish_two(offset, carry, index=index):
                hop_two(index, lax.rem(dev + offset, per_group), dev).wait_send()
                source = lax.rem(dev + per_group - offset, per_group)
                hop_two(index, source, source).wait_recv()
                return carry

            lax.fori_loop(1, per_group, finish_two, 0)

    mids = [shapes[index] for index in wholes]
    results = pl.pallas_call(
        kernel,
        out_shape=shapes + mids,
        in_specs=[pl.BlockSpec(memory_space=pl.ANY)] * count,
        out_specs=[pl.BlockSpec(memory_space=pl.ANY)] * (count + len(wholes)),
        scratch_shapes=[
            pltpu.SemaphoreType.DMA((max(len(wholes), 1), groups)),
            pltpu.SemaphoreType.DMA((max(len(wholes), 1), groups)),
            pltpu.SemaphoreType.DMA((count, per_group)),
            pltpu.SemaphoreType.DMA((count, per_group)),
            pltpu.SemaphoreType.DMA(()),
        ],
        compiler_params=pltpu.CompilerParams(collective_id=collective_id, has_side_effects=True),
    )(*[blocks for blocks, _ in items])
    return [
        result.reshape(blocks.shape) for result, (blocks, _) in zip(results[:count], items)
    ]


def decode_kernel(
    source_ref, moved_ref,
    routed_ref, states_ref, arrived_ref, up_w_ref, up_b_ref, conv_w_ref, conv_b_ref, in_w_ref, in_b_ref, out_w_ref,
    out_b_ref, decoded_ref, new_ref, carried_ref,
):
    frame_count, slots, _ = routed_ref.shape
    step_count = 2 * frame_count
    rows = states_ref.shape[0]
    conv_taps = conv_w_ref.shape[0]
    res_taps = in_w_ref.shape[0]
    kept = rows - 2 - (res_taps - 1)
    base = pl.program_id(0) * slots

    carried_ref[...] = states_ref[...]

    def bring(slot, carry):
        @pl.when(moved_ref[base + slot] != 0)
        def _():
            source = source_ref[base + slot]
            for r in range(rows):
                carried_ref[r, pl.ds(slot, 1), :] = arrived_ref[source, pl.ds(r, 1), :]

        return carry

    lax.fori_loop(0, slots, bring, 0)

    def elu(value):
        return jnp.where(value > 0, value, jnp.exp(jnp.minimum(value, 0.0)) - 1.0)

    up_w = up_w_ref[...]
    up_b = up_b_ref[...]
    inputs = [routed_ref[f].astype(jnp.float32) for f in range(frame_count)]
    carried = [carried_ref[r] for r in range(rows)]
    upsampled = []
    for f in range(frame_count):
        early_even = carried[0] if f == 0 else inputs[f - 1] * up_w[2:3]
        early_odd = carried[1] if f == 0 else inputs[f - 1] * up_w[3:4]
        upsampled.append((inputs[f] * up_w[0:1] + early_even) + up_b)
        upsampled.append((inputs[f] * up_w[1:2] + early_odd) + up_b)
    history = jnp.concatenate(
        [c.astype(jnp.bfloat16) for c in carried[2 : 2 + kept]] + [u.astype(jnp.bfloat16) for u in upsampled], axis=0
    )
    conv_out = None
    for tap in range(conv_taps):
        start = (conv_taps - 1 - tap) * slots
        term = jnp.dot(history[start : start + step_count * slots], conv_w_ref[tap], preferred_element_type=jnp.float32)
        conv_out = term if conv_out is None else conv_out + term
    conv_out = conv_out + conv_b_ref[...]
    active = elu(conv_out)
    res_rounded = jnp.concatenate(
        [c.astype(jnp.bfloat16) for c in carried[2 + kept :]] + [active.astype(jnp.bfloat16)], axis=0
    )
    inner = None
    for tap in range(res_taps):
        start = (res_taps - 1 - tap) * slots
        term = jnp.dot(res_rounded[start : start + step_count * slots], in_w_ref[tap], preferred_element_type=jnp.float32)
        inner = term if inner is None else inner + term
    squeezed = elu(inner + in_b_ref[...]).astype(jnp.bfloat16)
    summed = conv_out + jnp.dot(squeezed, out_w_ref[...], preferred_element_type=jnp.float32) + out_b_ref[...]
    decoded = summed.astype(jnp.bfloat16)
    for t in range(step_count):
        decoded_ref[:, t, :] = decoded[t * slots : (t + 1) * slots]
    new_ref[0] = inputs[frame_count - 1] * up_w[2:3]
    new_ref[1] = inputs[frame_count - 1] * up_w[3:4]
    for k in range(kept):
        row = history.shape[0] // slots - kept + k
        new_ref[2 + k] = history[row * slots : (row + 1) * slots].astype(jnp.float32)
    for k in range(res_taps - 1):
        row = step_count - (res_taps - 1) + k
        new_ref[2 + kept + k] = active[row * slots : (row + 1) * slots]


def decode(
    routed, states, arrived, source, moved, up_weight, up_bias, conv_weight, conv_bias, res_in_weight, res_in_bias,
    res_out_weight, res_out_bias,
):
    frame_count, conv_count, chan_width = routed.shape
    rows = states.shape[1]
    chunk = 32 if conv_count % 32 == 0 else conv_count
    whole = lambda shape: pl.BlockSpec(shape, lambda i, *_: (0,) * len(shape))
    states_t = jnp.transpose(states, (1, 0, 2))
    decoded, new_t = pl.pallas_call(
        decode_kernel,
        grid_spec=pltpu.PrefetchScalarGridSpec(
            num_scalar_prefetch=2,
            grid=(conv_count // chunk,),
            in_specs=[
                pl.BlockSpec((frame_count, chunk, chan_width), lambda i, *_: (0, i, 0)),
                pl.BlockSpec((rows, chunk, chan_width), lambda i, *_: (0, i, 0)),
                whole(arrived.shape),
                whole(up_weight.shape),
                whole((1, chan_width)),
                whole(conv_weight.shape),
                whole((1, chan_width)),
                whole(res_in_weight.shape),
                whole((1, res_in_weight.shape[2])),
                whole(res_out_weight.shape),
                whole((1, chan_width)),
            ],
            out_specs=(
                pl.BlockSpec((chunk, 2 * frame_count, chan_width), lambda i, *_: (i, 0, 0)),
                pl.BlockSpec((rows, chunk, chan_width), lambda i, *_: (0, i, 0)),
            ),
            scratch_shapes=[pltpu.VMEM((rows, chunk, chan_width), jnp.float32)],
        ),
        out_shape=(
            jax.ShapeDtypeStruct((conv_count, 2 * frame_count, chan_width), jnp.bfloat16),
            jax.ShapeDtypeStruct((rows, conv_count, chan_width), jnp.float32),
        ),
        compiler_params=pltpu.CompilerParams(vmem_limit_bytes=48 * 1024 * 1024),
    )(
        source, moved, routed, states_t, arrived, up_weight, up_bias.reshape(1, -1), conv_weight,
        conv_bias.reshape(1, -1), res_in_weight, res_in_bias.reshape(1, -1), res_out_weight, res_out_bias.reshape(1, -1),
    )
    return decoded, jnp.transpose(new_t, (1, 0, 2))


def local(
    codes,
    code_table,
    roster,
    old_slot,
    states,
    up_weight,
    up_bias,
    conv_weight,
    conv_bias,
    res_in_weight,
    res_in_bias,
    res_out_weight,
    res_out_bias,
):
    conv_count = roster.shape[0]
    per_group = lax.axis_size("dev")
    devices_all = lax.axis_size("grp") * per_group
    most = MOST
    group_first = lax.axis_index("grp") * per_group
    local_index = lax.axis_index("dev")
    positions = jnp.arange(conv_count, dtype=jnp.int32)
    earlier = positions[None, :] < positions[:, None]

    anchor = roster // conv_count
    row = roster % conv_count
    rank_in = jnp.sum(earlier & (anchor[None, :] == anchor[:, None]), axis=1).astype(jnp.int32)
    key = anchor * most + rank_in
    spots = jnp.arange(devices_all * most, dtype=jnp.int32)
    code_request = jnp.sum(jnp.where(key[None, :] == spots[:, None], row[None, :] + 1, 0), axis=1) - 1
    source_dev = old_slot // conv_count - group_first
    source_row = old_slot % conv_count
    moved = source_dev != local_index
    everyone = jnp.arange(devices_all, dtype=jnp.int32)
    state_request = (
        jnp.sum(
            jnp.where(
                moved[None, :] & (source_dev[None, :] + group_first == everyone[:, None]),
                source_row[None, :] + 1,
                0,
            ),
            axis=1,
        )
        - 1
    )
    request = jnp.concatenate(
        [code_request.reshape(devices_all, most), state_request.reshape(devices_all, 1)], axis=1
    )
    lanes = 128
    padded = jnp.zeros((devices_all, 1, lanes), jnp.int32).at[:, 0, : most + 1].set(request)
    (asked,) = exchange([(padded, True)], 0)
    asked = asked[:, 0, : most + 1]

    answer = jnp.take(codes, jnp.clip(asked[:, :most].reshape(-1), 0, conv_count - 1), axis=0)
    answer = jnp.zeros((devices_all, 1, lanes), jnp.int32).at[:, 0, : answer.size // devices_all].set(
        answer.reshape(devices_all, -1)
    )
    state_asked = lax.dynamic_slice_in_dim(asked[:, most], group_first, per_group)
    leaving = jnp.take(states, jnp.clip(state_asked, 0, conv_count - 1), axis=0)
    answered, arrived = exchange(
        [(answer, True), (leaving.reshape(per_group, -1, lanes), False)], 1
    )
    code_width = codes.shape[1]
    answered = answered[:, 0, : most * code_width].reshape(devices_all * most, code_width)
    my_codes = jnp.take(answered, key, axis=0)
    routed = embed_codes(my_codes, code_table)
    arrived = arrived.reshape(leaving.shape)
    return decode(
        routed,
        states,
        arrived,
        jnp.clip(source_dev, 0, per_group - 1),
        moved.astype(jnp.int32),
        up_weight,
        up_bias,
        conv_weight,
        conv_bias,
        res_in_weight,
        res_in_bias,
        res_out_weight,
        res_out_bias,
    )


def solution(mesh):
    in_specs = (
        P(("grp", "dev"), None),
        P(),
        P(("grp", "dev")),
        P(("grp", "dev")),
        P(("grp", "dev"), None, None),
        P(),
        P(),
        P(),
        P(),
        P(),
        P(),
        P(),
        P(),
    )
    out_specs = (P(("grp", "dev"), None, None), P(("grp", "dev"), None, None))
    return jax.shard_map(local, mesh=mesh, in_specs=in_specs, out_specs=out_specs, check_vma=False)
```

```python
import jax
import jax.numpy as jnp
from jax import lax
from jax.experimental import pallas as pl
from jax.experimental.pallas import tpu as pltpu
from jax.sharding import PartitionSpec as P

FRAMES = 4
MOST = 2


def embed_kernel(codes_ref, table_ref, out_ref, blocks, sems):
    books, rows = codes_ref.shape
    size = blocks.shape[1]

    def fetch(book):
        return pltpu.make_async_copy(table_ref.at[pl.ds(book * size, size)], blocks.at[book % 2], sems.at[book % 2])

    fetch(0).start()
    total = None
    for book in range(books):
        if book + 1 < books:
            fetch(book + 1).start()
        fetch(book).wait()
        entries = lax.broadcasted_iota(jnp.int32, (size, rows), 0)
        onehot = (codes_ref[book : book + 1, :] == entries).astype(jnp.bfloat16)
        term = lax.dot_general(
            onehot, blocks[book % 2], (((0,), (0,)), ((), ())), preferred_element_type=jnp.float32
        )
        total = term if total is None else total + term
    out_ref[...] = total.astype(jnp.bfloat16)


def embed_codes(codes, code_table):
    row_count = codes.shape[0]
    book_count = codes.shape[1] // FRAMES
    book_size = code_table.shape[0] // book_count
    chan_width = code_table.shape[1]
    by_book = codes.reshape(row_count, FRAMES, book_count).transpose(2, 1, 0).reshape(book_count, -1)
    rows = FRAMES * row_count
    summed = pl.pallas_call(
        embed_kernel,
        in_specs=[pl.BlockSpec(memory_space=pltpu.VMEM), pl.BlockSpec(memory_space=pl.ANY)],
        out_specs=pl.BlockSpec(memory_space=pltpu.VMEM),
        out_shape=jax.ShapeDtypeStruct((rows, chan_width), jnp.bfloat16),
        scratch_shapes=[
            pltpu.VMEM((2, book_size, chan_width), code_table.dtype),
            pltpu.SemaphoreType.DMA((2,)),
        ],
    )(by_book, code_table)
    return summed.reshape(FRAMES, row_count, chan_width)


def pick_rows(table, index, live):
    entries = jnp.arange(table.shape[0], dtype=jnp.int32)
    select = (index[:, None] == entries[None, :]) & live[:, None]
    if table.dtype == jnp.bfloat16:
        return jnp.dot(
            select.astype(jnp.bfloat16), table, preferred_element_type=jnp.float32
        ).astype(jnp.bfloat16)
    if table.dtype == jnp.int32:
        picked = jnp.dot(
            select.astype(jnp.float32), table.astype(jnp.float32), precision=lax.Precision.HIGHEST
        )
        return picked.astype(jnp.int32)
    return jnp.dot(select.astype(jnp.float32), table, precision=lax.Precision.HIGHEST)


def prefix_count(flags):
    width = flags.shape[-1]
    positions = jnp.arange(width, dtype=jnp.int32)
    upper = (positions[:, None] <= positions[None, :]).astype(jnp.float32)
    return jnp.dot(flags.astype(jnp.float32), upper).astype(jnp.int32)


def compact(flags, ranks, values, slots):
    spots = jnp.arange(slots, dtype=jnp.int32)
    hit = flags[..., None, :] & (ranks[..., None, :] == spots[:, None])
    picked = jnp.sum(jnp.where(hit, values[..., None, :], 0), axis=-1)
    return (picked, jnp.any(hit, axis=-1))


def exchange(items, collective_id):
    groups = lax.axis_size("grp")
    per_group = lax.axis_size("dev")
    count = len(items)
    shapes = []
    for blocks, whole in items:
        if whole:
            shapes.append(jax.ShapeDtypeStruct((groups, per_group) + blocks.shape[1:], blocks.dtype))
        else:
            shapes.append(jax.ShapeDtypeStruct(blocks.shape, blocks.dtype))
    wholes = [index for index, (_, whole) in enumerate(items) if whole]

    def kernel(*refs):
        x_refs = refs[:count]
        o_refs = refs[count : 2 * count]
        mid_refs = dict(zip(wholes, refs[2 * count : 2 * count + len(wholes)]))
        sems = refs[2 * count + len(wholes) :]
        first_send, first_recv, second_send, second_recv, own_sem = sems
        group = lax.axis_index("grp")
        dev = lax.axis_index("dev")
        barrier = pltpu.get_barrier_semaphore()
        across = len(wholes) > 0

        if across:
            def greet_group(offset, carry):
                peer = lax.rem(group + offset, groups)
                pl.semaphore_signal(barrier, inc=1, device_id=(peer, dev), device_id_type=pl.DeviceIdType.MESH)
                return carry

            lax.fori_loop(1, groups, greet_group, 0)

        def greet_dev(offset, carry):
            peer = lax.rem(dev + offset, per_group)
            pl.semaphore_signal(barrier, inc=1, device_id=(group, peer), device_id_type=pl.DeviceIdType.MESH)
            return carry

        lax.fori_loop(1, per_group, greet_dev, 0)
        pl.semaphore_wait(barrier, (groups - 1 if across else 0) + per_group - 1)

        def hop_one(slot, index, peer, place):
            return pltpu.make_async_remote_copy(
                src_ref=x_refs[index].at[pl.ds(peer * per_group, per_group)],
                dst_ref=mid_refs[index].at[place],
                send_sem=first_send.at[slot, peer],
                recv_sem=first_recv.at[slot, place],
                device_id=(peer, dev),
                device_id_type=pl.DeviceIdType.MESH,
            )

        def hop_two(index, peer, place):
            if items[index][1]:
                source = mid_refs[index].at[:, peer]
                target = o_refs[index].at[:, place]
            else:
                source = x_refs[index].at[peer]
                target = o_refs[index].at[place]
            return pltpu.make_async_remote_copy(
                src_ref=source,
                dst_ref=target,
                send_sem=second_send.at[index, peer],
                recv_sem=second_recv.at[index, place],
                device_id=(group, peer),
                device_id_type=pl.DeviceIdType.MESH,
            )

        for slot, index in enumerate(wholes):
            def send_one(offset, carry, slot=slot, index=index):
                hop_one(slot, index, lax.rem(group + offset, groups), group).start()
                return carry

            lax.fori_loop(1, groups, send_one, 0)
        for index, (_, whole) in enumerate(items):
            if not whole:
                def send_group(offset, carry, index=index):
                    hop_two(index, lax.rem(dev + offset, per_group), dev).start()
                    return carry

                lax.fori_loop(1, per_group, send_group, 0)
        for slot, index in enumerate(wholes):
            own = pltpu.make_async_copy(
                x_refs[index].at[pl.ds(group * per_group, per_group)], mid_refs[index].at[group], own_sem
            )
            own.start()
            own.wait()

            def finish_one(offset, carry, slot=slot, index=index):
                hop_one(slot, index, lax.rem(group + offset, groups), group).wait_send()
                source = lax.rem(group + groups - offset, groups)
                hop_one(slot, index, source, source).wait_recv()
                return carry

            lax.fori_loop(1, groups, finish_one, 0)

            def send_two(offset, carry, index=index):
                hop_two(index, lax.rem(dev + offset, per_group), dev).start()
                return carry

            lax.fori_loop(1, per_group, send_two, 0)
        for index, (_, whole) in enumerate(items):
            if whole:
                own = pltpu.make_async_copy(mid_refs[index].at[:, dev], o_refs[index].at[:, dev], own_sem)
            else:
                own = pltpu.make_async_copy(x_refs[index].at[dev], o_refs[index].at[dev], own_sem)
            own.start()
            own.wait()

            def finish_two(offset, carry, index=index):
                hop_two(index, lax.rem(dev + offset, per_group), dev).wait_send()
                source = lax.rem(dev + per_group - offset, per_group)
                hop_two(index, source, source).wait_recv()
                return carry

            lax.fori_loop(1, per_group, finish_two, 0)

    mids = [shapes[index] for index in wholes]
    results = pl.pallas_call(
        kernel,
        out_shape=shapes + mids,
        in_specs=[pl.BlockSpec(memory_space=pl.ANY)] * count,
        out_specs=[pl.BlockSpec(memory_space=pl.ANY)] * (count + len(wholes)),
        scratch_shapes=[
            pltpu.SemaphoreType.DMA((max(len(wholes), 1), groups)),
            pltpu.SemaphoreType.DMA((max(len(wholes), 1), groups)),
            pltpu.SemaphoreType.DMA((count, per_group)),
            pltpu.SemaphoreType.DMA((count, per_group)),
            pltpu.SemaphoreType.DMA(()),
        ],
        compiler_params=pltpu.CompilerParams(collective_id=collective_id, has_side_effects=True),
        cost_estimate=pl.CostEstimate(flops=0, transcendentals=0, bytes_accessed=48 * 1024 * 1024),
    )(*[blocks for blocks, _ in items])
    return [
        result.reshape(blocks.shape) for result, (blocks, _) in zip(results[:count], items)
    ]


def decode_kernel(
    source_ref, moved_ref,
    routed_ref, states_ref, arrived_ref, up_w_ref, up_b_ref, conv_w_ref, conv_b_ref, in_w_ref, in_b_ref, out_w_ref,
    out_b_ref, decoded_ref, new_ref, carried_ref,
):
    frame_count, slots, _ = routed_ref.shape
    step_count = 2 * frame_count
    rows = states_ref.shape[0]
    conv_taps = conv_w_ref.shape[0]
    res_taps = in_w_ref.shape[0]
    kept = rows - 2 - (res_taps - 1)
    base = pl.program_id(0) * slots

    carried_ref[...] = states_ref[...]

    def bring(slot, carry):
        @pl.when(moved_ref[base + slot] != 0)
        def _():
            source = source_ref[base + slot]
            for r in range(rows):
                carried_ref[r, pl.ds(slot, 1), :] = arrived_ref[source, pl.ds(r, 1), :]

        return carry

    lax.fori_loop(0, slots, bring, 0)

    def elu(value):
        return jnp.where(value > 0, value, jnp.exp(jnp.minimum(value, 0.0)) - 1.0)

    up_w = up_w_ref[...]
    up_b = up_b_ref[...]
    inputs = [routed_ref[f].astype(jnp.float32) for f in range(frame_count)]
    carried = [carried_ref[r] for r in range(rows)]
    upsampled = []
    for f in range(frame_count):
        early_even = carried[0] if f == 0 else inputs[f - 1] * up_w[2:3]
        early_odd = carried[1] if f == 0 else inputs[f - 1] * up_w[3:4]
        upsampled.append((inputs[f] * up_w[0:1] + early_even) + up_b)
        upsampled.append((inputs[f] * up_w[1:2] + early_odd) + up_b)
    history = jnp.concatenate(
        [c.astype(jnp.bfloat16) for c in carried[2 : 2 + kept]] + [u.astype(jnp.bfloat16) for u in upsampled], axis=0
    )
    conv_out = None
    for tap in range(conv_taps):
        start = (conv_taps - 1 - tap) * slots
        term = jnp.dot(history[start : start + step_count * slots], conv_w_ref[tap], preferred_element_type=jnp.float32)
        conv_out = term if conv_out is None else conv_out + term
    conv_out = conv_out + conv_b_ref[...]
    active = elu(conv_out)
    res_rounded = jnp.concatenate(
        [c.astype(jnp.bfloat16) for c in carried[2 + kept :]] + [active.astype(jnp.bfloat16)], axis=0
    )
    inner = None
    for tap in range(res_taps):
        start = (res_taps - 1 - tap) * slots
        term = jnp.dot(res_rounded[start : start + step_count * slots], in_w_ref[tap], preferred_element_type=jnp.float32)
        inner = term if inner is None else inner + term
    squeezed = elu(inner + in_b_ref[...]).astype(jnp.bfloat16)
    summed = conv_out + jnp.dot(squeezed, out_w_ref[...], preferred_element_type=jnp.float32) + out_b_ref[...]
    decoded = summed.astype(jnp.bfloat16)
    for t in range(step_count):
        decoded_ref[:, t, :] = decoded[t * slots : (t + 1) * slots]
    new_ref[0] = inputs[frame_count - 1] * up_w[2:3]
    new_ref[1] = inputs[frame_count - 1] * up_w[3:4]
    for k in range(kept):
        row = history.shape[0] // slots - kept + k
        new_ref[2 + k] = history[row * slots : (row + 1) * slots].astype(jnp.float32)
    for k in range(res_taps - 1):
        row = step_count - (res_taps - 1) + k
        new_ref[2 + kept + k] = active[row * slots : (row + 1) * slots]


def decode(
    routed, states, arrived, source, moved, up_weight, up_bias, conv_weight, conv_bias, res_in_weight, res_in_bias,
    res_out_weight, res_out_bias,
):
    frame_count, conv_count, chan_width = routed.shape
    rows = states.shape[1]
    chunk = 32 if conv_count % 32 == 0 else conv_count
    whole = lambda shape: pl.BlockSpec(shape, lambda i, *_: (0,) * len(shape))
    states_t = jnp.transpose(states, (1, 0, 2))
    decoded, new_t = pl.pallas_call(
        decode_kernel,
        grid_spec=pltpu.PrefetchScalarGridSpec(
            num_scalar_prefetch=2,
            grid=(conv_count // chunk,),
            in_specs=[
                pl.BlockSpec((frame_count, chunk, chan_width), lambda i, *_: (0, i, 0)),
                pl.BlockSpec((rows, chunk, chan_width), lambda i, *_: (0, i, 0)),
                whole(arrived.shape),
                whole(up_weight.shape),
                whole((1, chan_width)),
                whole(conv_weight.shape),
                whole((1, chan_width)),
                whole(res_in_weight.shape),
                whole((1, res_in_weight.shape[2])),
                whole(res_out_weight.shape),
                whole((1, chan_width)),
            ],
            out_specs=(
                pl.BlockSpec((chunk, 2 * frame_count, chan_width), lambda i, *_: (i, 0, 0)),
                pl.BlockSpec((rows, chunk, chan_width), lambda i, *_: (0, i, 0)),
            ),
            scratch_shapes=[pltpu.VMEM((rows, chunk, chan_width), jnp.float32)],
        ),
        out_shape=(
            jax.ShapeDtypeStruct((conv_count, 2 * frame_count, chan_width), jnp.bfloat16),
            jax.ShapeDtypeStruct((rows, conv_count, chan_width), jnp.float32),
        ),
        compiler_params=pltpu.CompilerParams(vmem_limit_bytes=48 * 1024 * 1024),
    )(
        source, moved, routed, states_t, arrived, up_weight, up_bias.reshape(1, -1), conv_weight,
        conv_bias.reshape(1, -1), res_in_weight, res_in_bias.reshape(1, -1), res_out_weight, res_out_bias.reshape(1, -1),
    )
    return decoded, jnp.transpose(new_t, (1, 0, 2))


def local(
    codes,
    code_table,
    roster,
    old_slot,
    states,
    up_weight,
    up_bias,
    conv_weight,
    conv_bias,
    res_in_weight,
    res_in_bias,
    res_out_weight,
    res_out_bias,
):
    conv_count = roster.shape[0]
    per_group = lax.axis_size("dev")
    devices_all = lax.axis_size("grp") * per_group
    most = MOST
    group_first = lax.axis_index("grp") * per_group
    local_index = lax.axis_index("dev")
    positions = jnp.arange(conv_count, dtype=jnp.int32)
    earlier = positions[None, :] < positions[:, None]

    anchor = roster // conv_count
    row = roster % conv_count
    rank_in = jnp.sum(earlier & (anchor[None, :] == anchor[:, None]), axis=1).astype(jnp.int32)
    key = anchor * most + rank_in
    spots = jnp.arange(devices_all * most, dtype=jnp.int32)
    code_request = jnp.sum(jnp.where(key[None, :] == spots[:, None], row[None, :] + 1, 0), axis=1) - 1
    source_dev = old_slot // conv_count - group_first
    source_row = old_slot % conv_count
    moved = source_dev != local_index
    everyone = jnp.arange(devices_all, dtype=jnp.int32)
    state_request = (
        jnp.sum(
            jnp.where(
                moved[None, :] & (source_dev[None, :] + group_first == everyone[:, None]),
                source_row[None, :] + 1,
                0,
            ),
            axis=1,
        )
        - 1
    )
    request = jnp.concatenate(
        [code_request.reshape(devices_all, most), state_request.reshape(devices_all, 1)], axis=1
    )
    lanes = 128
    padded = jnp.zeros((devices_all, 1, lanes), jnp.int32).at[:, 0, : most + 1].set(request)
    (asked,) = exchange([(padded, True)], 0)
    asked = asked[:, 0, : most + 1]

    answer = jnp.take(codes, jnp.clip(asked[:, :most].reshape(-1), 0, conv_count - 1), axis=0)
    answer = jnp.zeros((devices_all, 1, lanes), jnp.int32).at[:, 0, : answer.size // devices_all].set(
        answer.reshape(devices_all, -1)
    )
    state_asked = lax.dynamic_slice_in_dim(asked[:, most], group_first, per_group)
    leaving = jnp.take(states, jnp.clip(state_asked, 0, conv_count - 1), axis=0)
    answered, arrived = exchange(
        [(answer, True), (leaving, False)], 1
    )
    code_width = codes.shape[1]
    answered = answered[:, 0, : most * code_width].reshape(devices_all * most, code_width)
    my_codes = jnp.take(answered, key, axis=0)
    routed = embed_codes(my_codes, code_table)
    return decode(
        routed,
        states,
        arrived,
        jnp.clip(source_dev, 0, per_group - 1),
        moved.astype(jnp.int32),
        up_weight,
        up_bias,
        conv_weight,
        conv_bias,
        res_in_weight,
        res_in_bias,
        res_out_weight,
        res_out_bias,
    )


def solution(mesh):
    in_specs = (
        P(("grp", "dev"), None),
        P(),
        P(("grp", "dev")),
        P(("grp", "dev")),
        P(("grp", "dev"), None, None),
        P(),
        P(),
        P(),
        P(),
        P(),
        P(),
        P(),
        P(),
    )
    out_specs = (P(("grp", "dev"), None, None), P(("grp", "dev"), None, None))
    return jax.shard_map(local, mesh=mesh, in_specs=in_specs, out_specs=out_specs, check_vma=False)
```

```python
import jax
import jax.numpy as jnp
from jax import lax
from jax.experimental import pallas as pl
from jax.experimental.pallas import tpu as pltpu
from jax.sharding import PartitionSpec as P

FRAMES = 4
MOST = 2


def embed_kernel(codes_ref, table_ref, out_ref, blocks, sems):
    books, rows = codes_ref.shape
    size = blocks.shape[1]

    def fetch(book):
        return pltpu.make_async_copy(table_ref.at[pl.ds(book * size, size)], blocks.at[book % 2], sems.at[book % 2])

    fetch(0).start()
    by_row = jnp.transpose(codes_ref[...])
    total = None
    for book in range(books):
        if book + 1 < books:
            fetch(book + 1).start()
        fetch(book).wait()
        entries = lax.broadcasted_iota(jnp.int32, (rows, size), 1)
        onehot = (by_row[:, book : book + 1] == entries).astype(jnp.bfloat16)
        term = jnp.dot(onehot, blocks[book % 2], preferred_element_type=jnp.float32)
        total = term if total is None else total + term
    out_ref[...] = total.astype(jnp.bfloat16)


def embed_codes(codes, code_table):
    row_count = codes.shape[0]
    book_count = codes.shape[1] // FRAMES
    book_size = code_table.shape[0] // book_count
    chan_width = code_table.shape[1]
    by_book = codes.reshape(row_count, FRAMES, book_count).transpose(2, 1, 0).reshape(book_count, -1)
    rows = FRAMES * row_count
    summed = pl.pallas_call(
        embed_kernel,
        in_specs=[pl.BlockSpec(memory_space=pltpu.VMEM), pl.BlockSpec(memory_space=pl.ANY)],
        out_specs=pl.BlockSpec(memory_space=pltpu.VMEM),
        out_shape=jax.ShapeDtypeStruct((rows, chan_width), jnp.bfloat16),
        scratch_shapes=[
            pltpu.VMEM((2, book_size, chan_width), code_table.dtype),
            pltpu.SemaphoreType.DMA((2,)),
        ],
    )(by_book, code_table)
    return summed.reshape(FRAMES, row_count, chan_width)


def pick_rows(table, index, live):
    entries = jnp.arange(table.shape[0], dtype=jnp.int32)
    select = (index[:, None] == entries[None, :]) & live[:, None]
    if table.dtype == jnp.bfloat16:
        return jnp.dot(
            select.astype(jnp.bfloat16), table, preferred_element_type=jnp.float32
        ).astype(jnp.bfloat16)
    if table.dtype == jnp.int32:
        picked = jnp.dot(
            select.astype(jnp.float32), table.astype(jnp.float32), precision=lax.Precision.HIGHEST
        )
        return picked.astype(jnp.int32)
    return jnp.dot(select.astype(jnp.float32), table, precision=lax.Precision.HIGHEST)


def prefix_count(flags):
    width = flags.shape[-1]
    positions = jnp.arange(width, dtype=jnp.int32)
    upper = (positions[:, None] <= positions[None, :]).astype(jnp.float32)
    return jnp.dot(flags.astype(jnp.float32), upper).astype(jnp.int32)


def compact(flags, ranks, values, slots):
    spots = jnp.arange(slots, dtype=jnp.int32)
    hit = flags[..., None, :] & (ranks[..., None, :] == spots[:, None])
    picked = jnp.sum(jnp.where(hit, values[..., None, :], 0), axis=-1)
    return (picked, jnp.any(hit, axis=-1))


def exchange(items, collective_id):
    groups = lax.axis_size("grp")
    per_group = lax.axis_size("dev")
    count = len(items)
    shapes = []
    for blocks, whole in items:
        if whole:
            shapes.append(jax.ShapeDtypeStruct((groups, per_group) + blocks.shape[1:], blocks.dtype))
        else:
            shapes.append(jax.ShapeDtypeStruct(blocks.shape, blocks.dtype))
    wholes = [index for index, (_, whole) in enumerate(items) if whole]

    def kernel(*refs):
        x_refs = refs[:count]
        o_refs = refs[count : 2 * count]
        mid_refs = dict(zip(wholes, refs[2 * count : 2 * count + len(wholes)]))
        sems = refs[2 * count + len(wholes) :]
        first_send, first_recv, second_send, second_recv, own_sem = sems
        group = lax.axis_index("grp")
        dev = lax.axis_index("dev")
        barrier = pltpu.get_barrier_semaphore()
        across = len(wholes) > 0

        if across:
            def greet_group(offset, carry):
                peer = lax.rem(group + offset, groups)
                pl.semaphore_signal(barrier, inc=1, device_id=(peer, dev), device_id_type=pl.DeviceIdType.MESH)
                return carry

            lax.fori_loop(1, groups, greet_group, 0)

        def greet_dev(offset, carry):
            peer = lax.rem(dev + offset, per_group)
            pl.semaphore_signal(barrier, inc=1, device_id=(group, peer), device_id_type=pl.DeviceIdType.MESH)
            return carry

        lax.fori_loop(1, per_group, greet_dev, 0)
        pl.semaphore_wait(barrier, (groups - 1 if across else 0) + per_group - 1)

        def hop_one(slot, index, peer, place):
            return pltpu.make_async_remote_copy(
                src_ref=x_refs[index].at[pl.ds(peer * per_group, per_group)],
                dst_ref=mid_refs[index].at[place],
                send_sem=first_send.at[slot, peer],
                recv_sem=first_recv.at[slot, place],
                device_id=(peer, dev),
                device_id_type=pl.DeviceIdType.MESH,
            )

        def hop_two(index, peer, place):
            if items[index][1]:
                source = mid_refs[index].at[:, peer]
                target = o_refs[index].at[:, place]
            else:
                source = x_refs[index].at[peer]
                target = o_refs[index].at[place]
            return pltpu.make_async_remote_copy(
                src_ref=source,
                dst_ref=target,
                send_sem=second_send.at[index, peer],
                recv_sem=second_recv.at[index, place],
                device_id=(group, peer),
                device_id_type=pl.DeviceIdType.MESH,
            )

        for slot, index in enumerate(wholes):
            def send_one(offset, carry, slot=slot, index=index):
                hop_one(slot, index, lax.rem(group + offset, groups), group).start()
                return carry

            lax.fori_loop(1, groups, send_one, 0)
        for index, (_, whole) in enumerate(items):
            if not whole:
                def send_group(offset, carry, index=index):
                    hop_two(index, lax.rem(dev + offset, per_group), dev).start()
                    return carry

                lax.fori_loop(1, per_group, send_group, 0)
        for slot, index in enumerate(wholes):
            own = pltpu.make_async_copy(
                x_refs[index].at[pl.ds(group * per_group, per_group)], mid_refs[index].at[group], own_sem
            )
            own.start()
            own.wait()

            def finish_one(offset, carry, slot=slot, index=index):
                hop_one(slot, index, lax.rem(group + offset, groups), group).wait_send()
                source = lax.rem(group + groups - offset, groups)
                hop_one(slot, index, source, source).wait_recv()
                return carry

            lax.fori_loop(1, groups, finish_one, 0)

            def send_two(offset, carry, index=index):
                hop_two(index, lax.rem(dev + offset, per_group), dev).start()
                return carry

            lax.fori_loop(1, per_group, send_two, 0)
        for index, (_, whole) in enumerate(items):
            if whole:
                own = pltpu.make_async_copy(mid_refs[index].at[:, dev], o_refs[index].at[:, dev], own_sem)
            else:
                own = pltpu.make_async_copy(x_refs[index].at[dev], o_refs[index].at[dev], own_sem)
            own.start()
            own.wait()

            def finish_two(offset, carry, index=index):
                hop_two(index, lax.rem(dev + offset, per_group), dev).wait_send()
                source = lax.rem(dev + per_group - offset, per_group)
                hop_two(index, source, source).wait_recv()
                return carry

            lax.fori_loop(1, per_group, finish_two, 0)

    mids = [shapes[index] for index in wholes]
    results = pl.pallas_call(
        kernel,
        out_shape=shapes + mids,
        in_specs=[pl.BlockSpec(memory_space=pl.ANY)] * count,
        out_specs=[pl.BlockSpec(memory_space=pl.ANY)] * (count + len(wholes)),
        scratch_shapes=[
            pltpu.SemaphoreType.DMA((max(len(wholes), 1), groups)),
            pltpu.SemaphoreType.DMA((max(len(wholes), 1), groups)),
            pltpu.SemaphoreType.DMA((count, per_group)),
            pltpu.SemaphoreType.DMA((count, per_group)),
            pltpu.SemaphoreType.DMA(()),
        ],
        compiler_params=pltpu.CompilerParams(collective_id=collective_id, has_side_effects=True),
        cost_estimate=pl.CostEstimate(flops=0, transcendentals=0, bytes_accessed=48 * 1024 * 1024),
    )(*[blocks for blocks, _ in items])
    return [
        result.reshape(blocks.shape) for result, (blocks, _) in zip(results[:count], items)
    ]


def decode_kernel(
    source_ref, moved_ref,
    routed_ref, states_ref, arrived_ref, arrived_low_ref, up_w_ref, up_b_ref, conv_w_ref, conv_b_ref, in_w_ref, in_b_ref, out_w_ref,
    out_b_ref, decoded_ref, new_ref, carried_ref,
):
    frame_count, slots, _ = routed_ref.shape
    step_count = 2 * frame_count
    rows = states_ref.shape[0]
    conv_taps = conv_w_ref.shape[0]
    res_taps = in_w_ref.shape[0]
    kept = rows - 2 - (res_taps - 1)
    base = pl.program_id(0) * slots

    carried_ref[...] = states_ref[...]

    def bring(slot, carry):
        @pl.when(moved_ref[base + slot] != 0)
        def _():
            source = source_ref[base + slot]
            pieces = carried_ref.shape[2] // arrived_ref.shape[2]
            for r in range(rows):
                if r < 2:
                    row = arrived_ref[source, pl.ds(r * pieces, pieces), :]
                else:
                    row = arrived_low_ref[source, pl.ds((r - 2) * pieces, pieces), :].astype(jnp.float32)
                carried_ref[r, pl.ds(slot, 1), :] = jnp.concatenate(
                    [row[k : k + 1] for k in range(pieces)], axis=1
                )

        return carry

    lax.fori_loop(0, slots, bring, 0)

    def elu(value):
        return jnp.where(value > 0, value, jnp.exp(jnp.minimum(value, 0.0)) - 1.0)

    up_w = up_w_ref[...]
    up_b = up_b_ref[...]
    inputs = [routed_ref[f].astype(jnp.float32) for f in range(frame_count)]
    carried = [carried_ref[r] for r in range(rows)]
    upsampled = []
    for f in range(frame_count):
        early_even = carried[0] if f == 0 else inputs[f - 1] * up_w[2:3]
        early_odd = carried[1] if f == 0 else inputs[f - 1] * up_w[3:4]
        upsampled.append((inputs[f] * up_w[0:1] + early_even) + up_b)
        upsampled.append((inputs[f] * up_w[1:2] + early_odd) + up_b)
    history = jnp.concatenate(
        [c.astype(jnp.bfloat16) for c in carried[2 : 2 + kept]] + [u.astype(jnp.bfloat16) for u in upsampled], axis=0
    )
    conv_out = None
    for tap in range(conv_taps):
        start = (conv_taps - 1 - tap) * slots
        term = jnp.dot(history[start : start + step_count * slots], conv_w_ref[tap], preferred_element_type=jnp.float32)
        conv_out = term if conv_out is None else conv_out + term
    conv_out = conv_out + conv_b_ref[...]
    active = elu(conv_out)
    res_rounded = jnp.concatenate(
        [c.astype(jnp.bfloat16) for c in carried[2 + kept :]] + [active.astype(jnp.bfloat16)], axis=0
    )
    inner = None
    for tap in range(res_taps):
        start = (res_taps - 1 - tap) * slots
        term = jnp.dot(res_rounded[start : start + step_count * slots], in_w_ref[tap], preferred_element_type=jnp.float32)
        inner = term if inner is None else inner + term
    squeezed = elu(inner + in_b_ref[...]).astype(jnp.bfloat16)
    summed = conv_out + jnp.dot(squeezed, out_w_ref[...], preferred_element_type=jnp.float32) + out_b_ref[...]
    decoded = summed.astype(jnp.bfloat16)
    for t in range(step_count):
        decoded_ref[:, t, :] = decoded[t * slots : (t + 1) * slots]
    new_ref[0] = inputs[frame_count - 1] * up_w[2:3]
    new_ref[1] = inputs[frame_count - 1] * up_w[3:4]
    for k in range(kept):
        row = history.shape[0] // slots - kept + k
        new_ref[2 + k] = history[row * slots : (row + 1) * slots].astype(jnp.float32)
    for k in range(res_taps - 1):
        row = step_count - (res_taps - 1) + k
        new_ref[2 + kept + k] = active[row * slots : (row + 1) * slots]


def decode(
    routed, states, arrived, arrived_low, source, moved, up_weight, up_bias, conv_weight, conv_bias, res_in_weight, res_in_bias,
    res_out_weight, res_out_bias,
):
    frame_count, conv_count, chan_width = routed.shape
    rows = states.shape[1]
    chunk = 32 if conv_count % 32 == 0 else conv_count
    whole = lambda shape: pl.BlockSpec(shape, lambda i, *_: (0,) * len(shape))
    states_t = jnp.transpose(states, (1, 0, 2))
    decoded, new_t = pl.pallas_call(
        decode_kernel,
        grid_spec=pltpu.PrefetchScalarGridSpec(
            num_scalar_prefetch=2,
            grid=(conv_count // chunk,),
            in_specs=[
                pl.BlockSpec((frame_count, chunk, chan_width), lambda i, *_: (0, i, 0)),
                pl.BlockSpec((rows, chunk, chan_width), lambda i, *_: (0, i, 0)),
                whole(arrived.shape),
                whole(arrived_low.shape),
                whole(up_weight.shape),
                whole((1, chan_width)),
                whole(conv_weight.shape),
                whole((1, chan_width)),
                whole(res_in_weight.shape),
                whole((1, res_in_weight.shape[2])),
                whole(res_out_weight.shape),
                whole((1, chan_width)),
            ],
            out_specs=(
                pl.BlockSpec((chunk, 2 * frame_count, chan_width), lambda i, *_: (i, 0, 0)),
                pl.BlockSpec((rows, chunk, chan_width), lambda i, *_: (0, i, 0)),
            ),
            scratch_shapes=[pltpu.VMEM((rows, chunk, chan_width), jnp.float32)],
        ),
        out_shape=(
            jax.ShapeDtypeStruct((conv_count, 2 * frame_count, chan_width), jnp.bfloat16),
            jax.ShapeDtypeStruct((rows, conv_count, chan_width), jnp.float32),
        ),
        compiler_params=pltpu.CompilerParams(vmem_limit_bytes=48 * 1024 * 1024),
    )(
        source, moved, routed, states_t, arrived, arrived_low, up_weight, up_bias.reshape(1, -1), conv_weight,
        conv_bias.reshape(1, -1), res_in_weight, res_in_bias.reshape(1, -1), res_out_weight, res_out_bias.reshape(1, -1),
    )
    return decoded, jnp.transpose(new_t, (1, 0, 2))


def local(
    codes,
    code_table,
    roster,
    old_slot,
    states,
    up_weight,
    up_bias,
    conv_weight,
    conv_bias,
    res_in_weight,
    res_in_bias,
    res_out_weight,
    res_out_bias,
):
    conv_count = roster.shape[0]
    per_group = lax.axis_size("dev")
    devices_all = lax.axis_size("grp") * per_group
    most = MOST
    group_first = lax.axis_index("grp") * per_group
    local_index = lax.axis_index("dev")
    positions = jnp.arange(conv_count, dtype=jnp.int32)
    earlier = positions[None, :] < positions[:, None]

    anchor = roster // conv_count
    row = roster % conv_count
    rank_in = jnp.sum(earlier & (anchor[None, :] == anchor[:, None]), axis=1).astype(jnp.int32)
    key = anchor * most + rank_in
    spots = jnp.arange(devices_all * most, dtype=jnp.int32)
    code_request = jnp.sum(jnp.where(key[None, :] == spots[:, None], row[None, :] + 1, 0), axis=1) - 1
    source_dev = old_slot // conv_count - group_first
    source_row = old_slot % conv_count
    moved = source_dev != local_index
    everyone = jnp.arange(devices_all, dtype=jnp.int32)
    state_request = (
        jnp.sum(
            jnp.where(
                moved[None, :] & (source_dev[None, :] + group_first == everyone[:, None]),
                source_row[None, :] + 1,
                0,
            ),
            axis=1,
        )
        - 1
    )
    request = jnp.concatenate(
        [code_request.reshape(devices_all, most), state_request.reshape(devices_all, 1)], axis=1
    )
    lanes = 128
    padded = jnp.zeros((devices_all, 1, lanes), jnp.int32).at[:, 0, : most + 1].set(request)
    (asked,) = exchange([(padded, True)], 0)
    asked = asked[:, 0, : most + 1]

    answer = jnp.take(codes, jnp.clip(asked[:, :most].reshape(-1), 0, conv_count - 1), axis=0)
    answer = jnp.zeros((devices_all, 1, lanes), jnp.int32).at[:, 0, : answer.size // devices_all].set(
        answer.reshape(devices_all, -1)
    )
    state_asked = lax.dynamic_slice_in_dim(asked[:, most], group_first, per_group)
    leaving = jnp.take(states, jnp.clip(state_asked, 0, conv_count - 1), axis=0)
    leaving_high = leaving[:, :2].reshape(per_group, -1, lanes)
    leaving_low = leaving[:, 2:].astype(jnp.bfloat16).reshape(per_group, -1, lanes)
    answered, arrived, arrived_low = exchange(
        [(answer, True), (leaving_high, False), (leaving_low, False)], 1
    )
    code_width = codes.shape[1]
    answered = answered[:, 0, : most * code_width].reshape(devices_all * most, code_width)
    my_codes = jnp.take(answered, key, axis=0)
    routed = embed_codes(my_codes, code_table)
    return decode(
        routed,
        states,
        arrived,
        arrived_low,
        jnp.clip(source_dev, 0, per_group - 1),
        moved.astype(jnp.int32),
        up_weight,
        up_bias,
        conv_weight,
        conv_bias,
        res_in_weight,
        res_in_bias,
        res_out_weight,
        res_out_bias,
    )


def solution(mesh):
    in_specs = (
        P(("grp", "dev"), None),
        P(),
        P(("grp", "dev")),
        P(("grp", "dev")),
        P(("grp", "dev"), None, None),
        P(),
        P(),
        P(),
        P(),
        P(),
        P(),
        P(),
        P(),
    )
    out_specs = (P(("grp", "dev"), None, None), P(("grp", "dev"), None, None))
    return jax.shard_map(local, mesh=mesh, in_specs=in_specs, out_specs=out_specs, check_vma=False)
```

```python
import jax
import jax.numpy as jnp
from jax import lax
from jax.experimental import pallas as pl
from jax.experimental.pallas import tpu as pltpu
from jax.sharding import PartitionSpec as P

FRAMES = 4
MOST = 2


def embed_kernel(codes_ref, table_ref, out_ref, blocks, sems):
    books, rows = codes_ref.shape
    size = blocks.shape[1]

    def fetch(book):
        return pltpu.make_async_copy(table_ref.at[pl.ds(book * size, size)], blocks.at[book], sems.at[book])

    for book in range(books):
        fetch(book).start()
    by_row = jnp.transpose(codes_ref[...])
    total = None
    for book in range(books):
        fetch(book).wait()
        entries = lax.broadcasted_iota(jnp.int32, (rows, size), 1)
        onehot = (by_row[:, book : book + 1] == entries).astype(jnp.bfloat16)
        term = jnp.dot(onehot, blocks[book], preferred_element_type=jnp.float32)
        total = term if total is None else total + term
    out_ref[...] = total.astype(jnp.bfloat16)


def embed_codes(codes, code_table):
    row_count = codes.shape[0]
    book_count = codes.shape[1] // FRAMES
    book_size = code_table.shape[0] // book_count
    chan_width = code_table.shape[1]
    by_book = codes.reshape(row_count, FRAMES, book_count).transpose(2, 1, 0).reshape(book_count, -1)
    rows = FRAMES * row_count
    summed = pl.pallas_call(
        embed_kernel,
        in_specs=[pl.BlockSpec(memory_space=pltpu.VMEM), pl.BlockSpec(memory_space=pl.ANY)],
        out_specs=pl.BlockSpec(memory_space=pltpu.VMEM),
        out_shape=jax.ShapeDtypeStruct((rows, chan_width), jnp.bfloat16),
        scratch_shapes=[
            pltpu.VMEM((book_count, book_size, chan_width), code_table.dtype),
            pltpu.SemaphoreType.DMA((book_count,)),
        ],
    )(by_book, code_table)
    return summed.reshape(FRAMES, row_count, chan_width)


def pick_rows(table, index, live):
    entries = jnp.arange(table.shape[0], dtype=jnp.int32)
    select = (index[:, None] == entries[None, :]) & live[:, None]
    if table.dtype == jnp.bfloat16:
        return jnp.dot(
            select.astype(jnp.bfloat16), table, preferred_element_type=jnp.float32
        ).astype(jnp.bfloat16)
    if table.dtype == jnp.int32:
        picked = jnp.dot(
            select.astype(jnp.float32), table.astype(jnp.float32), precision=lax.Precision.HIGHEST
        )
        return picked.astype(jnp.int32)
    return jnp.dot(select.astype(jnp.float32), table, precision=lax.Precision.HIGHEST)


def prefix_count(flags):
    width = flags.shape[-1]
    positions = jnp.arange(width, dtype=jnp.int32)
    upper = (positions[:, None] <= positions[None, :]).astype(jnp.float32)
    return jnp.dot(flags.astype(jnp.float32), upper).astype(jnp.int32)


def compact(flags, ranks, values, slots):
    spots = jnp.arange(slots, dtype=jnp.int32)
    hit = flags[..., None, :] & (ranks[..., None, :] == spots[:, None])
    picked = jnp.sum(jnp.where(hit, values[..., None, :], 0), axis=-1)
    return (picked, jnp.any(hit, axis=-1))


def exchange(items, collective_id):
    groups = lax.axis_size("grp")
    per_group = lax.axis_size("dev")
    count = len(items)
    shapes = []
    for blocks, whole in items:
        if whole:
            shapes.append(jax.ShapeDtypeStruct((groups, per_group) + blocks.shape[1:], blocks.dtype))
        else:
            shapes.append(jax.ShapeDtypeStruct(blocks.shape, blocks.dtype))
    wholes = [index for index, (_, whole) in enumerate(items) if whole]

    def kernel(*refs):
        x_refs = refs[:count]
        o_refs = refs[count : 2 * count]
        mid_refs = dict(zip(wholes, refs[2 * count : 2 * count + len(wholes)]))
        sems = refs[2 * count + len(wholes) :]
        first_send, first_recv, second_send, second_recv, own_sem = sems
        group = lax.axis_index("grp")
        dev = lax.axis_index("dev")
        barrier = pltpu.get_barrier_semaphore()
        across = len(wholes) > 0

        if across:
            def greet_group(offset, carry):
                peer = lax.rem(group + offset, groups)
                pl.semaphore_signal(barrier, inc=1, device_id=(peer, dev), device_id_type=pl.DeviceIdType.MESH)
                return carry

            lax.fori_loop(1, groups, greet_group, 0)

        def greet_dev(offset, carry):
            peer = lax.rem(dev + offset, per_group)
            pl.semaphore_signal(barrier, inc=1, device_id=(group, peer), device_id_type=pl.DeviceIdType.MESH)
            return carry

        lax.fori_loop(1, per_group, greet_dev, 0)
        pl.semaphore_wait(barrier, (groups - 1 if across else 0) + per_group - 1)

        def hop_one(slot, index, peer, place):
            return pltpu.make_async_remote_copy(
                src_ref=x_refs[index].at[pl.ds(peer * per_group, per_group)],
                dst_ref=mid_refs[index].at[place],
                send_sem=first_send.at[slot, peer],
                recv_sem=first_recv.at[slot, place],
                device_id=(peer, dev),
                device_id_type=pl.DeviceIdType.MESH,
            )

        def hop_two(index, peer, place):
            if items[index][1]:
                source = mid_refs[index].at[:, peer]
                target = o_refs[index].at[:, place]
            else:
                source = x_refs[index].at[peer]
                target = o_refs[index].at[place]
            return pltpu.make_async_remote_copy(
                src_ref=source,
                dst_ref=target,
                send_sem=second_send.at[index, peer],
                recv_sem=second_recv.at[index, place],
                device_id=(group, peer),
                device_id_type=pl.DeviceIdType.MESH,
            )

        for slot, index in enumerate(wholes):
            def send_one(offset, carry, slot=slot, index=index):
                hop_one(slot, index, lax.rem(group + offset, groups), group).start()
                return carry

            lax.fori_loop(1, groups, send_one, 0)
        for index, (_, whole) in enumerate(items):
            if not whole:
                def send_group(offset, carry, index=index):
                    hop_two(index, lax.rem(dev + offset, per_group), dev).start()
                    return carry

                lax.fori_loop(1, per_group, send_group, 0)
        for slot, index in enumerate(wholes):
            own = pltpu.make_async_copy(
                x_refs[index].at[pl.ds(group * per_group, per_group)], mid_refs[index].at[group], own_sem
            )
            own.start()
            own.wait()

            def finish_one(offset, carry, slot=slot, index=index):
                hop_one(slot, index, lax.rem(group + offset, groups), group).wait_send()
                source = lax.rem(group + groups - offset, groups)
                hop_one(slot, index, source, source).wait_recv()
                return carry

            lax.fori_loop(1, groups, finish_one, 0)

            def send_two(offset, carry, index=index):
                hop_two(index, lax.rem(dev + offset, per_group), dev).start()
                return carry

            lax.fori_loop(1, per_group, send_two, 0)
        for index, (_, whole) in enumerate(items):
            if whole:
                own = pltpu.make_async_copy(mid_refs[index].at[:, dev], o_refs[index].at[:, dev], own_sem)
            else:
                own = pltpu.make_async_copy(x_refs[index].at[dev], o_refs[index].at[dev], own_sem)
            own.start()
            own.wait()

            def finish_two(offset, carry, index=index):
                hop_two(index, lax.rem(dev + offset, per_group), dev).wait_send()
                source = lax.rem(dev + per_group - offset, per_group)
                hop_two(index, source, source).wait_recv()
                return carry

            lax.fori_loop(1, per_group, finish_two, 0)

    mids = [shapes[index] for index in wholes]
    results = pl.pallas_call(
        kernel,
        out_shape=shapes + mids,
        in_specs=[pl.BlockSpec(memory_space=pl.ANY)] * count,
        out_specs=[pl.BlockSpec(memory_space=pl.ANY)] * (count + len(wholes)),
        scratch_shapes=[
            pltpu.SemaphoreType.DMA((max(len(wholes), 1), groups)),
            pltpu.SemaphoreType.DMA((max(len(wholes), 1), groups)),
            pltpu.SemaphoreType.DMA((count, per_group)),
            pltpu.SemaphoreType.DMA((count, per_group)),
            pltpu.SemaphoreType.DMA(()),
        ],
        compiler_params=pltpu.CompilerParams(collective_id=collective_id, has_side_effects=True),
        cost_estimate=pl.CostEstimate(flops=0, transcendentals=0, bytes_accessed=48 * 1024 * 1024),
    )(*[blocks for blocks, _ in items])
    return [
        result.reshape(blocks.shape) for result, (blocks, _) in zip(results[:count], items)
    ]


def decode_kernel(
    source_ref, moved_ref,
    routed_ref, states_ref, arrived_ref, arrived_low_ref, up_w_ref, up_b_ref, conv_w_ref, conv_b_ref, in_w_ref, in_b_ref, out_w_ref,
    out_b_ref, decoded_ref, new_ref, carried_ref,
):
    frame_count, slots, _ = routed_ref.shape
    step_count = 2 * frame_count
    rows = states_ref.shape[0]
    conv_taps = conv_w_ref.shape[0]
    res_taps = in_w_ref.shape[0]
    kept = rows - 2 - (res_taps - 1)
    base = pl.program_id(0) * slots

    carried_ref[...] = states_ref[...]

    def bring(slot, carry):
        @pl.when(moved_ref[base + slot] != 0)
        def _():
            source = source_ref[base + slot]
            pieces = carried_ref.shape[2] // arrived_ref.shape[2]
            for r in range(rows):
                if r < 2:
                    row = arrived_ref[source, pl.ds(r * pieces, pieces), :]
                else:
                    row = arrived_low_ref[source, pl.ds((r - 2) * pieces, pieces), :].astype(jnp.float32)
                carried_ref[r, pl.ds(slot, 1), :] = jnp.concatenate(
                    [row[k : k + 1] for k in range(pieces)], axis=1
                )

        return carry

    lax.fori_loop(0, slots, bring, 0)

    def elu(value):
        return jnp.where(value > 0, value, jnp.exp(jnp.minimum(value, 0.0)) - 1.0)

    up_w = up_w_ref[...]
    up_b = up_b_ref[...]
    inputs = [routed_ref[f].astype(jnp.float32) for f in range(frame_count)]
    carried = [carried_ref[r] for r in range(rows)]
    upsampled = []
    for f in range(frame_count):
        early_even = carried[0] if f == 0 else inputs[f - 1] * up_w[2:3]
        early_odd = carried[1] if f == 0 else inputs[f - 1] * up_w[3:4]
        upsampled.append((inputs[f] * up_w[0:1] + early_even) + up_b)
        upsampled.append((inputs[f] * up_w[1:2] + early_odd) + up_b)
    history = jnp.concatenate(
        [c.astype(jnp.bfloat16) for c in carried[2 : 2 + kept]] + [u.astype(jnp.bfloat16) for u in upsampled], axis=0
    )
    conv_out = None
    for tap in range(conv_taps):
        start = (conv_taps - 1 - tap) * slots
        term = jnp.dot(history[start : start + step_count * slots], conv_w_ref[tap], preferred_element_type=jnp.float32)
        conv_out = term if conv_out is None else conv_out + term
    conv_out = conv_out + conv_b_ref[...]
    active = elu(conv_out)
    res_rounded = jnp.concatenate(
        [c.astype(jnp.bfloat16) for c in carried[2 + kept :]] + [active.astype(jnp.bfloat16)], axis=0
    )
    inner = None
    for tap in range(res_taps):
        start = (res_taps - 1 - tap) * slots
        term = jnp.dot(res_rounded[start : start + step_count * slots], in_w_ref[tap], preferred_element_type=jnp.float32)
        inner = term if inner is None else inner + term
    squeezed = elu(inner + in_b_ref[...]).astype(jnp.bfloat16)
    summed = conv_out + jnp.dot(squeezed, out_w_ref[...], preferred_element_type=jnp.float32) + out_b_ref[...]
    decoded = summed.astype(jnp.bfloat16)
    for t in range(step_count):
        decoded_ref[:, t, :] = decoded[t * slots : (t + 1) * slots]
    new_ref[0] = inputs[frame_count - 1] * up_w[2:3]
    new_ref[1] = inputs[frame_count - 1] * up_w[3:4]
    for k in range(kept):
        row = history.shape[0] // slots - kept + k
        new_ref[2 + k] = history[row * slots : (row + 1) * slots].astype(jnp.float32)
    for k in range(res_taps - 1):
        row = step_count - (res_taps - 1) + k
        new_ref[2 + kept + k] = active[row * slots : (row + 1) * slots]


def decode(
    routed, states, arrived, arrived_low, source, moved, up_weight, up_bias, conv_weight, conv_bias, res_in_weight, res_in_bias,
    res_out_weight, res_out_bias,
):
    frame_count, conv_count, chan_width = routed.shape
    rows = states.shape[1]
    chunk = 32 if conv_count % 32 == 0 else conv_count
    whole = lambda shape: pl.BlockSpec(shape, lambda i, *_: (0,) * len(shape))
    states_t = jnp.transpose(states, (1, 0, 2))
    decoded, new_t = pl.pallas_call(
        decode_kernel,
        grid_spec=pltpu.PrefetchScalarGridSpec(
            num_scalar_prefetch=2,
            grid=(conv_count // chunk,),
            in_specs=[
                pl.BlockSpec((frame_count, chunk, chan_width), lambda i, *_: (0, i, 0)),
                pl.BlockSpec((rows, chunk, chan_width), lambda i, *_: (0, i, 0)),
                whole(arrived.shape),
                whole(arrived_low.shape),
                whole(up_weight.shape),
                whole((1, chan_width)),
                whole(conv_weight.shape),
                whole((1, chan_width)),
                whole(res_in_weight.shape),
                whole((1, res_in_weight.shape[2])),
                whole(res_out_weight.shape),
                whole((1, chan_width)),
            ],
            out_specs=(
                pl.BlockSpec((chunk, 2 * frame_count, chan_width), lambda i, *_: (i, 0, 0)),
                pl.BlockSpec((rows, chunk, chan_width), lambda i, *_: (0, i, 0)),
            ),
            scratch_shapes=[pltpu.VMEM((rows, chunk, chan_width), jnp.float32)],
        ),
        out_shape=(
            jax.ShapeDtypeStruct((conv_count, 2 * frame_count, chan_width), jnp.bfloat16),
            jax.ShapeDtypeStruct((rows, conv_count, chan_width), jnp.float32),
        ),
        compiler_params=pltpu.CompilerParams(vmem_limit_bytes=48 * 1024 * 1024),
    )(
        source, moved, routed, states_t, arrived, arrived_low, up_weight, up_bias.reshape(1, -1), conv_weight,
        conv_bias.reshape(1, -1), res_in_weight, res_in_bias.reshape(1, -1), res_out_weight, res_out_bias.reshape(1, -1),
    )
    return decoded, jnp.transpose(new_t, (1, 0, 2))


def local(
    codes,
    code_table,
    roster,
    old_slot,
    states,
    up_weight,
    up_bias,
    conv_weight,
    conv_bias,
    res_in_weight,
    res_in_bias,
    res_out_weight,
    res_out_bias,
):
    conv_count = roster.shape[0]
    per_group = lax.axis_size("dev")
    devices_all = lax.axis_size("grp") * per_group
    most = MOST
    group_first = lax.axis_index("grp") * per_group
    local_index = lax.axis_index("dev")
    positions = jnp.arange(conv_count, dtype=jnp.int32)
    earlier = positions[None, :] < positions[:, None]

    anchor = roster // conv_count
    row = roster % conv_count
    rank_in = jnp.sum(earlier & (anchor[None, :] == anchor[:, None]), axis=1).astype(jnp.int32)
    key = anchor * most + rank_in
    spots = jnp.arange(devices_all * most, dtype=jnp.int32)
    code_request = jnp.sum(jnp.where(key[None, :] == spots[:, None], row[None, :] + 1, 0), axis=1) - 1
    source_dev = old_slot // conv_count - group_first
    source_row = old_slot % conv_count
    moved = source_dev != local_index
    everyone = jnp.arange(devices_all, dtype=jnp.int32)
    state_request = (
        jnp.sum(
            jnp.where(
                moved[None, :] & (source_dev[None, :] + group_first == everyone[:, None]),
                source_row[None, :] + 1,
                0,
            ),
            axis=1,
        )
        - 1
    )
    request = jnp.concatenate(
        [code_request.reshape(devices_all, most), state_request.reshape(devices_all, 1)], axis=1
    )
    lanes = 128
    padded = jnp.pad(request, ((0, 0), (0, lanes - most - 1))).reshape(devices_all, 1, lanes)
    (asked,) = exchange([(padded, True)], 0)
    asked = asked[:, 0, : most + 1]

    answer = jnp.take(codes, jnp.clip(asked[:, :most].reshape(-1), 0, conv_count - 1), axis=0)
    answer = answer.reshape(devices_all, -1)
    answer = jnp.pad(answer, ((0, 0), (0, lanes - answer.shape[1]))).reshape(devices_all, 1, lanes)
    state_asked = lax.dynamic_slice_in_dim(asked[:, most], group_first, per_group)
    leaving = jnp.take(states, jnp.clip(state_asked, 0, conv_count - 1), axis=0)
    leaving_high = leaving[:, :2].reshape(per_group, -1, lanes)
    leaving_low = leaving[:, 2:].astype(jnp.bfloat16).reshape(per_group, -1, lanes)
    answered, arrived, arrived_low = exchange(
        [(answer, True), (leaving_high, False), (leaving_low, False)], 1
    )
    code_width = codes.shape[1]
    answered = answered[:, 0, : most * code_width].reshape(devices_all * most, code_width)
    my_codes = jnp.take(answered, key, axis=0)
    routed = embed_codes(my_codes, code_table)
    return decode(
        routed,
        states,
        arrived,
        arrived_low,
        jnp.clip(source_dev, 0, per_group - 1),
        moved.astype(jnp.int32),
        up_weight,
        up_bias,
        conv_weight,
        conv_bias,
        res_in_weight,
        res_in_bias,
        res_out_weight,
        res_out_bias,
    )


def solution(mesh):
    in_specs = (
        P(("grp", "dev"), None),
        P(),
        P(("grp", "dev")),
        P(("grp", "dev")),
        P(("grp", "dev"), None, None),
        P(),
        P(),
        P(),
        P(),
        P(),
        P(),
        P(),
        P(),
    )
    out_specs = (P(("grp", "dev"), None, None), P(("grp", "dev"), None, None))
    return jax.shard_map(local, mesh=mesh, in_specs=in_specs, out_specs=out_specs, check_vma=False)
```

```python
import jax
import jax.numpy as jnp
from jax import lax
from jax.experimental import pallas as pl
from jax.experimental.pallas import tpu as pltpu
from jax.sharding import PartitionSpec as P

FRAMES = 4
MOST = 2


def embed_kernel(codes_ref, table_ref, out_ref, blocks, sems):
    books, rows = codes_ref.shape
    size = blocks.shape[1]

    def fetch(book):
        return pltpu.make_async_copy(table_ref.at[pl.ds(book * size, size)], blocks.at[book], sems.at[book])

    for book in range(books):
        fetch(book).start()
    by_row = jnp.transpose(codes_ref[...])
    total = None
    for book in range(books):
        fetch(book).wait()
        entries = lax.broadcasted_iota(jnp.int32, (rows, size), 1)
        onehot = (by_row[:, book : book + 1] == entries).astype(jnp.bfloat16)
        term = jnp.dot(onehot, blocks[book], preferred_element_type=jnp.float32)
        total = term if total is None else total + term
    out_ref[...] = total.astype(jnp.bfloat16)


def embed_codes(codes, code_table):
    row_count = codes.shape[0]
    book_count = codes.shape[1] // FRAMES
    book_size = code_table.shape[0] // book_count
    chan_width = code_table.shape[1]
    by_book = codes.reshape(row_count, FRAMES, book_count).transpose(2, 1, 0).reshape(book_count, -1)
    rows = FRAMES * row_count
    summed = pl.pallas_call(
        embed_kernel,
        in_specs=[pl.BlockSpec(memory_space=pltpu.VMEM), pl.BlockSpec(memory_space=pl.ANY)],
        out_specs=pl.BlockSpec(memory_space=pltpu.VMEM),
        out_shape=jax.ShapeDtypeStruct((rows, chan_width), jnp.bfloat16),
        scratch_shapes=[
            pltpu.VMEM((book_count, book_size, chan_width), code_table.dtype),
            pltpu.SemaphoreType.DMA((book_count,)),
        ],
    )(by_book, code_table)
    return summed.reshape(FRAMES, row_count, chan_width)


def pick_rows(table, index, live):
    entries = jnp.arange(table.shape[0], dtype=jnp.int32)
    select = (index[:, None] == entries[None, :]) & live[:, None]
    if table.dtype == jnp.bfloat16:
        return jnp.dot(
            select.astype(jnp.bfloat16), table, preferred_element_type=jnp.float32
        ).astype(jnp.bfloat16)
    if table.dtype == jnp.int32:
        picked = jnp.dot(
            select.astype(jnp.float32), table.astype(jnp.float32), precision=lax.Precision.HIGHEST
        )
        return picked.astype(jnp.int32)
    return jnp.dot(select.astype(jnp.float32), table, precision=lax.Precision.HIGHEST)


def prefix_count(flags):
    width = flags.shape[-1]
    positions = jnp.arange(width, dtype=jnp.int32)
    upper = (positions[:, None] <= positions[None, :]).astype(jnp.float32)
    return jnp.dot(flags.astype(jnp.float32), upper).astype(jnp.int32)


def compact(flags, ranks, values, slots):
    spots = jnp.arange(slots, dtype=jnp.int32)
    hit = flags[..., None, :] & (ranks[..., None, :] == spots[:, None])
    picked = jnp.sum(jnp.where(hit, values[..., None, :], 0), axis=-1)
    return (picked, jnp.any(hit, axis=-1))


def exchange(items, collective_id):
    groups = lax.axis_size("grp")
    per_group = lax.axis_size("dev")
    count = len(items)
    shapes = []
    for blocks, whole in items:
        if whole:
            shapes.append(jax.ShapeDtypeStruct((groups, per_group) + blocks.shape[1:], blocks.dtype))
        else:
            shapes.append(jax.ShapeDtypeStruct(blocks.shape, blocks.dtype))
    wholes = [index for index, (_, whole) in enumerate(items) if whole]

    def kernel(*refs):
        x_refs = refs[:count]
        o_refs = refs[count : 2 * count]
        mid_refs = dict(zip(wholes, refs[2 * count : 2 * count + len(wholes)]))
        sems = refs[2 * count + len(wholes) :]
        first_send, first_recv, second_send, second_recv, own_sem = sems
        group = lax.axis_index("grp")
        dev = lax.axis_index("dev")
        barrier = pltpu.get_barrier_semaphore()
        across = len(wholes) > 0

        if across:
            def greet_group(offset, carry):
                peer = lax.rem(group + offset, groups)
                pl.semaphore_signal(barrier, inc=1, device_id=(peer, dev), device_id_type=pl.DeviceIdType.MESH)
                return carry

            lax.fori_loop(1, groups, greet_group, 0)

        def greet_dev(offset, carry):
            peer = lax.rem(dev + offset, per_group)
            pl.semaphore_signal(barrier, inc=1, device_id=(group, peer), device_id_type=pl.DeviceIdType.MESH)
            return carry

        lax.fori_loop(1, per_group, greet_dev, 0)
        pl.semaphore_wait(barrier, (groups - 1 if across else 0) + per_group - 1)

        def hop_one(slot, index, peer, place):
            return pltpu.make_async_remote_copy(
                src_ref=x_refs[index].at[pl.ds(peer * per_group, per_group)],
                dst_ref=mid_refs[index].at[place],
                send_sem=first_send.at[slot, peer],
                recv_sem=first_recv.at[slot, place],
                device_id=(peer, dev),
                device_id_type=pl.DeviceIdType.MESH,
            )

        def hop_two(index, peer, place):
            if items[index][1]:
                source = mid_refs[index].at[:, peer]
                target = o_refs[index].at[:, place]
            else:
                source = x_refs[index].at[peer]
                target = o_refs[index].at[place]
            return pltpu.make_async_remote_copy(
                src_ref=source,
                dst_ref=target,
                send_sem=second_send.at[index, peer],
                recv_sem=second_recv.at[index, place],
                device_id=(group, peer),
                device_id_type=pl.DeviceIdType.MESH,
            )

        for slot, index in enumerate(wholes):
            def send_one(offset, carry, slot=slot, index=index):
                hop_one(slot, index, lax.rem(group + offset, groups), group).start()
                return carry

            lax.fori_loop(1, groups, send_one, 0)
        for index, (_, whole) in enumerate(items):
            if not whole:
                def send_group(offset, carry, index=index):
                    hop_two(index, lax.rem(dev + offset, per_group), dev).start()
                    return carry

                lax.fori_loop(1, per_group, send_group, 0)
        for slot, index in enumerate(wholes):
            own = pltpu.make_async_copy(
                x_refs[index].at[pl.ds(group * per_group, per_group)], mid_refs[index].at[group], own_sem
            )
            own.start()
            own.wait()

            def finish_one(offset, carry, slot=slot, index=index):
                hop_one(slot, index, lax.rem(group + offset, groups), group).wait_send()
                source = lax.rem(group + groups - offset, groups)
                hop_one(slot, index, source, source).wait_recv()
                return carry

            lax.fori_loop(1, groups, finish_one, 0)

            def send_two(offset, carry, index=index):
                hop_two(index, lax.rem(dev + offset, per_group), dev).start()
                return carry

            lax.fori_loop(1, per_group, send_two, 0)
        for index, (_, whole) in enumerate(items):
            if whole:
                own = pltpu.make_async_copy(mid_refs[index].at[:, dev], o_refs[index].at[:, dev], own_sem)
            else:
                own = pltpu.make_async_copy(x_refs[index].at[dev], o_refs[index].at[dev], own_sem)
            own.start()
            own.wait()

            def finish_two(offset, carry, index=index):
                hop_two(index, lax.rem(dev + offset, per_group), dev).wait_send()
                source = lax.rem(dev + per_group - offset, per_group)
                hop_two(index, source, source).wait_recv()
                return carry

            lax.fori_loop(1, per_group, finish_two, 0)

    mids = [shapes[index] for index in wholes]
    results = pl.pallas_call(
        kernel,
        out_shape=shapes + mids,
        in_specs=[pl.BlockSpec(memory_space=pl.ANY)] * count,
        out_specs=[pl.BlockSpec(memory_space=pl.ANY)] * (count + len(wholes)),
        scratch_shapes=[
            pltpu.SemaphoreType.DMA((max(len(wholes), 1), groups)),
            pltpu.SemaphoreType.DMA((max(len(wholes), 1), groups)),
            pltpu.SemaphoreType.DMA((count, per_group)),
            pltpu.SemaphoreType.DMA((count, per_group)),
            pltpu.SemaphoreType.DMA(()),
        ],
        compiler_params=pltpu.CompilerParams(collective_id=collective_id, has_side_effects=True),
        cost_estimate=pl.CostEstimate(flops=0, transcendentals=0, bytes_accessed=48 * 1024 * 1024),
    )(*[blocks for blocks, _ in items])
    return [
        result.reshape(blocks.shape) for result, (blocks, _) in zip(results[:count], items)
    ]


def exchange_hops(blocks, collective_id):
    groups = lax.axis_size("grp")
    per_group = lax.axis_size("dev")
    rows = 4 if per_group % 4 == 0 else 1
    cols = per_group // rows
    tail = blocks.shape[1:]
    first = jax.ShapeDtypeStruct((groups, rows, cols) + tail, blocks.dtype)
    second = jax.ShapeDtypeStruct((rows, groups, cols) + tail, blocks.dtype)

    def kernel(x_ref, out_ref, mid_one, mid_two, send_sems, recv_sems, own_sem):
        group = lax.axis_index("grp")
        dev = lax.axis_index("dev")
        row = dev // cols
        col = dev % cols
        barrier = pltpu.get_barrier_semaphore()
        stages = (
            (groups, lambda peer: (peer, dev), group),
            (rows, lambda peer: (group, peer * cols + col), row),
            (cols, lambda peer: (group, row * cols + peer), col),
        )
        for size, device, me in stages:
            def greet(offset, carry, size=size, device=device, me=me):
                pl.semaphore_signal(
                    barrier, inc=1, device_id=device(lax.rem(me + offset, size)), device_id_type=pl.DeviceIdType.MESH
                )
                return carry

            lax.fori_loop(1, size, greet, 0)
        pl.semaphore_wait(barrier, groups + rows + cols - 3)

        def views(stage, peer, place):
            if stage == 0:
                return x_ref.at[peer], mid_one.at[place]
            if stage == 1:
                return mid_one.at[:, peer], mid_two.at[place]
            return mid_two.at[:, :, peer], out_ref.at[:, :, place]

        for stage, (size, device, me) in enumerate(stages):
            def copy(peer, place, stage=stage, device=device):
                source, target = views(stage, peer, place)
                return pltpu.make_async_remote_copy(
                    src_ref=source,
                    dst_ref=target,
                    send_sem=send_sems.at[stage, peer],
                    recv_sem=recv_sems.at[stage, place],
                    device_id=device(peer),
                    device_id_type=pl.DeviceIdType.MESH,
                )

            def send(offset, carry, size=size, me=me, copy=copy):
                copy(lax.rem(me + offset, size), me).start()
                return carry

            lax.fori_loop(1, size, send, 0)
            source, target = views(stage, me, me)
            if stage == 0:
                own = pltpu.make_async_copy(x_ref.at[group], mid_one.at[group], own_sem)
            else:
                own = pltpu.make_async_copy(source, target, own_sem)
            own.start()
            own.wait()

            def finish(offset, carry, size=size, me=me, copy=copy):
                copy(lax.rem(me + offset, size), me).wait_send()
                source = lax.rem(me + size - offset, size)
                copy(source, source).wait_recv()
                return carry

            lax.fori_loop(1, size, finish, 0)

    widest = max(groups, rows, cols)
    result, _, _ = pl.pallas_call(
        kernel,
        out_shape=[jax.ShapeDtypeStruct((rows, groups, cols) + tail, blocks.dtype), first, second],
        in_specs=[pl.BlockSpec(memory_space=pl.ANY)],
        out_specs=[pl.BlockSpec(memory_space=pl.ANY)] * 3,
        scratch_shapes=[
            pltpu.SemaphoreType.DMA((3, widest)),
            pltpu.SemaphoreType.DMA((3, widest)),
            pltpu.SemaphoreType.DMA(()),
        ],
        compiler_params=pltpu.CompilerParams(collective_id=collective_id, has_side_effects=True),
        cost_estimate=pl.CostEstimate(flops=0, transcendentals=0, bytes_accessed=48 * 1024 * 1024),
    )(blocks.reshape((groups, rows, cols) + tail))
    return jnp.transpose(result, (1, 0) + tuple(range(2, result.ndim))).reshape(blocks.shape)


def decode_kernel(
    source_ref, moved_ref,
    routed_ref, states_ref, arrived_ref, arrived_low_ref, up_w_ref, up_b_ref, conv_w_ref, conv_b_ref, in_w_ref, in_b_ref, out_w_ref,
    out_b_ref, decoded_ref, new_ref, carried_ref,
):
    frame_count, slots, _ = routed_ref.shape
    step_count = 2 * frame_count
    rows = states_ref.shape[0]
    conv_taps = conv_w_ref.shape[0]
    res_taps = in_w_ref.shape[0]
    kept = rows - 2 - (res_taps - 1)
    base = pl.program_id(0) * slots

    carried_ref[...] = states_ref[...]

    def bring(slot, carry):
        @pl.when(moved_ref[base + slot] != 0)
        def _():
            source = source_ref[base + slot]
            pieces = carried_ref.shape[2] // arrived_ref.shape[2]
            for r in range(rows):
                if r < 2:
                    row = arrived_ref[source, pl.ds(r * pieces, pieces), :]
                else:
                    row = arrived_low_ref[source, pl.ds((r - 2) * pieces, pieces), :].astype(jnp.float32)
                carried_ref[r, pl.ds(slot, 1), :] = jnp.concatenate(
                    [row[k : k + 1] for k in range(pieces)], axis=1
                )

        return carry

    lax.fori_loop(0, slots, bring, 0)

    def elu(value):
        return jnp.where(value > 0, value, jnp.exp(jnp.minimum(value, 0.0)) - 1.0)

    up_w = up_w_ref[...]
    up_b = up_b_ref[...]
    inputs = [routed_ref[f].astype(jnp.float32) for f in range(frame_count)]
    carried = [carried_ref[r] for r in range(rows)]
    upsampled = []
    for f in range(frame_count):
        early_even = carried[0] if f == 0 else inputs[f - 1] * up_w[2:3]
        early_odd = carried[1] if f == 0 else inputs[f - 1] * up_w[3:4]
        upsampled.append((inputs[f] * up_w[0:1] + early_even) + up_b)
        upsampled.append((inputs[f] * up_w[1:2] + early_odd) + up_b)
    history = jnp.concatenate(
        [c.astype(jnp.bfloat16) for c in carried[2 : 2 + kept]] + [u.astype(jnp.bfloat16) for u in upsampled], axis=0
    )
    conv_out = None
    for tap in range(conv_taps):
        start = (conv_taps - 1 - tap) * slots
        term = jnp.dot(history[start : start + step_count * slots], conv_w_ref[tap], preferred_element_type=jnp.float32)
        conv_out = term if conv_out is None else conv_out + term
    conv_out = conv_out + conv_b_ref[...]
    active = elu(conv_out)
    res_rounded = jnp.concatenate(
        [c.astype(jnp.bfloat16) for c in carried[2 + kept :]] + [active.astype(jnp.bfloat16)], axis=0
    )
    inner = None
    for tap in range(res_taps):
        start = (res_taps - 1 - tap) * slots
        term = jnp.dot(res_rounded[start : start + step_count * slots], in_w_ref[tap], preferred_element_type=jnp.float32)
        inner = term if inner is None else inner + term
    squeezed = elu(inner + in_b_ref[...]).astype(jnp.bfloat16)
    summed = conv_out + jnp.dot(squeezed, out_w_ref[...], preferred_element_type=jnp.float32) + out_b_ref[...]
    decoded = summed.astype(jnp.bfloat16)
    for t in range(step_count):
        decoded_ref[:, t, :] = decoded[t * slots : (t + 1) * slots]
    new_ref[0] = inputs[frame_count - 1] * up_w[2:3]
    new_ref[1] = inputs[frame_count - 1] * up_w[3:4]
    for k in range(kept):
        row = history.shape[0] // slots - kept + k
        new_ref[2 + k] = history[row * slots : (row + 1) * slots].astype(jnp.float32)
    for k in range(res_taps - 1):
        row = step_count - (res_taps - 1) + k
        new_ref[2 + kept + k] = active[row * slots : (row + 1) * slots]


def decode(
    routed, states, arrived, arrived_low, source, moved, up_weight, up_bias, conv_weight, conv_bias, res_in_weight, res_in_bias,
    res_out_weight, res_out_bias,
):
    frame_count, conv_count, chan_width = routed.shape
    rows = states.shape[1]
    chunk = 32 if conv_count % 32 == 0 else conv_count
    whole = lambda shape: pl.BlockSpec(shape, lambda i, *_: (0,) * len(shape))
    states_t = jnp.transpose(states, (1, 0, 2))
    decoded, new_t = pl.pallas_call(
        decode_kernel,
        grid_spec=pltpu.PrefetchScalarGridSpec(
            num_scalar_prefetch=2,
            grid=(conv_count // chunk,),
            in_specs=[
                pl.BlockSpec((frame_count, chunk, chan_width), lambda i, *_: (0, i, 0)),
                pl.BlockSpec((rows, chunk, chan_width), lambda i, *_: (0, i, 0)),
                whole(arrived.shape),
                whole(arrived_low.shape),
                whole(up_weight.shape),
                whole((1, chan_width)),
                whole(conv_weight.shape),
                whole((1, chan_width)),
                whole(res_in_weight.shape),
                whole((1, res_in_weight.shape[2])),
                whole(res_out_weight.shape),
                whole((1, chan_width)),
            ],
            out_specs=(
                pl.BlockSpec((chunk, 2 * frame_count, chan_width), lambda i, *_: (i, 0, 0)),
                pl.BlockSpec((rows, chunk, chan_width), lambda i, *_: (0, i, 0)),
            ),
            scratch_shapes=[pltpu.VMEM((rows, chunk, chan_width), jnp.float32)],
        ),
        out_shape=(
            jax.ShapeDtypeStruct((conv_count, 2 * frame_count, chan_width), jnp.bfloat16),
            jax.ShapeDtypeStruct((rows, conv_count, chan_width), jnp.float32),
        ),
        compiler_params=pltpu.CompilerParams(vmem_limit_bytes=48 * 1024 * 1024),
    )(
        source, moved, routed, states_t, arrived, arrived_low, up_weight, up_bias.reshape(1, -1), conv_weight,
        conv_bias.reshape(1, -1), res_in_weight, res_in_bias.reshape(1, -1), res_out_weight, res_out_bias.reshape(1, -1),
    )
    return decoded, jnp.transpose(new_t, (1, 0, 2))


def local(
    codes,
    code_table,
    roster,
    old_slot,
    states,
    up_weight,
    up_bias,
    conv_weight,
    conv_bias,
    res_in_weight,
    res_in_bias,
    res_out_weight,
    res_out_bias,
):
    conv_count = roster.shape[0]
    per_group = lax.axis_size("dev")
    devices_all = lax.axis_size("grp") * per_group
    most = MOST
    group_first = lax.axis_index("grp") * per_group
    local_index = lax.axis_index("dev")
    positions = jnp.arange(conv_count, dtype=jnp.int32)
    earlier = positions[None, :] < positions[:, None]

    anchor = roster // conv_count
    row = roster % conv_count
    rank_in = jnp.sum(earlier & (anchor[None, :] == anchor[:, None]), axis=1).astype(jnp.int32)
    key = anchor * most + rank_in
    spots = jnp.arange(devices_all * most, dtype=jnp.int32)
    code_request = jnp.sum(jnp.where(key[None, :] == spots[:, None], row[None, :] + 1, 0), axis=1) - 1
    source_dev = old_slot // conv_count - group_first
    source_row = old_slot % conv_count
    moved = source_dev != local_index
    everyone = jnp.arange(devices_all, dtype=jnp.int32)
    state_request = (
        jnp.sum(
            jnp.where(
                moved[None, :] & (source_dev[None, :] + group_first == everyone[:, None]),
                source_row[None, :] + 1,
                0,
            ),
            axis=1,
        )
        - 1
    )
    request = jnp.concatenate(
        [code_request.reshape(devices_all, most), state_request.reshape(devices_all, 1)], axis=1
    )
    lanes = 128
    padded = jnp.pad(request, ((0, 0), (0, lanes - most - 1))).reshape(devices_all, 1, lanes)
    asked = exchange_hops(padded, 0)
    asked = asked[:, 0, : most + 1]

    answer = jnp.take(codes, jnp.clip(asked[:, :most].reshape(-1), 0, conv_count - 1), axis=0)
    answer = answer.reshape(devices_all, -1)
    answer = jnp.pad(answer, ((0, 0), (0, lanes - answer.shape[1]))).reshape(devices_all, 1, lanes)
    state_asked = lax.dynamic_slice_in_dim(asked[:, most], group_first, per_group)
    leaving = jnp.take(states, jnp.clip(state_asked, 0, conv_count - 1), axis=0)
    leaving_high = leaving[:, :2].reshape(per_group, -1, lanes)
    leaving_low = leaving[:, 2:].astype(jnp.bfloat16).reshape(per_group, -1, lanes)
    answered, arrived, arrived_low = exchange(
        [(answer, True), (leaving_high, False), (leaving_low, False)], 1
    )
    code_width = codes.shape[1]
    answered = answered[:, 0, : most * code_width].reshape(devices_all * most, code_width)
    my_codes = jnp.take(answered, key, axis=0)
    routed = embed_codes(my_codes, code_table)
    return decode(
        routed,
        states,
        arrived,
        arrived_low,
        jnp.clip(source_dev, 0, per_group - 1),
        moved.astype(jnp.int32),
        up_weight,
        up_bias,
        conv_weight,
        conv_bias,
        res_in_weight,
        res_in_bias,
        res_out_weight,
        res_out_bias,
    )


def solution(mesh):
    in_specs = (
        P(("grp", "dev"), None),
        P(),
        P(("grp", "dev")),
        P(("grp", "dev")),
        P(("grp", "dev"), None, None),
        P(),
        P(),
        P(),
        P(),
        P(),
        P(),
        P(),
        P(),
    )
    out_specs = (P(("grp", "dev"), None, None), P(("grp", "dev"), None, None))
    return jax.shard_map(local, mesh=mesh, in_specs=in_specs, out_specs=out_specs, check_vma=False)
```

```python
import jax
import jax.numpy as jnp
from jax import lax
from jax.experimental import pallas as pl
from jax.experimental.pallas import tpu as pltpu
from jax.sharding import PartitionSpec as P

FRAMES = 4
MOST = 2


def embed_kernel(codes_ref, table_ref, out_ref, blocks, sems):
    books, rows = codes_ref.shape
    size = blocks.shape[1]

    def fetch(book):
        return pltpu.make_async_copy(table_ref.at[pl.ds(book * size, size)], blocks.at[book], sems.at[book])

    for book in range(books):
        fetch(book).start()
    by_row = jnp.transpose(codes_ref[...])
    total = None
    for book in range(books):
        fetch(book).wait()
        entries = lax.broadcasted_iota(jnp.int32, (rows, size), 1)
        onehot = (by_row[:, book : book + 1] == entries).astype(jnp.bfloat16)
        term = jnp.dot(onehot, blocks[book], preferred_element_type=jnp.float32)
        total = term if total is None else total + term
    out_ref[...] = total.astype(jnp.bfloat16)


def embed_codes(codes, code_table):
    row_count = codes.shape[0]
    book_count = codes.shape[1] // FRAMES
    book_size = code_table.shape[0] // book_count
    chan_width = code_table.shape[1]
    by_book = codes.reshape(row_count, FRAMES, book_count).transpose(2, 1, 0).reshape(book_count, -1)
    rows = FRAMES * row_count
    summed = pl.pallas_call(
        embed_kernel,
        in_specs=[pl.BlockSpec(memory_space=pltpu.VMEM), pl.BlockSpec(memory_space=pl.ANY)],
        out_specs=pl.BlockSpec(memory_space=pltpu.VMEM),
        out_shape=jax.ShapeDtypeStruct((rows, chan_width), jnp.bfloat16),
        scratch_shapes=[
            pltpu.VMEM((book_count, book_size, chan_width), code_table.dtype),
            pltpu.SemaphoreType.DMA((book_count,)),
        ],
    )(by_book, code_table)
    return summed.reshape(FRAMES, row_count, chan_width)


def pick_rows(table, index, live):
    entries = jnp.arange(table.shape[0], dtype=jnp.int32)
    select = (index[:, None] == entries[None, :]) & live[:, None]
    if table.dtype == jnp.bfloat16:
        return jnp.dot(
            select.astype(jnp.bfloat16), table, preferred_element_type=jnp.float32
        ).astype(jnp.bfloat16)
    if table.dtype == jnp.int32:
        picked = jnp.dot(
            select.astype(jnp.float32), table.astype(jnp.float32), precision=lax.Precision.HIGHEST
        )
        return picked.astype(jnp.int32)
    return jnp.dot(select.astype(jnp.float32), table, precision=lax.Precision.HIGHEST)


def prefix_count(flags):
    width = flags.shape[-1]
    positions = jnp.arange(width, dtype=jnp.int32)
    upper = (positions[:, None] <= positions[None, :]).astype(jnp.float32)
    return jnp.dot(flags.astype(jnp.float32), upper).astype(jnp.int32)


def compact(flags, ranks, values, slots):
    spots = jnp.arange(slots, dtype=jnp.int32)
    hit = flags[..., None, :] & (ranks[..., None, :] == spots[:, None])
    picked = jnp.sum(jnp.where(hit, values[..., None, :], 0), axis=-1)
    return (picked, jnp.any(hit, axis=-1))


def exchange(items, collective_id):
    groups = lax.axis_size("grp")
    per_group = lax.axis_size("dev")
    count = len(items)
    shapes = []
    for blocks, whole in items:
        if whole:
            shapes.append(jax.ShapeDtypeStruct((groups, per_group) + blocks.shape[1:], blocks.dtype))
        else:
            shapes.append(jax.ShapeDtypeStruct(blocks.shape, blocks.dtype))
    wholes = [index for index, (_, whole) in enumerate(items) if whole]

    def kernel(*refs):
        x_refs = refs[:count]
        o_refs = refs[count : 2 * count]
        mid_refs = dict(zip(wholes, refs[2 * count : 2 * count + len(wholes)]))
        sems = refs[2 * count + len(wholes) :]
        first_send, first_recv, second_send, second_recv, own_sem = sems
        group = lax.axis_index("grp")
        dev = lax.axis_index("dev")
        barrier = pltpu.get_barrier_semaphore()
        across = len(wholes) > 0

        if across:
            def greet_group(offset, carry):
                peer = lax.rem(group + offset, groups)
                pl.semaphore_signal(barrier, inc=1, device_id=(peer, dev), device_id_type=pl.DeviceIdType.MESH)
                return carry

            lax.fori_loop(1, groups, greet_group, 0)

        def greet_dev(offset, carry):
            peer = lax.rem(dev + offset, per_group)
            pl.semaphore_signal(barrier, inc=1, device_id=(group, peer), device_id_type=pl.DeviceIdType.MESH)
            return carry

        lax.fori_loop(1, per_group, greet_dev, 0)
        pl.semaphore_wait(barrier, (groups - 1 if across else 0) + per_group - 1)

        def hop_one(slot, index, peer, place):
            return pltpu.make_async_remote_copy(
                src_ref=x_refs[index].at[pl.ds(peer * per_group, per_group)],
                dst_ref=mid_refs[index].at[place],
                send_sem=first_send.at[slot, peer],
                recv_sem=first_recv.at[slot, place],
                device_id=(peer, dev),
                device_id_type=pl.DeviceIdType.MESH,
            )

        def hop_two(index, peer, place):
            if items[index][1]:
                source = mid_refs[index].at[:, peer]
                target = o_refs[index].at[:, place]
            else:
                source = x_refs[index].at[peer]
                target = o_refs[index].at[place]
            return pltpu.make_async_remote_copy(
                src_ref=source,
                dst_ref=target,
                send_sem=second_send.at[index, peer],
                recv_sem=second_recv.at[index, place],
                device_id=(group, peer),
                device_id_type=pl.DeviceIdType.MESH,
            )

        for slot, index in enumerate(wholes):
            def send_one(offset, carry, slot=slot, index=index):
                hop_one(slot, index, lax.rem(group + offset, groups), group).start()
                return carry

            lax.fori_loop(1, groups, send_one, 0)
        for index, (_, whole) in enumerate(items):
            if not whole:
                def send_group(offset, carry, index=index):
                    hop_two(index, lax.rem(dev + offset, per_group), dev).start()
                    return carry

                lax.fori_loop(1, per_group, send_group, 0)
        for slot, index in enumerate(wholes):
            own = pltpu.make_async_copy(
                x_refs[index].at[pl.ds(group * per_group, per_group)], mid_refs[index].at[group], own_sem
            )
            own.start()
            own.wait()

            def finish_one(offset, carry, slot=slot, index=index):
                hop_one(slot, index, lax.rem(group + offset, groups), group).wait_send()
                source = lax.rem(group + groups - offset, groups)
                hop_one(slot, index, source, source).wait_recv()
                return carry

            lax.fori_loop(1, groups, finish_one, 0)

            def send_two(offset, carry, index=index):
                hop_two(index, lax.rem(dev + offset, per_group), dev).start()
                return carry

            lax.fori_loop(1, per_group, send_two, 0)
        for index, (_, whole) in enumerate(items):
            if whole:
                own = pltpu.make_async_copy(mid_refs[index].at[:, dev], o_refs[index].at[:, dev], own_sem)
            else:
                own = pltpu.make_async_copy(x_refs[index].at[dev], o_refs[index].at[dev], own_sem)
            own.start()
            own.wait()

            def finish_two(offset, carry, index=index):
                hop_two(index, lax.rem(dev + offset, per_group), dev).wait_send()
                source = lax.rem(dev + per_group - offset, per_group)
                hop_two(index, source, source).wait_recv()
                return carry

            lax.fori_loop(1, per_group, finish_two, 0)

    mids = [shapes[index] for index in wholes]
    results = pl.pallas_call(
        kernel,
        out_shape=shapes + mids,
        in_specs=[pl.BlockSpec(memory_space=pl.ANY)] * count,
        out_specs=[pl.BlockSpec(memory_space=pl.ANY)] * (count + len(wholes)),
        scratch_shapes=[
            pltpu.SemaphoreType.DMA((max(len(wholes), 1), groups)),
            pltpu.SemaphoreType.DMA((max(len(wholes), 1), groups)),
            pltpu.SemaphoreType.DMA((count, per_group)),
            pltpu.SemaphoreType.DMA((count, per_group)),
            pltpu.SemaphoreType.DMA(()),
        ],
        compiler_params=pltpu.CompilerParams(collective_id=collective_id, has_side_effects=True),
        cost_estimate=pl.CostEstimate(flops=0, transcendentals=0, bytes_accessed=48 * 1024 * 1024),
    )(*[blocks for blocks, _ in items])
    return [
        result.reshape(blocks.shape) for result, (blocks, _) in zip(results[:count], items)
    ]


def decode_kernel(
    source_ref, moved_ref,
    routed_ref, states_ref, arrived_ref, arrived_low_ref, up_w_ref, up_b_ref, conv_w_ref, conv_b_ref, in_w_ref, in_b_ref, out_w_ref,
    out_b_ref, decoded_ref, new_ref, carried_ref,
):
    frame_count, slots, _ = routed_ref.shape
    step_count = 2 * frame_count
    rows = states_ref.shape[0]
    conv_taps = conv_w_ref.shape[0]
    res_taps = in_w_ref.shape[0]
    kept = rows - 2 - (res_taps - 1)
    base = pl.program_id(0) * slots

    carried_ref[...] = states_ref[...]

    def bring(slot, carry):
        @pl.when(moved_ref[base + slot] != 0)
        def _():
            source = source_ref[base + slot]
            pieces = carried_ref.shape[2] // arrived_ref.shape[2]
            for r in range(rows):
                if r < 2:
                    row = arrived_ref[source, pl.ds(r * pieces, pieces), :]
                else:
                    row = arrived_low_ref[source, pl.ds((r - 2) * pieces, pieces), :].astype(jnp.float32)
                carried_ref[r, pl.ds(slot, 1), :] = jnp.concatenate(
                    [row[k : k + 1] for k in range(pieces)], axis=1
                )

        return carry

    lax.fori_loop(0, slots, bring, 0)

    def elu(value):
        return jnp.where(value > 0, value, jnp.exp(jnp.minimum(value, 0.0)) - 1.0)

    up_w = up_w_ref[...]
    up_b = up_b_ref[...]
    inputs = [routed_ref[f].astype(jnp.float32) for f in range(frame_count)]
    carried = [carried_ref[r] for r in range(rows)]
    upsampled = []
    for f in range(frame_count):
        early_even = carried[0] if f == 0 else inputs[f - 1] * up_w[2:3]
        early_odd = carried[1] if f == 0 else inputs[f - 1] * up_w[3:4]
        upsampled.append((inputs[f] * up_w[0:1] + early_even) + up_b)
        upsampled.append((inputs[f] * up_w[1:2] + early_odd) + up_b)
    history = jnp.concatenate(
        [c.astype(jnp.bfloat16) for c in carried[2 : 2 + kept]] + [u.astype(jnp.bfloat16) for u in upsampled], axis=0
    )
    conv_out = None
    for tap in range(conv_taps):
        start = (conv_taps - 1 - tap) * slots
        term = jnp.dot(history[start : start + step_count * slots], conv_w_ref[tap], preferred_element_type=jnp.float32)
        conv_out = term if conv_out is None else conv_out + term
    conv_out = conv_out + conv_b_ref[...]
    active = elu(conv_out)
    res_rounded = jnp.concatenate(
        [c.astype(jnp.bfloat16) for c in carried[2 + kept :]] + [active.astype(jnp.bfloat16)], axis=0
    )
    inner = None
    for tap in range(res_taps):
        start = (res_taps - 1 - tap) * slots
        term = jnp.dot(res_rounded[start : start + step_count * slots], in_w_ref[tap], preferred_element_type=jnp.float32)
        inner = term if inner is None else inner + term
    squeezed = elu(inner + in_b_ref[...]).astype(jnp.bfloat16)
    summed = conv_out + jnp.dot(squeezed, out_w_ref[...], preferred_element_type=jnp.float32) + out_b_ref[...]
    decoded = summed.astype(jnp.bfloat16)
    for t in range(step_count):
        decoded_ref[:, t, :] = decoded[t * slots : (t + 1) * slots]
    new_ref[0] = inputs[frame_count - 1] * up_w[2:3]
    new_ref[1] = inputs[frame_count - 1] * up_w[3:4]
    for k in range(kept):
        row = history.shape[0] // slots - kept + k
        new_ref[2 + k] = history[row * slots : (row + 1) * slots].astype(jnp.float32)
    for k in range(res_taps - 1):
        row = step_count - (res_taps - 1) + k
        new_ref[2 + kept + k] = active[row * slots : (row + 1) * slots]


def decode(
    routed, states, arrived, arrived_low, source, moved, up_weight, up_bias, conv_weight, conv_bias, res_in_weight, res_in_bias,
    res_out_weight, res_out_bias,
):
    frame_count, conv_count, chan_width = routed.shape
    rows = states.shape[1]
    chunk = 48 if conv_count % 48 == 0 else conv_count
    whole = lambda shape: pl.BlockSpec(shape, lambda i, *_: (0,) * len(shape))
    states_t = jnp.transpose(states, (1, 0, 2))
    decoded, new_t = pl.pallas_call(
        decode_kernel,
        grid_spec=pltpu.PrefetchScalarGridSpec(
            num_scalar_prefetch=2,
            grid=(conv_count // chunk,),
            in_specs=[
                pl.BlockSpec((frame_count, chunk, chan_width), lambda i, *_: (0, i, 0)),
                pl.BlockSpec((rows, chunk, chan_width), lambda i, *_: (0, i, 0)),
                whole(arrived.shape),
                whole(arrived_low.shape),
                whole(up_weight.shape),
                whole((1, chan_width)),
                whole(conv_weight.shape),
                whole((1, chan_width)),
                whole(res_in_weight.shape),
                whole((1, res_in_weight.shape[2])),
                whole(res_out_weight.shape),
                whole((1, chan_width)),
            ],
            out_specs=(
                pl.BlockSpec((chunk, 2 * frame_count, chan_width), lambda i, *_: (i, 0, 0)),
                pl.BlockSpec((rows, chunk, chan_width), lambda i, *_: (0, i, 0)),
            ),
            scratch_shapes=[pltpu.VMEM((rows, chunk, chan_width), jnp.float32)],
        ),
        out_shape=(
            jax.ShapeDtypeStruct((conv_count, 2 * frame_count, chan_width), jnp.bfloat16),
            jax.ShapeDtypeStruct((rows, conv_count, chan_width), jnp.float32),
        ),
        compiler_params=pltpu.CompilerParams(vmem_limit_bytes=48 * 1024 * 1024),
    )(
        source, moved, routed, states_t, arrived, arrived_low, up_weight, up_bias.reshape(1, -1), conv_weight,
        conv_bias.reshape(1, -1), res_in_weight, res_in_bias.reshape(1, -1), res_out_weight, res_out_bias.reshape(1, -1),
    )
    return decoded, jnp.transpose(new_t, (1, 0, 2))


def local(
    codes,
    code_table,
    roster,
    old_slot,
    states,
    up_weight,
    up_bias,
    conv_weight,
    conv_bias,
    res_in_weight,
    res_in_bias,
    res_out_weight,
    res_out_bias,
):
    conv_count = roster.shape[0]
    per_group = lax.axis_size("dev")
    devices_all = lax.axis_size("grp") * per_group
    most = MOST
    group_first = lax.axis_index("grp") * per_group
    local_index = lax.axis_index("dev")
    positions = jnp.arange(conv_count, dtype=jnp.int32)
    earlier = positions[None, :] < positions[:, None]

    anchor = roster // conv_count
    row = roster % conv_count
    rank_in = jnp.sum(earlier & (anchor[None, :] == anchor[:, None]), axis=1).astype(jnp.int32)
    key = anchor * most + rank_in
    spots = jnp.arange(devices_all * most, dtype=jnp.int32)
    code_request = jnp.sum(jnp.where(key[None, :] == spots[:, None], row[None, :] + 1, 0), axis=1) - 1
    source_dev = old_slot // conv_count - group_first
    source_row = old_slot % conv_count
    moved = source_dev != local_index
    everyone = jnp.arange(devices_all, dtype=jnp.int32)
    state_request = (
        jnp.sum(
            jnp.where(
                moved[None, :] & (source_dev[None, :] + group_first == everyone[:, None]),
                source_row[None, :] + 1,
                0,
            ),
            axis=1,
        )
        - 1
    )
    request = jnp.concatenate(
        [code_request.reshape(devices_all, most), state_request.reshape(devices_all, 1)], axis=1
    )
    lanes = 128
    padded = jnp.pad(request, ((0, 0), (0, lanes - most - 1))).reshape(devices_all, 1, lanes)
    (asked,) = exchange([(padded, True)], 0)
    asked = asked[:, 0, : most + 1]

    answer = jnp.take(codes, jnp.clip(asked[:, :most].reshape(-1), 0, conv_count - 1), axis=0)
    answer = answer.reshape(devices_all, -1)
    answer = jnp.pad(answer, ((0, 0), (0, lanes - answer.shape[1]))).reshape(devices_all, 1, lanes)
    state_asked = lax.dynamic_slice_in_dim(asked[:, most], group_first, per_group)
    leaving = jnp.take(states, jnp.clip(state_asked, 0, conv_count - 1), axis=0)
    leaving_high = leaving[:, :2].reshape(per_group, -1, lanes)
    leaving_low = leaving[:, 2:].astype(jnp.bfloat16).reshape(per_group, -1, lanes)
    answered, arrived, arrived_low = exchange(
        [(answer, True), (leaving_high, False), (leaving_low, False)], 1
    )
    code_width = codes.shape[1]
    answered = answered[:, 0, : most * code_width].reshape(devices_all * most, code_width)
    my_codes = jnp.take(answered, key, axis=0)
    routed = embed_codes(my_codes, code_table)
    return decode(
        routed,
        states,
        arrived,
        arrived_low,
        jnp.clip(source_dev, 0, per_group - 1),
        moved.astype(jnp.int32),
        up_weight,
        up_bias,
        conv_weight,
        conv_bias,
        res_in_weight,
        res_in_bias,
        res_out_weight,
        res_out_bias,
    )


def solution(mesh):
    in_specs = (
        P(("grp", "dev"), None),
        P(),
        P(("grp", "dev")),
        P(("grp", "dev")),
        P(("grp", "dev"), None, None),
        P(),
        P(),
        P(),
        P(),
        P(),
        P(),
        P(),
        P(),
    )
    out_specs = (P(("grp", "dev"), None, None), P(("grp", "dev"), None, None))
    return jax.shard_map(local, mesh=mesh, in_specs=in_specs, out_specs=out_specs, check_vma=False)
```

```python
import jax
import jax.numpy as jnp
from jax import lax
from jax.experimental import pallas as pl
from jax.experimental.pallas import tpu as pltpu
from jax.sharding import PartitionSpec as P

FRAMES = 4
MOST = 2


def embed_kernel(codes_ref, table_ref, out_ref, blocks, sems):
    books, rows = codes_ref.shape
    size = blocks.shape[1]

    def fetch(book):
        return pltpu.make_async_copy(table_ref.at[pl.ds(book * size, size)], blocks.at[book], sems.at[book])

    for book in range(books):
        fetch(book).start()
    by_row = jnp.transpose(codes_ref[...])
    total = None
    for book in range(books):
        fetch(book).wait()
        entries = lax.broadcasted_iota(jnp.int32, (rows, size), 1)
        onehot = (by_row[:, book : book + 1] == entries).astype(jnp.bfloat16)
        term = jnp.dot(onehot, blocks[book], preferred_element_type=jnp.float32)
        total = term if total is None else total + term
    out_ref[...] = total.astype(jnp.bfloat16)


def embed_codes(codes, code_table):
    row_count = codes.shape[0]
    book_count = codes.shape[1] // FRAMES
    book_size = code_table.shape[0] // book_count
    chan_width = code_table.shape[1]
    by_book = codes.reshape(row_count, FRAMES, book_count).transpose(2, 1, 0).reshape(book_count, -1)
    rows = FRAMES * row_count
    summed = pl.pallas_call(
        embed_kernel,
        in_specs=[pl.BlockSpec(memory_space=pltpu.VMEM), pl.BlockSpec(memory_space=pl.ANY)],
        out_specs=pl.BlockSpec(memory_space=pltpu.VMEM),
        out_shape=jax.ShapeDtypeStruct((rows, chan_width), jnp.bfloat16),
        scratch_shapes=[
            pltpu.VMEM((book_count, book_size, chan_width), code_table.dtype),
            pltpu.SemaphoreType.DMA((book_count,)),
        ],
    )(by_book, code_table)
    return summed.reshape(FRAMES, row_count, chan_width)


def pick_rows(table, index, live):
    entries = jnp.arange(table.shape[0], dtype=jnp.int32)
    select = (index[:, None] == entries[None, :]) & live[:, None]
    if table.dtype == jnp.bfloat16:
        return jnp.dot(
            select.astype(jnp.bfloat16), table, preferred_element_type=jnp.float32
        ).astype(jnp.bfloat16)
    if table.dtype == jnp.int32:
        picked = jnp.dot(
            select.astype(jnp.float32), table.astype(jnp.float32), precision=lax.Precision.HIGHEST
        )
        return picked.astype(jnp.int32)
    return jnp.dot(select.astype(jnp.float32), table, precision=lax.Precision.HIGHEST)


def prefix_count(flags):
    width = flags.shape[-1]
    positions = jnp.arange(width, dtype=jnp.int32)
    upper = (positions[:, None] <= positions[None, :]).astype(jnp.float32)
    return jnp.dot(flags.astype(jnp.float32), upper).astype(jnp.int32)


def compact(flags, ranks, values, slots):
    spots = jnp.arange(slots, dtype=jnp.int32)
    hit = flags[..., None, :] & (ranks[..., None, :] == spots[:, None])
    picked = jnp.sum(jnp.where(hit, values[..., None, :], 0), axis=-1)
    return (picked, jnp.any(hit, axis=-1))


def exchange(items, collective_id):
    groups = lax.axis_size("grp")
    per_group = lax.axis_size("dev")
    count = len(items)
    shapes = []
    for blocks, whole in items:
        if whole:
            shapes.append(jax.ShapeDtypeStruct((groups, per_group) + blocks.shape[1:], blocks.dtype))
        else:
            shapes.append(jax.ShapeDtypeStruct(blocks.shape, blocks.dtype))
    wholes = [index for index, (_, whole) in enumerate(items) if whole]

    def kernel(*refs):
        x_refs = refs[:count]
        o_refs = refs[count : 2 * count]
        mid_refs = dict(zip(wholes, refs[2 * count : 2 * count + len(wholes)]))
        sems = refs[2 * count + len(wholes) :]
        first_send, first_recv, second_send, second_recv, own_sem = sems
        group = lax.axis_index("grp")
        dev = lax.axis_index("dev")
        barrier = pltpu.get_barrier_semaphore()
        across = len(wholes) > 0

        if across:
            def greet_group(offset, carry):
                peer = lax.rem(group + offset, groups)
                pl.semaphore_signal(barrier, inc=1, device_id=(peer, dev), device_id_type=pl.DeviceIdType.MESH)
                return carry

            lax.fori_loop(1, groups, greet_group, 0)

        def greet_dev(offset, carry):
            peer = lax.rem(dev + offset, per_group)
            pl.semaphore_signal(barrier, inc=1, device_id=(group, peer), device_id_type=pl.DeviceIdType.MESH)
            return carry

        lax.fori_loop(1, per_group, greet_dev, 0)
        pl.semaphore_wait(barrier, (groups - 1 if across else 0) + per_group - 1)

        def hop_one(slot, index, peer, place):
            return pltpu.make_async_remote_copy(
                src_ref=x_refs[index].at[pl.ds(peer * per_group, per_group)],
                dst_ref=mid_refs[index].at[place],
                send_sem=first_send.at[slot, peer],
                recv_sem=first_recv.at[slot, place],
                device_id=(peer, dev),
                device_id_type=pl.DeviceIdType.MESH,
            )

        def hop_two(index, peer, place):
            if items[index][1]:
                source = mid_refs[index].at[:, peer]
                target = o_refs[index].at[:, place]
            else:
                source = x_refs[index].at[peer]
                target = o_refs[index].at[place]
            return pltpu.make_async_remote_copy(
                src_ref=source,
                dst_ref=target,
                send_sem=second_send.at[index, peer],
                recv_sem=second_recv.at[index, place],
                device_id=(group, peer),
                device_id_type=pl.DeviceIdType.MESH,
            )

        for slot, index in enumerate(wholes):
            def send_one(offset, carry, slot=slot, index=index):
                hop_one(slot, index, lax.rem(group + offset, groups), group).start()
                return carry

            lax.fori_loop(1, groups, send_one, 0)
        for index, (_, whole) in enumerate(items):
            if not whole:
                def send_group(offset, carry, index=index):
                    hop_two(index, lax.rem(dev + offset, per_group), dev).start()
                    return carry

                lax.fori_loop(1, per_group, send_group, 0)
        for slot, index in enumerate(wholes):
            own = pltpu.make_async_copy(
                x_refs[index].at[pl.ds(group * per_group, per_group)], mid_refs[index].at[group], own_sem
            )
            own.start()
            own.wait()

            def finish_one(offset, carry, slot=slot, index=index):
                hop_one(slot, index, lax.rem(group + offset, groups), group).wait_send()
                source = lax.rem(group + groups - offset, groups)
                hop_one(slot, index, source, source).wait_recv()
                return carry

            lax.fori_loop(1, groups, finish_one, 0)

            def send_two(offset, carry, index=index):
                hop_two(index, lax.rem(dev + offset, per_group), dev).start()
                return carry

            lax.fori_loop(1, per_group, send_two, 0)
        for index, (_, whole) in enumerate(items):
            if whole:
                own = pltpu.make_async_copy(mid_refs[index].at[:, dev], o_refs[index].at[:, dev], own_sem)
            else:
                own = pltpu.make_async_copy(x_refs[index].at[dev], o_refs[index].at[dev], own_sem)
            own.start()
            own.wait()

            def finish_two(offset, carry, index=index):
                hop_two(index, lax.rem(dev + offset, per_group), dev).wait_send()
                source = lax.rem(dev + per_group - offset, per_group)
                hop_two(index, source, source).wait_recv()
                return carry

            lax.fori_loop(1, per_group, finish_two, 0)

    mids = [shapes[index] for index in wholes]
    results = pl.pallas_call(
        kernel,
        out_shape=shapes + mids,
        in_specs=[pl.BlockSpec(memory_space=pl.ANY)] * count,
        out_specs=[pl.BlockSpec(memory_space=pl.ANY)] * (count + len(wholes)),
        scratch_shapes=[
            pltpu.SemaphoreType.DMA((max(len(wholes), 1), groups)),
            pltpu.SemaphoreType.DMA((max(len(wholes), 1), groups)),
            pltpu.SemaphoreType.DMA((count, per_group)),
            pltpu.SemaphoreType.DMA((count, per_group)),
            pltpu.SemaphoreType.DMA(()),
        ],
        compiler_params=pltpu.CompilerParams(collective_id=collective_id, has_side_effects=True),
        cost_estimate=pl.CostEstimate(flops=0, transcendentals=0, bytes_accessed=48 * 1024 * 1024),
    )(*[blocks for blocks, _ in items])
    return [
        result.reshape(blocks.shape) for result, (blocks, _) in zip(results[:count], items)
    ]


def decode_kernel(
    source_ref, moved_ref,
    routed_ref, states_ref, arrived_ref, arrived_low_ref, up_w_ref, up_b_ref, conv_w_ref, conv_b_ref, in_w_ref, in_b_ref, out_w_ref,
    out_b_ref, decoded_ref, new_ref, carried_ref,
):
    frame_count, slots, _ = routed_ref.shape
    step_count = 2 * frame_count
    rows = states_ref.shape[0]
    conv_taps = conv_w_ref.shape[0]
    res_taps = in_w_ref.shape[0]
    kept = rows - 2 - (res_taps - 1)
    base = pl.program_id(0) * slots

    carried_ref[...] = states_ref[...]

    def bring(slot, carry):
        @pl.when(moved_ref[base + slot] != 0)
        def _():
            source = source_ref[base + slot]
            pieces = carried_ref.shape[2] // arrived_ref.shape[2]
            for r in range(rows):
                if r < 2:
                    row = arrived_ref[source, pl.ds(r * pieces, pieces), :]
                else:
                    row = arrived_low_ref[source, pl.ds((r - 2) * pieces, pieces), :].astype(jnp.float32)
                carried_ref[r, pl.ds(slot, 1), :] = jnp.concatenate(
                    [row[k : k + 1] for k in range(pieces)], axis=1
                )

        return carry

    lax.fori_loop(0, slots, bring, 0)

    def elu(value):
        return jnp.where(value > 0, value, jnp.exp(jnp.minimum(value, 0.0)) - 1.0)

    up_w = up_w_ref[...]
    up_b = up_b_ref[...]
    inputs = [routed_ref[f].astype(jnp.float32) for f in range(frame_count)]
    carried = [carried_ref[r] for r in range(rows)]
    upsampled = []
    for f in range(frame_count):
        early_even = carried[0] if f == 0 else inputs[f - 1] * up_w[2:3]
        early_odd = carried[1] if f == 0 else inputs[f - 1] * up_w[3:4]
        upsampled.append((inputs[f] * up_w[0:1] + early_even) + up_b)
        upsampled.append((inputs[f] * up_w[1:2] + early_odd) + up_b)
    history = jnp.concatenate(
        [c.astype(jnp.bfloat16) for c in carried[2 : 2 + kept]] + [u.astype(jnp.bfloat16) for u in upsampled], axis=0
    )
    conv_out = None
    for tap in range(conv_taps):
        start = (conv_taps - 1 - tap) * slots
        term = jnp.dot(history[start : start + step_count * slots], conv_w_ref[tap], preferred_element_type=jnp.float32)
        conv_out = term if conv_out is None else conv_out + term
    conv_out = conv_out + conv_b_ref[...]
    active = elu(conv_out)
    res_rounded = jnp.concatenate(
        [c.astype(jnp.bfloat16) for c in carried[2 + kept :]] + [active.astype(jnp.bfloat16)], axis=0
    )
    inner = None
    for tap in range(res_taps):
        start = (res_taps - 1 - tap) * slots
        term = jnp.dot(res_rounded[start : start + step_count * slots], in_w_ref[tap], preferred_element_type=jnp.float32)
        inner = term if inner is None else inner + term
    squeezed = elu(inner + in_b_ref[...]).astype(jnp.bfloat16)
    summed = conv_out + jnp.dot(squeezed, out_w_ref[...], preferred_element_type=jnp.float32) + out_b_ref[...]
    decoded = summed.astype(jnp.bfloat16)
    for t in range(step_count):
        decoded_ref[:, t, :] = decoded[t * slots : (t + 1) * slots]
    new_ref[0] = inputs[frame_count - 1] * up_w[2:3]
    new_ref[1] = inputs[frame_count - 1] * up_w[3:4]
    for k in range(kept):
        row = history.shape[0] // slots - kept + k
        new_ref[2 + k] = history[row * slots : (row + 1) * slots].astype(jnp.float32)
    for k in range(res_taps - 1):
        row = step_count - (res_taps - 1) + k
        new_ref[2 + kept + k] = active[row * slots : (row + 1) * slots]


def decode(
    routed, states, arrived, arrived_low, source, moved, up_weight, up_bias, conv_weight, conv_bias, res_in_weight, res_in_bias,
    res_out_weight, res_out_bias,
):
    frame_count, conv_count, chan_width = routed.shape
    rows = states.shape[1]
    chunk = conv_count
    whole = lambda shape: pl.BlockSpec(shape, lambda i, *_: (0,) * len(shape))
    states_t = jnp.transpose(states, (1, 0, 2))
    decoded, new_t = pl.pallas_call(
        decode_kernel,
        grid_spec=pltpu.PrefetchScalarGridSpec(
            num_scalar_prefetch=2,
            grid=(conv_count // chunk,),
            in_specs=[
                pl.BlockSpec((frame_count, chunk, chan_width), lambda i, *_: (0, i, 0)),
                pl.BlockSpec((rows, chunk, chan_width), lambda i, *_: (0, i, 0)),
                whole(arrived.shape),
                whole(arrived_low.shape),
                whole(up_weight.shape),
                whole((1, chan_width)),
                whole(conv_weight.shape),
                whole((1, chan_width)),
                whole(res_in_weight.shape),
                whole((1, res_in_weight.shape[2])),
                whole(res_out_weight.shape),
                whole((1, chan_width)),
            ],
            out_specs=(
                pl.BlockSpec((chunk, 2 * frame_count, chan_width), lambda i, *_: (i, 0, 0)),
                pl.BlockSpec((rows, chunk, chan_width), lambda i, *_: (0, i, 0)),
            ),
            scratch_shapes=[pltpu.VMEM((rows, chunk, chan_width), jnp.float32)],
        ),
        out_shape=(
            jax.ShapeDtypeStruct((conv_count, 2 * frame_count, chan_width), jnp.bfloat16),
            jax.ShapeDtypeStruct((rows, conv_count, chan_width), jnp.float32),
        ),
        compiler_params=pltpu.CompilerParams(vmem_limit_bytes=48 * 1024 * 1024),
    )(
        source, moved, routed, states_t, arrived, arrived_low, up_weight, up_bias.reshape(1, -1), conv_weight,
        conv_bias.reshape(1, -1), res_in_weight, res_in_bias.reshape(1, -1), res_out_weight, res_out_bias.reshape(1, -1),
    )
    return decoded, jnp.transpose(new_t, (1, 0, 2))


def local(
    codes,
    code_table,
    roster,
    old_slot,
    states,
    up_weight,
    up_bias,
    conv_weight,
    conv_bias,
    res_in_weight,
    res_in_bias,
    res_out_weight,
    res_out_bias,
):
    conv_count = roster.shape[0]
    per_group = lax.axis_size("dev")
    devices_all = lax.axis_size("grp") * per_group
    most = MOST
    group_first = lax.axis_index("grp") * per_group
    local_index = lax.axis_index("dev")
    positions = jnp.arange(conv_count, dtype=jnp.int32)
    earlier = positions[None, :] < positions[:, None]

    anchor = roster // conv_count
    row = roster % conv_count
    rank_in = jnp.sum(earlier & (anchor[None, :] == anchor[:, None]), axis=1).astype(jnp.int32)
    key = anchor * most + rank_in
    spots = jnp.arange(devices_all * most, dtype=jnp.int32)
    code_request = jnp.sum(jnp.where(key[None, :] == spots[:, None], row[None, :] + 1, 0), axis=1) - 1
    source_dev = old_slot // conv_count - group_first
    source_row = old_slot % conv_count
    moved = source_dev != local_index
    everyone = jnp.arange(devices_all, dtype=jnp.int32)
    state_request = (
        jnp.sum(
            jnp.where(
                moved[None, :] & (source_dev[None, :] + group_first == everyone[:, None]),
                source_row[None, :] + 1,
                0,
            ),
            axis=1,
        )
        - 1
    )
    request = jnp.concatenate(
        [code_request.reshape(devices_all, most), state_request.reshape(devices_all, 1)], axis=1
    )
    lanes = 128
    padded = jnp.pad(request, ((0, 0), (0, lanes - most - 1))).reshape(devices_all, 1, lanes)
    (asked,) = exchange([(padded, True)], 0)
    asked = asked[:, 0, : most + 1]

    answer = jnp.take(codes, jnp.clip(asked[:, :most].reshape(-1), 0, conv_count - 1), axis=0)
    answer = answer.reshape(devices_all, -1)
    answer = jnp.pad(answer, ((0, 0), (0, lanes - answer.shape[1]))).reshape(devices_all, 1, lanes)
    state_asked = lax.dynamic_slice_in_dim(asked[:, most], group_first, per_group)
    leaving = jnp.take(states, jnp.clip(state_asked, 0, conv_count - 1), axis=0)
    leaving_high = leaving[:, :2].reshape(per_group, -1, lanes)
    leaving_low = leaving[:, 2:].astype(jnp.bfloat16).reshape(per_group, -1, lanes)
    answered, arrived, arrived_low = exchange(
        [(answer, True), (leaving_high, False), (leaving_low, False)], 1
    )
    code_width = codes.shape[1]
    answered = answered[:, 0, : most * code_width].reshape(devices_all * most, code_width)
    my_codes = jnp.take(answered, key, axis=0)
    routed = embed_codes(my_codes, code_table)
    return decode(
        routed,
        states,
        arrived,
        arrived_low,
        jnp.clip(source_dev, 0, per_group - 1),
        moved.astype(jnp.int32),
        up_weight,
        up_bias,
        conv_weight,
        conv_bias,
        res_in_weight,
        res_in_bias,
        res_out_weight,
        res_out_bias,
    )


def solution(mesh):
    in_specs = (
        P(("grp", "dev"), None),
        P(),
        P(("grp", "dev")),
        P(("grp", "dev")),
        P(("grp", "dev"), None, None),
        P(),
        P(),
        P(),
        P(),
        P(),
        P(),
        P(),
        P(),
    )
    out_specs = (P(("grp", "dev"), None, None), P(("grp", "dev"), None, None))
    return jax.shard_map(local, mesh=mesh, in_specs=in_specs, out_specs=out_specs, check_vma=False)
```

```python
import jax
import jax.numpy as jnp
from jax import lax
from jax.experimental import pallas as pl
from jax.experimental.pallas import tpu as pltpu
from jax.sharding import PartitionSpec as P

FRAMES = 4
MOST = 2


def embed_kernel(codes_ref, table_ref, out_ref, blocks, sems):
    books, rows = codes_ref.shape
    size = blocks.shape[1]

    def fetch(book):
        return pltpu.make_async_copy(table_ref.at[pl.ds(book * size, size)], blocks.at[book], sems.at[book])

    for book in range(books):
        fetch(book).start()
    by_row = jnp.transpose(codes_ref[...])
    total = None
    for book in range(books):
        fetch(book).wait()
        entries = lax.broadcasted_iota(jnp.int32, (rows, size), 1)
        onehot = (by_row[:, book : book + 1] == entries).astype(jnp.bfloat16)
        term = jnp.dot(onehot, blocks[book], preferred_element_type=jnp.float32)
        total = term if total is None else total + term
    out_ref[...] = total.astype(jnp.bfloat16)


def embed_codes(codes, code_table):
    row_count = codes.shape[0]
    book_count = codes.shape[1] // FRAMES
    book_size = code_table.shape[0] // book_count
    chan_width = code_table.shape[1]
    by_book = codes.reshape(row_count, FRAMES, book_count).transpose(2, 1, 0).reshape(book_count, -1)
    rows = FRAMES * row_count
    summed = pl.pallas_call(
        embed_kernel,
        in_specs=[pl.BlockSpec(memory_space=pltpu.VMEM), pl.BlockSpec(memory_space=pl.ANY)],
        out_specs=pl.BlockSpec(memory_space=pltpu.VMEM),
        out_shape=jax.ShapeDtypeStruct((rows, chan_width), jnp.bfloat16),
        scratch_shapes=[
            pltpu.VMEM((book_count, book_size, chan_width), code_table.dtype),
            pltpu.SemaphoreType.DMA((book_count,)),
        ],
    )(by_book, code_table)
    return summed.reshape(FRAMES, row_count, chan_width)


def pick_rows(table, index, live):
    entries = jnp.arange(table.shape[0], dtype=jnp.int32)
    select = (index[:, None] == entries[None, :]) & live[:, None]
    if table.dtype == jnp.bfloat16:
        return jnp.dot(
            select.astype(jnp.bfloat16), table, preferred_element_type=jnp.float32
        ).astype(jnp.bfloat16)
    if table.dtype == jnp.int32:
        picked = jnp.dot(
            select.astype(jnp.float32), table.astype(jnp.float32), precision=lax.Precision.HIGHEST
        )
        return picked.astype(jnp.int32)
    return jnp.dot(select.astype(jnp.float32), table, precision=lax.Precision.HIGHEST)


def prefix_count(flags):
    width = flags.shape[-1]
    positions = jnp.arange(width, dtype=jnp.int32)
    upper = (positions[:, None] <= positions[None, :]).astype(jnp.float32)
    return jnp.dot(flags.astype(jnp.float32), upper).astype(jnp.int32)


def compact(flags, ranks, values, slots):
    spots = jnp.arange(slots, dtype=jnp.int32)
    hit = flags[..., None, :] & (ranks[..., None, :] == spots[:, None])
    picked = jnp.sum(jnp.where(hit, values[..., None, :], 0), axis=-1)
    return (picked, jnp.any(hit, axis=-1))


def exchange(items, collective_id):
    groups = lax.axis_size("grp")
    per_group = lax.axis_size("dev")
    count = len(items)
    shapes = []
    for blocks, whole in items:
        if whole:
            shapes.append(jax.ShapeDtypeStruct((groups, per_group) + blocks.shape[1:], blocks.dtype))
        else:
            shapes.append(jax.ShapeDtypeStruct(blocks.shape, blocks.dtype))
    wholes = [index for index, (_, whole) in enumerate(items) if whole]

    def kernel(*refs):
        x_refs = refs[:count]
        o_refs = refs[count : 2 * count]
        mid_refs = dict(zip(wholes, refs[2 * count : 2 * count + len(wholes)]))
        sems = refs[2 * count + len(wholes) :]
        first_send, first_recv, second_send, second_recv, own_sem = sems
        group = lax.axis_index("grp")
        dev = lax.axis_index("dev")
        barrier = pltpu.get_barrier_semaphore()
        across = len(wholes) > 0

        if across:
            def greet_group(offset, carry):
                peer = lax.rem(group + offset, groups)
                pl.semaphore_signal(barrier, inc=1, device_id=(peer, dev), device_id_type=pl.DeviceIdType.MESH)
                return carry

            lax.fori_loop(1, groups, greet_group, 0)

        def greet_dev(offset, carry):
            peer = lax.rem(dev + offset, per_group)
            pl.semaphore_signal(barrier, inc=1, device_id=(group, peer), device_id_type=pl.DeviceIdType.MESH)
            return carry

        lax.fori_loop(1, per_group, greet_dev, 0)
        pl.semaphore_wait(barrier, (groups - 1 if across else 0) + per_group - 1)

        def hop_one(slot, index, peer, place):
            return pltpu.make_async_remote_copy(
                src_ref=x_refs[index].at[pl.ds(peer * per_group, per_group)],
                dst_ref=mid_refs[index].at[place],
                send_sem=first_send.at[slot, peer],
                recv_sem=first_recv.at[slot, place],
                device_id=(peer, dev),
                device_id_type=pl.DeviceIdType.MESH,
            )

        def hop_two(index, peer, place):
            if items[index][1]:
                source = mid_refs[index].at[:, peer]
                target = o_refs[index].at[:, place]
            else:
                source = x_refs[index].at[peer]
                target = o_refs[index].at[place]
            return pltpu.make_async_remote_copy(
                src_ref=source,
                dst_ref=target,
                send_sem=second_send.at[index, peer],
                recv_sem=second_recv.at[index, place],
                device_id=(group, peer),
                device_id_type=pl.DeviceIdType.MESH,
            )

        for slot, index in enumerate(wholes):
            def send_one(offset, carry, slot=slot, index=index):
                hop_one(slot, index, lax.rem(group + offset, groups), group).start()
                return carry

            lax.fori_loop(1, groups, send_one, 0)
        for index, (_, whole) in enumerate(items):
            if not whole:
                def send_group(offset, carry, index=index):
                    hop_two(index, lax.rem(dev + offset, per_group), dev).start()
                    return carry

                lax.fori_loop(1, per_group, send_group, 0)
        for slot, index in enumerate(wholes):
            own = pltpu.make_async_copy(
                x_refs[index].at[pl.ds(group * per_group, per_group)], mid_refs[index].at[group], own_sem
            )
            own.start()
            own.wait()

            def finish_one(offset, carry, slot=slot, index=index):
                hop_one(slot, index, lax.rem(group + offset, groups), group).wait_send()
                source = lax.rem(group + groups - offset, groups)
                hop_one(slot, index, source, source).wait_recv()
                return carry

            lax.fori_loop(1, groups, finish_one, 0)

            def send_two(offset, carry, index=index):
                hop_two(index, lax.rem(dev + offset, per_group), dev).start()
                return carry

            lax.fori_loop(1, per_group, send_two, 0)
        for index, (_, whole) in enumerate(items):
            if whole:
                own = pltpu.make_async_copy(mid_refs[index].at[:, dev], o_refs[index].at[:, dev], own_sem)
            else:
                own = pltpu.make_async_copy(x_refs[index].at[dev], o_refs[index].at[dev], own_sem)
            own.start()
            own.wait()

            def finish_two(offset, carry, index=index):
                hop_two(index, lax.rem(dev + offset, per_group), dev).wait_send()
                source = lax.rem(dev + per_group - offset, per_group)
                hop_two(index, source, source).wait_recv()
                return carry

            lax.fori_loop(1, per_group, finish_two, 0)

    mids = [shapes[index] for index in wholes]
    results = pl.pallas_call(
        kernel,
        out_shape=shapes + mids,
        in_specs=[pl.BlockSpec(memory_space=pl.ANY)] * count,
        out_specs=[pl.BlockSpec(memory_space=pl.ANY)] * (count + len(wholes)),
        scratch_shapes=[
            pltpu.SemaphoreType.DMA((max(len(wholes), 1), groups)),
            pltpu.SemaphoreType.DMA((max(len(wholes), 1), groups)),
            pltpu.SemaphoreType.DMA((count, per_group)),
            pltpu.SemaphoreType.DMA((count, per_group)),
            pltpu.SemaphoreType.DMA(()),
        ],
        compiler_params=pltpu.CompilerParams(collective_id=collective_id, has_side_effects=True),
        cost_estimate=pl.CostEstimate(flops=0, transcendentals=0, bytes_accessed=48 * 1024 * 1024),
    )(*[blocks for blocks, _ in items])
    return [
        result.reshape(blocks.shape) for result, (blocks, _) in zip(results[:count], items)
    ]


def decode_kernel(
    source_ref, moved_ref,
    routed_ref, states_ref, arrived_ref, arrived_low_ref, up_w_ref, up_b_ref, conv_w_ref, conv_b_ref, in_w_ref, in_b_ref, out_w_ref,
    out_b_ref, decoded_ref, new_ref, carried_ref,
):
    frame_count, slots, _ = routed_ref.shape
    step_count = 2 * frame_count
    rows = states_ref.shape[0]
    conv_taps = conv_w_ref.shape[0]
    res_taps = in_w_ref.shape[0]
    kept = rows - 2 - (res_taps - 1)
    base = pl.program_id(0) * slots

    carried_ref[...] = states_ref[...]

    def bring(slot, carry):
        @pl.when(moved_ref[base + slot] != 0)
        def _():
            source = source_ref[base + slot]
            pieces = carried_ref.shape[2] // arrived_ref.shape[2]
            for r in range(rows):
                if r < 2:
                    row = arrived_ref[source, pl.ds(r * pieces, pieces), :]
                else:
                    row = arrived_low_ref[source, pl.ds((r - 2) * pieces, pieces), :].astype(jnp.float32)
                carried_ref[r, pl.ds(slot, 1), :] = jnp.concatenate(
                    [row[k : k + 1] for k in range(pieces)], axis=1
                )

        return carry

    lax.fori_loop(0, slots, bring, 0)

    def elu(value):
        return jnp.where(value > 0, value, jnp.exp(jnp.minimum(value, 0.0)) - 1.0)

    up_w = up_w_ref[...]
    up_b = up_b_ref[...]
    inputs = [routed_ref[f].astype(jnp.float32) for f in range(frame_count)]
    carried = [carried_ref[r] for r in range(rows)]
    upsampled = []
    for f in range(frame_count):
        early_even = carried[0] if f == 0 else inputs[f - 1] * up_w[2:3]
        early_odd = carried[1] if f == 0 else inputs[f - 1] * up_w[3:4]
        upsampled.append((inputs[f] * up_w[0:1] + early_even) + up_b)
        upsampled.append((inputs[f] * up_w[1:2] + early_odd) + up_b)
    history = jnp.concatenate(
        [c.astype(jnp.bfloat16) for c in carried[2 : 2 + kept]] + [u.astype(jnp.bfloat16) for u in upsampled], axis=0
    )
    conv_out = None
    for tap in range(conv_taps):
        start = (conv_taps - 1 - tap) * slots
        term = jnp.dot(history[start : start + step_count * slots], conv_w_ref[tap], preferred_element_type=jnp.float32)
        conv_out = term if conv_out is None else conv_out + term
    conv_out = conv_out + conv_b_ref[...]
    active = elu(conv_out)
    res_rounded = jnp.concatenate(
        [c.astype(jnp.bfloat16) for c in carried[2 + kept :]] + [active.astype(jnp.bfloat16)], axis=0
    )
    inner = None
    for tap in range(res_taps):
        start = (res_taps - 1 - tap) * slots
        term = jnp.dot(res_rounded[start : start + step_count * slots], in_w_ref[tap], preferred_element_type=jnp.float32)
        inner = term if inner is None else inner + term
    squeezed = elu(inner + in_b_ref[...]).astype(jnp.bfloat16)
    summed = conv_out + jnp.dot(squeezed, out_w_ref[...], preferred_element_type=jnp.float32) + out_b_ref[...]
    decoded = summed.astype(jnp.bfloat16)
    for t in range(step_count):
        decoded_ref[t] = decoded[t * slots : (t + 1) * slots]
    new_ref[0] = inputs[frame_count - 1] * up_w[2:3]
    new_ref[1] = inputs[frame_count - 1] * up_w[3:4]
    for k in range(kept):
        row = history.shape[0] // slots - kept + k
        new_ref[2 + k] = history[row * slots : (row + 1) * slots].astype(jnp.float32)
    for k in range(res_taps - 1):
        row = step_count - (res_taps - 1) + k
        new_ref[2 + kept + k] = active[row * slots : (row + 1) * slots]


def decode(
    routed, states, arrived, arrived_low, source, moved, up_weight, up_bias, conv_weight, conv_bias, res_in_weight, res_in_bias,
    res_out_weight, res_out_bias,
):
    frame_count, conv_count, chan_width = routed.shape
    rows = states.shape[1]
    chunk = conv_count
    whole = lambda shape: pl.BlockSpec(shape, lambda i, *_: (0,) * len(shape))
    states_t = jnp.transpose(states, (1, 0, 2))
    decoded, new_t = pl.pallas_call(
        decode_kernel,
        grid_spec=pltpu.PrefetchScalarGridSpec(
            num_scalar_prefetch=2,
            grid=(conv_count // chunk,),
            in_specs=[
                pl.BlockSpec((frame_count, chunk, chan_width), lambda i, *_: (0, i, 0)),
                pl.BlockSpec((rows, chunk, chan_width), lambda i, *_: (0, i, 0)),
                whole(arrived.shape),
                whole(arrived_low.shape),
                whole(up_weight.shape),
                whole((1, chan_width)),
                whole(conv_weight.shape),
                whole((1, chan_width)),
                whole(res_in_weight.shape),
                whole((1, res_in_weight.shape[2])),
                whole(res_out_weight.shape),
                whole((1, chan_width)),
            ],
            out_specs=(
                pl.BlockSpec((2 * frame_count, chunk, chan_width), lambda i, *_: (0, i, 0)),
                pl.BlockSpec((rows, chunk, chan_width), lambda i, *_: (0, i, 0)),
            ),
            scratch_shapes=[pltpu.VMEM((rows, chunk, chan_width), jnp.float32)],
        ),
        out_shape=(
            jax.ShapeDtypeStruct((2 * frame_count, conv_count, chan_width), jnp.bfloat16),
            jax.ShapeDtypeStruct((rows, conv_count, chan_width), jnp.float32),
        ),
        compiler_params=pltpu.CompilerParams(vmem_limit_bytes=48 * 1024 * 1024),
    )(
        source, moved, routed, states_t, arrived, arrived_low, up_weight, up_bias.reshape(1, -1), conv_weight,
        conv_bias.reshape(1, -1), res_in_weight, res_in_bias.reshape(1, -1), res_out_weight, res_out_bias.reshape(1, -1),
    )
    return jnp.transpose(decoded, (1, 0, 2)), jnp.transpose(new_t, (1, 0, 2))


def local(
    codes,
    code_table,
    roster,
    old_slot,
    states,
    up_weight,
    up_bias,
    conv_weight,
    conv_bias,
    res_in_weight,
    res_in_bias,
    res_out_weight,
    res_out_bias,
):
    conv_count = roster.shape[0]
    per_group = lax.axis_size("dev")
    devices_all = lax.axis_size("grp") * per_group
    most = MOST
    group_first = lax.axis_index("grp") * per_group
    local_index = lax.axis_index("dev")
    positions = jnp.arange(conv_count, dtype=jnp.int32)
    earlier = positions[None, :] < positions[:, None]

    anchor = roster // conv_count
    row = roster % conv_count
    rank_in = jnp.sum(earlier & (anchor[None, :] == anchor[:, None]), axis=1).astype(jnp.int32)
    key = anchor * most + rank_in
    spots = jnp.arange(devices_all * most, dtype=jnp.int32)
    code_request = jnp.sum(jnp.where(key[None, :] == spots[:, None], row[None, :] + 1, 0), axis=1) - 1
    source_dev = old_slot // conv_count - group_first
    source_row = old_slot % conv_count
    moved = source_dev != local_index
    everyone = jnp.arange(devices_all, dtype=jnp.int32)
    state_request = (
        jnp.sum(
            jnp.where(
                moved[None, :] & (source_dev[None, :] + group_first == everyone[:, None]),
                source_row[None, :] + 1,
                0,
            ),
            axis=1,
        )
        - 1
    )
    request = jnp.concatenate(
        [code_request.reshape(devices_all, most), state_request.reshape(devices_all, 1)], axis=1
    )
    lanes = 128
    padded = jnp.pad(request, ((0, 0), (0, lanes - most - 1))).reshape(devices_all, 1, lanes)
    (asked,) = exchange([(padded, True)], 0)
    asked = asked[:, 0, : most + 1]

    answer = jnp.take(codes, jnp.clip(asked[:, :most].reshape(-1), 0, conv_count - 1), axis=0)
    answer = answer.reshape(devices_all, -1)
    answer = jnp.pad(answer, ((0, 0), (0, lanes - answer.shape[1]))).reshape(devices_all, 1, lanes)
    state_asked = lax.dynamic_slice_in_dim(asked[:, most], group_first, per_group)
    leaving = jnp.take(states, jnp.clip(state_asked, 0, conv_count - 1), axis=0)
    leaving_high = leaving[:, :2].reshape(per_group, -1, lanes)
    leaving_low = leaving[:, 2:].astype(jnp.bfloat16).reshape(per_group, -1, lanes)
    answered, arrived, arrived_low = exchange(
        [(answer, True), (leaving_high, False), (leaving_low, False)], 1
    )
    code_width = codes.shape[1]
    answered = answered[:, 0, : most * code_width].reshape(devices_all * most, code_width)
    my_codes = jnp.take(answered, key, axis=0)
    routed = embed_codes(my_codes, code_table)
    return decode(
        routed,
        states,
        arrived,
        arrived_low,
        jnp.clip(source_dev, 0, per_group - 1),
        moved.astype(jnp.int32),
        up_weight,
        up_bias,
        conv_weight,
        conv_bias,
        res_in_weight,
        res_in_bias,
        res_out_weight,
        res_out_bias,
    )


def solution(mesh):
    in_specs = (
        P(("grp", "dev"), None),
        P(),
        P(("grp", "dev")),
        P(("grp", "dev")),
        P(("grp", "dev"), None, None),
        P(),
        P(),
        P(),
        P(),
        P(),
        P(),
        P(),
        P(),
    )
    out_specs = (P(("grp", "dev"), None, None), P(("grp", "dev"), None, None))
    return jax.shard_map(local, mesh=mesh, in_specs=in_specs, out_specs=out_specs, check_vma=False)
```

```python
import jax
import jax.numpy as jnp
from jax import lax
from jax.experimental import pallas as pl
from jax.experimental.pallas import tpu as pltpu
from jax.sharding import PartitionSpec as P

FRAMES = 4
MOST = 2


def embed_kernel(anchor_ref, answered_ref, rank_ref, table_ref, out_ref, blocks, sems, mine_ref):
    books = blocks.shape[0]
    size = blocks.shape[1]
    slots = rank_ref.shape[0]

    def fetch(book):
        return pltpu.make_async_copy(table_ref.at[pl.ds(book * size, size)], blocks.at[book], sems.at[book])

    for book in range(books):
        fetch(book).start()

    def pick(slot, carry):
        mine_ref[pl.ds(slot, 1), :] = answered_ref[anchor_ref[slot]]
        return carry

    lax.fori_loop(0, slots, pick, 0)
    mine = mine_ref[...]
    width = books * FRAMES
    own = jnp.where(rank_ref[...] == 0, mine[:, :width], mine[:, width : 2 * width])
    by_row = jnp.concatenate([own[:, f * books : (f + 1) * books] for f in range(FRAMES)], axis=0)
    rows = by_row.shape[0]
    total = None
    for book in range(books):
        fetch(book).wait()
        entries = lax.broadcasted_iota(jnp.int32, (rows, size), 1)
        onehot = (by_row[:, book : book + 1] == entries).astype(jnp.bfloat16)
        term = jnp.dot(onehot, blocks[book], preferred_element_type=jnp.float32)
        total = term if total is None else total + term
    out_ref[...] = total.astype(jnp.bfloat16)


def embed_codes(answered, anchor, rank, code_table, code_width):
    row_count = anchor.shape[0]
    book_count = code_width // FRAMES
    book_size = code_table.shape[0] // book_count
    chan_width = code_table.shape[1]
    rows = FRAMES * row_count
    summed = pl.pallas_call(
        embed_kernel,
        in_specs=[
            pl.BlockSpec(memory_space=pltpu.SMEM),
            pl.BlockSpec(memory_space=pltpu.VMEM),
            pl.BlockSpec(memory_space=pltpu.VMEM),
            pl.BlockSpec(memory_space=pl.ANY),
        ],
        out_specs=pl.BlockSpec(memory_space=pltpu.VMEM),
        out_shape=jax.ShapeDtypeStruct((rows, chan_width), jnp.bfloat16),
        scratch_shapes=[
            pltpu.VMEM((book_count, book_size, chan_width), code_table.dtype),
            pltpu.SemaphoreType.DMA((book_count,)),
            pltpu.VMEM((row_count, answered.shape[-1]), answered.dtype),
        ],
    )(anchor, answered, rank.reshape(-1, 1), code_table)
    return summed.reshape(FRAMES, row_count, chan_width)


def pick_rows(table, index, live):
    entries = jnp.arange(table.shape[0], dtype=jnp.int32)
    select = (index[:, None] == entries[None, :]) & live[:, None]
    if table.dtype == jnp.bfloat16:
        return jnp.dot(
            select.astype(jnp.bfloat16), table, preferred_element_type=jnp.float32
        ).astype(jnp.bfloat16)
    if table.dtype == jnp.int32:
        picked = jnp.dot(
            select.astype(jnp.float32), table.astype(jnp.float32), precision=lax.Precision.HIGHEST
        )
        return picked.astype(jnp.int32)
    return jnp.dot(select.astype(jnp.float32), table, precision=lax.Precision.HIGHEST)


def prefix_count(flags):
    width = flags.shape[-1]
    positions = jnp.arange(width, dtype=jnp.int32)
    upper = (positions[:, None] <= positions[None, :]).astype(jnp.float32)
    return jnp.dot(flags.astype(jnp.float32), upper).astype(jnp.int32)


def compact(flags, ranks, values, slots):
    spots = jnp.arange(slots, dtype=jnp.int32)
    hit = flags[..., None, :] & (ranks[..., None, :] == spots[:, None])
    picked = jnp.sum(jnp.where(hit, values[..., None, :], 0), axis=-1)
    return (picked, jnp.any(hit, axis=-1))


def exchange(items, collective_id):
    groups = lax.axis_size("grp")
    per_group = lax.axis_size("dev")
    count = len(items)
    shapes = []
    for blocks, whole in items:
        if whole:
            shapes.append(jax.ShapeDtypeStruct((groups, per_group) + blocks.shape[1:], blocks.dtype))
        else:
            shapes.append(jax.ShapeDtypeStruct(blocks.shape, blocks.dtype))
    wholes = [index for index, (_, whole) in enumerate(items) if whole]

    def kernel(*refs):
        x_refs = refs[:count]
        o_refs = refs[count : 2 * count]
        mid_refs = dict(zip(wholes, refs[2 * count : 2 * count + len(wholes)]))
        sems = refs[2 * count + len(wholes) :]
        first_send, first_recv, second_send, second_recv, own_sem = sems
        group = lax.axis_index("grp")
        dev = lax.axis_index("dev")
        barrier = pltpu.get_barrier_semaphore()
        across = len(wholes) > 0

        if across:
            def greet_group(offset, carry):
                peer = lax.rem(group + offset, groups)
                pl.semaphore_signal(barrier, inc=1, device_id=(peer, dev), device_id_type=pl.DeviceIdType.MESH)
                return carry

            lax.fori_loop(1, groups, greet_group, 0)

        def greet_dev(offset, carry):
            peer = lax.rem(dev + offset, per_group)
            pl.semaphore_signal(barrier, inc=1, device_id=(group, peer), device_id_type=pl.DeviceIdType.MESH)
            return carry

        lax.fori_loop(1, per_group, greet_dev, 0)
        pl.semaphore_wait(barrier, (groups - 1 if across else 0) + per_group - 1)

        def hop_one(slot, index, peer, place):
            return pltpu.make_async_remote_copy(
                src_ref=x_refs[index].at[pl.ds(peer * per_group, per_group)],
                dst_ref=mid_refs[index].at[place],
                send_sem=first_send.at[slot, peer],
                recv_sem=first_recv.at[slot, place],
                device_id=(peer, dev),
                device_id_type=pl.DeviceIdType.MESH,
            )

        def hop_two(index, peer, place):
            if items[index][1]:
                source = mid_refs[index].at[:, peer]
                target = o_refs[index].at[:, place]
            else:
                source = x_refs[index].at[peer]
                target = o_refs[index].at[place]
            return pltpu.make_async_remote_copy(
                src_ref=source,
                dst_ref=target,
                send_sem=second_send.at[index, peer],
                recv_sem=second_recv.at[index, place],
                device_id=(group, peer),
                device_id_type=pl.DeviceIdType.MESH,
            )

        for slot, index in enumerate(wholes):
            def send_one(offset, carry, slot=slot, index=index):
                hop_one(slot, index, lax.rem(group + offset, groups), group).start()
                return carry

            lax.fori_loop(1, groups, send_one, 0)
        for index, (_, whole) in enumerate(items):
            if not whole:
                def send_group(offset, carry, index=index):
                    hop_two(index, lax.rem(dev + offset, per_group), dev).start()
                    return carry

                lax.fori_loop(1, per_group, send_group, 0)
        for slot, index in enumerate(wholes):
            own = pltpu.make_async_copy(
                x_refs[index].at[pl.ds(group * per_group, per_group)], mid_refs[index].at[group], own_sem
            )
            own.start()
            own.wait()

            def finish_one(offset, carry, slot=slot, index=index):
                hop_one(slot, index, lax.rem(group + offset, groups), group).wait_send()
                source = lax.rem(group + groups - offset, groups)
                hop_one(slot, index, source, source).wait_recv()
                return carry

            lax.fori_loop(1, groups, finish_one, 0)

            def send_two(offset, carry, index=index):
                hop_two(index, lax.rem(dev + offset, per_group), dev).start()
                return carry

            lax.fori_loop(1, per_group, send_two, 0)
        for index, (_, whole) in enumerate(items):
            if whole:
                own = pltpu.make_async_copy(mid_refs[index].at[:, dev], o_refs[index].at[:, dev], own_sem)
            else:
                own = pltpu.make_async_copy(x_refs[index].at[dev], o_refs[index].at[dev], own_sem)
            own.start()
            own.wait()

            def finish_two(offset, carry, index=index):
                hop_two(index, lax.rem(dev + offset, per_group), dev).wait_send()
                source = lax.rem(dev + per_group - offset, per_group)
                hop_two(index, source, source).wait_recv()
                return carry

            lax.fori_loop(1, per_group, finish_two, 0)

    mids = [shapes[index] for index in wholes]
    results = pl.pallas_call(
        kernel,
        out_shape=shapes + mids,
        in_specs=[pl.BlockSpec(memory_space=pl.ANY)] * count,
        out_specs=[pl.BlockSpec(memory_space=pl.ANY)] * (count + len(wholes)),
        scratch_shapes=[
            pltpu.SemaphoreType.DMA((max(len(wholes), 1), groups)),
            pltpu.SemaphoreType.DMA((max(len(wholes), 1), groups)),
            pltpu.SemaphoreType.DMA((count, per_group)),
            pltpu.SemaphoreType.DMA((count, per_group)),
            pltpu.SemaphoreType.DMA(()),
        ],
        compiler_params=pltpu.CompilerParams(collective_id=collective_id, has_side_effects=True),
        cost_estimate=pl.CostEstimate(flops=0, transcendentals=0, bytes_accessed=48 * 1024 * 1024),
    )(*[blocks for blocks, _ in items])
    return [
        result.reshape(blocks.shape) for result, (blocks, _) in zip(results[:count], items)
    ]


def decode_kernel(
    source_ref, moved_ref,
    routed_ref, states_ref, arrived_ref, arrived_low_ref, up_w_ref, up_b_ref, conv_w_ref, conv_b_ref, in_w_ref, in_b_ref, out_w_ref,
    out_b_ref, decoded_ref, new_ref, carried_ref,
):
    frame_count, slots, _ = routed_ref.shape
    step_count = 2 * frame_count
    rows = states_ref.shape[0]
    conv_taps = conv_w_ref.shape[0]
    res_taps = in_w_ref.shape[0]
    kept = rows - 2 - (res_taps - 1)
    base = pl.program_id(0) * slots

    carried_ref[...] = states_ref[...]

    def bring(slot, carry):
        @pl.when(moved_ref[base + slot] != 0)
        def _():
            source = source_ref[base + slot]
            pieces = carried_ref.shape[2] // arrived_ref.shape[2]
            for r in range(rows):
                if r < 2:
                    row = arrived_ref[source, pl.ds(r * pieces, pieces), :]
                else:
                    row = arrived_low_ref[source, pl.ds((r - 2) * pieces, pieces), :].astype(jnp.float32)
                carried_ref[r, pl.ds(slot, 1), :] = jnp.concatenate(
                    [row[k : k + 1] for k in range(pieces)], axis=1
                )

        return carry

    lax.fori_loop(0, slots, bring, 0)

    def elu(value):
        return jnp.where(value > 0, value, jnp.exp(jnp.minimum(value, 0.0)) - 1.0)

    up_w = up_w_ref[...]
    up_b = up_b_ref[...]
    inputs = [routed_ref[f].astype(jnp.float32) for f in range(frame_count)]
    carried = [carried_ref[r] for r in range(rows)]
    upsampled = []
    for f in range(frame_count):
        early_even = carried[0] if f == 0 else inputs[f - 1] * up_w[2:3]
        early_odd = carried[1] if f == 0 else inputs[f - 1] * up_w[3:4]
        upsampled.append((inputs[f] * up_w[0:1] + early_even) + up_b)
        upsampled.append((inputs[f] * up_w[1:2] + early_odd) + up_b)
    history = jnp.concatenate(
        [c.astype(jnp.bfloat16) for c in carried[2 : 2 + kept]] + [u.astype(jnp.bfloat16) for u in upsampled], axis=0
    )
    conv_out = None
    for tap in range(conv_taps):
        start = (conv_taps - 1 - tap) * slots
        term = jnp.dot(history[start : start + step_count * slots], conv_w_ref[tap], preferred_element_type=jnp.float32)
        conv_out = term if conv_out is None else conv_out + term
    conv_out = conv_out + conv_b_ref[...]
    active = elu(conv_out)
    res_rounded = jnp.concatenate(
        [c.astype(jnp.bfloat16) for c in carried[2 + kept :]] + [active.astype(jnp.bfloat16)], axis=0
    )
    inner = None
    for tap in range(res_taps):
        start = (res_taps - 1 - tap) * slots
        term = jnp.dot(res_rounded[start : start + step_count * slots], in_w_ref[tap], preferred_element_type=jnp.float32)
        inner = term if inner is None else inner + term
    squeezed = elu(inner + in_b_ref[...]).astype(jnp.bfloat16)
    summed = conv_out + jnp.dot(squeezed, out_w_ref[...], preferred_element_type=jnp.float32) + out_b_ref[...]
    decoded = summed.astype(jnp.bfloat16)
    for t in range(step_count):
        decoded_ref[:, t, :] = decoded[t * slots : (t + 1) * slots]
    new_ref[0] = inputs[frame_count - 1] * up_w[2:3]
    new_ref[1] = inputs[frame_count - 1] * up_w[3:4]
    for k in range(kept):
        row = history.shape[0] // slots - kept + k
        new_ref[2 + k] = history[row * slots : (row + 1) * slots].astype(jnp.float32)
    for k in range(res_taps - 1):
        row = step_count - (res_taps - 1) + k
        new_ref[2 + kept + k] = active[row * slots : (row + 1) * slots]


def decode(
    routed, states, arrived, arrived_low, source, moved, up_weight, up_bias, conv_weight, conv_bias, res_in_weight, res_in_bias,
    res_out_weight, res_out_bias,
):
    frame_count, conv_count, chan_width = routed.shape
    rows = states.shape[1]
    chunk = conv_count
    whole = lambda shape: pl.BlockSpec(shape, lambda i, *_: (0,) * len(shape))
    states_t = jnp.transpose(states, (1, 0, 2))
    decoded, new_t = pl.pallas_call(
        decode_kernel,
        grid_spec=pltpu.PrefetchScalarGridSpec(
            num_scalar_prefetch=2,
            grid=(conv_count // chunk,),
            in_specs=[
                pl.BlockSpec((frame_count, chunk, chan_width), lambda i, *_: (0, i, 0)),
                pl.BlockSpec((rows, chunk, chan_width), lambda i, *_: (0, i, 0)),
                whole(arrived.shape),
                whole(arrived_low.shape),
                whole(up_weight.shape),
                whole((1, chan_width)),
                whole(conv_weight.shape),
                whole((1, chan_width)),
                whole(res_in_weight.shape),
                whole((1, res_in_weight.shape[2])),
                whole(res_out_weight.shape),
                whole((1, chan_width)),
            ],
            out_specs=(
                pl.BlockSpec((chunk, 2 * frame_count, chan_width), lambda i, *_: (i, 0, 0)),
                pl.BlockSpec((rows, chunk, chan_width), lambda i, *_: (0, i, 0)),
            ),
            scratch_shapes=[pltpu.VMEM((rows, chunk, chan_width), jnp.float32)],
        ),
        out_shape=(
            jax.ShapeDtypeStruct((conv_count, 2 * frame_count, chan_width), jnp.bfloat16),
            jax.ShapeDtypeStruct((rows, conv_count, chan_width), jnp.float32),
        ),
        compiler_params=pltpu.CompilerParams(vmem_limit_bytes=48 * 1024 * 1024),
    )(
        source, moved, routed, states_t, arrived, arrived_low, up_weight, up_bias.reshape(1, -1), conv_weight,
        conv_bias.reshape(1, -1), res_in_weight, res_in_bias.reshape(1, -1), res_out_weight, res_out_bias.reshape(1, -1),
    )
    return decoded, jnp.transpose(new_t, (1, 0, 2))


def local(
    codes,
    code_table,
    roster,
    old_slot,
    states,
    up_weight,
    up_bias,
    conv_weight,
    conv_bias,
    res_in_weight,
    res_in_bias,
    res_out_weight,
    res_out_bias,
):
    conv_count = roster.shape[0]
    per_group = lax.axis_size("dev")
    devices_all = lax.axis_size("grp") * per_group
    most = MOST
    group_first = lax.axis_index("grp") * per_group
    local_index = lax.axis_index("dev")
    positions = jnp.arange(conv_count, dtype=jnp.int32)
    earlier = positions[None, :] < positions[:, None]

    anchor = roster // conv_count
    row = roster % conv_count
    rank_in = jnp.sum(earlier & (anchor[None, :] == anchor[:, None]), axis=1).astype(jnp.int32)
    key = anchor * most + rank_in
    spots = jnp.arange(devices_all * most, dtype=jnp.int32)
    code_request = jnp.sum(jnp.where(key[None, :] == spots[:, None], row[None, :] + 1, 0), axis=1) - 1
    source_dev = old_slot // conv_count - group_first
    source_row = old_slot % conv_count
    moved = source_dev != local_index
    everyone = jnp.arange(devices_all, dtype=jnp.int32)
    state_request = (
        jnp.sum(
            jnp.where(
                moved[None, :] & (source_dev[None, :] + group_first == everyone[:, None]),
                source_row[None, :] + 1,
                0,
            ),
            axis=1,
        )
        - 1
    )
    request = jnp.concatenate(
        [code_request.reshape(devices_all, most), state_request.reshape(devices_all, 1)], axis=1
    )
    lanes = 128
    padded = jnp.pad(request, ((0, 0), (0, lanes - most - 1))).reshape(devices_all, 1, lanes)
    (asked,) = exchange([(padded, True)], 0)
    asked = asked[:, 0, : most + 1]

    answer = jnp.take(codes, jnp.clip(asked[:, :most].reshape(-1), 0, conv_count - 1), axis=0)
    answer = answer.reshape(devices_all, -1)
    answer = jnp.pad(answer, ((0, 0), (0, lanes - answer.shape[1]))).reshape(devices_all, 1, lanes)
    state_asked = lax.dynamic_slice_in_dim(asked[:, most], group_first, per_group)
    leaving = jnp.take(states, jnp.clip(state_asked, 0, conv_count - 1), axis=0)
    leaving_high = leaving[:, :2].reshape(per_group, -1, lanes)
    leaving_low = leaving[:, 2:].astype(jnp.bfloat16).reshape(per_group, -1, lanes)
    answered, arrived, arrived_low = exchange(
        [(answer, True), (leaving_high, False), (leaving_low, False)], 1
    )
    code_width = codes.shape[1]
    routed = embed_codes(answered, anchor, rank_in, code_table, code_width)
    return decode(
        routed,
        states,
        arrived,
        arrived_low,
        jnp.clip(source_dev, 0, per_group - 1),
        moved.astype(jnp.int32),
        up_weight,
        up_bias,
        conv_weight,
        conv_bias,
        res_in_weight,
        res_in_bias,
        res_out_weight,
        res_out_bias,
    )


def solution(mesh):
    in_specs = (
        P(("grp", "dev"), None),
        P(),
        P(("grp", "dev")),
        P(("grp", "dev")),
        P(("grp", "dev"), None, None),
        P(),
        P(),
        P(),
        P(),
        P(),
        P(),
        P(),
        P(),
    )
    out_specs = (P(("grp", "dev"), None, None), P(("grp", "dev"), None, None))
    return jax.shard_map(local, mesh=mesh, in_specs=in_specs, out_specs=out_specs, check_vma=False)
```

```python
import jax
import jax.numpy as jnp
from jax import lax
from jax.experimental import pallas as pl
from jax.experimental.pallas import tpu as pltpu
from jax.sharding import PartitionSpec as P

FRAMES = 4
MOST = 2


def embed_kernel(anchor_ref, answered_ref, rank_ref, table_ref, out_ref, blocks, sems, mine_ref):
    books = blocks.shape[0]
    size = blocks.shape[1]
    slots = rank_ref.shape[0]

    def fetch(book):
        return pltpu.make_async_copy(table_ref.at[pl.ds(book * size, size)], blocks.at[book], sems.at[book])

    for book in range(books):
        fetch(book).start()

    def pick(slot, carry):
        mine_ref[pl.ds(slot, 1), :] = answered_ref[anchor_ref[slot]]
        return carry

    lax.fori_loop(0, slots, pick, 0)
    mine = mine_ref[...]
    width = books * FRAMES
    own = jnp.where(rank_ref[...] == 0, mine[:, :width], mine[:, width : 2 * width])
    by_row = jnp.concatenate([own[:, f * books : (f + 1) * books] for f in range(FRAMES)], axis=0)
    rows = by_row.shape[0]
    total = None
    for book in range(books):
        fetch(book).wait()
        entries = lax.broadcasted_iota(jnp.int32, (rows, size), 1)
        onehot = (by_row[:, book : book + 1] == entries).astype(jnp.bfloat16)
        term = jnp.dot(onehot, blocks[book], preferred_element_type=jnp.float32)
        total = term if total is None else total + term
    out_ref[...] = total.astype(jnp.bfloat16)


def embed_codes(answered, anchor, rank, code_table, code_width):
    row_count = anchor.shape[0]
    book_count = code_width // FRAMES
    book_size = code_table.shape[0] // book_count
    chan_width = code_table.shape[1]
    rows = FRAMES * row_count
    summed = pl.pallas_call(
        embed_kernel,
        in_specs=[
            pl.BlockSpec(memory_space=pltpu.SMEM),
            pl.BlockSpec(memory_space=pltpu.VMEM),
            pl.BlockSpec(memory_space=pltpu.VMEM),
            pl.BlockSpec(memory_space=pl.ANY),
        ],
        out_specs=pl.BlockSpec(memory_space=pltpu.VMEM),
        out_shape=jax.ShapeDtypeStruct((rows, chan_width), jnp.bfloat16),
        scratch_shapes=[
            pltpu.VMEM((book_count, book_size, chan_width), code_table.dtype),
            pltpu.SemaphoreType.DMA((book_count,)),
            pltpu.VMEM((row_count, answered.shape[-1]), answered.dtype),
        ],
    )(anchor, answered, rank.reshape(-1, 1), code_table)
    return summed.reshape(FRAMES, row_count, chan_width)


def pick_rows(table, index, live):
    entries = jnp.arange(table.shape[0], dtype=jnp.int32)
    select = (index[:, None] == entries[None, :]) & live[:, None]
    if table.dtype == jnp.bfloat16:
        return jnp.dot(
            select.astype(jnp.bfloat16), table, preferred_element_type=jnp.float32
        ).astype(jnp.bfloat16)
    if table.dtype == jnp.int32:
        picked = jnp.dot(
            select.astype(jnp.float32), table.astype(jnp.float32), precision=lax.Precision.HIGHEST
        )
        return picked.astype(jnp.int32)
    return jnp.dot(select.astype(jnp.float32), table, precision=lax.Precision.HIGHEST)


def prefix_count(flags):
    width = flags.shape[-1]
    positions = jnp.arange(width, dtype=jnp.int32)
    upper = (positions[:, None] <= positions[None, :]).astype(jnp.float32)
    return jnp.dot(flags.astype(jnp.float32), upper).astype(jnp.int32)


def compact(flags, ranks, values, slots):
    spots = jnp.arange(slots, dtype=jnp.int32)
    hit = flags[..., None, :] & (ranks[..., None, :] == spots[:, None])
    picked = jnp.sum(jnp.where(hit, values[..., None, :], 0), axis=-1)
    return (picked, jnp.any(hit, axis=-1))


def exchange(items, collective_id):
    groups = lax.axis_size("grp")
    per_group = lax.axis_size("dev")
    count = len(items)
    shapes = []
    for blocks, whole in items:
        if whole:
            shapes.append(jax.ShapeDtypeStruct((groups, per_group) + blocks.shape[1:], blocks.dtype))
        else:
            shapes.append(jax.ShapeDtypeStruct(blocks.shape, blocks.dtype))
    wholes = [index for index, (_, whole) in enumerate(items) if whole]

    def kernel(*refs):
        x_refs = refs[:count]
        o_refs = refs[count : 2 * count]
        mid_refs = dict(zip(wholes, refs[2 * count : 2 * count + len(wholes)]))
        sems = refs[2 * count + len(wholes) :]
        first_send, first_recv, second_send, second_recv, own_sem = sems
        group = lax.axis_index("grp")
        dev = lax.axis_index("dev")
        barrier = pltpu.get_barrier_semaphore()
        across = len(wholes) > 0

        if across:
            def greet_group(offset, carry):
                peer = lax.rem(group + offset, groups)
                pl.semaphore_signal(barrier, inc=1, device_id=(peer, dev), device_id_type=pl.DeviceIdType.MESH)
                return carry

            lax.fori_loop(1, groups, greet_group, 0)

        def greet_dev(offset, carry):
            peer = lax.rem(dev + offset, per_group)
            pl.semaphore_signal(barrier, inc=1, device_id=(group, peer), device_id_type=pl.DeviceIdType.MESH)
            return carry

        lax.fori_loop(1, per_group, greet_dev, 0)
        pl.semaphore_wait(barrier, (groups - 1 if across else 0) + per_group - 1)

        def hop_one(slot, index, peer, place):
            return pltpu.make_async_remote_copy(
                src_ref=x_refs[index].at[pl.ds(peer * per_group, per_group)],
                dst_ref=mid_refs[index].at[place],
                send_sem=first_send.at[slot, peer],
                recv_sem=first_recv.at[slot, place],
                device_id=(peer, dev),
                device_id_type=pl.DeviceIdType.MESH,
            )

        def hop_two(index, peer, place):
            if items[index][1]:
                source = mid_refs[index].at[:, peer]
                target = o_refs[index].at[:, place]
            else:
                source = x_refs[index].at[peer]
                target = o_refs[index].at[place]
            return pltpu.make_async_remote_copy(
                src_ref=source,
                dst_ref=target,
                send_sem=second_send.at[index, peer],
                recv_sem=second_recv.at[index, place],
                device_id=(group, peer),
                device_id_type=pl.DeviceIdType.MESH,
            )

        for slot, index in enumerate(wholes):
            def send_one(offset, carry, slot=slot, index=index):
                hop_one(slot, index, lax.rem(group + offset, groups), group).start()
                return carry

            lax.fori_loop(1, groups, send_one, 0)
        for index, (_, whole) in enumerate(items):
            if not whole:
                def send_group(offset, carry, index=index):
                    hop_two(index, lax.rem(dev + offset, per_group), dev).start()
                    return carry

                lax.fori_loop(1, per_group, send_group, 0)
        for slot, index in enumerate(wholes):
            own = pltpu.make_async_copy(
                x_refs[index].at[pl.ds(group * per_group, per_group)], mid_refs[index].at[group], own_sem
            )
            own.start()
            own.wait()

            def finish_one(offset, carry, slot=slot, index=index):
                hop_one(slot, index, lax.rem(group + offset, groups), group).wait_send()
                source = lax.rem(group + groups - offset, groups)
                hop_one(slot, index, source, source).wait_recv()
                return carry

            lax.fori_loop(1, groups, finish_one, 0)

            def send_two(offset, carry, index=index):
                hop_two(index, lax.rem(dev + offset, per_group), dev).start()
                return carry

            lax.fori_loop(1, per_group, send_two, 0)
        for index, (_, whole) in enumerate(items):
            if whole:
                own = pltpu.make_async_copy(mid_refs[index].at[:, dev], o_refs[index].at[:, dev], own_sem)
            else:
                own = pltpu.make_async_copy(x_refs[index].at[dev], o_refs[index].at[dev], own_sem)
            own.start()
            own.wait()

            def finish_two(offset, carry, index=index):
                hop_two(index, lax.rem(dev + offset, per_group), dev).wait_send()
                source = lax.rem(dev + per_group - offset, per_group)
                hop_two(index, source, source).wait_recv()
                return carry

            lax.fori_loop(1, per_group, finish_two, 0)

    mids = [shapes[index] for index in wholes]
    results = pl.pallas_call(
        kernel,
        out_shape=shapes + mids,
        in_specs=[pl.BlockSpec(memory_space=pl.ANY)] * count,
        out_specs=[pl.BlockSpec(memory_space=pl.ANY)] * (count + len(wholes)),
        scratch_shapes=[
            pltpu.SemaphoreType.DMA((max(len(wholes), 1), groups)),
            pltpu.SemaphoreType.DMA((max(len(wholes), 1), groups)),
            pltpu.SemaphoreType.DMA((count, per_group)),
            pltpu.SemaphoreType.DMA((count, per_group)),
            pltpu.SemaphoreType.DMA(()),
        ],
        compiler_params=pltpu.CompilerParams(collective_id=collective_id, has_side_effects=True),
        cost_estimate=pl.CostEstimate(flops=0, transcendentals=0, bytes_accessed=48 * 1024 * 1024),
    )(*[blocks for blocks, _ in items])
    return [
        result.reshape(blocks.shape) for result, (blocks, _) in zip(results[:count], items)
    ]


def pack_kernel(asked_ref, states_ref, high_ref, low_ref, low_scratch):
    peers = high_ref.shape[0]
    rows, slots, width = states_ref.shape
    lanes = high_ref.shape[2]
    pieces = width // lanes

    def one(peer, carry):
        index = jnp.clip(asked_ref[peer], 0, slots - 1)
        for r in range(rows):
            line = states_ref[r, pl.ds(index, 1), :]
            for k in range(pieces):
                piece = line[:, k * lanes : (k + 1) * lanes]
                if r < 2:
                    high_ref[peer, pl.ds(r * pieces + k, 1), :] = piece
                else:
                    low_scratch[peer, pl.ds((r - 2) * pieces + k, 1), :] = piece
        return carry

    lax.fori_loop(0, peers, one, 0)
    low_ref[...] = low_scratch[...].astype(low_ref.dtype)


def pack_leaving(asked, states_t, lanes):
    peers = asked.shape[0]
    rows, _, width = states_t.shape
    pieces = width // lanes
    return pl.pallas_call(
        pack_kernel,
        in_specs=[pl.BlockSpec(memory_space=pltpu.SMEM), pl.BlockSpec(memory_space=pltpu.VMEM)],
        out_specs=[pl.BlockSpec(memory_space=pltpu.VMEM)] * 2,
        out_shape=[
            jax.ShapeDtypeStruct((peers, 2 * pieces, lanes), states_t.dtype),
            jax.ShapeDtypeStruct((peers, (rows - 2) * pieces, lanes), jnp.bfloat16),
        ],
        scratch_shapes=[pltpu.VMEM((peers, (rows - 2) * pieces, lanes), jnp.float32)],
    )(asked, states_t)


def decode_kernel(
    source_ref, moved_ref,
    routed_ref, states_ref, arrived_ref, arrived_low_ref, up_w_ref, up_b_ref, conv_w_ref, conv_b_ref, in_w_ref, in_b_ref, out_w_ref,
    out_b_ref, decoded_ref, new_ref, carried_ref,
):
    frame_count, slots, _ = routed_ref.shape
    step_count = 2 * frame_count
    rows = states_ref.shape[0]
    conv_taps = conv_w_ref.shape[0]
    res_taps = in_w_ref.shape[0]
    kept = rows - 2 - (res_taps - 1)
    base = pl.program_id(0) * slots

    carried_ref[...] = states_ref[...]

    def bring(slot, carry):
        @pl.when(moved_ref[base + slot] != 0)
        def _():
            source = source_ref[base + slot]
            pieces = carried_ref.shape[2] // arrived_ref.shape[2]
            for r in range(rows):
                if r < 2:
                    row = arrived_ref[source, pl.ds(r * pieces, pieces), :]
                else:
                    row = arrived_low_ref[source, pl.ds((r - 2) * pieces, pieces), :].astype(jnp.float32)
                carried_ref[r, pl.ds(slot, 1), :] = jnp.concatenate(
                    [row[k : k + 1] for k in range(pieces)], axis=1
                )

        return carry

    lax.fori_loop(0, slots, bring, 0)

    def elu(value):
        return jnp.where(value > 0, value, jnp.exp(jnp.minimum(value, 0.0)) - 1.0)

    up_w = up_w_ref[...]
    up_b = up_b_ref[...]
    inputs = [routed_ref[f].astype(jnp.float32) for f in range(frame_count)]
    carried = [carried_ref[r] for r in range(rows)]
    upsampled = []
    for f in range(frame_count):
        early_even = carried[0] if f == 0 else inputs[f - 1] * up_w[2:3]
        early_odd = carried[1] if f == 0 else inputs[f - 1] * up_w[3:4]
        upsampled.append((inputs[f] * up_w[0:1] + early_even) + up_b)
        upsampled.append((inputs[f] * up_w[1:2] + early_odd) + up_b)
    history = jnp.concatenate(
        [c.astype(jnp.bfloat16) for c in carried[2 : 2 + kept]] + [u.astype(jnp.bfloat16) for u in upsampled], axis=0
    )
    conv_out = None
    for tap in range(conv_taps):
        start = (conv_taps - 1 - tap) * slots
        term = jnp.dot(history[start : start + step_count * slots], conv_w_ref[tap], preferred_element_type=jnp.float32)
        conv_out = term if conv_out is None else conv_out + term
    conv_out = conv_out + conv_b_ref[...]
    active = elu(conv_out)
    res_rounded = jnp.concatenate(
        [c.astype(jnp.bfloat16) for c in carried[2 + kept :]] + [active.astype(jnp.bfloat16)], axis=0
    )
    inner = None
    for tap in range(res_taps):
        start = (res_taps - 1 - tap) * slots
        term = jnp.dot(res_rounded[start : start + step_count * slots], in_w_ref[tap], preferred_element_type=jnp.float32)
        inner = term if inner is None else inner + term
    squeezed = elu(inner + in_b_ref[...]).astype(jnp.bfloat16)
    summed = conv_out + jnp.dot(squeezed, out_w_ref[...], preferred_element_type=jnp.float32) + out_b_ref[...]
    decoded = summed.astype(jnp.bfloat16)
    for t in range(step_count):
        decoded_ref[:, t, :] = decoded[t * slots : (t + 1) * slots]
    new_ref[0] = inputs[frame_count - 1] * up_w[2:3]
    new_ref[1] = inputs[frame_count - 1] * up_w[3:4]
    for k in range(kept):
        row = history.shape[0] // slots - kept + k
        new_ref[2 + k] = history[row * slots : (row + 1) * slots].astype(jnp.float32)
    for k in range(res_taps - 1):
        row = step_count - (res_taps - 1) + k
        new_ref[2 + kept + k] = active[row * slots : (row + 1) * slots]


def decode(
    routed, states, arrived, arrived_low, source, moved, up_weight, up_bias, conv_weight, conv_bias, res_in_weight, res_in_bias,
    res_out_weight, res_out_bias,
):
    frame_count, conv_count, chan_width = routed.shape
    rows = states.shape[1]
    chunk = conv_count
    whole = lambda shape: pl.BlockSpec(shape, lambda i, *_: (0,) * len(shape))
    states_t = jnp.transpose(states, (1, 0, 2))
    decoded, new_t = pl.pallas_call(
        decode_kernel,
        grid_spec=pltpu.PrefetchScalarGridSpec(
            num_scalar_prefetch=2,
            grid=(conv_count // chunk,),
            in_specs=[
                pl.BlockSpec((frame_count, chunk, chan_width), lambda i, *_: (0, i, 0)),
                pl.BlockSpec((rows, chunk, chan_width), lambda i, *_: (0, i, 0)),
                whole(arrived.shape),
                whole(arrived_low.shape),
                whole(up_weight.shape),
                whole((1, chan_width)),
                whole(conv_weight.shape),
                whole((1, chan_width)),
                whole(res_in_weight.shape),
                whole((1, res_in_weight.shape[2])),
                whole(res_out_weight.shape),
                whole((1, chan_width)),
            ],
            out_specs=(
                pl.BlockSpec((chunk, 2 * frame_count, chan_width), lambda i, *_: (i, 0, 0)),
                pl.BlockSpec((rows, chunk, chan_width), lambda i, *_: (0, i, 0)),
            ),
            scratch_shapes=[pltpu.VMEM((rows, chunk, chan_width), jnp.float32)],
        ),
        out_shape=(
            jax.ShapeDtypeStruct((conv_count, 2 * frame_count, chan_width), jnp.bfloat16),
            jax.ShapeDtypeStruct((rows, conv_count, chan_width), jnp.float32),
        ),
        compiler_params=pltpu.CompilerParams(vmem_limit_bytes=48 * 1024 * 1024),
    )(
        source, moved, routed, states_t, arrived, arrived_low, up_weight, up_bias.reshape(1, -1), conv_weight,
        conv_bias.reshape(1, -1), res_in_weight, res_in_bias.reshape(1, -1), res_out_weight, res_out_bias.reshape(1, -1),
    )
    return decoded, jnp.transpose(new_t, (1, 0, 2))


def local(
    codes,
    code_table,
    roster,
    old_slot,
    states,
    up_weight,
    up_bias,
    conv_weight,
    conv_bias,
    res_in_weight,
    res_in_bias,
    res_out_weight,
    res_out_bias,
):
    conv_count = roster.shape[0]
    per_group = lax.axis_size("dev")
    devices_all = lax.axis_size("grp") * per_group
    most = MOST
    group_first = lax.axis_index("grp") * per_group
    local_index = lax.axis_index("dev")
    positions = jnp.arange(conv_count, dtype=jnp.int32)
    earlier = positions[None, :] < positions[:, None]

    anchor = roster // conv_count
    row = roster % conv_count
    rank_in = jnp.sum(earlier & (anchor[None, :] == anchor[:, None]), axis=1).astype(jnp.int32)
    key = anchor * most + rank_in
    spots = jnp.arange(devices_all * most, dtype=jnp.int32)
    code_request = jnp.sum(jnp.where(key[None, :] == spots[:, None], row[None, :] + 1, 0), axis=1) - 1
    source_dev = old_slot // conv_count - group_first
    source_row = old_slot % conv_count
    moved = source_dev != local_index
    everyone = jnp.arange(devices_all, dtype=jnp.int32)
    state_request = (
        jnp.sum(
            jnp.where(
                moved[None, :] & (source_dev[None, :] + group_first == everyone[:, None]),
                source_row[None, :] + 1,
                0,
            ),
            axis=1,
        )
        - 1
    )
    request = jnp.concatenate(
        [code_request.reshape(devices_all, most), state_request.reshape(devices_all, 1)], axis=1
    )
    lanes = 128
    padded = jnp.pad(request, ((0, 0), (0, lanes - most - 1))).reshape(devices_all, 1, lanes)
    (asked,) = exchange([(padded, True)], 0)
    asked = asked[:, 0, : most + 1]

    answer = jnp.take(codes, jnp.clip(asked[:, :most].reshape(-1), 0, conv_count - 1), axis=0)
    answer = answer.reshape(devices_all, -1)
    answer = jnp.pad(answer, ((0, 0), (0, lanes - answer.shape[1]))).reshape(devices_all, 1, lanes)
    state_asked = lax.dynamic_slice_in_dim(asked[:, most], group_first, per_group)
    leaving_high, leaving_low = pack_leaving(state_asked, jnp.transpose(states, (1, 0, 2)), lanes)
    answered, arrived, arrived_low = exchange(
        [(answer, True), (leaving_high, False), (leaving_low, False)], 1
    )
    code_width = codes.shape[1]
    routed = embed_codes(answered, anchor, rank_in, code_table, code_width)
    return decode(
        routed,
        states,
        arrived,
        arrived_low,
        jnp.clip(source_dev, 0, per_group - 1),
        moved.astype(jnp.int32),
        up_weight,
        up_bias,
        conv_weight,
        conv_bias,
        res_in_weight,
        res_in_bias,
        res_out_weight,
        res_out_bias,
    )


def solution(mesh):
    in_specs = (
        P(("grp", "dev"), None),
        P(),
        P(("grp", "dev")),
        P(("grp", "dev")),
        P(("grp", "dev"), None, None),
        P(),
        P(),
        P(),
        P(),
        P(),
        P(),
        P(),
        P(),
    )
    out_specs = (P(("grp", "dev"), None, None), P(("grp", "dev"), None, None))
    return jax.shard_map(local, mesh=mesh, in_specs=in_specs, out_specs=out_specs, check_vma=False)
```

```python
import jax
import jax.numpy as jnp
from jax import lax
from jax.experimental import pallas as pl
from jax.experimental.pallas import tpu as pltpu
from jax.sharding import PartitionSpec as P

FRAMES = 4
MOST = 2


def embed_kernel(anchor_ref, answered_ref, rank_ref, table_ref, out_ref, blocks, sems, mine_ref):
    books = blocks.shape[0]
    size = blocks.shape[1]
    slots = rank_ref.shape[0]

    def fetch(book):
        return pltpu.make_async_copy(table_ref.at[pl.ds(book * size, size)], blocks.at[book], sems.at[book])

    for book in range(books):
        fetch(book).start()

    def pick(slot, carry):
        mine_ref[pl.ds(slot, 1), :] = answered_ref[anchor_ref[slot]]
        return carry

    lax.fori_loop(0, slots, pick, 0)
    mine = mine_ref[...]
    width = books * FRAMES
    own = jnp.where(rank_ref[...] == 0, mine[:, :width], mine[:, width : 2 * width])
    by_row = jnp.concatenate([own[:, f * books : (f + 1) * books] for f in range(FRAMES)], axis=0)
    rows = by_row.shape[0]
    total = None
    for book in range(books):
        fetch(book).wait()
        entries = lax.broadcasted_iota(jnp.int32, (rows, size), 1)
        onehot = (by_row[:, book : book + 1] == entries).astype(jnp.bfloat16)
        term = jnp.dot(onehot, blocks[book], preferred_element_type=jnp.float32)
        total = term if total is None else total + term
    out_ref[...] = total.astype(jnp.bfloat16)


def embed_codes(answered, anchor, rank, code_table, code_width):
    row_count = anchor.shape[0]
    book_count = code_width // FRAMES
    book_size = code_table.shape[0] // book_count
    chan_width = code_table.shape[1]
    rows = FRAMES * row_count
    summed = pl.pallas_call(
        embed_kernel,
        in_specs=[
            pl.BlockSpec(memory_space=pltpu.SMEM),
            pl.BlockSpec(memory_space=pltpu.VMEM),
            pl.BlockSpec(memory_space=pltpu.VMEM),
            pl.BlockSpec(memory_space=pl.ANY),
        ],
        out_specs=pl.BlockSpec(memory_space=pltpu.VMEM),
        out_shape=jax.ShapeDtypeStruct((rows, chan_width), jnp.bfloat16),
        scratch_shapes=[
            pltpu.VMEM((book_count, book_size, chan_width), code_table.dtype),
            pltpu.SemaphoreType.DMA((book_count,)),
            pltpu.VMEM((row_count, answered.shape[-1]), answered.dtype),
        ],
    )(anchor, answered, rank.reshape(-1, 1), code_table)
    return summed.reshape(FRAMES, row_count, chan_width)


def pick_rows(table, index, live):
    entries = jnp.arange(table.shape[0], dtype=jnp.int32)
    select = (index[:, None] == entries[None, :]) & live[:, None]
    if table.dtype == jnp.bfloat16:
        return jnp.dot(
            select.astype(jnp.bfloat16), table, preferred_element_type=jnp.float32
        ).astype(jnp.bfloat16)
    if table.dtype == jnp.int32:
        picked = jnp.dot(
            select.astype(jnp.float32), table.astype(jnp.float32), precision=lax.Precision.HIGHEST
        )
        return picked.astype(jnp.int32)
    return jnp.dot(select.astype(jnp.float32), table, precision=lax.Precision.HIGHEST)


def prefix_count(flags):
    width = flags.shape[-1]
    positions = jnp.arange(width, dtype=jnp.int32)
    upper = (positions[:, None] <= positions[None, :]).astype(jnp.float32)
    return jnp.dot(flags.astype(jnp.float32), upper).astype(jnp.int32)


def compact(flags, ranks, values, slots):
    spots = jnp.arange(slots, dtype=jnp.int32)
    hit = flags[..., None, :] & (ranks[..., None, :] == spots[:, None])
    picked = jnp.sum(jnp.where(hit, values[..., None, :], 0), axis=-1)
    return (picked, jnp.any(hit, axis=-1))


def exchange(items, collective_id):
    groups = lax.axis_size("grp")
    per_group = lax.axis_size("dev")
    count = len(items)
    shapes = []
    for blocks, whole in items:
        if whole:
            shapes.append(jax.ShapeDtypeStruct((groups, per_group) + blocks.shape[1:], blocks.dtype))
        else:
            shapes.append(jax.ShapeDtypeStruct(blocks.shape, blocks.dtype))
    wholes = [index for index, (_, whole) in enumerate(items) if whole]

    def kernel(*refs):
        x_refs = refs[:count]
        o_refs = refs[count : 2 * count]
        mid_refs = dict(zip(wholes, refs[2 * count : 2 * count + len(wholes)]))
        sems = refs[2 * count + len(wholes) :]
        first_send, first_recv, second_send, second_recv, own_sem = sems
        group = lax.axis_index("grp")
        dev = lax.axis_index("dev")
        barrier = pltpu.get_barrier_semaphore()
        across = len(wholes) > 0

        if across:
            def greet_group(offset, carry):
                peer = lax.rem(group + offset, groups)
                pl.semaphore_signal(barrier, inc=1, device_id=(peer, dev), device_id_type=pl.DeviceIdType.MESH)
                return carry

            lax.fori_loop(1, groups, greet_group, 0)

        def greet_dev(offset, carry):
            peer = lax.rem(dev + offset, per_group)
            pl.semaphore_signal(barrier, inc=1, device_id=(group, peer), device_id_type=pl.DeviceIdType.MESH)
            return carry

        lax.fori_loop(1, per_group, greet_dev, 0)
        pl.semaphore_wait(barrier, (groups - 1 if across else 0) + per_group - 1)

        def hop_one(slot, index, peer, place):
            return pltpu.make_async_remote_copy(
                src_ref=x_refs[index].at[pl.ds(peer * per_group, per_group)],
                dst_ref=mid_refs[index].at[place],
                send_sem=first_send.at[slot, peer],
                recv_sem=first_recv.at[slot, place],
                device_id=(peer, dev),
                device_id_type=pl.DeviceIdType.MESH,
            )

        def hop_two(index, peer, place):
            if items[index][1]:
                source = mid_refs[index].at[:, peer]
                target = o_refs[index].at[:, place]
            else:
                source = x_refs[index].at[peer]
                target = o_refs[index].at[place]
            return pltpu.make_async_remote_copy(
                src_ref=source,
                dst_ref=target,
                send_sem=second_send.at[index, peer],
                recv_sem=second_recv.at[index, place],
                device_id=(group, peer),
                device_id_type=pl.DeviceIdType.MESH,
            )

        for slot, index in enumerate(wholes):
            def send_one(offset, carry, slot=slot, index=index):
                hop_one(slot, index, lax.rem(group + offset, groups), group).start()
                return carry

            lax.fori_loop(1, groups, send_one, 0)
        for index, (_, whole) in enumerate(items):
            if not whole:
                def send_group(offset, carry, index=index):
                    hop_two(index, lax.rem(dev + offset, per_group), dev).start()
                    return carry

                lax.fori_loop(1, per_group, send_group, 0)
        for slot, index in enumerate(wholes):
            own = pltpu.make_async_copy(
                x_refs[index].at[pl.ds(group * per_group, per_group)], mid_refs[index].at[group], own_sem
            )
            own.start()
            own.wait()

            def finish_one(offset, carry, slot=slot, index=index):
                hop_one(slot, index, lax.rem(group + offset, groups), group).wait_send()
                source = lax.rem(group + groups - offset, groups)
                hop_one(slot, index, source, source).wait_recv()
                return carry

            lax.fori_loop(1, groups, finish_one, 0)

            def send_two(offset, carry, index=index):
                hop_two(index, lax.rem(dev + offset, per_group), dev).start()
                return carry

            lax.fori_loop(1, per_group, send_two, 0)
        for index, (_, whole) in enumerate(items):
            if whole:
                own = pltpu.make_async_copy(mid_refs[index].at[:, dev], o_refs[index].at[:, dev], own_sem)
            else:
                own = pltpu.make_async_copy(x_refs[index].at[dev], o_refs[index].at[dev], own_sem)
            own.start()
            own.wait()

            def finish_two(offset, carry, index=index):
                hop_two(index, lax.rem(dev + offset, per_group), dev).wait_send()
                source = lax.rem(dev + per_group - offset, per_group)
                hop_two(index, source, source).wait_recv()
                return carry

            lax.fori_loop(1, per_group, finish_two, 0)

    mids = [shapes[index] for index in wholes]
    results = pl.pallas_call(
        kernel,
        out_shape=shapes + mids,
        in_specs=[pl.BlockSpec(memory_space=pl.ANY)] * count,
        out_specs=[pl.BlockSpec(memory_space=pl.ANY)] * (count + len(wholes)),
        scratch_shapes=[
            pltpu.SemaphoreType.DMA((max(len(wholes), 1), groups)),
            pltpu.SemaphoreType.DMA((max(len(wholes), 1), groups)),
            pltpu.SemaphoreType.DMA((count, per_group)),
            pltpu.SemaphoreType.DMA((count, per_group)),
            pltpu.SemaphoreType.DMA(()),
        ],
        compiler_params=pltpu.CompilerParams(collective_id=collective_id, has_side_effects=True),
        cost_estimate=pl.CostEstimate(flops=0, transcendentals=0, bytes_accessed=48 * 1024 * 1024),
    )(*[blocks for blocks, _ in items])
    return [
        result.reshape(blocks.shape) for result, (blocks, _) in zip(results[:count], items)
    ]


def pack_kernel(asked_ref, states_ref, high_ref, low_ref, lines_ref, low_scratch, sem):
    peers = high_ref.shape[0]
    rows, slots, width = states_ref.shape
    lanes = high_ref.shape[2]
    pieces = width // lanes
    first = lax.axis_index("grp") * peers

    def fetch(peer, carry):
        index = jnp.clip(asked_ref[first + peer, 0, 2], 0, slots - 1)
        pltpu.make_async_copy(states_ref.at[:, pl.ds(index, 1), :], lines_ref.at[:, pl.ds(peer, 1), :], sem).start()
        return carry

    lax.fori_loop(0, peers, fetch, 0)
    pltpu.make_async_copy(lines_ref, lines_ref, sem).wait()

    def one(peer, carry):
        for r in range(rows):
            line = lines_ref[r, pl.ds(peer, 1), :]
            for k in range(pieces):
                piece = line[:, k * lanes : (k + 1) * lanes]
                if r < 2:
                    high_ref[peer, pl.ds(r * pieces + k, 1), :] = piece
                else:
                    low_scratch[peer, pl.ds((r - 2) * pieces + k, 1), :] = piece
        return carry

    lax.fori_loop(0, peers, one, 0)
    low_ref[...] = low_scratch[...].astype(low_ref.dtype)


def pack_leaving(asked, states_t, lanes, peers):
    rows, _, width = states_t.shape
    pieces = width // lanes
    return pl.pallas_call(
        pack_kernel,
        in_specs=[pl.BlockSpec(memory_space=pltpu.SMEM), pl.BlockSpec(memory_space=pl.ANY)],
        out_specs=[pl.BlockSpec(memory_space=pltpu.VMEM)] * 2,
        out_shape=[
            jax.ShapeDtypeStruct((peers, 2 * pieces, lanes), states_t.dtype),
            jax.ShapeDtypeStruct((peers, (rows - 2) * pieces, lanes), jnp.bfloat16),
        ],
        scratch_shapes=[
            pltpu.VMEM((rows, peers, width), states_t.dtype),
            pltpu.VMEM((peers, (rows - 2) * pieces, lanes), jnp.float32),
            pltpu.SemaphoreType.DMA(()),
        ],
    )(asked, states_t)


def decode_kernel(
    source_ref, moved_ref,
    routed_ref, states_ref, arrived_ref, arrived_low_ref, up_w_ref, up_b_ref, conv_w_ref, conv_b_ref, in_w_ref, in_b_ref, out_w_ref,
    out_b_ref, decoded_ref, new_ref, carried_ref,
):
    frame_count, slots, _ = routed_ref.shape
    step_count = 2 * frame_count
    rows = states_ref.shape[0]
    conv_taps = conv_w_ref.shape[0]
    res_taps = in_w_ref.shape[0]
    kept = rows - 2 - (res_taps - 1)
    base = pl.program_id(0) * slots

    carried_ref[...] = states_ref[...]

    def bring(slot, carry):
        @pl.when(moved_ref[base + slot] != 0)
        def _():
            source = source_ref[base + slot]
            pieces = carried_ref.shape[2] // arrived_ref.shape[2]
            for r in range(rows):
                if r < 2:
                    row = arrived_ref[source, pl.ds(r * pieces, pieces), :]
                else:
                    row = arrived_low_ref[source, pl.ds((r - 2) * pieces, pieces), :].astype(jnp.float32)
                carried_ref[r, pl.ds(slot, 1), :] = jnp.concatenate(
                    [row[k : k + 1] for k in range(pieces)], axis=1
                )

        return carry

    lax.fori_loop(0, slots, bring, 0)

    def elu(value):
        return jnp.where(value > 0, value, jnp.exp(jnp.minimum(value, 0.0)) - 1.0)

    up_w = up_w_ref[...]
    up_b = up_b_ref[...]
    inputs = [routed_ref[f].astype(jnp.float32) for f in range(frame_count)]
    carried = [carried_ref[r] for r in range(rows)]
    upsampled = []
    for f in range(frame_count):
        early_even = carried[0] if f == 0 else inputs[f - 1] * up_w[2:3]
        early_odd = carried[1] if f == 0 else inputs[f - 1] * up_w[3:4]
        upsampled.append((inputs[f] * up_w[0:1] + early_even) + up_b)
        upsampled.append((inputs[f] * up_w[1:2] + early_odd) + up_b)
    history = jnp.concatenate(
        [c.astype(jnp.bfloat16) for c in carried[2 : 2 + kept]] + [u.astype(jnp.bfloat16) for u in upsampled], axis=0
    )
    conv_out = None
    for tap in range(conv_taps):
        start = (conv_taps - 1 - tap) * slots
        term = jnp.dot(history[start : start + step_count * slots], conv_w_ref[tap], preferred_element_type=jnp.float32)
        conv_out = term if conv_out is None else conv_out + term
    conv_out = conv_out + conv_b_ref[...]
    active = elu(conv_out)
    res_rounded = jnp.concatenate(
        [c.astype(jnp.bfloat16) for c in carried[2 + kept :]] + [active.astype(jnp.bfloat16)], axis=0
    )
    inner = None
    for tap in range(res_taps):
        start = (res_taps - 1 - tap) * slots
        term = jnp.dot(res_rounded[start : start + step_count * slots], in_w_ref[tap], preferred_element_type=jnp.float32)
        inner = term if inner is None else inner + term
    squeezed = elu(inner + in_b_ref[...]).astype(jnp.bfloat16)
    summed = conv_out + jnp.dot(squeezed, out_w_ref[...], preferred_element_type=jnp.float32) + out_b_ref[...]
    decoded = summed.astype(jnp.bfloat16)
    for t in range(step_count):
        decoded_ref[:, t, :] = decoded[t * slots : (t + 1) * slots]
    new_ref[0] = inputs[frame_count - 1] * up_w[2:3]
    new_ref[1] = inputs[frame_count - 1] * up_w[3:4]
    for k in range(kept):
        row = history.shape[0] // slots - kept + k
        new_ref[2 + k] = history[row * slots : (row + 1) * slots].astype(jnp.float32)
    for k in range(res_taps - 1):
        row = step_count - (res_taps - 1) + k
        new_ref[2 + kept + k] = active[row * slots : (row + 1) * slots]


def decode(
    routed, states, arrived, arrived_low, source, moved, up_weight, up_bias, conv_weight, conv_bias, res_in_weight, res_in_bias,
    res_out_weight, res_out_bias,
):
    frame_count, conv_count, chan_width = routed.shape
    rows = states.shape[1]
    chunk = conv_count
    whole = lambda shape: pl.BlockSpec(shape, lambda i, *_: (0,) * len(shape))
    states_t = jnp.transpose(states, (1, 0, 2))
    decoded, new_t = pl.pallas_call(
        decode_kernel,
        grid_spec=pltpu.PrefetchScalarGridSpec(
            num_scalar_prefetch=2,
            grid=(conv_count // chunk,),
            in_specs=[
                pl.BlockSpec((frame_count, chunk, chan_width), lambda i, *_: (0, i, 0)),
                pl.BlockSpec((rows, chunk, chan_width), lambda i, *_: (0, i, 0)),
                whole(arrived.shape),
                whole(arrived_low.shape),
                whole(up_weight.shape),
                whole((1, chan_width)),
                whole(conv_weight.shape),
                whole((1, chan_width)),
                whole(res_in_weight.shape),
                whole((1, res_in_weight.shape[2])),
                whole(res_out_weight.shape),
                whole((1, chan_width)),
            ],
            out_specs=(
                pl.BlockSpec((chunk, 2 * frame_count, chan_width), lambda i, *_: (i, 0, 0)),
                pl.BlockSpec((rows, chunk, chan_width), lambda i, *_: (0, i, 0)),
            ),
            scratch_shapes=[pltpu.VMEM((rows, chunk, chan_width), jnp.float32)],
        ),
        out_shape=(
            jax.ShapeDtypeStruct((conv_count, 2 * frame_count, chan_width), jnp.bfloat16),
            jax.ShapeDtypeStruct((rows, conv_count, chan_width), jnp.float32),
        ),
        compiler_params=pltpu.CompilerParams(vmem_limit_bytes=48 * 1024 * 1024),
    )(
        source, moved, routed, states_t, arrived, arrived_low, up_weight, up_bias.reshape(1, -1), conv_weight,
        conv_bias.reshape(1, -1), res_in_weight, res_in_bias.reshape(1, -1), res_out_weight, res_out_bias.reshape(1, -1),
    )
    return decoded, jnp.transpose(new_t, (1, 0, 2))


def local(
    codes,
    code_table,
    roster,
    old_slot,
    states,
    up_weight,
    up_bias,
    conv_weight,
    conv_bias,
    res_in_weight,
    res_in_bias,
    res_out_weight,
    res_out_bias,
):
    conv_count = roster.shape[0]
    per_group = lax.axis_size("dev")
    devices_all = lax.axis_size("grp") * per_group
    most = MOST
    group_first = lax.axis_index("grp") * per_group
    local_index = lax.axis_index("dev")
    positions = jnp.arange(conv_count, dtype=jnp.int32)
    earlier = positions[None, :] < positions[:, None]

    anchor = roster // conv_count
    row = roster % conv_count
    rank_in = jnp.sum(earlier & (anchor[None, :] == anchor[:, None]), axis=1).astype(jnp.int32)
    key = anchor * most + rank_in
    spots = jnp.arange(devices_all * most, dtype=jnp.int32)
    code_request = jnp.sum(jnp.where(key[None, :] == spots[:, None], row[None, :] + 1, 0), axis=1) - 1
    source_dev = old_slot // conv_count - group_first
    source_row = old_slot % conv_count
    moved = source_dev != local_index
    everyone = jnp.arange(devices_all, dtype=jnp.int32)
    state_request = (
        jnp.sum(
            jnp.where(
                moved[None, :] & (source_dev[None, :] + group_first == everyone[:, None]),
                source_row[None, :] + 1,
                0,
            ),
            axis=1,
        )
        - 1
    )
    request = jnp.concatenate(
        [code_request.reshape(devices_all, most), state_request.reshape(devices_all, 1)], axis=1
    )
    lanes = 128
    padded = jnp.pad(request, ((0, 0), (0, lanes - most - 1))).reshape(devices_all, 1, lanes)
    (asked,) = exchange([(padded, True)], 0)
    asked_blocks = asked
    asked = asked[:, 0, : most + 1]

    answer = jnp.take(codes, jnp.clip(asked[:, :most].reshape(-1), 0, conv_count - 1), axis=0)
    answer = answer.reshape(devices_all, -1)
    answer = jnp.pad(answer, ((0, 0), (0, lanes - answer.shape[1]))).reshape(devices_all, 1, lanes)
    leaving_high, leaving_low = pack_leaving(asked_blocks, jnp.transpose(states, (1, 0, 2)), lanes, per_group)
    answered, arrived, arrived_low = exchange(
        [(answer, True), (leaving_high, False), (leaving_low, False)], 1
    )
    code_width = codes.shape[1]
    routed = embed_codes(answered, anchor, rank_in, code_table, code_width)
    return decode(
        routed,
        states,
        arrived,
        arrived_low,
        jnp.clip(source_dev, 0, per_group - 1),
        moved.astype(jnp.int32),
        up_weight,
        up_bias,
        conv_weight,
        conv_bias,
        res_in_weight,
        res_in_bias,
        res_out_weight,
        res_out_bias,
    )


def solution(mesh):
    in_specs = (
        P(("grp", "dev"), None),
        P(),
        P(("grp", "dev")),
        P(("grp", "dev")),
        P(("grp", "dev"), None, None),
        P(),
        P(),
        P(),
        P(),
        P(),
        P(),
        P(),
        P(),
    )
    out_specs = (P(("grp", "dev"), None, None), P(("grp", "dev"), None, None))
    return jax.shard_map(local, mesh=mesh, in_specs=in_specs, out_specs=out_specs, check_vma=False)
```

```python
import jax
import jax.numpy as jnp
from jax import lax
from jax.experimental import pallas as pl
from jax.experimental.pallas import tpu as pltpu
from jax.sharding import PartitionSpec as P

FRAMES = 4
MOST = 2


def embed_kernel(anchor_ref, answered_ref, rank_ref, table_ref, out_ref, blocks, sems, mine_ref):
    books = blocks.shape[0]
    size = blocks.shape[1]
    slots = rank_ref.shape[0]

    def fetch(book):
        return pltpu.make_async_copy(table_ref.at[pl.ds(book * size, size)], blocks.at[book], sems.at[book])

    for book in range(books):
        fetch(book).start()

    def pick(slot, carry):
        mine_ref[pl.ds(slot, 1), :] = answered_ref[anchor_ref[slot]]
        return carry

    lax.fori_loop(0, slots, pick, 0)
    mine = mine_ref[...]
    width = books * FRAMES
    own = jnp.where(rank_ref[...] == 0, mine[:, :width], mine[:, width : 2 * width])
    by_row = jnp.concatenate([own[:, f * books : (f + 1) * books] for f in range(FRAMES)], axis=0)
    rows = by_row.shape[0]
    entries = lax.broadcasted_iota(jnp.int32, (rows, size), 1)
    total = None
    for book in range(books):
        fetch(book).wait()
        onehot = (by_row[:, book : book + 1] == entries).astype(jnp.bfloat16)
        term = jnp.dot(onehot, blocks[book], preferred_element_type=jnp.float32)
        total = term if total is None else total + term
    out_ref[...] = total.astype(jnp.bfloat16)


def embed_codes(answered, anchor, rank, code_table, code_width):
    row_count = anchor.shape[0]
    book_count = code_width // FRAMES
    book_size = code_table.shape[0] // book_count
    chan_width = code_table.shape[1]
    rows = FRAMES * row_count
    summed = pl.pallas_call(
        embed_kernel,
        in_specs=[
            pl.BlockSpec(memory_space=pltpu.SMEM),
            pl.BlockSpec(memory_space=pltpu.VMEM),
            pl.BlockSpec(memory_space=pltpu.VMEM),
            pl.BlockSpec(memory_space=pl.ANY),
        ],
        out_specs=pl.BlockSpec(memory_space=pltpu.VMEM),
        out_shape=jax.ShapeDtypeStruct((rows, chan_width), jnp.bfloat16),
        scratch_shapes=[
            pltpu.VMEM((book_count, book_size, chan_width), code_table.dtype),
            pltpu.SemaphoreType.DMA((book_count,)),
            pltpu.VMEM((row_count, answered.shape[-1]), answered.dtype),
        ],
    )(anchor, answered, rank.reshape(-1, 1), code_table)
    return summed.reshape(FRAMES, row_count, chan_width)


def pick_rows(table, index, live):
    entries = jnp.arange(table.shape[0], dtype=jnp.int32)
    select = (index[:, None] == entries[None, :]) & live[:, None]
    if table.dtype == jnp.bfloat16:
        return jnp.dot(
            select.astype(jnp.bfloat16), table, preferred_element_type=jnp.float32
        ).astype(jnp.bfloat16)
    if table.dtype == jnp.int32:
        picked = jnp.dot(
            select.astype(jnp.float32), table.astype(jnp.float32), precision=lax.Precision.HIGHEST
        )
        return picked.astype(jnp.int32)
    return jnp.dot(select.astype(jnp.float32), table, precision=lax.Precision.HIGHEST)


def prefix_count(flags):
    width = flags.shape[-1]
    positions = jnp.arange(width, dtype=jnp.int32)
    upper = (positions[:, None] <= positions[None, :]).astype(jnp.float32)
    return jnp.dot(flags.astype(jnp.float32), upper).astype(jnp.int32)


def compact(flags, ranks, values, slots):
    spots = jnp.arange(slots, dtype=jnp.int32)
    hit = flags[..., None, :] & (ranks[..., None, :] == spots[:, None])
    picked = jnp.sum(jnp.where(hit, values[..., None, :], 0), axis=-1)
    return (picked, jnp.any(hit, axis=-1))


def exchange(items, collective_id):
    groups = lax.axis_size("grp")
    per_group = lax.axis_size("dev")
    count = len(items)
    shapes = []
    for blocks, whole in items:
        if whole:
            shapes.append(jax.ShapeDtypeStruct((groups, per_group) + blocks.shape[1:], blocks.dtype))
        else:
            shapes.append(jax.ShapeDtypeStruct(blocks.shape, blocks.dtype))
    wholes = [index for index, (_, whole) in enumerate(items) if whole]

    def kernel(*refs):
        x_refs = refs[:count]
        o_refs = refs[count : 2 * count]
        mid_refs = dict(zip(wholes, refs[2 * count : 2 * count + len(wholes)]))
        sems = refs[2 * count + len(wholes) :]
        first_send, first_recv, second_send, second_recv, own_sem = sems
        group = lax.axis_index("grp")
        dev = lax.axis_index("dev")
        barrier = pltpu.get_barrier_semaphore()
        across = len(wholes) > 0

        if across:
            def greet_group(offset, carry):
                peer = lax.rem(group + offset, groups)
                pl.semaphore_signal(barrier, inc=1, device_id=(peer, dev), device_id_type=pl.DeviceIdType.MESH)
                return carry

            lax.fori_loop(1, groups, greet_group, 0)

        def greet_dev(offset, carry):
            peer = lax.rem(dev + offset, per_group)
            pl.semaphore_signal(barrier, inc=1, device_id=(group, peer), device_id_type=pl.DeviceIdType.MESH)
            return carry

        lax.fori_loop(1, per_group, greet_dev, 0)
        pl.semaphore_wait(barrier, (groups - 1 if across else 0) + per_group - 1)

        def hop_one(slot, index, peer, place):
            return pltpu.make_async_remote_copy(
                src_ref=x_refs[index].at[pl.ds(peer * per_group, per_group)],
                dst_ref=mid_refs[index].at[place],
                send_sem=first_send.at[slot, peer],
                recv_sem=first_recv.at[slot, place],
                device_id=(peer, dev),
                device_id_type=pl.DeviceIdType.MESH,
            )

        def hop_two(index, peer, place):
            if items[index][1]:
                source = mid_refs[index].at[:, peer]
                target = o_refs[index].at[:, place]
            else:
                source = x_refs[index].at[peer]
                target = o_refs[index].at[place]
            return pltpu.make_async_remote_copy(
                src_ref=source,
                dst_ref=target,
                send_sem=second_send.at[index, peer],
                recv_sem=second_recv.at[index, place],
                device_id=(group, peer),
                device_id_type=pl.DeviceIdType.MESH,
            )

        for slot, index in enumerate(wholes):
            def send_one(offset, carry, slot=slot, index=index):
                hop_one(slot, index, lax.rem(group + offset, groups), group).start()
                return carry

            lax.fori_loop(1, groups, send_one, 0)
        for index, (_, whole) in enumerate(items):
            if not whole:
                def send_group(offset, carry, index=index):
                    hop_two(index, lax.rem(dev + offset, per_group), dev).start()
                    return carry

                lax.fori_loop(1, per_group, send_group, 0)
        for slot, index in enumerate(wholes):
            own = pltpu.make_async_copy(
                x_refs[index].at[pl.ds(group * per_group, per_group)], mid_refs[index].at[group], own_sem
            )
            own.start()
            own.wait()

            def finish_one(offset, carry, slot=slot, index=index):
                hop_one(slot, index, lax.rem(group + offset, groups), group).wait_send()
                source = lax.rem(group + groups - offset, groups)
                hop_one(slot, index, source, source).wait_recv()
                return carry

            lax.fori_loop(1, groups, finish_one, 0)

            def send_two(offset, carry, index=index):
                hop_two(index, lax.rem(dev + offset, per_group), dev).start()
                return carry

            lax.fori_loop(1, per_group, send_two, 0)
        for index, (_, whole) in enumerate(items):
            if whole:
                own = pltpu.make_async_copy(mid_refs[index].at[:, dev], o_refs[index].at[:, dev], own_sem)
            else:
                own = pltpu.make_async_copy(x_refs[index].at[dev], o_refs[index].at[dev], own_sem)
            own.start()
            own.wait()

            def finish_two(offset, carry, index=index):
                hop_two(index, lax.rem(dev + offset, per_group), dev).wait_send()
                source = lax.rem(dev + per_group - offset, per_group)
                hop_two(index, source, source).wait_recv()
                return carry

            lax.fori_loop(1, per_group, finish_two, 0)

    mids = [shapes[index] for index in wholes]
    results = pl.pallas_call(
        kernel,
        out_shape=shapes + mids,
        in_specs=[pl.BlockSpec(memory_space=pl.ANY)] * count,
        out_specs=[pl.BlockSpec(memory_space=pl.ANY)] * (count + len(wholes)),
        scratch_shapes=[
            pltpu.SemaphoreType.DMA((max(len(wholes), 1), groups)),
            pltpu.SemaphoreType.DMA((max(len(wholes), 1), groups)),
            pltpu.SemaphoreType.DMA((count, per_group)),
            pltpu.SemaphoreType.DMA((count, per_group)),
            pltpu.SemaphoreType.DMA(()),
        ],
        compiler_params=pltpu.CompilerParams(collective_id=collective_id, has_side_effects=True),
        cost_estimate=pl.CostEstimate(flops=0, transcendentals=0, bytes_accessed=48 * 1024 * 1024),
    )(*[blocks for blocks, _ in items])
    return [
        result.reshape(blocks.shape) for result, (blocks, _) in zip(results[:count], items)
    ]


def pack_kernel(asked_ref, states_ref, high_ref, low_ref, low_scratch):
    peers = high_ref.shape[0]
    rows, slots, width = states_ref.shape
    lanes = high_ref.shape[2]
    pieces = width // lanes

    def one(peer, carry):
        index = jnp.clip(asked_ref[peer], 0, slots - 1)
        for r in range(rows):
            line = states_ref[r, pl.ds(index, 1), :]
            for k in range(pieces):
                piece = line[:, k * lanes : (k + 1) * lanes]
                if r < 2:
                    high_ref[peer, pl.ds(r * pieces + k, 1), :] = piece
                else:
                    low_scratch[peer, pl.ds((r - 2) * pieces + k, 1), :] = piece
        return carry

    lax.fori_loop(0, peers, one, 0)
    low_ref[...] = low_scratch[...].astype(low_ref.dtype)


def pack_leaving(asked, states_t, lanes):
    peers = asked.shape[0]
    rows, _, width = states_t.shape
    pieces = width // lanes
    return pl.pallas_call(
        pack_kernel,
        in_specs=[pl.BlockSpec(memory_space=pltpu.SMEM), pl.BlockSpec(memory_space=pltpu.VMEM)],
        out_specs=[pl.BlockSpec(memory_space=pltpu.VMEM)] * 2,
        out_shape=[
            jax.ShapeDtypeStruct((peers, 2 * pieces, lanes), states_t.dtype),
            jax.ShapeDtypeStruct((peers, (rows - 2) * pieces, lanes), jnp.bfloat16),
        ],
        scratch_shapes=[pltpu.VMEM((peers, (rows - 2) * pieces, lanes), jnp.float32)],
    )(asked, states_t)


def decode_kernel(
    source_ref, moved_ref,
    routed_ref, states_ref, arrived_ref, arrived_low_ref, up_w_ref, up_b_ref, conv_w_ref, conv_b_ref, in_w_ref, in_b_ref, out_w_ref,
    out_b_ref, decoded_ref, new_ref, carried_ref,
):
    frame_count, slots, _ = routed_ref.shape
    step_count = 2 * frame_count
    rows = states_ref.shape[0]
    conv_taps = conv_w_ref.shape[0]
    res_taps = in_w_ref.shape[0]
    kept = rows - 2 - (res_taps - 1)
    base = pl.program_id(0) * slots

    carried_ref[...] = states_ref[...]

    def bring(slot, carry):
        @pl.when(moved_ref[base + slot] != 0)
        def _():
            source = source_ref[base + slot]
            pieces = carried_ref.shape[2] // arrived_ref.shape[2]
            for r in range(rows):
                if r < 2:
                    row = arrived_ref[source, pl.ds(r * pieces, pieces), :]
                else:
                    row = arrived_low_ref[source, pl.ds((r - 2) * pieces, pieces), :].astype(jnp.float32)
                carried_ref[r, pl.ds(slot, 1), :] = jnp.concatenate(
                    [row[k : k + 1] for k in range(pieces)], axis=1
                )

        return carry

    lax.fori_loop(0, slots, bring, 0)

    def elu(value):
        return jnp.where(value > 0, value, jnp.exp(jnp.minimum(value, 0.0)) - 1.0)

    up_w = up_w_ref[...]
    up_b = up_b_ref[...]
    inputs = [routed_ref[f].astype(jnp.float32) for f in range(frame_count)]
    carried = [carried_ref[r] for r in range(rows)]
    upsampled = []
    for f in range(frame_count):
        early_even = carried[0] if f == 0 else inputs[f - 1] * up_w[2:3]
        early_odd = carried[1] if f == 0 else inputs[f - 1] * up_w[3:4]
        upsampled.append((inputs[f] * up_w[0:1] + early_even) + up_b)
        upsampled.append((inputs[f] * up_w[1:2] + early_odd) + up_b)
    history = jnp.concatenate(
        [c.astype(jnp.bfloat16) for c in carried[2 : 2 + kept]] + [u.astype(jnp.bfloat16) for u in upsampled], axis=0
    )
    conv_out = None
    for tap in range(conv_taps):
        start = (conv_taps - 1 - tap) * slots
        term = jnp.dot(history[start : start + step_count * slots], conv_w_ref[tap], preferred_element_type=jnp.float32)
        conv_out = term if conv_out is None else conv_out + term
    conv_out = conv_out + conv_b_ref[...]
    active = elu(conv_out)
    res_rounded = jnp.concatenate(
        [c.astype(jnp.bfloat16) for c in carried[2 + kept :]] + [active.astype(jnp.bfloat16)], axis=0
    )
    inner = None
    for tap in range(res_taps):
        start = (res_taps - 1 - tap) * slots
        term = jnp.dot(res_rounded[start : start + step_count * slots], in_w_ref[tap], preferred_element_type=jnp.float32)
        inner = term if inner is None else inner + term
    squeezed = elu(inner + in_b_ref[...]).astype(jnp.bfloat16)
    summed = conv_out + jnp.dot(squeezed, out_w_ref[...], preferred_element_type=jnp.float32) + out_b_ref[...]
    decoded = summed.astype(jnp.bfloat16)
    for t in range(step_count):
        decoded_ref[:, t, :] = decoded[t * slots : (t + 1) * slots]
    new_ref[0] = inputs[frame_count - 1] * up_w[2:3]
    new_ref[1] = inputs[frame_count - 1] * up_w[3:4]
    for k in range(kept):
        row = history.shape[0] // slots - kept + k
        new_ref[2 + k] = history[row * slots : (row + 1) * slots].astype(jnp.float32)
    for k in range(res_taps - 1):
        row = step_count - (res_taps - 1) + k
        new_ref[2 + kept + k] = active[row * slots : (row + 1) * slots]


def decode(
    routed, states, arrived, arrived_low, source, moved, up_weight, up_bias, conv_weight, conv_bias, res_in_weight, res_in_bias,
    res_out_weight, res_out_bias,
):
    frame_count, conv_count, chan_width = routed.shape
    rows = states.shape[1]
    chunk = conv_count
    whole = lambda shape: pl.BlockSpec(shape, lambda i, *_: (0,) * len(shape))
    states_t = jnp.transpose(states, (1, 0, 2))
    decoded, new_t = pl.pallas_call(
        decode_kernel,
        grid_spec=pltpu.PrefetchScalarGridSpec(
            num_scalar_prefetch=2,
            grid=(conv_count // chunk,),
            in_specs=[
                pl.BlockSpec((frame_count, chunk, chan_width), lambda i, *_: (0, i, 0)),
                pl.BlockSpec((rows, chunk, chan_width), lambda i, *_: (0, i, 0)),
                whole(arrived.shape),
                whole(arrived_low.shape),
                whole(up_weight.shape),
                whole((1, chan_width)),
                whole(conv_weight.shape),
                whole((1, chan_width)),
                whole(res_in_weight.shape),
                whole((1, res_in_weight.shape[2])),
                whole(res_out_weight.shape),
                whole((1, chan_width)),
            ],
            out_specs=(
                pl.BlockSpec((chunk, 2 * frame_count, chan_width), lambda i, *_: (i, 0, 0)),
                pl.BlockSpec((rows, chunk, chan_width), lambda i, *_: (0, i, 0)),
            ),
            scratch_shapes=[pltpu.VMEM((rows, chunk, chan_width), jnp.float32)],
        ),
        out_shape=(
            jax.ShapeDtypeStruct((conv_count, 2 * frame_count, chan_width), jnp.bfloat16),
            jax.ShapeDtypeStruct((rows, conv_count, chan_width), jnp.float32),
        ),
        compiler_params=pltpu.CompilerParams(vmem_limit_bytes=48 * 1024 * 1024),
    )(
        source, moved, routed, states_t, arrived, arrived_low, up_weight, up_bias.reshape(1, -1), conv_weight,
        conv_bias.reshape(1, -1), res_in_weight, res_in_bias.reshape(1, -1), res_out_weight, res_out_bias.reshape(1, -1),
    )
    return decoded, jnp.transpose(new_t, (1, 0, 2))


def local(
    codes,
    code_table,
    roster,
    old_slot,
    states,
    up_weight,
    up_bias,
    conv_weight,
    conv_bias,
    res_in_weight,
    res_in_bias,
    res_out_weight,
    res_out_bias,
):
    conv_count = roster.shape[0]
    per_group = lax.axis_size("dev")
    devices_all = lax.axis_size("grp") * per_group
    most = MOST
    group_first = lax.axis_index("grp") * per_group
    local_index = lax.axis_index("dev")
    positions = jnp.arange(conv_count, dtype=jnp.int32)
    earlier = positions[None, :] < positions[:, None]

    anchor = roster // conv_count
    row = roster % conv_count
    rank_in = jnp.sum(earlier & (anchor[None, :] == anchor[:, None]), axis=1).astype(jnp.int32)
    key = anchor * most + rank_in
    spots = jnp.arange(devices_all * most, dtype=jnp.int32)
    code_request = jnp.sum(jnp.where(key[None, :] == spots[:, None], row[None, :] + 1, 0), axis=1) - 1
    source_dev = old_slot // conv_count - group_first
    source_row = old_slot % conv_count
    moved = source_dev != local_index
    everyone = jnp.arange(devices_all, dtype=jnp.int32)
    state_request = (
        jnp.sum(
            jnp.where(
                moved[None, :] & (source_dev[None, :] + group_first == everyone[:, None]),
                source_row[None, :] + 1,
                0,
            ),
            axis=1,
        )
        - 1
    )
    request = jnp.concatenate(
        [code_request.reshape(devices_all, most), state_request.reshape(devices_all, 1)], axis=1
    )
    lanes = 128
    padded = jnp.pad(request, ((0, 0), (0, lanes - most - 1))).reshape(devices_all, 1, lanes)
    (asked,) = exchange([(padded, True)], 0)
    asked = asked[:, 0, : most + 1]

    answer = jnp.take(codes, jnp.clip(asked[:, :most].reshape(-1), 0, conv_count - 1), axis=0)
    answer = answer.reshape(devices_all, -1)
    answer = jnp.pad(answer, ((0, 0), (0, lanes - answer.shape[1]))).reshape(devices_all, 1, lanes)
    state_asked = lax.dynamic_slice_in_dim(asked[:, most], group_first, per_group)
    leaving_high, leaving_low = pack_leaving(state_asked, jnp.transpose(states, (1, 0, 2)), lanes)
    answered, arrived, arrived_low = exchange(
        [(answer, True), (leaving_high, False), (leaving_low, False)], 1
    )
    code_width = codes.shape[1]
    routed = embed_codes(answered, anchor, rank_in, code_table, code_width)
    return decode(
        routed,
        states,
        arrived,
        arrived_low,
        jnp.clip(source_dev, 0, per_group - 1),
        moved.astype(jnp.int32),
        up_weight,
        up_bias,
        conv_weight,
        conv_bias,
        res_in_weight,
        res_in_bias,
        res_out_weight,
        res_out_bias,
    )


def solution(mesh):
    in_specs = (
        P(("grp", "dev"), None),
        P(),
        P(("grp", "dev")),
        P(("grp", "dev")),
        P(("grp", "dev"), None, None),
        P(),
        P(),
        P(),
        P(),
        P(),
        P(),
        P(),
        P(),
    )
    out_specs = (P(("grp", "dev"), None, None), P(("grp", "dev"), None, None))
    return jax.shard_map(local, mesh=mesh, in_specs=in_specs, out_specs=out_specs, check_vma=False)
```

```python
import jax
import jax.numpy as jnp
from jax import lax
from jax.experimental import pallas as pl
from jax.experimental.pallas import tpu as pltpu
from jax.sharding import PartitionSpec as P

FRAMES = 4
MOST = 2


def embed_kernel(anchor_ref, answered_ref, rank_ref, table_ref, out_ref, blocks, sems, mine_ref):
    books = blocks.shape[0]
    size = blocks.shape[1]
    slots = rank_ref.shape[0]

    def fetch(book):
        return pltpu.make_async_copy(table_ref.at[pl.ds(book * size, size)], blocks.at[book], sems.at[book])

    for book in range(books):
        fetch(book).start()

    def pick(slot, carry):
        mine_ref[pl.ds(slot, 1), :] = answered_ref[anchor_ref[slot]]
        return carry

    lax.fori_loop(0, slots, pick, 0)
    mine = mine_ref[...]
    width = books * FRAMES
    own = jnp.where(rank_ref[...] == 0, mine[:, :width], mine[:, width : 2 * width])
    by_row = jnp.concatenate([own[:, f * books : (f + 1) * books] for f in range(FRAMES)], axis=0)
    rows = by_row.shape[0]
    total = None
    for book in range(books):
        fetch(book).wait()
        entries = lax.broadcasted_iota(jnp.int32, (rows, size), 1)
        onehot = (by_row[:, book : book + 1] == entries).astype(jnp.bfloat16)
        term = jnp.dot(onehot, blocks[book], preferred_element_type=jnp.float32)
        total = term if total is None else total + term
    out_ref[...] = total.astype(jnp.bfloat16)


def embed_codes(answered, anchor, rank, code_table, code_width):
    row_count = anchor.shape[0]
    book_count = code_width // FRAMES
    book_size = code_table.shape[0] // book_count
    chan_width = code_table.shape[1]
    rows = FRAMES * row_count
    summed = pl.pallas_call(
        embed_kernel,
        in_specs=[
            pl.BlockSpec(memory_space=pltpu.SMEM),
            pl.BlockSpec(memory_space=pltpu.VMEM),
            pl.BlockSpec(memory_space=pltpu.VMEM),
            pl.BlockSpec(memory_space=pl.ANY),
        ],
        out_specs=pl.BlockSpec(memory_space=pltpu.VMEM),
        out_shape=jax.ShapeDtypeStruct((rows, chan_width), jnp.bfloat16),
        scratch_shapes=[
            pltpu.VMEM((book_count, book_size, chan_width), code_table.dtype),
            pltpu.SemaphoreType.DMA((book_count,)),
            pltpu.VMEM((row_count, answered.shape[-1]), answered.dtype),
        ],
    )(anchor, answered, rank.reshape(-1, 1), code_table)
    return summed.reshape(FRAMES, row_count, chan_width)


def pick_rows(table, index, live):
    entries = jnp.arange(table.shape[0], dtype=jnp.int32)
    select = (index[:, None] == entries[None, :]) & live[:, None]
    if table.dtype == jnp.bfloat16:
        return jnp.dot(
            select.astype(jnp.bfloat16), table, preferred_element_type=jnp.float32
        ).astype(jnp.bfloat16)
    if table.dtype == jnp.int32:
        picked = jnp.dot(
            select.astype(jnp.float32), table.astype(jnp.float32), precision=lax.Precision.HIGHEST
        )
        return picked.astype(jnp.int32)
    return jnp.dot(select.astype(jnp.float32), table, precision=lax.Precision.HIGHEST)


def prefix_count(flags):
    width = flags.shape[-1]
    positions = jnp.arange(width, dtype=jnp.int32)
    upper = (positions[:, None] <= positions[None, :]).astype(jnp.float32)
    return jnp.dot(flags.astype(jnp.float32), upper).astype(jnp.int32)


def compact(flags, ranks, values, slots):
    spots = jnp.arange(slots, dtype=jnp.int32)
    hit = flags[..., None, :] & (ranks[..., None, :] == spots[:, None])
    picked = jnp.sum(jnp.where(hit, values[..., None, :], 0), axis=-1)
    return (picked, jnp.any(hit, axis=-1))


def exchange(items, collective_id):
    groups = lax.axis_size("grp")
    per_group = lax.axis_size("dev")
    count = len(items)
    shapes = []
    for blocks, whole in items:
        if whole:
            shapes.append(jax.ShapeDtypeStruct((groups, per_group) + blocks.shape[1:], blocks.dtype))
        else:
            shapes.append(jax.ShapeDtypeStruct(blocks.shape, blocks.dtype))
    wholes = [index for index, (_, whole) in enumerate(items) if whole]

    def kernel(*refs):
        x_refs = refs[:count]
        o_refs = refs[count : 2 * count]
        mid_refs = dict(zip(wholes, refs[2 * count : 2 * count + len(wholes)]))
        sems = refs[2 * count + len(wholes) :]
        first_send, first_recv, second_send, second_recv, own_sem = sems
        group = lax.axis_index("grp")
        dev = lax.axis_index("dev")
        barrier = pltpu.get_barrier_semaphore()
        across = len(wholes) > 0

        if across:
            def greet_group(offset, carry):
                peer = lax.rem(group + offset, groups)
                pl.semaphore_signal(barrier, inc=1, device_id=(peer, dev), device_id_type=pl.DeviceIdType.MESH)
                return carry

            lax.fori_loop(1, groups, greet_group, 0)

        def greet_dev(offset, carry):
            peer = lax.rem(dev + offset, per_group)
            pl.semaphore_signal(barrier, inc=1, device_id=(group, peer), device_id_type=pl.DeviceIdType.MESH)
            return carry

        lax.fori_loop(1, per_group, greet_dev, 0)
        pl.semaphore_wait(barrier, (groups - 1 if across else 0) + per_group - 1)

        def hop_one(slot, index, peer, place):
            return pltpu.make_async_remote_copy(
                src_ref=x_refs[index].at[pl.ds(peer * per_group, per_group)],
                dst_ref=mid_refs[index].at[place],
                send_sem=first_send.at[slot, peer],
                recv_sem=first_recv.at[slot, place],
                device_id=(peer, dev),
                device_id_type=pl.DeviceIdType.MESH,
            )

        def hop_two(index, peer, place):
            if items[index][1]:
                source = mid_refs[index].at[:, peer]
                target = o_refs[index].at[:, place]
            else:
                source = x_refs[index].at[peer]
                target = o_refs[index].at[place]
            return pltpu.make_async_remote_copy(
                src_ref=source,
                dst_ref=target,
                send_sem=second_send.at[index, peer],
                recv_sem=second_recv.at[index, place],
                device_id=(group, peer),
                device_id_type=pl.DeviceIdType.MESH,
            )

        for slot, index in enumerate(wholes):
            def send_one(offset, carry, slot=slot, index=index):
                hop_one(slot, index, lax.rem(group + offset, groups), group).start()
                return carry

            lax.fori_loop(1, groups, send_one, 0)
        for index, (_, whole) in enumerate(items):
            if not whole:
                def send_group(offset, carry, index=index):
                    hop_two(index, lax.rem(dev + offset, per_group), dev).start()
                    return carry

                lax.fori_loop(1, per_group, send_group, 0)
        for slot, index in enumerate(wholes):
            own = pltpu.make_async_copy(
                x_refs[index].at[pl.ds(group * per_group, per_group)], mid_refs[index].at[group], own_sem
            )
            own.start()
            own.wait()

            def finish_one(offset, carry, slot=slot, index=index):
                hop_one(slot, index, lax.rem(group + offset, groups), group).wait_send()
                source = lax.rem(group + groups - offset, groups)
                hop_one(slot, index, source, source).wait_recv()
                return carry

            lax.fori_loop(1, groups, finish_one, 0)

            def send_two(offset, carry, index=index):
                hop_two(index, lax.rem(dev + offset, per_group), dev).start()
                return carry

            lax.fori_loop(1, per_group, send_two, 0)
        for index, (_, whole) in enumerate(items):
            if whole:
                own = pltpu.make_async_copy(mid_refs[index].at[:, dev], o_refs[index].at[:, dev], own_sem)
            else:
                own = pltpu.make_async_copy(x_refs[index].at[dev], o_refs[index].at[dev], own_sem)
            own.start()
            own.wait()

            def finish_two(offset, carry, index=index):
                hop_two(index, lax.rem(dev + offset, per_group), dev).wait_send()
                source = lax.rem(dev + per_group - offset, per_group)
                hop_two(index, source, source).wait_recv()
                return carry

            lax.fori_loop(1, per_group, finish_two, 0)

    mids = [shapes[index] for index in wholes]
    results = pl.pallas_call(
        kernel,
        out_shape=shapes + mids,
        in_specs=[pl.BlockSpec(memory_space=pl.ANY)] * count,
        out_specs=[pl.BlockSpec(memory_space=pl.ANY)] * (count + len(wholes)),
        scratch_shapes=[
            pltpu.SemaphoreType.DMA((max(len(wholes), 1), groups)),
            pltpu.SemaphoreType.DMA((max(len(wholes), 1), groups)),
            pltpu.SemaphoreType.DMA((count, per_group)),
            pltpu.SemaphoreType.DMA((count, per_group)),
            pltpu.SemaphoreType.DMA(()),
        ],
        compiler_params=pltpu.CompilerParams(collective_id=collective_id, has_side_effects=True),
        cost_estimate=pl.CostEstimate(flops=0, transcendentals=0, bytes_accessed=48 * 1024 * 1024),
    )(*[blocks for blocks, _ in items])
    return [
        result.reshape(blocks.shape) for result, (blocks, _) in zip(results[:count], items)
    ]


def pack_kernel(asked_ref, states_ref, high_ref, low_ref, low_scratch):
    peers = high_ref.shape[0]
    rows, slots, width = states_ref.shape
    lanes = high_ref.shape[2]
    pieces = width // lanes

    def one(peer, carry):
        index = jnp.clip(asked_ref[peer], 0, slots - 1)
        for r in range(rows):
            line = states_ref[r, pl.ds(index, 1), :]
            for k in range(pieces):
                piece = line[:, k * lanes : (k + 1) * lanes]
                if r < 2:
                    high_ref[peer, pl.ds(r * pieces + k, 1), :] = piece
                else:
                    low_scratch[peer, pl.ds((r - 2) * pieces + k, 1), :] = piece
        return carry

    lax.fori_loop(0, peers, one, 0)
    low_ref[...] = low_scratch[...].astype(low_ref.dtype)


def pack_leaving(asked, states_t, lanes):
    peers = asked.shape[0]
    rows, _, width = states_t.shape
    pieces = width // lanes
    return pl.pallas_call(
        pack_kernel,
        in_specs=[pl.BlockSpec(memory_space=pltpu.SMEM), pl.BlockSpec(memory_space=pltpu.VMEM)],
        out_specs=[pl.BlockSpec(memory_space=pltpu.VMEM)] * 2,
        out_shape=[
            jax.ShapeDtypeStruct((peers, 2 * pieces, lanes), states_t.dtype),
            jax.ShapeDtypeStruct((peers, (rows - 2) * pieces, lanes), jnp.bfloat16),
        ],
        scratch_shapes=[pltpu.VMEM((peers, (rows - 2) * pieces, lanes), jnp.float32)],
    )(asked, states_t)


def decode_kernel(
    source_ref, moved_ref,
    routed_ref, states_ref, arrived_ref, arrived_low_ref, up_w_ref, up_b_ref, conv_w_ref, conv_b_ref, in_w_ref, in_b_ref, out_w_ref,
    out_b_ref, decoded_ref, new_ref, carried_ref,
):
    frame_count, slots, _ = routed_ref.shape
    step_count = 2 * frame_count
    rows = states_ref.shape[0]
    conv_taps = conv_w_ref.shape[0]
    res_taps = in_w_ref.shape[0]
    kept = rows - 2 - (res_taps - 1)
    base = pl.program_id(0) * slots

    carried_ref[...] = states_ref[...]

    def bring(slot, carry):
        @pl.when(moved_ref[base + slot] != 0)
        def _():
            source = source_ref[base + slot]
            pieces = carried_ref.shape[2] // arrived_ref.shape[2]
            for r in range(rows):
                if r < 2:
                    row = arrived_ref[source, pl.ds(r * pieces, pieces), :]
                else:
                    row = arrived_low_ref[source, pl.ds((r - 2) * pieces, pieces), :].astype(jnp.float32)
                carried_ref[r, pl.ds(slot, 1), :] = jnp.concatenate(
                    [row[k : k + 1] for k in range(pieces)], axis=1
                )

        return carry

    lax.fori_loop(0, slots, bring, 0, unroll=8)

    def elu(value):
        return jnp.where(value > 0, value, jnp.exp(jnp.minimum(value, 0.0)) - 1.0)

    up_w = up_w_ref[...]
    up_b = up_b_ref[...]
    inputs = [routed_ref[f].astype(jnp.float32) for f in range(frame_count)]
    carried = [carried_ref[r] for r in range(rows)]
    upsampled = []
    for f in range(frame_count):
        early_even = carried[0] if f == 0 else inputs[f - 1] * up_w[2:3]
        early_odd = carried[1] if f == 0 else inputs[f - 1] * up_w[3:4]
        upsampled.append((inputs[f] * up_w[0:1] + early_even) + up_b)
        upsampled.append((inputs[f] * up_w[1:2] + early_odd) + up_b)
    history = jnp.concatenate(
        [c.astype(jnp.bfloat16) for c in carried[2 : 2 + kept]] + [u.astype(jnp.bfloat16) for u in upsampled], axis=0
    )
    conv_out = None
    for tap in range(conv_taps):
        start = (conv_taps - 1 - tap) * slots
        term = jnp.dot(history[start : start + step_count * slots], conv_w_ref[tap], preferred_element_type=jnp.float32)
        conv_out = term if conv_out is None else conv_out + term
    conv_out = conv_out + conv_b_ref[...]
    active = elu(conv_out)
    res_rounded = jnp.concatenate(
        [c.astype(jnp.bfloat16) for c in carried[2 + kept :]] + [active.astype(jnp.bfloat16)], axis=0
    )
    inner = None
    for tap in range(res_taps):
        start = (res_taps - 1 - tap) * slots
        term = jnp.dot(res_rounded[start : start + step_count * slots], in_w_ref[tap], preferred_element_type=jnp.float32)
        inner = term if inner is None else inner + term
    squeezed = elu(inner + in_b_ref[...]).astype(jnp.bfloat16)
    summed = conv_out + jnp.dot(squeezed, out_w_ref[...], preferred_element_type=jnp.float32) + out_b_ref[...]
    decoded = summed.astype(jnp.bfloat16)
    for t in range(step_count):
        decoded_ref[:, t, :] = decoded[t * slots : (t + 1) * slots]
    new_ref[0] = inputs[frame_count - 1] * up_w[2:3]
    new_ref[1] = inputs[frame_count - 1] * up_w[3:4]
    for k in range(kept):
        row = history.shape[0] // slots - kept + k
        new_ref[2 + k] = history[row * slots : (row + 1) * slots].astype(jnp.float32)
    for k in range(res_taps - 1):
        row = step_count - (res_taps - 1) + k
        new_ref[2 + kept + k] = active[row * slots : (row + 1) * slots]


def decode(
    routed, states, arrived, arrived_low, source, moved, up_weight, up_bias, conv_weight, conv_bias, res_in_weight, res_in_bias,
    res_out_weight, res_out_bias,
):
    frame_count, conv_count, chan_width = routed.shape
    rows = states.shape[1]
    chunk = conv_count
    whole = lambda shape: pl.BlockSpec(shape, lambda i, *_: (0,) * len(shape))
    states_t = jnp.transpose(states, (1, 0, 2))
    decoded, new_t = pl.pallas_call(
        decode_kernel,
        grid_spec=pltpu.PrefetchScalarGridSpec(
            num_scalar_prefetch=2,
            grid=(conv_count // chunk,),
            in_specs=[
                pl.BlockSpec((frame_count, chunk, chan_width), lambda i, *_: (0, i, 0)),
                pl.BlockSpec((rows, chunk, chan_width), lambda i, *_: (0, i, 0)),
                whole(arrived.shape),
                whole(arrived_low.shape),
                whole(up_weight.shape),
                whole((1, chan_width)),
                whole(conv_weight.shape),
                whole((1, chan_width)),
                whole(res_in_weight.shape),
                whole((1, res_in_weight.shape[2])),
                whole(res_out_weight.shape),
                whole((1, chan_width)),
            ],
            out_specs=(
                pl.BlockSpec((chunk, 2 * frame_count, chan_width), lambda i, *_: (i, 0, 0)),
                pl.BlockSpec((rows, chunk, chan_width), lambda i, *_: (0, i, 0)),
            ),
            scratch_shapes=[pltpu.VMEM((rows, chunk, chan_width), jnp.float32)],
        ),
        out_shape=(
            jax.ShapeDtypeStruct((conv_count, 2 * frame_count, chan_width), jnp.bfloat16),
            jax.ShapeDtypeStruct((rows, conv_count, chan_width), jnp.float32),
        ),
        compiler_params=pltpu.CompilerParams(vmem_limit_bytes=48 * 1024 * 1024),
    )(
        source, moved, routed, states_t, arrived, arrived_low, up_weight, up_bias.reshape(1, -1), conv_weight,
        conv_bias.reshape(1, -1), res_in_weight, res_in_bias.reshape(1, -1), res_out_weight, res_out_bias.reshape(1, -1),
    )
    return decoded, jnp.transpose(new_t, (1, 0, 2))


def local(
    codes,
    code_table,
    roster,
    old_slot,
    states,
    up_weight,
    up_bias,
    conv_weight,
    conv_bias,
    res_in_weight,
    res_in_bias,
    res_out_weight,
    res_out_bias,
):
    conv_count = roster.shape[0]
    per_group = lax.axis_size("dev")
    devices_all = lax.axis_size("grp") * per_group
    most = MOST
    group_first = lax.axis_index("grp") * per_group
    local_index = lax.axis_index("dev")
    positions = jnp.arange(conv_count, dtype=jnp.int32)
    earlier = positions[None, :] < positions[:, None]

    anchor = roster // conv_count
    row = roster % conv_count
    rank_in = jnp.sum(earlier & (anchor[None, :] == anchor[:, None]), axis=1).astype(jnp.int32)
    key = anchor * most + rank_in
    spots = jnp.arange(devices_all * most, dtype=jnp.int32)
    code_request = jnp.sum(jnp.where(key[None, :] == spots[:, None], row[None, :] + 1, 0), axis=1) - 1
    source_dev = old_slot // conv_count - group_first
    source_row = old_slot % conv_count
    moved = source_dev != local_index
    everyone = jnp.arange(devices_all, dtype=jnp.int32)
    state_request = (
        jnp.sum(
            jnp.where(
                moved[None, :] & (source_dev[None, :] + group_first == everyone[:, None]),
                source_row[None, :] + 1,
                0,
            ),
            axis=1,
        )
        - 1
    )
    request = jnp.concatenate(
        [code_request.reshape(devices_all, most), state_request.reshape(devices_all, 1)], axis=1
    )
    lanes = 128
    padded = jnp.pad(request, ((0, 0), (0, lanes - most - 1))).reshape(devices_all, 1, lanes)
    (asked,) = exchange([(padded, True)], 0)
    asked = asked[:, 0, : most + 1]

    answer = jnp.take(codes, jnp.clip(asked[:, :most].reshape(-1), 0, conv_count - 1), axis=0)
    answer = answer.reshape(devices_all, -1)
    answer = jnp.pad(answer, ((0, 0), (0, lanes - answer.shape[1]))).reshape(devices_all, 1, lanes)
    state_asked = lax.dynamic_slice_in_dim(asked[:, most], group_first, per_group)
    leaving_high, leaving_low = pack_leaving(state_asked, jnp.transpose(states, (1, 0, 2)), lanes)
    answered, arrived, arrived_low = exchange(
        [(answer, True), (leaving_high, False), (leaving_low, False)], 1
    )
    code_width = codes.shape[1]
    routed = embed_codes(answered, anchor, rank_in, code_table, code_width)
    return decode(
        routed,
        states,
        arrived,
        arrived_low,
        jnp.clip(source_dev, 0, per_group - 1),
        moved.astype(jnp.int32),
        up_weight,
        up_bias,
        conv_weight,
        conv_bias,
        res_in_weight,
        res_in_bias,
        res_out_weight,
        res_out_bias,
    )


def solution(mesh):
    in_specs = (
        P(("grp", "dev"), None),
        P(),
        P(("grp", "dev")),
        P(("grp", "dev")),
        P(("grp", "dev"), None, None),
        P(),
        P(),
        P(),
        P(),
        P(),
        P(),
        P(),
        P(),
    )
    out_specs = (P(("grp", "dev"), None, None), P(("grp", "dev"), None, None))
    return jax.shard_map(local, mesh=mesh, in_specs=in_specs, out_specs=out_specs, check_vma=False)
```

```python
import jax
import jax.numpy as jnp
from jax import lax
from jax.experimental import pallas as pl
from jax.experimental.pallas import tpu as pltpu
from jax.sharding import PartitionSpec as P

FRAMES = 4
MOST = 2


def embed_kernel(anchor_ref, answered_ref, rank_ref, table_ref, out_ref, blocks, sems, mine_ref):
    books = blocks.shape[0]
    size = blocks.shape[1]
    slots = rank_ref.shape[0]

    def fetch(book):
        return pltpu.make_async_copy(table_ref.at[pl.ds(book * size, size)], blocks.at[book], sems.at[book])

    for book in range(books):
        fetch(book).start()

    def pick(slot, carry):
        mine_ref[pl.ds(slot, 1), :] = answered_ref[anchor_ref[slot]]
        return carry

    lax.fori_loop(0, slots, pick, 0)
    mine = mine_ref[...]
    width = books * FRAMES
    own = jnp.where(rank_ref[...] == 0, mine[:, :width], mine[:, width : 2 * width])
    by_row = jnp.concatenate([own[:, f * books : (f + 1) * books] for f in range(FRAMES)], axis=0)
    rows = by_row.shape[0]
    total = None
    for book in range(books):
        fetch(book).wait()
        entries = lax.broadcasted_iota(jnp.int32, (rows, size), 1)
        onehot = (by_row[:, book : book + 1] == entries).astype(jnp.bfloat16)
        term = jnp.dot(onehot, blocks[book], preferred_element_type=jnp.float32)
        total = term if total is None else total + term
    out_ref[...] = total.astype(jnp.bfloat16)


def embed_codes(answered, anchor, rank, code_table, code_width):
    row_count = anchor.shape[0]
    book_count = code_width // FRAMES
    book_size = code_table.shape[0] // book_count
    chan_width = code_table.shape[1]
    rows = FRAMES * row_count
    summed = pl.pallas_call(
        embed_kernel,
        in_specs=[
            pl.BlockSpec(memory_space=pltpu.SMEM),
            pl.BlockSpec(memory_space=pltpu.VMEM),
            pl.BlockSpec(memory_space=pltpu.VMEM),
            pl.BlockSpec(memory_space=pl.ANY),
        ],
        out_specs=pl.BlockSpec(memory_space=pltpu.VMEM),
        out_shape=jax.ShapeDtypeStruct((rows, chan_width), jnp.bfloat16),
        scratch_shapes=[
            pltpu.VMEM((book_count, book_size, chan_width), code_table.dtype),
            pltpu.SemaphoreType.DMA((book_count,)),
            pltpu.VMEM((row_count, answered.shape[-1]), answered.dtype),
        ],
    )(anchor, answered, rank.reshape(-1, 1), code_table)
    return summed.reshape(FRAMES, row_count, chan_width)


def pick_rows(table, index, live):
    entries = jnp.arange(table.shape[0], dtype=jnp.int32)
    select = (index[:, None] == entries[None, :]) & live[:, None]
    if table.dtype == jnp.bfloat16:
        return jnp.dot(
            select.astype(jnp.bfloat16), table, preferred_element_type=jnp.float32
        ).astype(jnp.bfloat16)
    if table.dtype == jnp.int32:
        picked = jnp.dot(
            select.astype(jnp.float32), table.astype(jnp.float32), precision=lax.Precision.HIGHEST
        )
        return picked.astype(jnp.int32)
    return jnp.dot(select.astype(jnp.float32), table, precision=lax.Precision.HIGHEST)


def prefix_count(flags):
    width = flags.shape[-1]
    positions = jnp.arange(width, dtype=jnp.int32)
    upper = (positions[:, None] <= positions[None, :]).astype(jnp.float32)
    return jnp.dot(flags.astype(jnp.float32), upper).astype(jnp.int32)


def compact(flags, ranks, values, slots):
    spots = jnp.arange(slots, dtype=jnp.int32)
    hit = flags[..., None, :] & (ranks[..., None, :] == spots[:, None])
    picked = jnp.sum(jnp.where(hit, values[..., None, :], 0), axis=-1)
    return (picked, jnp.any(hit, axis=-1))


def exchange(items, collective_id):
    groups = lax.axis_size("grp")
    per_group = lax.axis_size("dev")
    count = len(items)
    shapes = []
    for blocks, whole in items:
        if whole:
            shapes.append(jax.ShapeDtypeStruct((groups, per_group) + blocks.shape[1:], blocks.dtype))
        else:
            shapes.append(jax.ShapeDtypeStruct(blocks.shape, blocks.dtype))
    wholes = [index for index, (_, whole) in enumerate(items) if whole]

    def kernel(*refs):
        x_refs = refs[:count]
        o_refs = refs[count : 2 * count]
        mid_refs = dict(zip(wholes, refs[2 * count : 2 * count + len(wholes)]))
        sems = refs[2 * count + len(wholes) :]
        first_send, first_recv, second_send, second_recv, own_sem = sems
        group = lax.axis_index("grp")
        dev = lax.axis_index("dev")
        barrier = pltpu.get_barrier_semaphore()
        across = len(wholes) > 0

        if across:
            def greet_group(offset, carry):
                peer = lax.rem(group + offset, groups)
                pl.semaphore_signal(barrier, inc=1, device_id=(peer, dev), device_id_type=pl.DeviceIdType.MESH)
                return carry

            lax.fori_loop(1, groups, greet_group, 0)

        def greet_dev(offset, carry):
            peer = lax.rem(dev + offset, per_group)
            pl.semaphore_signal(barrier, inc=1, device_id=(group, peer), device_id_type=pl.DeviceIdType.MESH)
            return carry

        lax.fori_loop(1, per_group, greet_dev, 0)
        pl.semaphore_wait(barrier, (groups - 1 if across else 0) + per_group - 1)

        def hop_one(slot, index, peer, place):
            return pltpu.make_async_remote_copy(
                src_ref=x_refs[index].at[pl.ds(peer * per_group, per_group)],
                dst_ref=mid_refs[index].at[place],
                send_sem=first_send.at[slot, peer],
                recv_sem=first_recv.at[slot, place],
                device_id=(peer, dev),
                device_id_type=pl.DeviceIdType.MESH,
            )

        def hop_two(index, peer, place):
            if items[index][1]:
                source = mid_refs[index].at[:, peer]
                target = o_refs[index].at[:, place]
            else:
                source = x_refs[index].at[peer]
                target = o_refs[index].at[place]
            return pltpu.make_async_remote_copy(
                src_ref=source,
                dst_ref=target,
                send_sem=second_send.at[index, peer],
                recv_sem=second_recv.at[index, place],
                device_id=(group, peer),
                device_id_type=pl.DeviceIdType.MESH,
            )

        for slot, index in enumerate(wholes):
            def send_one(offset, carry, slot=slot, index=index):
                hop_one(slot, index, lax.rem(group + offset, groups), group).start()
                return carry

            lax.fori_loop(1, groups, send_one, 0)
        for index, (_, whole) in enumerate(items):
            if not whole:
                def send_group(offset, carry, index=index):
                    hop_two(index, lax.rem(dev + offset, per_group), dev).start()
                    return carry

                lax.fori_loop(1, per_group, send_group, 0)
        for slot, index in enumerate(wholes):
            own = pltpu.make_async_copy(
                x_refs[index].at[pl.ds(group * per_group, per_group)], mid_refs[index].at[group], own_sem
            )
            own.start()
            own.wait()

            def finish_one(offset, carry, slot=slot, index=index):
                hop_one(slot, index, lax.rem(group + offset, groups), group).wait_send()
                source = lax.rem(group + groups - offset, groups)
                hop_one(slot, index, source, source).wait_recv()
                return carry

            lax.fori_loop(1, groups, finish_one, 0)

            def send_two(offset, carry, index=index):
                hop_two(index, lax.rem(dev + offset, per_group), dev).start()
                return carry

            lax.fori_loop(1, per_group, send_two, 0)
        for index, (_, whole) in enumerate(items):
            if whole:
                own = pltpu.make_async_copy(mid_refs[index].at[:, dev], o_refs[index].at[:, dev], own_sem)
            else:
                own = pltpu.make_async_copy(x_refs[index].at[dev], o_refs[index].at[dev], own_sem)
            own.start()
            own.wait()

            def finish_two(offset, carry, index=index):
                hop_two(index, lax.rem(dev + offset, per_group), dev).wait_send()
                source = lax.rem(dev + per_group - offset, per_group)
                hop_two(index, source, source).wait_recv()
                return carry

            lax.fori_loop(1, per_group, finish_two, 0)

    mids = [shapes[index] for index in wholes]
    results = pl.pallas_call(
        kernel,
        out_shape=shapes + mids,
        in_specs=[pl.BlockSpec(memory_space=pl.ANY)] * count,
        out_specs=[pl.BlockSpec(memory_space=pl.ANY)] * (count + len(wholes)),
        scratch_shapes=[
            pltpu.SemaphoreType.DMA((max(len(wholes), 1), groups)),
            pltpu.SemaphoreType.DMA((max(len(wholes), 1), groups)),
            pltpu.SemaphoreType.DMA((count, per_group)),
            pltpu.SemaphoreType.DMA((count, per_group)),
            pltpu.SemaphoreType.DMA(()),
        ],
        compiler_params=pltpu.CompilerParams(collective_id=collective_id, has_side_effects=True),
        cost_estimate=pl.CostEstimate(flops=0, transcendentals=0, bytes_accessed=48 * 1024 * 1024),
    )(*[blocks for blocks, _ in items])
    return [
        result.reshape(blocks.shape) for result, (blocks, _) in zip(results[:count], items)
    ]


def pack_kernel(asked_ref, states_ref, high_ref, low_ref, low_scratch):
    peers = high_ref.shape[0]
    rows, slots, width = states_ref.shape
    lanes = high_ref.shape[2]
    pieces = width // lanes

    def one(peer, carry):
        index = jnp.clip(asked_ref[peer], 0, slots - 1)
        for r in range(rows):
            line = states_ref[r, pl.ds(index, 1), :]
            for k in range(pieces):
                piece = line[:, k * lanes : (k + 1) * lanes]
                if r < 2:
                    high_ref[peer, pl.ds(r * pieces + k, 1), :] = piece
                else:
                    low_scratch[peer, pl.ds((r - 2) * pieces + k, 1), :] = piece
        return carry

    lax.fori_loop(0, peers, one, 0)
    low_ref[...] = low_scratch[...].astype(low_ref.dtype)


def pack_leaving(asked, states_t, lanes):
    peers = asked.shape[0]
    rows, _, width = states_t.shape
    pieces = width // lanes
    return pl.pallas_call(
        pack_kernel,
        in_specs=[pl.BlockSpec(memory_space=pltpu.SMEM), pl.BlockSpec(memory_space=pltpu.VMEM)],
        out_specs=[pl.BlockSpec(memory_space=pltpu.VMEM)] * 2,
        out_shape=[
            jax.ShapeDtypeStruct((peers, 2 * pieces, lanes), states_t.dtype),
            jax.ShapeDtypeStruct((peers, (rows - 2) * pieces, lanes), jnp.bfloat16),
        ],
        scratch_shapes=[pltpu.VMEM((peers, (rows - 2) * pieces, lanes), jnp.float32)],
    )(asked, states_t)


def decode_kernel(
    source_ref, moved_ref,
    routed_ref, states_ref, arrived_ref, arrived_low_ref, up_w_ref, up_b_ref, conv_w_ref, conv_b_ref, in_w_ref, in_b_ref, out_w_ref,
    out_b_ref, decoded_ref, new_ref, carried_ref,
):
    frame_count, slots, _ = routed_ref.shape
    step_count = 2 * frame_count
    rows = states_ref.shape[0]
    conv_taps = conv_w_ref.shape[0]
    res_taps = in_w_ref.shape[0]
    kept = rows - 2 - (res_taps - 1)
    base = pl.program_id(0) * slots

    carried_ref[...] = states_ref[...]

    def bring(slot, carry):
        @pl.when(moved_ref[base + slot] != 0)
        def _():
            source = source_ref[base + slot]
            pieces = carried_ref.shape[2] // arrived_ref.shape[2]
            for r in range(rows):
                if r < 2:
                    row = arrived_ref[source, pl.ds(r * pieces, pieces), :]
                else:
                    row = arrived_low_ref[source, pl.ds((r - 2) * pieces, pieces), :].astype(jnp.float32)
                carried_ref[r, pl.ds(slot, 1), :] = jnp.concatenate(
                    [row[k : k + 1] for k in range(pieces)], axis=1
                )

        return carry

    lax.fori_loop(0, slots, bring, 0, unroll=32)

    def elu(value):
        return jnp.where(value > 0, value, jnp.exp(jnp.minimum(value, 0.0)) - 1.0)

    up_w = up_w_ref[...]
    up_b = up_b_ref[...]
    inputs = [routed_ref[f].astype(jnp.float32) for f in range(frame_count)]
    carried = [carried_ref[r] for r in range(rows)]
    upsampled = []
    for f in range(frame_count):
        early_even = carried[0] if f == 0 else inputs[f - 1] * up_w[2:3]
        early_odd = carried[1] if f == 0 else inputs[f - 1] * up_w[3:4]
        upsampled.append((inputs[f] * up_w[0:1] + early_even) + up_b)
        upsampled.append((inputs[f] * up_w[1:2] + early_odd) + up_b)
    history = jnp.concatenate(
        [c.astype(jnp.bfloat16) for c in carried[2 : 2 + kept]] + [u.astype(jnp.bfloat16) for u in upsampled], axis=0
    )
    conv_out = None
    for tap in range(conv_taps):
        start = (conv_taps - 1 - tap) * slots
        term = jnp.dot(history[start : start + step_count * slots], conv_w_ref[tap], preferred_element_type=jnp.float32)
        conv_out = term if conv_out is None else conv_out + term
    conv_out = conv_out + conv_b_ref[...]
    active = elu(conv_out)
    res_rounded = jnp.concatenate(
        [c.astype(jnp.bfloat16) for c in carried[2 + kept :]] + [active.astype(jnp.bfloat16)], axis=0
    )
    inner = None
    for tap in range(res_taps):
        start = (res_taps - 1 - tap) * slots
        term = jnp.dot(res_rounded[start : start + step_count * slots], in_w_ref[tap], preferred_element_type=jnp.float32)
        inner = term if inner is None else inner + term
    squeezed = elu(inner + in_b_ref[...]).astype(jnp.bfloat16)
    summed = conv_out + jnp.dot(squeezed, out_w_ref[...], preferred_element_type=jnp.float32) + out_b_ref[...]
    decoded = summed.astype(jnp.bfloat16)
    for t in range(step_count):
        decoded_ref[:, t, :] = decoded[t * slots : (t + 1) * slots]
    new_ref[0] = inputs[frame_count - 1] * up_w[2:3]
    new_ref[1] = inputs[frame_count - 1] * up_w[3:4]
    for k in range(kept):
        row = history.shape[0] // slots - kept + k
        new_ref[2 + k] = history[row * slots : (row + 1) * slots].astype(jnp.float32)
    for k in range(res_taps - 1):
        row = step_count - (res_taps - 1) + k
        new_ref[2 + kept + k] = active[row * slots : (row + 1) * slots]


def decode(
    routed, states, arrived, arrived_low, source, moved, up_weight, up_bias, conv_weight, conv_bias, res_in_weight, res_in_bias,
    res_out_weight, res_out_bias,
):
    frame_count, conv_count, chan_width = routed.shape
    rows = states.shape[1]
    chunk = conv_count
    whole = lambda shape: pl.BlockSpec(shape, lambda i, *_: (0,) * len(shape))
    states_t = jnp.transpose(states, (1, 0, 2))
    decoded, new_t = pl.pallas_call(
        decode_kernel,
        grid_spec=pltpu.PrefetchScalarGridSpec(
            num_scalar_prefetch=2,
            grid=(conv_count // chunk,),
            in_specs=[
                pl.BlockSpec((frame_count, chunk, chan_width), lambda i, *_: (0, i, 0)),
                pl.BlockSpec((rows, chunk, chan_width), lambda i, *_: (0, i, 0)),
                whole(arrived.shape),
                whole(arrived_low.shape),
                whole(up_weight.shape),
                whole((1, chan_width)),
                whole(conv_weight.shape),
                whole((1, chan_width)),
                whole(res_in_weight.shape),
                whole((1, res_in_weight.shape[2])),
                whole(res_out_weight.shape),
                whole((1, chan_width)),
            ],
            out_specs=(
                pl.BlockSpec((chunk, 2 * frame_count, chan_width), lambda i, *_: (i, 0, 0)),
                pl.BlockSpec((rows, chunk, chan_width), lambda i, *_: (0, i, 0)),
            ),
            scratch_shapes=[pltpu.VMEM((rows, chunk, chan_width), jnp.float32)],
        ),
        out_shape=(
            jax.ShapeDtypeStruct((conv_count, 2 * frame_count, chan_width), jnp.bfloat16),
            jax.ShapeDtypeStruct((rows, conv_count, chan_width), jnp.float32),
        ),
        compiler_params=pltpu.CompilerParams(vmem_limit_bytes=48 * 1024 * 1024),
    )(
        source, moved, routed, states_t, arrived, arrived_low, up_weight, up_bias.reshape(1, -1), conv_weight,
        conv_bias.reshape(1, -1), res_in_weight, res_in_bias.reshape(1, -1), res_out_weight, res_out_bias.reshape(1, -1),
    )
    return decoded, jnp.transpose(new_t, (1, 0, 2))


def local(
    codes,
    code_table,
    roster,
    old_slot,
    states,
    up_weight,
    up_bias,
    conv_weight,
    conv_bias,
    res_in_weight,
    res_in_bias,
    res_out_weight,
    res_out_bias,
):
    conv_count = roster.shape[0]
    per_group = lax.axis_size("dev")
    devices_all = lax.axis_size("grp") * per_group
    most = MOST
    group_first = lax.axis_index("grp") * per_group
    local_index = lax.axis_index("dev")
    positions = jnp.arange(conv_count, dtype=jnp.int32)
    earlier = positions[None, :] < positions[:, None]

    anchor = roster // conv_count
    row = roster % conv_count
    rank_in = jnp.sum(earlier & (anchor[None, :] == anchor[:, None]), axis=1).astype(jnp.int32)
    key = anchor * most + rank_in
    spots = jnp.arange(devices_all * most, dtype=jnp.int32)
    code_request = jnp.sum(jnp.where(key[None, :] == spots[:, None], row[None, :] + 1, 0), axis=1) - 1
    source_dev = old_slot // conv_count - group_first
    source_row = old_slot % conv_count
    moved = source_dev != local_index
    everyone = jnp.arange(devices_all, dtype=jnp.int32)
    state_request = (
        jnp.sum(
            jnp.where(
                moved[None, :] & (source_dev[None, :] + group_first == everyone[:, None]),
                source_row[None, :] + 1,
                0,
            ),
            axis=1,
        )
        - 1
    )
    request = jnp.concatenate(
        [code_request.reshape(devices_all, most), state_request.reshape(devices_all, 1)], axis=1
    )
    lanes = 128
    padded = jnp.pad(request, ((0, 0), (0, lanes - most - 1))).reshape(devices_all, 1, lanes)
    (asked,) = exchange([(padded, True)], 0)
    asked = asked[:, 0, : most + 1]

    answer = jnp.take(codes, jnp.clip(asked[:, :most].reshape(-1), 0, conv_count - 1), axis=0)
    answer = answer.reshape(devices_all, -1)
    answer = jnp.pad(answer, ((0, 0), (0, lanes - answer.shape[1]))).reshape(devices_all, 1, lanes)
    state_asked = lax.dynamic_slice_in_dim(asked[:, most], group_first, per_group)
    leaving_high, leaving_low = pack_leaving(state_asked, jnp.transpose(states, (1, 0, 2)), lanes)
    answered, arrived, arrived_low = exchange(
        [(answer, True), (leaving_high, False), (leaving_low, False)], 1
    )
    code_width = codes.shape[1]
    routed = embed_codes(answered, anchor, rank_in, code_table, code_width)
    return decode(
        routed,
        states,
        arrived,
        arrived_low,
        jnp.clip(source_dev, 0, per_group - 1),
        moved.astype(jnp.int32),
        up_weight,
        up_bias,
        conv_weight,
        conv_bias,
        res_in_weight,
        res_in_bias,
        res_out_weight,
        res_out_bias,
    )


def solution(mesh):
    in_specs = (
        P(("grp", "dev"), None),
        P(),
        P(("grp", "dev")),
        P(("grp", "dev")),
        P(("grp", "dev"), None, None),
        P(),
        P(),
        P(),
        P(),
        P(),
        P(),
        P(),
        P(),
    )
    out_specs = (P(("grp", "dev"), None, None), P(("grp", "dev"), None, None))
    return jax.shard_map(local, mesh=mesh, in_specs=in_specs, out_specs=out_specs, check_vma=False)
```

```python
import jax
import jax.numpy as jnp
from jax import lax
from jax.experimental import pallas as pl
from jax.experimental.pallas import tpu as pltpu
from jax.sharding import PartitionSpec as P

FRAMES = 4
MOST = 2


def embed_kernel(anchor_ref, answered_ref, rank_ref, table_ref, out_ref, blocks, sems, mine_ref):
    books = blocks.shape[0]
    size = blocks.shape[1]
    slots = rank_ref.shape[0]

    def fetch(book):
        return pltpu.make_async_copy(table_ref.at[pl.ds(book * size, size)], blocks.at[book], sems.at[book])

    for book in range(books):
        fetch(book).start()

    def pick(slot, carry):
        mine_ref[pl.ds(slot, 1), :] = answered_ref[anchor_ref[slot]]
        return carry

    lax.fori_loop(0, slots, pick, 0, unroll=8)
    mine = mine_ref[...]
    width = books * FRAMES
    own = jnp.where(rank_ref[...] == 0, mine[:, :width], mine[:, width : 2 * width])
    by_row = jnp.concatenate([own[:, f * books : (f + 1) * books] for f in range(FRAMES)], axis=0)
    rows = by_row.shape[0]
    total = None
    for book in range(books):
        fetch(book).wait()
        entries = lax.broadcasted_iota(jnp.int32, (rows, size), 1)
        onehot = (by_row[:, book : book + 1] == entries).astype(jnp.bfloat16)
        term = jnp.dot(onehot, blocks[book], preferred_element_type=jnp.float32)
        total = term if total is None else total + term
    out_ref[...] = total.astype(jnp.bfloat16)


def embed_codes(answered, anchor, rank, code_table, code_width):
    row_count = anchor.shape[0]
    book_count = code_width // FRAMES
    book_size = code_table.shape[0] // book_count
    chan_width = code_table.shape[1]
    rows = FRAMES * row_count
    summed = pl.pallas_call(
        embed_kernel,
        in_specs=[
            pl.BlockSpec(memory_space=pltpu.SMEM),
            pl.BlockSpec(memory_space=pltpu.VMEM),
            pl.BlockSpec(memory_space=pltpu.VMEM),
            pl.BlockSpec(memory_space=pl.ANY),
        ],
        out_specs=pl.BlockSpec(memory_space=pltpu.VMEM),
        out_shape=jax.ShapeDtypeStruct((rows, chan_width), jnp.bfloat16),
        scratch_shapes=[
            pltpu.VMEM((book_count, book_size, chan_width), code_table.dtype),
            pltpu.SemaphoreType.DMA((book_count,)),
            pltpu.VMEM((row_count, answered.shape[-1]), answered.dtype),
        ],
    )(anchor, answered, rank.reshape(-1, 1), code_table)
    return summed.reshape(FRAMES, row_count, chan_width)


def pick_rows(table, index, live):
    entries = jnp.arange(table.shape[0], dtype=jnp.int32)
    select = (index[:, None] == entries[None, :]) & live[:, None]
    if table.dtype == jnp.bfloat16:
        return jnp.dot(
            select.astype(jnp.bfloat16), table, preferred_element_type=jnp.float32
        ).astype(jnp.bfloat16)
    if table.dtype == jnp.int32:
        picked = jnp.dot(
            select.astype(jnp.float32), table.astype(jnp.float32), precision=lax.Precision.HIGHEST
        )
        return picked.astype(jnp.int32)
    return jnp.dot(select.astype(jnp.float32), table, precision=lax.Precision.HIGHEST)


def prefix_count(flags):
    width = flags.shape[-1]
    positions = jnp.arange(width, dtype=jnp.int32)
    upper = (positions[:, None] <= positions[None, :]).astype(jnp.float32)
    return jnp.dot(flags.astype(jnp.float32), upper).astype(jnp.int32)


def compact(flags, ranks, values, slots):
    spots = jnp.arange(slots, dtype=jnp.int32)
    hit = flags[..., None, :] & (ranks[..., None, :] == spots[:, None])
    picked = jnp.sum(jnp.where(hit, values[..., None, :], 0), axis=-1)
    return (picked, jnp.any(hit, axis=-1))


def exchange(items, collective_id):
    groups = lax.axis_size("grp")
    per_group = lax.axis_size("dev")
    count = len(items)
    shapes = []
    for blocks, whole in items:
        if whole:
            shapes.append(jax.ShapeDtypeStruct((groups, per_group) + blocks.shape[1:], blocks.dtype))
        else:
            shapes.append(jax.ShapeDtypeStruct(blocks.shape, blocks.dtype))
    wholes = [index for index, (_, whole) in enumerate(items) if whole]

    def kernel(*refs):
        x_refs = refs[:count]
        o_refs = refs[count : 2 * count]
        mid_refs = dict(zip(wholes, refs[2 * count : 2 * count + len(wholes)]))
        sems = refs[2 * count + len(wholes) :]
        first_send, first_recv, second_send, second_recv, own_sem = sems
        group = lax.axis_index("grp")
        dev = lax.axis_index("dev")
        barrier = pltpu.get_barrier_semaphore()
        across = len(wholes) > 0

        if across:
            def greet_group(offset, carry):
                peer = lax.rem(group + offset, groups)
                pl.semaphore_signal(barrier, inc=1, device_id=(peer, dev), device_id_type=pl.DeviceIdType.MESH)
                return carry

            lax.fori_loop(1, groups, greet_group, 0)

        def greet_dev(offset, carry):
            peer = lax.rem(dev + offset, per_group)
            pl.semaphore_signal(barrier, inc=1, device_id=(group, peer), device_id_type=pl.DeviceIdType.MESH)
            return carry

        lax.fori_loop(1, per_group, greet_dev, 0)
        pl.semaphore_wait(barrier, (groups - 1 if across else 0) + per_group - 1)

        def hop_one(slot, index, peer, place):
            return pltpu.make_async_remote_copy(
                src_ref=x_refs[index].at[pl.ds(peer * per_group, per_group)],
                dst_ref=mid_refs[index].at[place],
                send_sem=first_send.at[slot, peer],
                recv_sem=first_recv.at[slot, place],
                device_id=(peer, dev),
                device_id_type=pl.DeviceIdType.MESH,
            )

        def hop_two(index, peer, place):
            if items[index][1]:
                source = mid_refs[index].at[:, peer]
                target = o_refs[index].at[:, place]
            else:
                source = x_refs[index].at[peer]
                target = o_refs[index].at[place]
            return pltpu.make_async_remote_copy(
                src_ref=source,
                dst_ref=target,
                send_sem=second_send.at[index, peer],
                recv_sem=second_recv.at[index, place],
                device_id=(group, peer),
                device_id_type=pl.DeviceIdType.MESH,
            )

        for slot, index in enumerate(wholes):
            def send_one(offset, carry, slot=slot, index=index):
                hop_one(slot, index, lax.rem(group + offset, groups), group).start()
                return carry

            lax.fori_loop(1, groups, send_one, 0)
        for index, (_, whole) in enumerate(items):
            if not whole:
                def send_group(offset, carry, index=index):
                    hop_two(index, lax.rem(dev + offset, per_group), dev).start()
                    return carry

                lax.fori_loop(1, per_group, send_group, 0)
        for slot, index in enumerate(wholes):
            own = pltpu.make_async_copy(
                x_refs[index].at[pl.ds(group * per_group, per_group)], mid_refs[index].at[group], own_sem
            )
            own.start()
            own.wait()

            def finish_one(offset, carry, slot=slot, index=index):
                hop_one(slot, index, lax.rem(group + offset, groups), group).wait_send()
                source = lax.rem(group + groups - offset, groups)
                hop_one(slot, index, source, source).wait_recv()
                return carry

            lax.fori_loop(1, groups, finish_one, 0)

            def send_two(offset, carry, index=index):
                hop_two(index, lax.rem(dev + offset, per_group), dev).start()
                return carry

            lax.fori_loop(1, per_group, send_two, 0)
        for index, (_, whole) in enumerate(items):
            if whole:
                own = pltpu.make_async_copy(mid_refs[index].at[:, dev], o_refs[index].at[:, dev], own_sem)
            else:
                own = pltpu.make_async_copy(x_refs[index].at[dev], o_refs[index].at[dev], own_sem)
            own.start()
            own.wait()

            def finish_two(offset, carry, index=index):
                hop_two(index, lax.rem(dev + offset, per_group), dev).wait_send()
                source = lax.rem(dev + per_group - offset, per_group)
                hop_two(index, source, source).wait_recv()
                return carry

            lax.fori_loop(1, per_group, finish_two, 0)

    mids = [shapes[index] for index in wholes]
    results = pl.pallas_call(
        kernel,
        out_shape=shapes + mids,
        in_specs=[pl.BlockSpec(memory_space=pl.ANY)] * count,
        out_specs=[pl.BlockSpec(memory_space=pl.ANY)] * (count + len(wholes)),
        scratch_shapes=[
            pltpu.SemaphoreType.DMA((max(len(wholes), 1), groups)),
            pltpu.SemaphoreType.DMA((max(len(wholes), 1), groups)),
            pltpu.SemaphoreType.DMA((count, per_group)),
            pltpu.SemaphoreType.DMA((count, per_group)),
            pltpu.SemaphoreType.DMA(()),
        ],
        compiler_params=pltpu.CompilerParams(collective_id=collective_id, has_side_effects=True),
        cost_estimate=pl.CostEstimate(flops=0, transcendentals=0, bytes_accessed=48 * 1024 * 1024),
    )(*[blocks for blocks, _ in items])
    return [
        result.reshape(blocks.shape) for result, (blocks, _) in zip(results[:count], items)
    ]


def pack_kernel(asked_ref, states_ref, high_ref, low_ref, low_scratch):
    peers = high_ref.shape[0]
    rows, slots, width = states_ref.shape
    lanes = high_ref.shape[2]
    pieces = width // lanes

    def one(peer, carry):
        index = jnp.clip(asked_ref[peer], 0, slots - 1)
        for r in range(rows):
            line = states_ref[r, pl.ds(index, 1), :]
            for k in range(pieces):
                piece = line[:, k * lanes : (k + 1) * lanes]
                if r < 2:
                    high_ref[peer, pl.ds(r * pieces + k, 1), :] = piece
                else:
                    low_scratch[peer, pl.ds((r - 2) * pieces + k, 1), :] = piece
        return carry

    lax.fori_loop(0, peers, one, 0, unroll=8)
    low_ref[...] = low_scratch[...].astype(low_ref.dtype)


def pack_leaving(asked, states_t, lanes):
    peers = asked.shape[0]
    rows, _, width = states_t.shape
    pieces = width // lanes
    return pl.pallas_call(
        pack_kernel,
        in_specs=[pl.BlockSpec(memory_space=pltpu.SMEM), pl.BlockSpec(memory_space=pltpu.VMEM)],
        out_specs=[pl.BlockSpec(memory_space=pltpu.VMEM)] * 2,
        out_shape=[
            jax.ShapeDtypeStruct((peers, 2 * pieces, lanes), states_t.dtype),
            jax.ShapeDtypeStruct((peers, (rows - 2) * pieces, lanes), jnp.bfloat16),
        ],
        scratch_shapes=[pltpu.VMEM((peers, (rows - 2) * pieces, lanes), jnp.float32)],
    )(asked, states_t)


def decode_kernel(
    source_ref, moved_ref,
    routed_ref, states_ref, arrived_ref, arrived_low_ref, up_w_ref, up_b_ref, conv_w_ref, conv_b_ref, in_w_ref, in_b_ref, out_w_ref,
    out_b_ref, decoded_ref, new_ref, carried_ref,
):
    frame_count, slots, _ = routed_ref.shape
    step_count = 2 * frame_count
    rows = states_ref.shape[0]
    conv_taps = conv_w_ref.shape[0]
    res_taps = in_w_ref.shape[0]
    kept = rows - 2 - (res_taps - 1)
    base = pl.program_id(0) * slots

    carried_ref[...] = states_ref[...]

    def bring(slot, carry):
        @pl.when(moved_ref[base + slot] != 0)
        def _():
            source = source_ref[base + slot]
            pieces = carried_ref.shape[2] // arrived_ref.shape[2]
            for r in range(rows):
                if r < 2:
                    row = arrived_ref[source, pl.ds(r * pieces, pieces), :]
                else:
                    row = arrived_low_ref[source, pl.ds((r - 2) * pieces, pieces), :].astype(jnp.float32)
                carried_ref[r, pl.ds(slot, 1), :] = jnp.concatenate(
                    [row[k : k + 1] for k in range(pieces)], axis=1
                )

        return carry

    lax.fori_loop(0, slots, bring, 0, unroll=8)

    def elu(value):
        return jnp.where(value > 0, value, jnp.exp(jnp.minimum(value, 0.0)) - 1.0)

    up_w = up_w_ref[...]
    up_b = up_b_ref[...]
    inputs = [routed_ref[f].astype(jnp.float32) for f in range(frame_count)]
    carried = [carried_ref[r] for r in range(rows)]
    upsampled = []
    for f in range(frame_count):
        early_even = carried[0] if f == 0 else inputs[f - 1] * up_w[2:3]
        early_odd = carried[1] if f == 0 else inputs[f - 1] * up_w[3:4]
        upsampled.append((inputs[f] * up_w[0:1] + early_even) + up_b)
        upsampled.append((inputs[f] * up_w[1:2] + early_odd) + up_b)
    history = jnp.concatenate(
        [c.astype(jnp.bfloat16) for c in carried[2 : 2 + kept]] + [u.astype(jnp.bfloat16) for u in upsampled], axis=0
    )
    conv_out = None
    for tap in range(conv_taps):
        start = (conv_taps - 1 - tap) * slots
        term = jnp.dot(history[start : start + step_count * slots], conv_w_ref[tap], preferred_element_type=jnp.float32)
        conv_out = term if conv_out is None else conv_out + term
    conv_out = conv_out + conv_b_ref[...]
    active = elu(conv_out)
    res_rounded = jnp.concatenate(
        [c.astype(jnp.bfloat16) for c in carried[2 + kept :]] + [active.astype(jnp.bfloat16)], axis=0
    )
    inner = None
    for tap in range(res_taps):
        start = (res_taps - 1 - tap) * slots
        term = jnp.dot(res_rounded[start : start + step_count * slots], in_w_ref[tap], preferred_element_type=jnp.float32)
        inner = term if inner is None else inner + term
    squeezed = elu(inner + in_b_ref[...]).astype(jnp.bfloat16)
    summed = conv_out + jnp.dot(squeezed, out_w_ref[...], preferred_element_type=jnp.float32) + out_b_ref[...]
    decoded = summed.astype(jnp.bfloat16)
    for t in range(step_count):
        decoded_ref[:, t, :] = decoded[t * slots : (t + 1) * slots]
    new_ref[0] = inputs[frame_count - 1] * up_w[2:3]
    new_ref[1] = inputs[frame_count - 1] * up_w[3:4]
    for k in range(kept):
        row = history.shape[0] // slots - kept + k
        new_ref[2 + k] = history[row * slots : (row + 1) * slots].astype(jnp.float32)
    for k in range(res_taps - 1):
        row = step_count - (res_taps - 1) + k
        new_ref[2 + kept + k] = active[row * slots : (row + 1) * slots]


def decode(
    routed, states, arrived, arrived_low, source, moved, up_weight, up_bias, conv_weight, conv_bias, res_in_weight, res_in_bias,
    res_out_weight, res_out_bias,
):
    frame_count, conv_count, chan_width = routed.shape
    rows = states.shape[1]
    chunk = conv_count
    whole = lambda shape: pl.BlockSpec(shape, lambda i, *_: (0,) * len(shape))
    states_t = jnp.transpose(states, (1, 0, 2))
    decoded, new_t = pl.pallas_call(
        decode_kernel,
        grid_spec=pltpu.PrefetchScalarGridSpec(
            num_scalar_prefetch=2,
            grid=(conv_count // chunk,),
            in_specs=[
                pl.BlockSpec((frame_count, chunk, chan_width), lambda i, *_: (0, i, 0)),
                pl.BlockSpec((rows, chunk, chan_width), lambda i, *_: (0, i, 0)),
                whole(arrived.shape),
                whole(arrived_low.shape),
                whole(up_weight.shape),
                whole((1, chan_width)),
                whole(conv_weight.shape),
                whole((1, chan_width)),
                whole(res_in_weight.shape),
                whole((1, res_in_weight.shape[2])),
                whole(res_out_weight.shape),
                whole((1, chan_width)),
            ],
            out_specs=(
                pl.BlockSpec((chunk, 2 * frame_count, chan_width), lambda i, *_: (i, 0, 0)),
                pl.BlockSpec((rows, chunk, chan_width), lambda i, *_: (0, i, 0)),
            ),
            scratch_shapes=[pltpu.VMEM((rows, chunk, chan_width), jnp.float32)],
        ),
        out_shape=(
            jax.ShapeDtypeStruct((conv_count, 2 * frame_count, chan_width), jnp.bfloat16),
            jax.ShapeDtypeStruct((rows, conv_count, chan_width), jnp.float32),
        ),
        compiler_params=pltpu.CompilerParams(vmem_limit_bytes=48 * 1024 * 1024),
    )(
        source, moved, routed, states_t, arrived, arrived_low, up_weight, up_bias.reshape(1, -1), conv_weight,
        conv_bias.reshape(1, -1), res_in_weight, res_in_bias.reshape(1, -1), res_out_weight, res_out_bias.reshape(1, -1),
    )
    return decoded, jnp.transpose(new_t, (1, 0, 2))


def local(
    codes,
    code_table,
    roster,
    old_slot,
    states,
    up_weight,
    up_bias,
    conv_weight,
    conv_bias,
    res_in_weight,
    res_in_bias,
    res_out_weight,
    res_out_bias,
):
    conv_count = roster.shape[0]
    per_group = lax.axis_size("dev")
    devices_all = lax.axis_size("grp") * per_group
    most = MOST
    group_first = lax.axis_index("grp") * per_group
    local_index = lax.axis_index("dev")
    positions = jnp.arange(conv_count, dtype=jnp.int32)
    earlier = positions[None, :] < positions[:, None]

    anchor = roster // conv_count
    row = roster % conv_count
    rank_in = jnp.sum(earlier & (anchor[None, :] == anchor[:, None]), axis=1).astype(jnp.int32)
    key = anchor * most + rank_in
    spots = jnp.arange(devices_all * most, dtype=jnp.int32)
    code_request = jnp.sum(jnp.where(key[None, :] == spots[:, None], row[None, :] + 1, 0), axis=1) - 1
    source_dev = old_slot // conv_count - group_first
    source_row = old_slot % conv_count
    moved = source_dev != local_index
    everyone = jnp.arange(devices_all, dtype=jnp.int32)
    state_request = (
        jnp.sum(
            jnp.where(
                moved[None, :] & (source_dev[None, :] + group_first == everyone[:, None]),
                source_row[None, :] + 1,
                0,
            ),
            axis=1,
        )
        - 1
    )
    request = jnp.concatenate(
        [code_request.reshape(devices_all, most), state_request.reshape(devices_all, 1)], axis=1
    )
    lanes = 128
    padded = jnp.pad(request, ((0, 0), (0, lanes - most - 1))).reshape(devices_all, 1, lanes)
    (asked,) = exchange([(padded, True)], 0)
    asked = asked[:, 0, : most + 1]

    answer = jnp.take(codes, jnp.clip(asked[:, :most].reshape(-1), 0, conv_count - 1), axis=0)
    answer = answer.reshape(devices_all, -1)
    answer = jnp.pad(answer, ((0, 0), (0, lanes - answer.shape[1]))).reshape(devices_all, 1, lanes)
    state_asked = lax.dynamic_slice_in_dim(asked[:, most], group_first, per_group)
    leaving_high, leaving_low = pack_leaving(state_asked, jnp.transpose(states, (1, 0, 2)), lanes)
    answered, arrived, arrived_low = exchange(
        [(answer, True), (leaving_high, False), (leaving_low, False)], 1
    )
    code_width = codes.shape[1]
    routed = embed_codes(answered, anchor, rank_in, code_table, code_width)
    return decode(
        routed,
        states,
        arrived,
        arrived_low,
        jnp.clip(source_dev, 0, per_group - 1),
        moved.astype(jnp.int32),
        up_weight,
        up_bias,
        conv_weight,
        conv_bias,
        res_in_weight,
        res_in_bias,
        res_out_weight,
        res_out_bias,
    )


def solution(mesh):
    in_specs = (
        P(("grp", "dev"), None),
        P(),
        P(("grp", "dev")),
        P(("grp", "dev")),
        P(("grp", "dev"), None, None),
        P(),
        P(),
        P(),
        P(),
        P(),
        P(),
        P(),
        P(),
    )
    out_specs = (P(("grp", "dev"), None, None), P(("grp", "dev"), None, None))
    return jax.shard_map(local, mesh=mesh, in_specs=in_specs, out_specs=out_specs, check_vma=False)
```

```python
import jax
import jax.numpy as jnp
from jax import lax
from jax.experimental import pallas as pl
from jax.experimental.pallas import tpu as pltpu
from jax.sharding import PartitionSpec as P

FRAMES = 4
MOST = 2


def embed_kernel(anchor_ref, answered_ref, rank_ref, table_ref, out_ref, blocks, sems, mine_ref):
    books = blocks.shape[0]
    size = blocks.shape[1]
    slots = rank_ref.shape[0]

    def fetch(book):
        return pltpu.make_async_copy(table_ref.at[pl.ds(book * size, size)], blocks.at[book], sems.at[book])

    for book in range(books):
        fetch(book).start()

    def pick(slot, carry):
        mine_ref[pl.ds(slot, 1), :] = answered_ref[anchor_ref[slot]]
        return carry

    lax.fori_loop(0, slots, pick, 0, unroll=8)
    mine = mine_ref[...]
    width = books * FRAMES
    own = jnp.where(rank_ref[...] == 0, mine[:, :width], mine[:, width : 2 * width])
    by_row = jnp.concatenate([own[:, f * books : (f + 1) * books] for f in range(FRAMES)], axis=0)
    rows = by_row.shape[0]
    total = None
    for book in range(books):
        fetch(book).wait()
        entries = lax.broadcasted_iota(jnp.int32, (rows, size), 1)
        onehot = (by_row[:, book : book + 1] == entries).astype(jnp.bfloat16)
        term = jnp.dot(onehot, blocks[book], preferred_element_type=jnp.float32)
        total = term if total is None else total + term
    out_ref[...] = total.astype(jnp.bfloat16)


def embed_codes(answered, anchor, rank, code_table, code_width):
    row_count = anchor.shape[0]
    book_count = code_width // FRAMES
    book_size = code_table.shape[0] // book_count
    chan_width = code_table.shape[1]
    rows = FRAMES * row_count
    summed = pl.pallas_call(
        embed_kernel,
        in_specs=[
            pl.BlockSpec(memory_space=pltpu.SMEM),
            pl.BlockSpec(memory_space=pltpu.VMEM),
            pl.BlockSpec(memory_space=pltpu.VMEM),
            pl.BlockSpec(memory_space=pl.ANY),
        ],
        out_specs=pl.BlockSpec(memory_space=pltpu.VMEM),
        out_shape=jax.ShapeDtypeStruct((rows, chan_width), jnp.bfloat16),
        scratch_shapes=[
            pltpu.VMEM((book_count, book_size, chan_width), code_table.dtype),
            pltpu.SemaphoreType.DMA((book_count,)),
            pltpu.VMEM((row_count, answered.shape[-1]), answered.dtype),
        ],
    )(anchor, answered, rank.reshape(-1, 1), code_table)
    return summed.reshape(FRAMES, row_count, chan_width)


def pick_rows(table, index, live):
    entries = jnp.arange(table.shape[0], dtype=jnp.int32)
    select = (index[:, None] == entries[None, :]) & live[:, None]
    if table.dtype == jnp.bfloat16:
        return jnp.dot(
            select.astype(jnp.bfloat16), table, preferred_element_type=jnp.float32
        ).astype(jnp.bfloat16)
    if table.dtype == jnp.int32:
        picked = jnp.dot(
            select.astype(jnp.float32), table.astype(jnp.float32), precision=lax.Precision.HIGHEST
        )
        return picked.astype(jnp.int32)
    return jnp.dot(select.astype(jnp.float32), table, precision=lax.Precision.HIGHEST)


def prefix_count(flags):
    width = flags.shape[-1]
    positions = jnp.arange(width, dtype=jnp.int32)
    upper = (positions[:, None] <= positions[None, :]).astype(jnp.float32)
    return jnp.dot(flags.astype(jnp.float32), upper).astype(jnp.int32)


def compact(flags, ranks, values, slots):
    spots = jnp.arange(slots, dtype=jnp.int32)
    hit = flags[..., None, :] & (ranks[..., None, :] == spots[:, None])
    picked = jnp.sum(jnp.where(hit, values[..., None, :], 0), axis=-1)
    return (picked, jnp.any(hit, axis=-1))


def exchange(items, collective_id):
    groups = lax.axis_size("grp")
    per_group = lax.axis_size("dev")
    count = len(items)
    shapes = []
    for blocks, whole in items:
        if whole:
            shapes.append(jax.ShapeDtypeStruct((groups, per_group) + blocks.shape[1:], blocks.dtype))
        else:
            shapes.append(jax.ShapeDtypeStruct(blocks.shape, blocks.dtype))
    wholes = [index for index, (_, whole) in enumerate(items) if whole]

    def kernel(*refs):
        x_refs = refs[:count]
        o_refs = refs[count : 2 * count]
        mid_refs = dict(zip(wholes, refs[2 * count : 2 * count + len(wholes)]))
        sems = refs[2 * count + len(wholes) :]
        first_send, first_recv, second_send, second_recv, own_sem = sems
        group = lax.axis_index("grp")
        dev = lax.axis_index("dev")
        barrier = pltpu.get_barrier_semaphore()
        across = len(wholes) > 0

        if across:
            def greet_group(offset, carry):
                peer = lax.rem(group + offset, groups)
                pl.semaphore_signal(barrier, inc=1, device_id=(peer, dev), device_id_type=pl.DeviceIdType.MESH)
                return carry

            lax.fori_loop(1, groups, greet_group, 0)

        def greet_dev(offset, carry):
            peer = lax.rem(dev + offset, per_group)
            pl.semaphore_signal(barrier, inc=1, device_id=(group, peer), device_id_type=pl.DeviceIdType.MESH)
            return carry

        lax.fori_loop(1, per_group, greet_dev, 0)
        pl.semaphore_wait(barrier, (groups - 1 if across else 0) + per_group - 1)

        def hop_one(slot, index, peer, place):
            return pltpu.make_async_remote_copy(
                src_ref=x_refs[index].at[pl.ds(peer * per_group, per_group)],
                dst_ref=mid_refs[index].at[place],
                send_sem=first_send.at[slot, peer],
                recv_sem=first_recv.at[slot, place],
                device_id=(peer, dev),
                device_id_type=pl.DeviceIdType.MESH,
            )

        def hop_two(index, peer, place):
            if items[index][1]:
                source = mid_refs[index].at[:, peer]
                target = o_refs[index].at[:, place]
            else:
                source = x_refs[index].at[peer]
                target = o_refs[index].at[place]
            return pltpu.make_async_remote_copy(
                src_ref=source,
                dst_ref=target,
                send_sem=second_send.at[index, peer],
                recv_sem=second_recv.at[index, place],
                device_id=(group, peer),
                device_id_type=pl.DeviceIdType.MESH,
            )

        for slot, index in enumerate(wholes):
            def send_one(offset, carry, slot=slot, index=index):
                hop_one(slot, index, lax.rem(group + offset, groups), group).start()
                return carry

            lax.fori_loop(1, groups, send_one, 0)
        for index, (_, whole) in enumerate(items):
            if not whole:
                def send_group(offset, carry, index=index):
                    hop_two(index, lax.rem(dev + offset, per_group), dev).start()
                    return carry

                lax.fori_loop(1, per_group, send_group, 0)
        for slot, index in enumerate(wholes):
            own = pltpu.make_async_copy(
                x_refs[index].at[pl.ds(group * per_group, per_group)], mid_refs[index].at[group], own_sem
            )
            own.start()
            own.wait()

            def finish_one(offset, carry, slot=slot, index=index):
                hop_one(slot, index, lax.rem(group + offset, groups), group).wait_send()
                source = lax.rem(group + groups - offset, groups)
                hop_one(slot, index, source, source).wait_recv()
                return carry

            lax.fori_loop(1, groups, finish_one, 0)

            def send_two(offset, carry, index=index):
                hop_two(index, lax.rem(dev + offset, per_group), dev).start()
                return carry

            lax.fori_loop(1, per_group, send_two, 0)
        for index, (_, whole) in enumerate(items):
            if whole:
                own = pltpu.make_async_copy(mid_refs[index].at[:, dev], o_refs[index].at[:, dev], own_sem)
            else:
                own = pltpu.make_async_copy(x_refs[index].at[dev], o_refs[index].at[dev], own_sem)
            own.start()
            own.wait()

            def finish_two(offset, carry, index=index):
                hop_two(index, lax.rem(dev + offset, per_group), dev).wait_send()
                source = lax.rem(dev + per_group - offset, per_group)
                hop_two(index, source, source).wait_recv()
                return carry

            lax.fori_loop(1, per_group, finish_two, 0)

    mids = [shapes[index] for index in wholes]
    results = pl.pallas_call(
        kernel,
        out_shape=shapes + mids,
        in_specs=[pl.BlockSpec(memory_space=pl.ANY)] * count,
        out_specs=[pl.BlockSpec(memory_space=pl.ANY)] * (count + len(wholes)),
        scratch_shapes=[
            pltpu.SemaphoreType.DMA((max(len(wholes), 1), groups)),
            pltpu.SemaphoreType.DMA((max(len(wholes), 1), groups)),
            pltpu.SemaphoreType.DMA((count, per_group)),
            pltpu.SemaphoreType.DMA((count, per_group)),
            pltpu.SemaphoreType.DMA(()),
        ],
        compiler_params=pltpu.CompilerParams(collective_id=collective_id, has_side_effects=True),
        cost_estimate=pl.CostEstimate(flops=0, transcendentals=0, bytes_accessed=48 * 1024 * 1024),
    )(*[blocks for blocks, _ in items])
    return [
        result.reshape(blocks.shape) for result, (blocks, _) in zip(results[:count], items)
    ]


def pack_kernel(asked_ref, states_ref, high_ref, low_ref, low_scratch):
    peers = high_ref.shape[0]
    rows, slots, width = states_ref.shape
    lanes = high_ref.shape[2]
    pieces = width // lanes

    def one(peer, carry):
        index = jnp.clip(asked_ref[peer], 0, slots - 1)
        for r in range(rows):
            line = states_ref[r, pl.ds(index, 1), :]
            for k in range(pieces):
                piece = line[:, k * lanes : (k + 1) * lanes]
                if r < 2:
                    high_ref[peer, pl.ds(r * pieces + k, 1), :] = piece
                else:
                    low_scratch[peer, pl.ds((r - 2) * pieces + k, 1), :] = piece
        return carry

    lax.fori_loop(0, peers, one, 0)
    low_ref[...] = low_scratch[...].astype(low_ref.dtype)


def pack_leaving(asked, states_t, lanes):
    peers = asked.shape[0]
    rows, _, width = states_t.shape
    pieces = width // lanes
    return pl.pallas_call(
        pack_kernel,
        in_specs=[pl.BlockSpec(memory_space=pltpu.SMEM), pl.BlockSpec(memory_space=pltpu.VMEM)],
        out_specs=[pl.BlockSpec(memory_space=pltpu.VMEM)] * 2,
        out_shape=[
            jax.ShapeDtypeStruct((peers, 2 * pieces, lanes), states_t.dtype),
            jax.ShapeDtypeStruct((peers, (rows - 2) * pieces, lanes), jnp.bfloat16),
        ],
        scratch_shapes=[pltpu.VMEM((peers, (rows - 2) * pieces, lanes), jnp.float32)],
    )(asked, states_t)


def decode_kernel(
    source_ref, moved_ref,
    routed_ref, states_ref, arrived_ref, arrived_low_ref, up_w_ref, up_b_ref, conv_w_ref, conv_b_ref, in_w_ref, in_b_ref, out_w_ref,
    out_b_ref, decoded_ref, new_ref, carried_ref,
):
    frame_count, slots, _ = routed_ref.shape
    step_count = 2 * frame_count
    rows = states_ref.shape[0]
    conv_taps = conv_w_ref.shape[0]
    res_taps = in_w_ref.shape[0]
    kept = rows - 2 - (res_taps - 1)
    base = pl.program_id(0) * slots

    carried_ref[...] = states_ref[...]

    def bring(slot, carry):
        @pl.when(moved_ref[base + slot] != 0)
        def _():
            source = source_ref[base + slot]
            pieces = carried_ref.shape[2] // arrived_ref.shape[2]
            for r in range(rows):
                if r < 2:
                    row = arrived_ref[source, pl.ds(r * pieces, pieces), :]
                else:
                    row = arrived_low_ref[source, pl.ds((r - 2) * pieces, pieces), :].astype(jnp.float32)
                carried_ref[r, pl.ds(slot, 1), :] = jnp.concatenate(
                    [row[k : k + 1] for k in range(pieces)], axis=1
                )

        return carry

    lax.fori_loop(0, slots, bring, 0, unroll=8)

    def elu(value):
        return jnp.where(value > 0, value, jnp.exp(jnp.minimum(value, 0.0)) - 1.0)

    up_w = up_w_ref[...]
    up_b = up_b_ref[...]
    inputs = [routed_ref[f].astype(jnp.float32) for f in range(frame_count)]
    carried = [carried_ref[r] for r in range(rows)]
    upsampled = []
    for f in range(frame_count):
        early_even = carried[0] if f == 0 else inputs[f - 1] * up_w[2:3]
        early_odd = carried[1] if f == 0 else inputs[f - 1] * up_w[3:4]
        upsampled.append((inputs[f] * up_w[0:1] + early_even) + up_b)
        upsampled.append((inputs[f] * up_w[1:2] + early_odd) + up_b)
    history = jnp.concatenate(
        [c.astype(jnp.bfloat16) for c in carried[2 : 2 + kept]] + [u.astype(jnp.bfloat16) for u in upsampled], axis=0
    )
    conv_out = None
    for tap in range(conv_taps):
        start = (conv_taps - 1 - tap) * slots
        term = jnp.dot(history[start : start + step_count * slots], conv_w_ref[tap], preferred_element_type=jnp.float32)
        conv_out = term if conv_out is None else conv_out + term
    conv_out = conv_out + conv_b_ref[...]
    active = elu(conv_out)
    res_rounded = jnp.concatenate(
        [c.astype(jnp.bfloat16) for c in carried[2 + kept :]] + [active.astype(jnp.bfloat16)], axis=0
    )
    inner = None
    for tap in range(res_taps):
        start = (res_taps - 1 - tap) * slots
        term = jnp.dot(res_rounded[start : start + step_count * slots], in_w_ref[tap], preferred_element_type=jnp.float32)
        inner = term if inner is None else inner + term
    squeezed = elu(inner + in_b_ref[...]).astype(jnp.bfloat16)
    summed = conv_out + jnp.dot(squeezed, out_w_ref[...], preferred_element_type=jnp.float32) + out_b_ref[...]
    decoded = summed.astype(jnp.bfloat16)
    for t in range(step_count):
        decoded_ref[:, t, :] = decoded[t * slots : (t + 1) * slots]
    new_ref[0] = inputs[frame_count - 1] * up_w[2:3]
    new_ref[1] = inputs[frame_count - 1] * up_w[3:4]
    for k in range(kept):
        row = history.shape[0] // slots - kept + k
        new_ref[2 + k] = history[row * slots : (row + 1) * slots].astype(jnp.float32)
    for k in range(res_taps - 1):
        row = step_count - (res_taps - 1) + k
        new_ref[2 + kept + k] = active[row * slots : (row + 1) * slots]


def decode(
    routed, states, arrived, arrived_low, source, moved, up_weight, up_bias, conv_weight, conv_bias, res_in_weight, res_in_bias,
    res_out_weight, res_out_bias,
):
    frame_count, conv_count, chan_width = routed.shape
    rows = states.shape[1]
    chunk = conv_count
    whole = lambda shape: pl.BlockSpec(shape, lambda i, *_: (0,) * len(shape))
    states_t = jnp.transpose(states, (1, 0, 2))
    decoded, new_t = pl.pallas_call(
        decode_kernel,
        grid_spec=pltpu.PrefetchScalarGridSpec(
            num_scalar_prefetch=2,
            grid=(conv_count // chunk,),
            in_specs=[
                pl.BlockSpec((frame_count, chunk, chan_width), lambda i, *_: (0, i, 0)),
                pl.BlockSpec((rows, chunk, chan_width), lambda i, *_: (0, i, 0)),
                whole(arrived.shape),
                whole(arrived_low.shape),
                whole(up_weight.shape),
                whole((1, chan_width)),
                whole(conv_weight.shape),
                whole((1, chan_width)),
                whole(res_in_weight.shape),
                whole((1, res_in_weight.shape[2])),
                whole(res_out_weight.shape),
                whole((1, chan_width)),
            ],
            out_specs=(
                pl.BlockSpec((chunk, 2 * frame_count, chan_width), lambda i, *_: (i, 0, 0)),
                pl.BlockSpec((rows, chunk, chan_width), lambda i, *_: (0, i, 0)),
            ),
            scratch_shapes=[pltpu.VMEM((rows, chunk, chan_width), jnp.float32)],
        ),
        out_shape=(
            jax.ShapeDtypeStruct((conv_count, 2 * frame_count, chan_width), jnp.bfloat16),
            jax.ShapeDtypeStruct((rows, conv_count, chan_width), jnp.float32),
        ),
        compiler_params=pltpu.CompilerParams(vmem_limit_bytes=48 * 1024 * 1024),
    )(
        source, moved, routed, states_t, arrived, arrived_low, up_weight, up_bias.reshape(1, -1), conv_weight,
        conv_bias.reshape(1, -1), res_in_weight, res_in_bias.reshape(1, -1), res_out_weight, res_out_bias.reshape(1, -1),
    )
    return decoded, jnp.transpose(new_t, (1, 0, 2))


def local(
    codes,
    code_table,
    roster,
    old_slot,
    states,
    up_weight,
    up_bias,
    conv_weight,
    conv_bias,
    res_in_weight,
    res_in_bias,
    res_out_weight,
    res_out_bias,
):
    conv_count = roster.shape[0]
    per_group = lax.axis_size("dev")
    devices_all = lax.axis_size("grp") * per_group
    most = MOST
    group_first = lax.axis_index("grp") * per_group
    local_index = lax.axis_index("dev")
    positions = jnp.arange(conv_count, dtype=jnp.int32)
    earlier = positions[None, :] < positions[:, None]

    anchor = roster // conv_count
    row = roster % conv_count
    rank_in = jnp.sum(earlier & (anchor[None, :] == anchor[:, None]), axis=1).astype(jnp.int32)
    key = anchor * most + rank_in
    spots = jnp.arange(devices_all * most, dtype=jnp.int32)
    code_request = jnp.sum(jnp.where(key[None, :] == spots[:, None], row[None, :] + 1, 0), axis=1) - 1
    source_dev = old_slot // conv_count - group_first
    source_row = old_slot % conv_count
    moved = source_dev != local_index
    everyone = jnp.arange(devices_all, dtype=jnp.int32)
    state_request = (
        jnp.sum(
            jnp.where(
                moved[None, :] & (source_dev[None, :] + group_first == everyone[:, None]),
                source_row[None, :] + 1,
                0,
            ),
            axis=1,
        )
        - 1
    )
    request = jnp.concatenate(
        [code_request.reshape(devices_all, most), state_request.reshape(devices_all, 1)], axis=1
    )
    lanes = 128
    padded = jnp.pad(request, ((0, 0), (0, lanes - most - 1))).reshape(devices_all, 1, lanes)
    (asked,) = exchange([(padded, True)], 0)
    asked = asked[:, 0, : most + 1]

    answer = jnp.take(codes, jnp.clip(asked[:, :most].reshape(-1), 0, conv_count - 1), axis=0)
    answer = answer.reshape(devices_all, -1)
    answer = jnp.pad(answer, ((0, 0), (0, lanes - answer.shape[1]))).reshape(devices_all, 1, lanes)
    state_asked = lax.dynamic_slice_in_dim(asked[:, most], group_first, per_group)
    leaving_high, leaving_low = pack_leaving(state_asked, jnp.transpose(states, (1, 0, 2)), lanes)
    answered, arrived, arrived_low = exchange(
        [(answer, True), (leaving_high, False), (leaving_low, False)], 1
    )
    code_width = codes.shape[1]
    routed = embed_codes(answered, anchor, rank_in, code_table, code_width)
    return decode(
        routed,
        states,
        arrived,
        arrived_low,
        jnp.clip(source_dev, 0, per_group - 1),
        moved.astype(jnp.int32),
        up_weight,
        up_bias,
        conv_weight,
        conv_bias,
        res_in_weight,
        res_in_bias,
        res_out_weight,
        res_out_bias,
    )


def solution(mesh):
    in_specs = (
        P(("grp", "dev"), None),
        P(),
        P(("grp", "dev")),
        P(("grp", "dev")),
        P(("grp", "dev"), None, None),
        P(),
        P(),
        P(),
        P(),
        P(),
        P(),
        P(),
        P(),
    )
    out_specs = (P(("grp", "dev"), None, None), P(("grp", "dev"), None, None))
    return jax.shard_map(local, mesh=mesh, in_specs=in_specs, out_specs=out_specs, check_vma=False)
```
